32 devices in a mesh: head: 4 (over y, x), seq: 8 (over z, core).
Axes of the slice: x: 2, y: 2, z: 4, core: 2. Of those that a mesh axis runs over, the one named last changes fastest.
Arguments:
- tokens: float32 [8, 1024, 1024], P('seq', 'head'), may hold values from -6 to 6
- patch_counts: int32 [8], P('seq'), may hold values from 256 to 874, as said below
- w_qkv: bfloat16 [1024, 3072], P(('head', 'seq')), may hold values from -0.1875 to 0.1875
- w_out: bfloat16 [1024, 1024], P(('head', 'seq')), may hold values from -3.453125 to 3.453125
- w_up: bfloat16 [1024, 4096], P(('head', 'seq')), may hold values from -0.1875 to 0.1875
- w_down: bfloat16 [4096, 1024], P(('head', 'seq')), may hold values from -0.09375 to 0.09375
- w_patch: bfloat16 [1024, 1024], P(('head', 'seq')), may hold values from -0.1875 to 0.1875
- w_class: bfloat16 [1024, 1024], P(('head', 'seq')), may hold values from -0.1875 to 0.1875
- norm_gains: bfloat16 [2, 1024], P(None, ('head', 'seq')), may hold values from 0.099609375 to 1.8984375
- mask_norm: float32 [2, 150], replicated, may hold values from 0.5 to 1.5
- grad_masks: float32 [8, 1024, 150], P('seq', 'head'), may hold values from -6 to 6
Outputs:
- class_masks: float32 [8, 1024, 150], P('seq', 'head')
- grad_tokens: float32 [8, 1024, 1024], P('seq', 'head')
- grad_w_qkv: float32 [1024, 3072], P(('head', 'seq'))
- grad_w_out: float32 [1024, 1024], P(('head', 'seq'))
- grad_w_up: float32 [1024, 4096], P(('head', 'seq'))
- grad_w_down: float32 [4096, 1024], P(('head', 'seq'))
- grad_w_patch: float32 [1024, 1024], P(('head', 'seq'))
- grad_w_class: float32 [1024, 1024], P(('head', 'seq'))
- grad_norm_gains: float32 [2, 1024], P(None, ('head', 'seq'))
- grad_mask_norm: float32 [2, 150], replicated
The draws below stay inside these ranges and needn't reach their ends.
Inputs may be any that keep to these rules, and one draw needn't show every extreme that they name: An image's slot holds its 150 class rows first, then patch_counts[i] patch rows, then padding; some image has 874 patches and some 1024 // 4.
All inputs are finite; a program needn't handle non-finite values.
Results may differ from the reference program's by a relative error of at most 0.02.
Values may be sent and summed in bfloat16 or wider, within the bound.
A program may use at most 192 MiB of HBM per device.

```python
import jax
import jax.numpy as jnp
from jax import lax

D = 1024
HEADS = 16
DH = 64
FF = 4096
CLS = 150
SLOT = 1024
IMAGES = 8


def draw_patch_counts(key, part):
    lowest = SLOT // 4
    highest = SLOT - CLS
    first_key, second_key = jax.random.split(key)
    values = jax.random.randint(first_key, (IMAGES,), lowest, highest + 1, dtype=jnp.int32)
    ranking = jax.random.permutation(second_key, IMAGES)
    values = values.at[ranking[0]].set(highest)
    values = values.at[ranking[1]].set(lowest)
    return values


def shard_levels(stream_key, dims, shards, least, high):
    level, own = 1.0, jax.random.fold_in(stream_key, 6)
    for axis_at, shards_of in shards:
        heights = jnp.exp(jax.random.uniform(jax.random.fold_in(own, axis_at), (shards_of,), jnp.float32, least / len(shards), high / len(shards)))
        level = level * jnp.repeat(heights, dims[axis_at] // shards_of).reshape([-1 if axis == axis_at else 1 for axis in range(len(dims))])
    return level


def bell_draw(stream_key, extent, scale, most, cuts=(), held_as=jnp.bfloat16):
    drawn = scale * jax.random.normal(stream_key, extent, jnp.float32)
    if cuts:
        drawn = drawn * shard_levels(stream_key, extent, cuts, -0.22, 0.18)
    return jnp.clip(drawn, -most, most).astype(held_as)


def setup_inputs(seed: int = 0) -> dict:
    key_of = jax.random.split(jax.random.key(seed), 12)
    tokens = bell_draw(key_of[0], (IMAGES, SLOT, D), 1.0, 6.0, ((0, 8), (1, 4)), jnp.float32)
    patch_counts = draw_patch_counts(jax.random.fold_in(key_of[11], 71), 0)
    w_qkv = bell_draw(key_of[2], (D, 3 * D), D ** -0.5, 0.1875, ((0, 32),))
    w_out = bell_draw(key_of[3], (D, D), ((SLOT // 3) ** 0.5 * D ** -0.5), 3.453125, ((0, 32),))
    w_up = bell_draw(key_of[4], (D, FF), D ** -0.5, 0.1875, ((0, 32),))
    w_down = bell_draw(key_of[5], (FF, D), FF ** -0.5, 0.09375, ((0, 32),))
    w_patch = bell_draw(key_of[6], (D, D), D ** -0.5, 0.1875, ((0, 32),))
    w_class = bell_draw(key_of[7], (D, D), D ** -0.5, 0.1875, ((0, 32),))
    norm_gains = jnp.clip(1.0 + 0.18 * jax.random.normal(key_of[8], (2, D), jnp.float32), 0.099609375, 1.8984375).astype(jnp.bfloat16)
    mask_norm = jnp.clip(jax.random.uniform(key_of[9], (2, CLS), jnp.float32, 0.5, 1.5), 0.5, 1.5)
    grad_masks = bell_draw(key_of[10], (IMAGES, SLOT, CLS), 1.0, 6.0, ((0, 8), (1, 4)), jnp.float32)
    return {"tokens": tokens, "patch_counts": patch_counts, "w_qkv": w_qkv, "w_out": w_out, "w_up": w_up, "w_down": w_down, "w_patch": w_patch, "w_class": w_class, "norm_gains": norm_gains, "mask_norm": mask_norm, "grad_masks": grad_masks}


@jax.custom_vjp
def low(v):
    return lax.optimization_barrier(v.astype(jnp.bfloat16)).astype(jnp.float32)

@jax.custom_vjp
def low_back(v):
    return v

def low_keep(v):
    return (low(v), None)

def low_pass(kept, grad):
    return (grad,)

def back_keep(v):
    return (v, None)

def back_low(kept, grad):
    return (low(grad),)
low.defvjp(low_keep, low_pass)
low_back.defvjp(back_keep, back_low)

def matmul(left, right):
    return jnp.dot(left, right, precision=lax.Precision.HIGHEST, preferred_element_type=jnp.float32)

def layer_norm(values, scaling):
    center = values - lax.optimization_barrier(jnp.mean(values, axis=-1, keepdims=True))
    spread = lax.optimization_barrier(jnp.mean(center * center, axis=-1, keepdims=True))
    return center * lax.rsqrt(spread + 1e-05) * scaling

def unit_rows(values):
    return values * lax.rsqrt(lax.optimization_barrier(jnp.sum(values * values, axis=-1, keepdims=True)) + 1e-06)

def image_layer(inputs, patches, qkv_weight, out_weight, up_weight, down_weight, patch_weight, class_weight, gain_pair, mask_pair):
    position = jnp.arange(SLOT, dtype=jnp.int32)
    live_keys = position < CLS + patches
    patch_rows = (position >= CLS) & live_keys
    normed = low(layer_norm(inputs, gain_pair[0]))
    triple = low_back(low(matmul(normed, qkv_weight))).reshape(SLOT, HEADS, 3, DH)
    queries = triple[:, :, 0]
    key_rows = triple[:, :, 1]
    values = triple[:, :, 2]
    scaling = DH ** (-0.5)
    block_rows = 512 if SLOT % 512 == 0 else SLOT

    def attend(query_block):
        scores = jnp.einsum('qhd,khd->hqk', query_block, key_rows, precision=lax.Precision.HIGHEST)
        scores = low_back(scores * scaling)
        scores = jnp.where(live_keys[None, None, :], scores, -1e+30)
        weights = jax.nn.softmax(scores, axis=-1)
        return jnp.einsum('hqk,khd->qhd', low(weights), values, precision=lax.Precision.HIGHEST)
    mixed = lax.map(jax.checkpoint(attend), queries.reshape(SLOT // block_rows, block_rows, HEADS, DH))
    mixed = low_back(low(mixed.reshape(SLOT, D)))
    second = inputs + low_back(matmul(mixed, out_weight))
    normed_two = low(layer_norm(second, gain_pair[1]))
    hidden = low_back(matmul(normed_two, up_weight))
    active = low(jax.nn.gelu(hidden, approximate=False))
    residual = second + low_back(matmul(active, down_weight))
    rounded = low(residual)
    patch_unit = low(unit_rows(low_back(matmul(rounded, patch_weight))))
    class_unit = low(unit_rows(low_back(matmul(rounded[:CLS], class_weight))))
    products = low_back(matmul(patch_unit, class_unit.T))
    mask_out = layer_norm(products, mask_pair[0]) + mask_pair[1]
    return jnp.where(patch_rows[:, None], mask_out, 0.0)

def reference(tokens, patch_counts, w_qkv, w_out, w_up, w_down, w_patch, w_class, norm_gains, mask_norm, grad_masks):

    def forward(inputs, qkv_weight, out_weight, up_weight, down_weight, patch_weight, class_weight, gain_pair, mask_pair):

        def scan_step(running, image_item):
            return (running, image_layer(image_item[0], image_item[1], qkv_weight, out_weight, up_weight, down_weight, patch_weight, class_weight, gain_pair, mask_pair))
        unused, mask_out = lax.scan(scan_step, jnp.zeros((), jnp.float32), (inputs, patch_counts))
        return mask_out
    class_masks, pullback = jax.vjp(forward, tokens, w_qkv.astype(jnp.float32), w_out.astype(jnp.float32), w_up.astype(jnp.float32), w_down.astype(jnp.float32), w_patch.astype(jnp.float32), w_class.astype(jnp.float32), norm_gains.astype(jnp.float32), mask_norm)
    gradients = pullback(grad_masks)
    return (class_masks, gradients[0], gradients[1], gradients[2], gradients[3], gradients[4], gradients[5], gradients[6], gradients[7], gradients[8])
```

```python
from functools import partial

import jax
import jax.numpy as jnp
from jax import lax
from jax.experimental import pallas as pl
from jax.experimental.pallas import tpu as pltpu
from jax.sharding import PartitionSpec as P

HEADS = 16
DH = 64
CLS = 150


def spread_2(value, axis, source):
    kept = jnp.where(lax.axis_index(axis) == source, value, 0).astype(value.dtype)
    return lax.psum(kept, axis)


def standardize(values):
    center = values - jnp.mean(values, axis=-1, keepdims=True)
    inverse = lax.rsqrt(jnp.mean(center * center, axis=-1, keepdims=True) + 1e-05)
    return (center * inverse, inverse)


def standard_back(normal, inverse, upstream):
    middle = jnp.mean(upstream, axis=-1, keepdims=True)
    along = jnp.mean(upstream * normal, axis=-1, keepdims=True)
    return inverse * (upstream - middle - normal * along)


def unit_scale(values):
    return lax.rsqrt(jnp.sum(values * values, axis=-1, keepdims=True) + 1e-06)


def unit_back(values, upstream):
    factor = unit_scale(values)
    direct = values * factor
    return factor * (upstream - direct * jnp.sum(upstream * direct, axis=-1, keepdims=True))


def block_scores(query_block, key_rows, key_live, scaling):
    scores = (
        jnp.einsum("qd,kd->qk", query_block, key_rows, preferred_element_type=jnp.float32) * scaling
    )
    return jnp.where(key_live, scores, -1e30)


def attend_head(queries, key_rows, values, key_live, scaling, blocks):
    head_width = queries.shape[-1]

    def single(query_block):
        scores = block_scores(query_block, key_rows, key_live, scaling)
        highest = jnp.max(scores, axis=-1, keepdims=True)
        weights_raw = jnp.exp(scores - highest)
        totals = jnp.sum(weights_raw, axis=-1, keepdims=True)
        weights = (weights_raw / totals).astype(jnp.bfloat16)
        output = jnp.einsum("qk,kd->qd", weights, values, preferred_element_type=jnp.float32)
        return (output.astype(jnp.bfloat16), (highest + jnp.log(totals))[:, 0])

    outputs, logsum = lax.map(single, queries.reshape(blocks, -1, head_width))
    return (outputs.reshape(-1, head_width), logsum.reshape(-1))


def attend_back(queries, key_rows, values, grad_out, logsum, key_live, scaling, blocks):
    head_width = queries.shape[-1]

    def single(running, pieces):
        grad_keys, grad_values = running
        query_block, grad_block, logsum_block = pieces
        scores = block_scores(query_block, key_rows, key_live, scaling)
        weights = jnp.exp(scores - logsum_block[:, None])
        grad_values = grad_values + jnp.einsum(
            "qk,qd->kd",
            weights.astype(jnp.bfloat16),
            grad_block,
            preferred_element_type=jnp.float32,
        )
        grad_weights = jnp.einsum(
            "qd,kd->qk", grad_block, values, preferred_element_type=jnp.float32
        )
        deltas = jnp.sum(grad_weights * weights, axis=-1, keepdims=True)
        grad_scores = (weights * (grad_weights - deltas)).astype(jnp.bfloat16)
        grad_query = (
            jnp.einsum("qk,kd->qd", grad_scores, key_rows, preferred_element_type=jnp.float32)
            * scaling
        )
        grad_keys = (
            grad_keys
            + jnp.einsum("qk,qd->kd", grad_scores, query_block, preferred_element_type=jnp.float32)
            * scaling
        )
        return ((grad_keys, grad_values), grad_query)

    zero_state = jnp.zeros(key_rows.shape, jnp.float32)
    pieces = (
        queries.reshape(blocks, -1, head_width),
        grad_out.reshape(blocks, -1, head_width),
        logsum.reshape(blocks, -1),
    )
    (grad_keys, grad_values), grad_queries = lax.scan(single, (zero_state, zero_state), pieces)
    return (grad_queries.reshape(-1, head_width), grad_keys, grad_values)


def body_general(
    tokens,
    patch_counts,
    w_qkv,
    w_out,
    w_up,
    w_down,
    w_patch,
    w_class,
    norm_gains,
    mask_norm,
    grad_masks,
):
    gains_rows = norm_gains.T
    gathered = (
        lax.all_gather(w_qkv, ("head", "seq"), axis=0, tiled=True),
        lax.all_gather(w_out, ("head", "seq"), axis=0, tiled=True),
        lax.all_gather(w_up, ("head", "seq"), axis=0, tiled=True),
        lax.all_gather(w_down, ("head", "seq"), axis=0, tiled=True),
        lax.all_gather(w_patch, ("head", "seq"), axis=0, tiled=True),
        lax.all_gather(w_class, ("head", "seq"), axis=0, tiled=True),
        lax.all_gather(gains_rows, ("head", "seq"), axis=0, tiled=True),
    )
    full_qkv, full_out, full_up, full_down, full_patch, full_class, full_gains = gathered
    gain_one = full_gains[:, 0].astype(jnp.float32)
    gain_two = full_gains[:, 1].astype(jnp.float32)
    image_count = tokens.shape[0]
    row_count = tokens.shape[1]
    groups = lax.axis_size("head")
    slot_rows = row_count * groups
    local_heads = HEADS // groups
    position = lax.axis_index("head") * row_count + jnp.arange(row_count, dtype=jnp.int32)
    live_limit = CLS + patch_counts
    patch_rows = ((position[None, :] >= CLS) & (position[None, :] < live_limit[:, None])).astype(
        jnp.float32
    )[:, :, None]
    key_live = (jnp.arange(slot_rows, dtype=jnp.int32)[None, :] < live_limit[:, None])[:, None, :]
    root_flag = (lax.axis_index("head") == 0).astype(jnp.float32)
    scaling = DH ** (-0.5)
    blocks = slot_rows // 512
    normal_one, inverse_one = standardize(tokens)
    normed_one = (normal_one * gain_one).astype(jnp.bfloat16)
    triple = jnp.einsum(
        "ird,dt->irt", normed_one, full_qkv, preferred_element_type=jnp.float32
    ).astype(jnp.bfloat16)
    spread = lax.all_to_all(triple, "head", split_axis=2, concat_axis=1, tiled=True).reshape(
        image_count, slot_rows, local_heads, 3, DH
    )
    image = 0
    outputs = []
    image_logsums = []
    for number in range(local_heads):
        output, logsum = attend_head(
            spread[image, :, number, 0],
            spread[image, :, number, 1],
            spread[image, :, number, 2],
            key_live[image],
            scaling,
            blocks,
        )
        outputs.append(output)
        image_logsums.append(logsum)
    image_outputs = [jnp.stack(outputs, axis=1).reshape(slot_rows, local_heads * DH)]
    logsums = [image_logsums]
    attended_heads = jnp.stack(image_outputs, axis=0)
    attended = lax.all_to_all(attended_heads, "head", split_axis=1, concat_axis=2, tiled=True)
    second = tokens + jnp.einsum(
        "ire,ed->ird", attended, full_out, preferred_element_type=jnp.float32
    )
    normal_two, inverse_two = standardize(second)
    normed_two = (normal_two * gain_two).astype(jnp.bfloat16)
    hidden = jnp.einsum("ird,df->irf", normed_two, full_up, preferred_element_type=jnp.float32)
    gelu_exact = partial(jax.nn.gelu, approximate=False)
    active = gelu_exact(hidden).astype(jnp.bfloat16)
    residual = second + jnp.einsum(
        "irf,fd->ird", active, full_down, preferred_element_type=jnp.float32
    )
    rounded = residual.astype(jnp.bfloat16)
    patch_proj = jnp.einsum("ird,de->ire", rounded, full_patch, preferred_element_type=jnp.float32)
    patch_unit = (patch_proj * unit_scale(patch_proj)).astype(jnp.bfloat16)
    class_proj = jnp.einsum(
        "ird,de->ire", rounded[:, :CLS], full_class, preferred_element_type=jnp.float32
    )
    class_unit = (class_proj * unit_scale(class_proj)).astype(jnp.bfloat16)
    classes = spread_2(class_unit, "head", 0)
    products = jnp.einsum("ird,icd->irc", patch_unit, classes, preferred_element_type=jnp.float32)
    normal_mask, inverse_mask = standardize(products)
    class_masks = (normal_mask * mask_norm[0] + mask_norm[1]) * patch_rows
    upstream = grad_masks * patch_rows
    norm_grads = lax.psum(
        jnp.stack([jnp.sum(upstream * normal_mask, axis=(0, 1)), jnp.sum(upstream, axis=(0, 1))]),
        ("head", "seq"),
    )
    d_products = standard_back(normal_mask, inverse_mask, upstream * mask_norm[0]).astype(
        jnp.bfloat16
    )
    d_patch_unit = jnp.einsum(
        "irc,icd->ird", d_products, classes, preferred_element_type=jnp.float32
    )
    class_part = jnp.einsum(
        "irc,ird->icd", d_products, patch_unit, preferred_element_type=jnp.float32
    )
    d_class_unit = lax.psum(class_part.astype(jnp.bfloat16), "head").astype(jnp.float32)
    d_patch_proj = unit_back(patch_proj, d_patch_unit).astype(jnp.bfloat16)
    d_class_proj = (unit_back(class_proj, d_class_unit) * root_flag).astype(jnp.bfloat16)
    regathered = (
        lax.all_gather(w_qkv, ("head", "seq"), axis=0, tiled=True),
        lax.all_gather(w_out, ("head", "seq"), axis=0, tiled=True),
        lax.all_gather(w_up, ("head", "seq"), axis=0, tiled=True),
        lax.all_gather(w_down, ("head", "seq"), axis=0, tiled=True),
        lax.all_gather(w_patch, ("head", "seq"), axis=0, tiled=True),
        lax.all_gather(w_class, ("head", "seq"), axis=0, tiled=True),
        lax.all_gather(gains_rows, ("head", "seq"), axis=0, tiled=True),
    )
    back_qkv, back_out, back_up, back_down, back_patch, back_class, back_gains = regathered
    back_one = back_gains[:, 0].astype(jnp.float32)
    back_two = back_gains[:, 1].astype(jnp.float32)
    grad_patch = jnp.einsum(
        "ird,ire->de", rounded, d_patch_proj, preferred_element_type=jnp.float32
    )
    grad_class = jnp.einsum(
        "ird,ire->de", rounded[:, :CLS], d_class_proj, preferred_element_type=jnp.float32
    )
    d_residual = jnp.einsum(
        "ire,de->ird", d_patch_proj, back_patch, preferred_element_type=jnp.float32
    )
    class_term = jnp.einsum(
        "ire,de->ird", d_class_proj, back_class, preferred_element_type=jnp.float32
    )
    d_residual = d_residual.at[:, :CLS].add(class_term)
    d_branch = d_residual.astype(jnp.bfloat16)
    grad_down = jnp.einsum("irf,ird->fd", active, d_branch, preferred_element_type=jnp.float32)
    d_active = jnp.einsum("ird,fd->irf", d_branch, back_down, preferred_element_type=jnp.float32)
    gelu_pull = jax.vjp(gelu_exact, hidden)[1]
    d_hidden = gelu_pull(d_active)[0].astype(jnp.bfloat16)
    grad_up = jnp.einsum("ird,irf->df", normed_two, d_hidden, preferred_element_type=jnp.float32)
    d_normed_two = jnp.einsum("irf,df->ird", d_hidden, back_up, preferred_element_type=jnp.float32)
    d_second = d_residual + standard_back(normal_two, inverse_two, d_normed_two * back_two)
    grad_gain_two = jnp.sum(d_normed_two * normal_two, axis=(0, 1))
    d_mix = d_second.astype(jnp.bfloat16)
    grad_out = jnp.einsum("ire,ird->ed", attended, d_mix, preferred_element_type=jnp.float32)
    d_attended = jnp.einsum(
        "ird,ed->ire", d_mix, back_out, preferred_element_type=jnp.float32
    ).astype(jnp.bfloat16)
    d_heads = lax.all_to_all(d_attended, "head", split_axis=2, concat_axis=1, tiled=True).reshape(
        image_count, slot_rows, local_heads, DH
    )
    image = 0
    head_grads = []
    for number in range(local_heads):
        grad_queries, grad_keys, grad_values = attend_back(
            spread[image, :, number, 0],
            spread[image, :, number, 1],
            spread[image, :, number, 2],
            d_heads[image, :, number],
            logsums[image][number],
            key_live[image],
            scaling,
            blocks,
        )
        head_grads.append(jnp.stack([grad_queries, grad_keys, grad_values], axis=1))
    image_grads = [jnp.stack(head_grads, axis=1).reshape(slot_rows, local_heads * 3 * DH)]
    d_spread = jnp.stack(image_grads, axis=0).astype(jnp.bfloat16)
    d_triple = lax.all_to_all(d_spread, "head", split_axis=1, concat_axis=2, tiled=True)
    grad_qkv = jnp.einsum("ird,irt->dt", normed_one, d_triple, preferred_element_type=jnp.float32)
    d_normed_one = jnp.einsum("irt,dt->ird", d_triple, back_qkv, preferred_element_type=jnp.float32)
    grad_inputs = d_second + standard_back(normal_one, inverse_one, d_normed_one * back_one)
    grad_gain_one = jnp.sum(d_normed_one * normal_one, axis=(0, 1))
    grad_gains = jnp.stack([grad_gain_one, grad_gain_two], axis=1)
    reduced = (
        lax.psum_scatter(grad_qkv, ("head", "seq"), scatter_dimension=0, tiled=True),
        lax.psum_scatter(grad_out, ("head", "seq"), scatter_dimension=0, tiled=True),
        lax.psum_scatter(grad_up, ("head", "seq"), scatter_dimension=0, tiled=True),
        lax.psum_scatter(grad_down, ("head", "seq"), scatter_dimension=0, tiled=True),
        lax.psum_scatter(grad_patch, ("head", "seq"), scatter_dimension=0, tiled=True),
        lax.psum_scatter(grad_class, ("head", "seq"), scatter_dimension=0, tiled=True),
        lax.psum_scatter(grad_gains, ("head", "seq"), scatter_dimension=0, tiled=True),
    )
    return (
        class_masks,
        grad_inputs,
        reduced[0],
        reduced[1],
        reduced[2],
        reduced[3],
        reduced[4],
        reduced[5],
        reduced[6].T,
        norm_grads,
    )


MESH = pl.DeviceIdType.MESH
LOG2E = 1.4426950408889634


def place():
    h = lax.axis_index("head")
    s = lax.axis_index("seq")
    return h // 2, h % 2, s // 2, s % 2


def device(y, x, z, c):
    return (y * 2 + x, z * 2 + c)


def greet(peers):
    barrier = pltpu.get_barrier_semaphore()
    for peer in peers:
        pl.semaphore_signal(barrier, inc=1, device_id=peer, device_id_type=MESH)
    pl.semaphore_wait(barrier, len(peers))


class Copies:
    def __init__(self, send_sem, recv_sem):
        self.send_sem, self.recv_sem, self.made = send_sem, recv_sem, []

    def start(self, source, target, peer):
        number = len(self.made)
        copy = pltpu.make_async_remote_copy(
            src_ref=source,
            dst_ref=target,
            send_sem=self.send_sem.at[number],
            recv_sem=self.recv_sem.at[number],
            device_id=peer,
            device_id_type=MESH,
        )
        copy.start()
        self.made.append(copy)
        return copy

    def drain(self):
        for copy in self.made:
            copy.wait_send()


def gather_kernel(names, *refs):
    count = len(names)
    shards, fulls = refs[:count], refs[count : 2 * count]
    send_sem, recv_sem, local_sem = refs[2 * count :]
    y, x, z, c = place()
    sibling, x_peer, y_peer = device(y, x, z, 1 - c), device(y, 1 - x, z, c), device(1 - y, x, z, c)
    z_peers = [device(y, x, (z + k) % 4, c) for k in (1, 2, 3)]
    greet([sibling, x_peer, y_peer] + z_peers)
    copies = Copies(send_sem, recv_sem)
    state = []
    for number in range(count):
        shard, full = shards[number], fulls[number]
        rows = shard.shape[0]
        own = pltpu.make_async_copy(shard, full.at[y, x, z, c], local_sem.at[number])
        own.start()
        entry = {"own": own, "first": []}
        if names[number] == "zfirst":
            for low, high in ((0, rows // 2), (rows // 2, rows)):
                part = full.at[y, x, z, c, low:high]
                entry["first"].append([copies.start(shard.at[low:high], part, peer) for peer in z_peers])
        else:
            entry["first"].append([copies.start(shard, full.at[y, x, z, c], x_peer)])
        state.append(entry)

    def second(number):
        entry, full = state[number], fulls[number]
        rows = shards[number].shape[0]
        half = rows // 2
        entry["own"].wait()
        for copy in entry["first"][0]:
            copy.wait_recv()
        if names[number] == "zfirst":
            piece = full.at[y, x, :, c, 0:half]
            entry["a"] = copies.start(piece, piece, x_peer)
            for copy in entry["first"][1]:
                copy.wait_recv()
            piece = full.at[y, x, :, c, half:rows]
            entry["b"] = copies.start(piece, piece, y_peer)
        else:
            piece = full.at[y, :, z, c]
            entry["a"] = copies.start(piece, piece, y_peer)

    def third(number):
        entry, full = state[number], fulls[number]
        rows = shards[number].shape[0]
        half = rows // 2
        entry["a"].wait_recv()
        if names[number] == "zfirst":
            piece = full.at[y, :, :, c, 0:half]
            entry["c"] = [copies.start(piece, piece, y_peer)]
            entry["b"].wait_recv()
            piece = full.at[:, x, :, c, half:rows]
            entry["c"].append(copies.start(piece, piece, x_peer))
        else:
            piece = full.at[:, :, z, c]
            entry["c"] = [copies.start(piece, piece, peer) for peer in z_peers]

    def fourth(number):
        entry, full = state[number], fulls[number]
        for copy in entry["c"]:
            copy.wait_recv()
        piece = full.at[:, :, :, c]
        entry["d"] = copies.start(piece, piece, sibling)

    stages = (second, third, fourth)
    for step in range(count + len(stages) - 1):
        for lag, stage in enumerate(stages):
            if 0 <= step - lag < count:
                stage(step - lag)
    for entry in state:
        entry["d"].wait_recv()
    copies.drain()


def gather_all(shards, orders):
    total = sum(11 if order == "zfirst" else 6 for order in orders)
    return pl.pallas_call(
        partial(gather_kernel, orders),
        out_shape=[jax.ShapeDtypeStruct((2, 2, 4, 2) + a.shape, a.dtype) for a in shards],
        in_specs=[pl.BlockSpec(memory_space=pl.ANY)] * len(shards),
        out_specs=[pl.BlockSpec(memory_space=pl.ANY)] * len(shards),
        scratch_shapes=[
            pltpu.SemaphoreType.DMA((total,)),
            pltpu.SemaphoreType.DMA((total,)),
            pltpu.SemaphoreType.DMA((len(shards),)),
        ],
        compiler_params=pltpu.CompilerParams(collective_id=1, has_side_effects=True),
        name="gather_all",
    )(*shards)


def reduce_kernel(orders, *refs):
    count = len(orders)
    partials, outs = refs[:count], refs[count : 2 * count]
    small_ref, small_out = refs[2 * count], refs[2 * count + 1]
    at = 2 * count + 2
    own, sib, one, two, three = [refs[at + i * count : at + (i + 1) * count] for i in range(5)]
    at += 5 * count
    small_own, small_got, send_sem, recv_sem, local_sem = refs[at:]
    y, x, z, c = place()
    sibling, x_peer, y_peer = device(y, x, z, 1 - c), device(y, 1 - x, z, c), device(1 - y, x, z, c)
    z_peers = [device(y, x, (z + k) % 4, c) for k in (1, 2, 3)]
    greet([sibling, x_peer, y_peer] + z_peers)
    copies = Copies(send_sem, recv_sem)
    state = []
    for number in range(count):
        local = pltpu.make_async_copy(
            partials[number].at[:, :, :, c], own[number], local_sem.at[number]
        )
        local.start()
        state.append(
            {"local": local, "s": copies.start(partials[number].at[:, :, :, 1 - c], sib[number], sibling)}
        )

    def add_in(total, extra, where, shards):
        def body(i, carry):
            index = where(i)
            total[index] = total[index] + extra(i)
            return carry

        lax.fori_loop(0, shards, body, 0)

    def first(number):
        entry, total, got = state[number], own[number], sib[number]
        rows = total.shape[3]
        half = rows // 2
        entry["local"].wait()
        entry["s"].wait_recv()
        add_in(total, lambda i: got[i // 8, i // 4 % 2, i % 4], lambda i: (i // 8, i // 4 % 2, i % 4), 16)
        if orders[number] == "zlast":
            entry["a"] = copies.start(
                total.at[1 - y, :, :, 0:half], one[number].at[0], y_peer
            )
            entry["b"] = copies.start(
                total.at[:, 1 - x, :, half:rows], one[number].at[1], x_peer
            )
        else:
            entry["a"] = [
                copies.start(total.at[:, :, (z + k) % 4], one[number].at[k - 1], z_peers[k - 1])
                for k in (1, 2, 3)
            ]

    def second(number):
        entry, total, got = state[number], own[number], one[number]
        rows = total.shape[3]
        half = rows // 2
        if orders[number] == "zlast":
            entry["a"].wait_recv()
            add_in(
                total,
                lambda i: got[0, i // 4, i % 4],
                lambda i: (y, i // 4, i % 4, slice(0, half)),
                8,
            )
            entry["c"] = copies.start(total.at[y, 1 - x, :, 0:half], two[number].at[0], x_peer)
            entry["b"].wait_recv()
            add_in(
                total,
                lambda i: got[1, i // 4, i % 4],
                lambda i: (i // 4, x, i % 4, slice(half, rows)),
                8,
            )
            entry["d"] = copies.start(total.at[1 - y, x, :, half:rows], two[number].at[1], y_peer)
        else:
            for copy in entry["a"]:
                copy.wait_recv()
            add_in(
                total,
                lambda i: got[0, i // 2, i % 2] + got[1, i // 2, i % 2] + got[2, i // 2, i % 2],
                lambda i: (i // 2, i % 2, z),
                4,
            )
            entry["c"] = copies.start(total.at[1 - y, :, z], two[number], y_peer)

    def third(number):
        entry, total, got = state[number], own[number], two[number]
        rows = total.shape[3]
        half = rows // 2
        entry["c"].wait_recv()
        if orders[number] == "zlast":
            add_in(total, lambda i: got[0, i], lambda i: (y, x, i, slice(0, half)), 4)
            entry["d"].wait_recv()
            add_in(total, lambda i: got[1, i], lambda i: (y, x, i, slice(half, rows)), 4)
            entry["e"] = [
                copies.start(total.at[y, x, (z + k) % 4], three[number].at[k - 1], z_peers[k - 1])
                for k in (1, 2, 3)
            ]
        else:
            add_in(total, lambda i: got[i], lambda i: (y, i, z), 2)
            entry["e"] = [copies.start(total.at[y, 1 - x, z], three[number], x_peer)]

    def fourth(number):
        entry, total, got, out = state[number], own[number], three[number], outs[number]
        for copy in entry["e"]:
            copy.wait_recv()
        value = total[y, x, z].astype(jnp.float32)
        if orders[number] == "zlast":
            for k in range(3):
                value = value + got[k].astype(jnp.float32)
        else:
            value = value + got[...].astype(jnp.float32)
        out[...] = value

    def small(step):
        if step == 0:
            small_own[...] = small_ref[...]
        elif step < 4:
            copies_small[-1].wait()
            small_own[...] = small_own[...] + small_got[step - 1]
        peer = (sibling, x_peer, y_peer)[step] if step < 3 else None
        if peer is not None:
            copy = pltpu.make_async_remote_copy(
                src_ref=small_own,
                dst_ref=small_got.at[step],
                send_sem=send_sem.at[total_copies + step],
                recv_sem=recv_sem.at[total_copies + step],
                device_id=peer,
                device_id_type=MESH,
            )
            copy.start()
            copies_small.append(copy)
        else:
            small_got[3 + z] = small_own[...]
            for k in (1, 2, 3):
                copy = pltpu.make_async_remote_copy(
                    src_ref=small_own,
                    dst_ref=small_got.at[3 + z],
                    send_sem=send_sem.at[total_copies + 2 + k],
                    recv_sem=recv_sem.at[total_copies + 2 + k],
                    device_id=z_peers[k - 1],
                    device_id_type=MESH,
                )
                copy.start()
                copies_small.append(copy)

    total_copies = copies_of(orders, 9, 6)
    copies_small = []
    stages = (first, second, third, fourth)
    for step in range(count + len(stages) - 1):
        for lag, stage in enumerate(stages):
            if 0 <= step - lag < count:
                stage(step - lag)
        if step < 4:
            small(step)
    for copy in copies_small[3:]:
        copy.wait()
    small_out[...] = small_got[3] + small_got[4] + small_got[5] + small_got[6]
    copies.drain()


def copies_of(orders, zlast, zfirst):
    return sum(zlast if order == "zlast" else zfirst for order in orders)


def reduce_all(partials, orders, small):
    count = len(partials)
    shapes = [a.shape[4:] for a in partials]

    def scratch(first, other):
        return [
            pltpu.VMEM((first(r) if o == "zlast" else other(r)) + (n,), jnp.bfloat16)
            for o, (r, n) in zip(orders, shapes)
        ]

    total = copies_of(orders, 9, 6) + 6
    vmem = pl.BlockSpec(memory_space=pltpu.VMEM)
    return pl.pallas_call(
        partial(reduce_wrap, orders),
        out_shape=[jax.ShapeDtypeStruct(shape, jnp.float32) for shape in shapes]
        + [jax.ShapeDtypeStruct(small.shape, jnp.float32)],
        in_specs=[pl.BlockSpec(memory_space=pl.ANY)] * count + [vmem],
        out_specs=[vmem] * (count + 1),
        scratch_shapes=scratch(lambda r: (2, 2, 4, r), lambda r: (2, 2, 4, r))
        + scratch(lambda r: (2, 2, 4, r), lambda r: (2, 2, 4, r))
        + scratch(lambda r: (2, 2, 4, r // 2), lambda r: (3, 2, 2, r))
        + scratch(lambda r: (2, 4, r // 2), lambda r: (2, r))
        + scratch(lambda r: (3, r), lambda r: (r,))
        + [
            pltpu.VMEM(small.shape, jnp.float32),
            pltpu.VMEM((7,) + small.shape, jnp.float32),
            pltpu.SemaphoreType.DMA((total,)),
            pltpu.SemaphoreType.DMA((total,)),
            pltpu.SemaphoreType.DMA((count,)),
        ],
        compiler_params=pltpu.CompilerParams(
            collective_id=2, has_side_effects=True, vmem_limit_bytes=60 * 2**20
        ),
        name="reduce_all",
    )(*partials, small)


def reduce_wrap(orders, *refs):
    count = len(orders)
    partials, small_ref = refs[:count], refs[count]
    outs, small_out = refs[count + 1 : 2 * count + 1], refs[2 * count + 1]
    reduce_kernel(orders, *partials, *outs, small_ref, small_out, *refs[2 * count + 2 :])


def plane_peer(h, rel):
    return h + (rel % 2) * (1 - 2 * (h % 2)) + (rel // 2) * (2 - 4 * (h // 2))


def attend_kernel(scaling, live_ref, triple, out, spread, logsum, staged, send_sem, recv_sem, local_sem):
    h, s = lax.axis_index("head"), lax.axis_index("seq")
    rows, slot_rows = triple.shape[0], spread.shape[0]
    wide = spread.shape[1]
    narrow = staged.shape[1]
    heads = narrow // DH
    greet([(plane_peer(h, rel), s) for rel in (1, 2, 3)])

    def into(rel):
        peer = plane_peer(h, rel)
        return pltpu.make_async_remote_copy(
            src_ref=triple.at[:, pl.ds(pl.multiple_of(peer * wide, 128), wide)],
            dst_ref=spread.at[pl.ds(pl.multiple_of(h * rows, rows), rows), :],
            send_sem=send_sem.at[rel - 1],
            recv_sem=recv_sem.at[rel - 1],
            device_id=(peer, s),
            device_id_type=MESH,
        )

    def back(rel):
        peer = plane_peer(h, rel)
        return pltpu.make_async_remote_copy(
            src_ref=staged.at[pl.ds(pl.multiple_of(peer * rows, rows), rows), :],
            dst_ref=out.at[:, pl.ds(pl.multiple_of(h * narrow, 128), narrow)],
            send_sem=send_sem.at[2 + rel],
            recv_sem=recv_sem.at[2 + rel],
            device_id=(peer, s),
            device_id_type=MESH,
        )

    moved = [into(rel) for rel in (3, 1, 2)]
    for copy in moved:
        copy.start()
    own = pltpu.make_async_copy(
        triple.at[:, pl.ds(pl.multiple_of(h * wide, 128), wide)],
        spread.at[pl.ds(pl.multiple_of(h * rows, rows), rows), :],
        local_sem,
    )
    own.start()
    own.wait()
    for copy in moved:
        copy.wait()
    live = live_ref[0]
    key_live = lax.broadcasted_iota(jnp.int32, (slot_rows, 1), 0) < live

    def block(turn, carry):
        rel = 3 - turn
        peer = plane_peer(h, rel)
        at = pl.ds(pl.multiple_of(peer * rows, rows), rows)
        for number in range(heads):
            base = number * 3 * DH
            queries = spread[at, base : base + DH]
            keys = spread[:, base + DH : base + 2 * DH]
            values = spread[:, base + 2 * DH : base + 3 * DH]
            scores = lax.dot_general(
                keys, queries, (((1,), (1,)), ((), ())), preferred_element_type=jnp.float32
            )
            scores = jnp.where(key_live, scores * (scaling * LOG2E), -1e30)
            highest = jnp.max(scores, axis=0, keepdims=True)
            raw = jnp.exp2(scores - highest)
            totals = jnp.sum(raw, axis=0, keepdims=True)
            weights = (raw * (1.0 / totals)).astype(jnp.bfloat16)
            mixed = lax.dot_general(
                values, weights, (((0,), (0,)), ((), ())), preferred_element_type=jnp.float32
            )
            staged[at, number * DH : (number + 1) * DH] = mixed.T.astype(jnp.bfloat16)
            logsum[number, at] = (highest + jnp.log2(totals))[0]

        @pl.when(rel > 0)
        def _():
            back(rel).start()

        return carry

    lax.fori_loop(0, 4, block, 0)
    own = pltpu.make_async_copy(
        staged.at[pl.ds(pl.multiple_of(h * rows, rows), rows), :],
        out.at[:, pl.ds(pl.multiple_of(h * narrow, 128), narrow)],
        local_sem,
    )
    own.start()
    own.wait()
    for rel in (3, 2, 1):
        back(rel).wait()


def attend(live, triple, scaling):
    rows, width = triple.shape
    slot_rows, wide = rows * 4, width // 4
    vmem = pl.BlockSpec(memory_space=pltpu.VMEM)
    return pl.pallas_call(
        partial(attend_kernel, scaling),
        out_shape=[
            jax.ShapeDtypeStruct((rows, width // 3), jnp.bfloat16),
            jax.ShapeDtypeStruct((slot_rows, wide), jnp.bfloat16),
            jax.ShapeDtypeStruct((8, slot_rows), jnp.float32),
        ],
        in_specs=[pl.BlockSpec(memory_space=pltpu.SMEM), vmem],
        out_specs=[vmem] * 3,
        scratch_shapes=[
            pltpu.VMEM((slot_rows, wide // 3), jnp.bfloat16),
            pltpu.SemaphoreType.DMA((6,)),
            pltpu.SemaphoreType.DMA((6,)),
            pltpu.SemaphoreType.DMA,
        ],
        compiler_params=pltpu.CompilerParams(
            collective_id=3, has_side_effects=True, vmem_limit_bytes=48 * 2**20
        ),
        name="attend",
    )(live, triple)


def attend_back_kernel(
    scaling, live_ref, d_rows, spread, logsum, d_triple, d_out, d_spread, grad_keys, grad_values, send_sem, recv_sem, local_sem
):
    h, s = lax.axis_index("head"), lax.axis_index("seq")
    rows, slot_rows = d_rows.shape[0], spread.shape[0]
    wide = spread.shape[1]
    narrow = d_out.shape[1]
    heads = narrow // DH
    greet([(plane_peer(h, rel), s) for rel in (1, 2, 3)])

    def into(rel):
        peer = plane_peer(h, rel)
        return pltpu.make_async_remote_copy(
            src_ref=d_rows.at[:, pl.ds(pl.multiple_of(peer * narrow, 128), narrow)],
            dst_ref=d_out.at[pl.ds(pl.multiple_of(h * rows, rows), rows), :],
            send_sem=send_sem.at[rel - 1],
            recv_sem=recv_sem.at[rel - 1],
            device_id=(peer, s),
            device_id_type=MESH,
        )

    def back(rel):
        peer = plane_peer(h, rel)
        return pltpu.make_async_remote_copy(
            src_ref=d_spread.at[pl.ds(pl.multiple_of(peer * rows, rows), rows), :],
            dst_ref=d_triple.at[:, pl.ds(pl.multiple_of(h * wide, 128), wide)],
            send_sem=send_sem.at[2 + rel],
            recv_sem=recv_sem.at[2 + rel],
            device_id=(peer, s),
            device_id_type=MESH,
        )

    moved = [into(rel) for rel in (3, 1, 2)]
    for copy in moved:
        copy.start()
    own = pltpu.make_async_copy(
        d_rows.at[:, pl.ds(pl.multiple_of(h * narrow, 128), narrow)],
        d_out.at[pl.ds(pl.multiple_of(h * rows, rows), rows), :],
        local_sem,
    )
    own.start()
    own.wait()
    for copy in moved:
        copy.wait()
    live = live_ref[0]
    key_live = lax.broadcasted_iota(jnp.int32, (slot_rows, 1), 0) < live

    for number in range(heads):
        base = number * 3 * DH
        grad_keys[...] = jnp.zeros_like(grad_keys)
        grad_values[...] = jnp.zeros_like(grad_values)

        def block(turn, carry, number=number, base=base):
            at = pl.ds(pl.multiple_of(turn * rows, rows), rows)
            queries = spread[at, base : base + DH]
            keys = spread[:, base + DH : base + 2 * DH]
            values = spread[:, base + 2 * DH : base + 3 * DH]
            grads = d_out[at, number * DH : (number + 1) * DH]
            scores = lax.dot_general(
                keys, queries, (((1,), (1,)), ((), ())), preferred_element_type=jnp.float32
            )
            powers = scores * (scaling * LOG2E) - logsum[number, at][None, :]
            weights = jnp.where(key_live, jnp.exp2(powers), 0.0)
            grad_values[...] += jnp.dot(
                weights.astype(jnp.bfloat16), grads, preferred_element_type=jnp.float32
            )
            grad_weights = lax.dot_general(
                values, grads, (((1,), (1,)), ((), ())), preferred_element_type=jnp.float32
            )
            deltas = jnp.sum(grad_weights * weights, axis=0, keepdims=True)
            grad_scores = (weights * (grad_weights - deltas)).astype(jnp.bfloat16)
            grad_keys[...] += jnp.dot(grad_scores, queries, preferred_element_type=jnp.float32)
            grad_queries = lax.dot_general(
                keys, grad_scores, (((0,), (0,)), ((), ())), preferred_element_type=jnp.float32
            )
            d_spread[at, base : base + DH] = (grad_queries.T * scaling).astype(jnp.bfloat16)
            return carry

        lax.fori_loop(0, 4, block, 0)
        d_spread[:, base + DH : base + 2 * DH] = (grad_keys[...] * scaling).astype(jnp.bfloat16)
        d_spread[:, base + 2 * DH : base + 3 * DH] = grad_values[...].astype(jnp.bfloat16)
    returned = [back(rel) for rel in (3, 1, 2)]
    for copy in returned:
        copy.start()
    own = pltpu.make_async_copy(
        d_spread.at[pl.ds(pl.multiple_of(h * rows, rows), rows), :],
        d_triple.at[:, pl.ds(pl.multiple_of(h * wide, 128), wide)],
        local_sem,
    )
    own.start()
    own.wait()
    for copy in returned:
        copy.wait()


def attend_backward(live, d_rows, spread, logsum, scaling):
    rows, features = d_rows.shape
    slot_rows, wide = spread.shape
    vmem = pl.BlockSpec(memory_space=pltpu.VMEM)
    return pl.pallas_call(
        partial(attend_back_kernel, scaling),
        out_shape=jax.ShapeDtypeStruct((rows, 3 * features), jnp.bfloat16),
        in_specs=[pl.BlockSpec(memory_space=pltpu.SMEM), vmem, vmem, vmem],
        out_specs=vmem,
        scratch_shapes=[
            pltpu.VMEM((slot_rows, wide // 3), jnp.bfloat16),
            pltpu.VMEM((slot_rows, wide), jnp.bfloat16),
            pltpu.VMEM((slot_rows, DH), jnp.float32),
            pltpu.VMEM((slot_rows, DH), jnp.float32),
            pltpu.SemaphoreType.DMA((6,)),
            pltpu.SemaphoreType.DMA((6,)),
            pltpu.SemaphoreType.DMA,
        ],
        compiler_params=pltpu.CompilerParams(
            collective_id=4, has_side_effects=True, vmem_limit_bytes=48 * 2**20
        ),
        name="attend_back",
    )(live, d_rows, spread, logsum)


def hop(value, pairs):
    return lax.ppermute(value, "head", pairs)


def matmul(left, right):
    return jnp.dot(left, right, preferred_element_type=jnp.float32)


def matmul_nt(left, right):
    return lax.dot_general(left, right, (((1,), (1,)), ((), ())), preferred_element_type=jnp.float32)


def matmul_tn(left, right):
    return lax.dot_general(left, right, (((0,), (0,)), ((), ())), preferred_element_type=jnp.float32)


def body_planned(
    tokens,
    patch_counts,
    w_qkv,
    w_out,
    w_up,
    w_down,
    w_patch,
    w_class,
    norm_gains,
    mask_norm,
    grad_masks,
):
    gain_tile = jnp.pad(norm_gains, ((0, 14), (0, 96)))
    orders = ("zfirst", "zfirst", "xfirst", "zfirst", "zfirst", "zfirst", "xfirst")
    shards = (gain_tile, w_qkv, w_out, w_up, w_down, w_patch, w_class)
    fulls = gather_all(shards, orders)
    full_gains = fulls[0].reshape(32, 16, 128)[:, :2, :32].transpose(1, 0, 2).reshape(2, 1024)
    full_qkv, full_out, full_up, full_down, full_patch, full_class = [
        a.reshape(-1, a.shape[-1]) for a in fulls[1:]
    ]
    gain_one = full_gains[0].astype(jnp.float32)
    gain_two = full_gains[1].astype(jnp.float32)
    tokens, grad_masks = tokens[0], grad_masks[0]
    row_count = tokens.shape[0]
    h = lax.axis_index("head")
    position = h * row_count + jnp.arange(row_count, dtype=jnp.int32)
    live = CLS + patch_counts
    patch_rows = ((position >= CLS) & (position < live[0])).astype(jnp.float32)[:, None]
    root_flag = (h == 0).astype(jnp.float32)
    scaling = DH ** (-0.5)

    normal_one, inverse_one = standardize(tokens)
    normed_one = (normal_one * gain_one).astype(jnp.bfloat16)
    triple = matmul(normed_one, full_qkv).astype(jnp.bfloat16)
    attended, spread, logsum = attend(live, triple, scaling)
    second = tokens + matmul(attended, full_out)
    normal_two, inverse_two = standardize(second)
    normed_two = (normal_two * gain_two).astype(jnp.bfloat16)
    hidden = matmul(normed_two, full_up)
    gelu_exact = partial(jax.nn.gelu, approximate=False)
    active = gelu_exact(hidden).astype(jnp.bfloat16)
    residual = second + matmul(active, full_down)
    rounded = residual.astype(jnp.bfloat16)
    class_rows = rounded[:CLS]
    class_proj = matmul(class_rows, full_class)
    class_unit = (class_proj * unit_scale(class_proj)).astype(jnp.bfloat16)
    arrived = [hop(class_unit, [(0, rel)]) for rel in (1, 2, 3)]
    patch_proj = matmul(rounded, full_patch)
    patch_unit = (patch_proj * unit_scale(patch_proj)).astype(jnp.bfloat16)
    classes = jnp.where(h == 0, class_unit, arrived[0] + arrived[1] + arrived[2])
    products = matmul_nt(patch_unit, classes)
    normal_mask, inverse_mask = standardize(products)
    class_masks = (normal_mask * mask_norm[0] + mask_norm[1]) * patch_rows
    upstream = grad_masks * patch_rows
    mask_sums = jnp.stack([jnp.sum(upstream * normal_mask, axis=0), jnp.sum(upstream, axis=0)])
    d_products = standard_back(normal_mask, inverse_mask, upstream * mask_norm[0]).astype(jnp.bfloat16)
    class_part = matmul_tn(d_products, patch_unit)
    class_sent = class_part.astype(jnp.bfloat16)
    parts = [hop(class_sent, [(rel, 0)]) for rel in (1, 2, 3)]
    d_patch_unit = matmul(d_products, classes)
    d_patch_proj = unit_back(patch_proj, d_patch_unit).astype(jnp.bfloat16)
    d_class_unit = class_part + (
        parts[0].astype(jnp.float32) + parts[1].astype(jnp.float32) + parts[2].astype(jnp.float32)
    )
    d_class_proj = (unit_back(class_proj, d_class_unit) * root_flag).astype(jnp.bfloat16)
    grad_patch = matmul_tn(rounded, d_patch_proj).astype(jnp.bfloat16)
    grad_class = matmul_tn(class_rows, d_class_proj).astype(jnp.bfloat16)
    d_residual = matmul_nt(d_patch_proj, full_patch)
    d_residual = d_residual.at[:CLS].add(matmul_nt(d_class_proj, full_class))
    d_branch = d_residual.astype(jnp.bfloat16)
    grad_down = matmul_tn(active, d_branch).astype(jnp.bfloat16)
    d_active = matmul_nt(d_branch, full_down)
    d_hidden = jax.vjp(gelu_exact, hidden)[1](d_active)[0].astype(jnp.bfloat16)
    grad_up = matmul_tn(normed_two, d_hidden).astype(jnp.bfloat16)
    d_normed_two = matmul_nt(d_hidden, full_up)
    d_second = d_residual + standard_back(normal_two, inverse_two, d_normed_two * gain_two)
    grad_gain_two = jnp.sum(d_normed_two * normal_two, axis=0)
    d_mix = d_second.astype(jnp.bfloat16)
    grad_out = matmul_tn(attended, d_mix).astype(jnp.bfloat16)
    d_attended = matmul_nt(d_mix, full_out).astype(jnp.bfloat16)
    d_triple = attend_backward(live, d_attended, spread, logsum, scaling)
    grad_qkv = matmul_tn(normed_one, d_triple).astype(jnp.bfloat16)
    d_normed_one = matmul_nt(d_triple, full_qkv)
    grad_inputs = d_second + standard_back(normal_one, inverse_one, d_normed_one * gain_one)
    grad_gain_one = jnp.sum(d_normed_one * normal_one, axis=0)
    small = jnp.concatenate(
        [jnp.stack([grad_gain_one, grad_gain_two]), jnp.pad(mask_sums, ((0, 0), (0, 1024 - CLS)))]
    )
    partials = [
        a.reshape(2, 2, 4, 2, a.shape[0] // 32, a.shape[1])
        for a in (grad_qkv, grad_out, grad_up, grad_down, grad_patch, grad_class)
    ]
    reduced = reduce_all(
        partials, ("zlast", "zfirst", "zlast", "zlast", "zlast", "zfirst"), small
    )
    sums = reduced[6]
    place_at = (h * 8 + lax.axis_index("seq")) * 32
    grad_gains = lax.dynamic_slice(sums, (0, place_at), (2, 32))
    return (
        class_masks[None],
        grad_inputs[None],
        *reduced[:6],
        grad_gains,
        sums[2:4, :CLS],
    )


def solution(mesh):
    planned = dict(mesh.shape) == {"head": 4, "seq": 8}
    return jax.shard_map(
        body_planned if planned else body_general,
        mesh=mesh,
        in_specs=(
            P("seq", "head", None),
            P("seq"),
            P(("head", "seq"), None),
            P(("head", "seq"), None),
            P(("head", "seq"), None),
            P(("head", "seq"), None),
            P(("head", "seq"), None),
            P(("head", "seq"), None),
            P(None, ("head", "seq")),
            P(),
            P("seq", "head", None),
        ),
        out_specs=(
            P("seq", "head", None),
            P("seq", "head", None),
            P(("head", "seq"), None),
            P(("head", "seq"), None),
            P(("head", "seq"), None),
            P(("head", "seq"), None),
            P(("head", "seq"), None),
            P(("head", "seq"), None),
            P(None, ("head", "seq")),
            P(),
        ),
        check_vma=False,
    )
```

```python
from functools import partial

import jax
import jax.numpy as jnp
from jax import lax
from jax.experimental import pallas as pl
from jax.experimental.pallas import tpu as pltpu
from jax.sharding import PartitionSpec as P

HEADS = 16
DH = 64
CLS = 150


def spread_2(value, axis, source):
    kept = jnp.where(lax.axis_index(axis) == source, value, 0).astype(value.dtype)
    return lax.psum(kept, axis)


def standardize(values):
    center = values - jnp.mean(values, axis=-1, keepdims=True)
    inverse = lax.rsqrt(jnp.mean(center * center, axis=-1, keepdims=True) + 1e-05)
    return (center * inverse, inverse)


def standard_back(normal, inverse, upstream):
    middle = jnp.mean(upstream, axis=-1, keepdims=True)
    along = jnp.mean(upstream * normal, axis=-1, keepdims=True)
    return inverse * (upstream - middle - normal * along)


def unit_scale(values):
    return lax.rsqrt(jnp.sum(values * values, axis=-1, keepdims=True) + 1e-06)


def unit_back(values, upstream):
    factor = unit_scale(values)
    direct = values * factor
    return factor * (upstream - direct * jnp.sum(upstream * direct, axis=-1, keepdims=True))


def block_scores(query_block, key_rows, key_live, scaling):
    scores = (
        jnp.einsum("qd,kd->qk", query_block, key_rows, preferred_element_type=jnp.float32) * scaling
    )
    return jnp.where(key_live, scores, -1e30)


def attend_head(queries, key_rows, values, key_live, scaling, blocks):
    head_width = queries.shape[-1]

    def single(query_block):
        scores = block_scores(query_block, key_rows, key_live, scaling)
        highest = jnp.max(scores, axis=-1, keepdims=True)
        weights_raw = jnp.exp(scores - highest)
        totals = jnp.sum(weights_raw, axis=-1, keepdims=True)
        weights = (weights_raw / totals).astype(jnp.bfloat16)
        output = jnp.einsum("qk,kd->qd", weights, values, preferred_element_type=jnp.float32)
        return (output.astype(jnp.bfloat16), (highest + jnp.log(totals))[:, 0])

    outputs, logsum = lax.map(single, queries.reshape(blocks, -1, head_width))
    return (outputs.reshape(-1, head_width), logsum.reshape(-1))


def attend_back(queries, key_rows, values, grad_out, logsum, key_live, scaling, blocks):
    head_width = queries.shape[-1]

    def single(running, pieces):
        grad_keys, grad_values = running
        query_block, grad_block, logsum_block = pieces
        scores = block_scores(query_block, key_rows, key_live, scaling)
        weights = jnp.exp(scores - logsum_block[:, None])
        grad_values = grad_values + jnp.einsum(
            "qk,qd->kd",
            weights.astype(jnp.bfloat16),
            grad_block,
            preferred_element_type=jnp.float32,
        )
        grad_weights = jnp.einsum(
            "qd,kd->qk", grad_block, values, preferred_element_type=jnp.float32
        )
        deltas = jnp.sum(grad_weights * weights, axis=-1, keepdims=True)
        grad_scores = (weights * (grad_weights - deltas)).astype(jnp.bfloat16)
        grad_query = (
            jnp.einsum("qk,kd->qd", grad_scores, key_rows, preferred_element_type=jnp.float32)
            * scaling
        )
        grad_keys = (
            grad_keys
            + jnp.einsum("qk,qd->kd", grad_scores, query_block, preferred_element_type=jnp.float32)
            * scaling
        )
        return ((grad_keys, grad_values), grad_query)

    zero_state = jnp.zeros(key_rows.shape, jnp.float32)
    pieces = (
        queries.reshape(blocks, -1, head_width),
        grad_out.reshape(blocks, -1, head_width),
        logsum.reshape(blocks, -1),
    )
    (grad_keys, grad_values), grad_queries = lax.scan(single, (zero_state, zero_state), pieces)
    return (grad_queries.reshape(-1, head_width), grad_keys, grad_values)


def body_general(
    tokens,
    patch_counts,
    w_qkv,
    w_out,
    w_up,
    w_down,
    w_patch,
    w_class,
    norm_gains,
    mask_norm,
    grad_masks,
):
    gains_rows = norm_gains.T
    gathered = (
        lax.all_gather(w_qkv, ("head", "seq"), axis=0, tiled=True),
        lax.all_gather(w_out, ("head", "seq"), axis=0, tiled=True),
        lax.all_gather(w_up, ("head", "seq"), axis=0, tiled=True),
        lax.all_gather(w_down, ("head", "seq"), axis=0, tiled=True),
        lax.all_gather(w_patch, ("head", "seq"), axis=0, tiled=True),
        lax.all_gather(w_class, ("head", "seq"), axis=0, tiled=True),
        lax.all_gather(gains_rows, ("head", "seq"), axis=0, tiled=True),
    )
    full_qkv, full_out, full_up, full_down, full_patch, full_class, full_gains = gathered
    gain_one = full_gains[:, 0].astype(jnp.float32)
    gain_two = full_gains[:, 1].astype(jnp.float32)
    image_count = tokens.shape[0]
    row_count = tokens.shape[1]
    groups = lax.axis_size("head")
    slot_rows = row_count * groups
    local_heads = HEADS // groups
    position = lax.axis_index("head") * row_count + jnp.arange(row_count, dtype=jnp.int32)
    live_limit = CLS + patch_counts
    patch_rows = ((position[None, :] >= CLS) & (position[None, :] < live_limit[:, None])).astype(
        jnp.float32
    )[:, :, None]
    key_live = (jnp.arange(slot_rows, dtype=jnp.int32)[None, :] < live_limit[:, None])[:, None, :]
    root_flag = (lax.axis_index("head") == 0).astype(jnp.float32)
    scaling = DH ** (-0.5)
    blocks = slot_rows // 512
    normal_one, inverse_one = standardize(tokens)
    normed_one = (normal_one * gain_one).astype(jnp.bfloat16)
    triple = jnp.einsum(
        "ird,dt->irt", normed_one, full_qkv, preferred_element_type=jnp.float32
    ).astype(jnp.bfloat16)
    spread = lax.all_to_all(triple, "head", split_axis=2, concat_axis=1, tiled=True).reshape(
        image_count, slot_rows, local_heads, 3, DH
    )
    image = 0
    outputs = []
    image_logsums = []
    for number in range(local_heads):
        output, logsum = attend_head(
            spread[image, :, number, 0],
            spread[image, :, number, 1],
            spread[image, :, number, 2],
            key_live[image],
            scaling,
            blocks,
        )
        outputs.append(output)
        image_logsums.append(logsum)
    image_outputs = [jnp.stack(outputs, axis=1).reshape(slot_rows, local_heads * DH)]
    logsums = [image_logsums]
    attended_heads = jnp.stack(image_outputs, axis=0)
    attended = lax.all_to_all(attended_heads, "head", split_axis=1, concat_axis=2, tiled=True)
    second = tokens + jnp.einsum(
        "ire,ed->ird", attended, full_out, preferred_element_type=jnp.float32
    )
    normal_two, inverse_two = standardize(second)
    normed_two = (normal_two * gain_two).astype(jnp.bfloat16)
    hidden = jnp.einsum("ird,df->irf", normed_two, full_up, preferred_element_type=jnp.float32)
    gelu_exact = partial(jax.nn.gelu, approximate=False)
    active = gelu_exact(hidden).astype(jnp.bfloat16)
    residual = second + jnp.einsum(
        "irf,fd->ird", active, full_down, preferred_element_type=jnp.float32
    )
    rounded = residual.astype(jnp.bfloat16)
    patch_proj = jnp.einsum("ird,de->ire", rounded, full_patch, preferred_element_type=jnp.float32)
    patch_unit = (patch_proj * unit_scale(patch_proj)).astype(jnp.bfloat16)
    class_proj = jnp.einsum(
        "ird,de->ire", rounded[:, :CLS], full_class, preferred_element_type=jnp.float32
    )
    class_unit = (class_proj * unit_scale(class_proj)).astype(jnp.bfloat16)
    classes = spread_2(class_unit, "head", 0)
    products = jnp.einsum("ird,icd->irc", patch_unit, classes, preferred_element_type=jnp.float32)
    normal_mask, inverse_mask = standardize(products)
    class_masks = (normal_mask * mask_norm[0] + mask_norm[1]) * patch_rows
    upstream = grad_masks * patch_rows
    norm_grads = lax.psum(
        jnp.stack([jnp.sum(upstream * normal_mask, axis=(0, 1)), jnp.sum(upstream, axis=(0, 1))]),
        ("head", "seq"),
    )
    d_products = standard_back(normal_mask, inverse_mask, upstream * mask_norm[0]).astype(
        jnp.bfloat16
    )
    d_patch_unit = jnp.einsum(
        "irc,icd->ird", d_products, classes, preferred_element_type=jnp.float32
    )
    class_part = jnp.einsum(
        "irc,ird->icd", d_products, patch_unit, preferred_element_type=jnp.float32
    )
    d_class_unit = lax.psum(class_part.astype(jnp.bfloat16), "head").astype(jnp.float32)
    d_patch_proj = unit_back(patch_proj, d_patch_unit).astype(jnp.bfloat16)
    d_class_proj = (unit_back(class_proj, d_class_unit) * root_flag).astype(jnp.bfloat16)
    regathered = (
        lax.all_gather(w_qkv, ("head", "seq"), axis=0, tiled=True),
        lax.all_gather(w_out, ("head", "seq"), axis=0, tiled=True),
        lax.all_gather(w_up, ("head", "seq"), axis=0, tiled=True),
        lax.all_gather(w_down, ("head", "seq"), axis=0, tiled=True),
        lax.all_gather(w_patch, ("head", "seq"), axis=0, tiled=True),
        lax.all_gather(w_class, ("head", "seq"), axis=0, tiled=True),
        lax.all_gather(gains_rows, ("head", "seq"), axis=0, tiled=True),
    )
    back_qkv, back_out, back_up, back_down, back_patch, back_class, back_gains = regathered
    back_one = back_gains[:, 0].astype(jnp.float32)
    back_two = back_gains[:, 1].astype(jnp.float32)
    grad_patch = jnp.einsum(
        "ird,ire->de", rounded, d_patch_proj, preferred_element_type=jnp.float32
    )
    grad_class = jnp.einsum(
        "ird,ire->de", rounded[:, :CLS], d_class_proj, preferred_element_type=jnp.float32
    )
    d_residual = jnp.einsum(
        "ire,de->ird", d_patch_proj, back_patch, preferred_element_type=jnp.float32
    )
    class_term = jnp.einsum(
        "ire,de->ird", d_class_proj, back_class, preferred_element_type=jnp.float32
    )
    d_residual = d_residual.at[:, :CLS].add(class_term)
    d_branch = d_residual.astype(jnp.bfloat16)
    grad_down = jnp.einsum("irf,ird->fd", active, d_branch, preferred_element_type=jnp.float32)
    d_active = jnp.einsum("ird,fd->irf", d_branch, back_down, preferred_element_type=jnp.float32)
    gelu_pull = jax.vjp(gelu_exact, hidden)[1]
    d_hidden = gelu_pull(d_active)[0].astype(jnp.bfloat16)
    grad_up = jnp.einsum("ird,irf->df", normed_two, d_hidden, preferred_element_type=jnp.float32)
    d_normed_two = jnp.einsum("irf,df->ird", d_hidden, back_up, preferred_element_type=jnp.float32)
    d_second = d_residual + standard_back(normal_two, inverse_two, d_normed_two * back_two)
    grad_gain_two = jnp.sum(d_normed_two * normal_two, axis=(0, 1))
    d_mix = d_second.astype(jnp.bfloat16)
    grad_out = jnp.einsum("ire,ird->ed", attended, d_mix, preferred_element_type=jnp.float32)
    d_attended = jnp.einsum(
        "ird,ed->ire", d_mix, back_out, preferred_element_type=jnp.float32
    ).astype(jnp.bfloat16)
    d_heads = lax.all_to_all(d_attended, "head", split_axis=2, concat_axis=1, tiled=True).reshape(
        image_count, slot_rows, local_heads, DH
    )
    image = 0
    head_grads = []
    for number in range(local_heads):
        grad_queries, grad_keys, grad_values = attend_back(
            spread[image, :, number, 0],
            spread[image, :, number, 1],
            spread[image, :, number, 2],
            d_heads[image, :, number],
            logsums[image][number],
            key_live[image],
            scaling,
            blocks,
        )
        head_grads.append(jnp.stack([grad_queries, grad_keys, grad_values], axis=1))
    image_grads = [jnp.stack(head_grads, axis=1).reshape(slot_rows, local_heads * 3 * DH)]
    d_spread = jnp.stack(image_grads, axis=0).astype(jnp.bfloat16)
    d_triple = lax.all_to_all(d_spread, "head", split_axis=1, concat_axis=2, tiled=True)
    grad_qkv = jnp.einsum("ird,irt->dt", normed_one, d_triple, preferred_element_type=jnp.float32)
    d_normed_one = jnp.einsum("irt,dt->ird", d_triple, back_qkv, preferred_element_type=jnp.float32)
    grad_inputs = d_second + standard_back(normal_one, inverse_one, d_normed_one * back_one)
    grad_gain_one = jnp.sum(d_normed_one * normal_one, axis=(0, 1))
    grad_gains = jnp.stack([grad_gain_one, grad_gain_two], axis=1)
    reduced = (
        lax.psum_scatter(grad_qkv, ("head", "seq"), scatter_dimension=0, tiled=True),
        lax.psum_scatter(grad_out, ("head", "seq"), scatter_dimension=0, tiled=True),
        lax.psum_scatter(grad_up, ("head", "seq"), scatter_dimension=0, tiled=True),
        lax.psum_scatter(grad_down, ("head", "seq"), scatter_dimension=0, tiled=True),
        lax.psum_scatter(grad_patch, ("head", "seq"), scatter_dimension=0, tiled=True),
        lax.psum_scatter(grad_class, ("head", "seq"), scatter_dimension=0, tiled=True),
        lax.psum_scatter(grad_gains, ("head", "seq"), scatter_dimension=0, tiled=True),
    )
    return (
        class_masks,
        grad_inputs,
        reduced[0],
        reduced[1],
        reduced[2],
        reduced[3],
        reduced[4],
        reduced[5],
        reduced[6].T,
        norm_grads,
    )


MESH = pl.DeviceIdType.MESH
LOG2E = 1.4426950408889634
SLOTS = 16


def device(y, x, z, c):
    return (y * 2 + x, z * 2 + c)


class Links:
    def __init__(self, send_sem, recv_sem):
        head, seq = lax.axis_index("head"), lax.axis_index("seq")
        self.y, self.x, self.z, self.c = head // 2, head % 2, seq // 2, seq % 2
        y, x, z, c = self.y, self.x, self.z, self.c
        self.sibling = device(y, x, z, 1 - c)
        self.along_x = device(y, 1 - x, z, c)
        self.along_y = device(1 - y, x, z, c)
        self.across = device(1 - y, 1 - x, z, c)
        self.along_z = [device(y, x, (z + k) % 4, c) for k in (1, 2, 3)]
        self.send_sem, self.recv_sem, self.count, self.made = send_sem, recv_sem, 0, []

    def greet(self):
        barrier = pltpu.get_barrier_semaphore()
        peers = [self.sibling, self.along_x, self.along_y, self.across] + self.along_z
        for peer in peers:
            pl.semaphore_signal(barrier, inc=1, device_id=peer, device_id_type=MESH)
        pl.semaphore_wait(barrier, len(peers))

    def plan(self, source, target, peer):
        number = self.count
        self.count += 1
        copy = pltpu.make_async_remote_copy(
            src_ref=source,
            dst_ref=target,
            send_sem=self.send_sem.at[number],
            recv_sem=self.recv_sem.at[number],
            device_id=peer,
            device_id_type=MESH,
        )
        self.made.append(copy)
        return copy

    def drain(self):
        for copy in self.made:
            copy.wait_send()


class Stage:
    def __init__(self, links, moves):
        self.copies = [links.plan(*move) for move in moves]

    def start(self):
        for copy in self.copies:
            copy.start()

    def wait(self):
        for copy in self.copies:
            copy.wait_recv()


def at_slots(slot, events):
    for number, event in enumerate(events):
        pl.when(slot == number)(event)


def front_kernel(scaling, *refs):
    (live_ref, normal, tile, qkv_shard, out_shard, up_shard, down_shard) = refs[:7]
    (attended, heads_ref, logsum, rows_ref, gains_ref, qkv, full_out, up, down) = refs[7:16]
    tiles, staged, send_sem, recv_sem, local_sem = refs[16:]
    links = Links(send_sem, recv_sem)
    y, x, z, c = links.y, links.x, links.z, links.c
    h = y * 2 + x
    rows = normal.shape[0]
    wide = qkv.shape[-1]
    narrow = staged.shape[1]
    heads = narrow // DH
    half_ff = up.shape[-1] // 2
    slot_rows = rows * 4
    plane = [(links.across, 3 - h, 3), (links.along_x, y * 2 + 1 - x, 1), (links.along_y, (1 - y) * 2 + x, 2)]

    def columns(start, size):
        return pl.ds(pl.multiple_of(start, 128), size)

    local = [
        pltpu.make_async_copy(tile, tiles.at[y, x, z, c], local_sem.at[0]),
        pltpu.make_async_copy(qkv_shard.at[:, columns(h * wide, wide)], qkv.at[y, x, z, c], local_sem.at[1]),
        pltpu.make_async_copy(out_shard, full_out.at[y, x, z, c], local_sem.at[2]),
        pltpu.make_async_copy(down_shard, down.at[y, z, c], local_sem.at[3]),
    ] + [
        pltpu.make_async_copy(
            up_shard.at[:, columns(k * 2 * half_ff + x * half_ff, half_ff)],
            up.at[y, x, z, c, :, k * half_ff : (k + 1) * half_ff],
            local_sem.at[4 + k],
        )
        for k in range(2)
    ]
    for copy in local:
        copy.start()
    gain_core = Stage(links, [(tile, tiles.at[y, x, z, c], links.sibling)])
    gain_z = Stage(links, [(tiles.at[y, x, z], tiles.at[y, x, z], peer) for peer in links.along_z])
    gain_plane = Stage(links, [(tiles.at[y, x], tiles.at[y, x], peer) for peer, _, _ in plane])
    qkv_plane = Stage(
        links, [(qkv_shard.at[:, columns(p * wide, wide)], qkv.at[y, x, z, c], peer) for peer, p, _ in plane]
    )
    qkv_z = Stage(links, [(qkv.at[:, :, z, c], qkv.at[:, :, z, c], peer) for peer in links.along_z])
    qkv_core = Stage(links, [(qkv.at[:, :, :, c], qkv.at[:, :, :, c], links.sibling)])
    up_x = [
        Stage(
            links,
            [
                (
                    up_shard.at[:, columns(k * 2 * half_ff + (1 - x) * half_ff, half_ff)],
                    up.at[y, x, z, c, :, k * half_ff : (k + 1) * half_ff],
                    links.along_x,
                )
            ],
        )
        for k in range(2)
    ]

    def up_part(k, *index):
        return up.at[(*index, slice(None), slice(k * half_ff, (k + 1) * half_ff))]

    up_z = [
        Stage(links, [(up_part(k, y, slice(None), z, c),) * 2 + (peer,) for peer in links.along_z]) for k in range(2)
    ]
    up_y = [
        Stage(links, [(up_part(k, y, slice(None), slice(None), c),) * 2 + (links.along_y,)]) for k in range(2)
    ]
    up_core = [
        Stage(links, [(up_part(k, slice(None), slice(None), slice(None), c),) * 2 + (links.sibling,)])
        for k in range(2)
    ]
    down_z = Stage(links, [(down_shard, down.at[y, z, c], peer) for peer in links.along_z])
    down_y = Stage(links, [(down.at[y, :, c], down.at[y, :, c], links.along_y)])
    down_core = Stage(links, [(down.at[:, :, c], down.at[:, :, c], links.sibling)])
    out_z = Stage(links, [(out_shard, full_out.at[y, x, z, c], peer) for peer in links.along_z])
    out_y = Stage(links, [(full_out.at[y, x, :, c], full_out.at[y, x, :, c], links.along_y)])
    out_x = Stage(links, [(full_out.at[:, x, :, c], full_out.at[:, x, :, c], links.along_x)])
    out_core = Stage(links, [(full_out.at[:, :, :, c], full_out.at[:, :, :, c], links.sibling)])

    def strip(p, low, high):
        return rows_ref.at[p, low:high]

    middle = rows // 2
    rows_x = [
        Stage(links, [(strip(h, low, high), strip(h, low, high), links.along_x)])
        for low, high in ((0, middle), (middle, rows))
    ]
    rows_y = [
        Stage(links, [(strip(h, low, high), strip(h, low, high), links.along_y)])
        for low, high in ((middle, rows), (0, middle))
    ]
    _, at_x, _ = plane[1]
    _, at_y, _ = plane[2]
    relay_y = Stage(links, [(strip(at_x, 0, middle), strip(at_x, 0, middle), links.along_y)])
    relay_x = Stage(links, [(strip(at_y, middle, rows), strip(at_y, middle, rows), links.along_x)])

    links.greet()
    gain_core.start()
    qkv_plane.start()
    up_x[0].start()
    up_x[1].start()
    local[0].wait()
    gain_core.wait()
    gain_z.start()
    out_z.start()
    gain_z.wait()
    gain_plane.start()
    local[1].wait()
    qkv_plane.wait()
    qkv_z.start()
    down_z.start()
    gain_plane.wait()
    for j in range(8):
        piece = tiles[j // 4, j // 2 % 2, (j % 2) * 2, 0].astype(jnp.float32)
        for i in range(1, 4):
            piece = piece + tiles[j // 4, j // 2 % 2, (j % 2) * 2 + i // 2, i % 2].astype(jnp.float32)
        gains_ref[:, j * 128 : (j + 1) * 128] = piece[0:8]
    rows_ref[h] = (normal[...] * gains_ref[0:1, :]).astype(jnp.bfloat16)
    for stage in (rows_x[0], rows_y[0], rows_x[1], rows_y[1]):
        stage.start()
    local[4].wait()
    local[5].wait()
    for k in range(2):
        up_x[k].wait()
        up_z[k].start()
    rows_x[0].wait()
    relay_y.start()
    rows_y[0].wait()
    relay_x.start()
    local[2].wait()
    out_z.wait()
    out_y.start()
    qkv_z.wait()
    qkv_core.start()
    qkv_core.wait()

    def project(p):
        weight = qkv[...].reshape(rows * 4, wide)
        piece = jnp.dot(rows_ref[p], weight, preferred_element_type=jnp.float32).astype(jnp.bfloat16)
        at = pl.ds(pl.multiple_of(p * rows, rows), rows)
        for number in range(3 * heads):
            heads_ref[number, at, :] = piece[:, number * DH : (number + 1) * DH]

    project(h)
    rows_x[1].wait()
    project(at_x)
    rows_y[1].wait()
    project(at_y)
    relay_y.wait()
    relay_x.wait()
    project(3 - h)

    live = live_ref[0]
    key_live = lax.broadcasted_iota(jnp.int32, (slot_rows, 1), 0) < live

    def back(rel):
        peer = h + (rel % 2) * (1 - 2 * x) + (rel // 2) * (2 - 4 * y)
        return pltpu.make_async_remote_copy(
            src_ref=staged.at[pl.ds(pl.multiple_of(peer * rows, rows), rows), :],
            dst_ref=attended.at[:, columns(h * narrow, narrow)],
            send_sem=send_sem.at[links.count - 1 + rel],
            recv_sem=recv_sem.at[links.count - 1 + rel],
            device_id=(peer, z * 2 + c),
            device_id_type=MESH,
        )

    def then(wait, start, extra=None):
        def run():
            if extra is not None:
                extra.wait()
            wait.wait()
            start.start()

        return run

    def nothing():
        pass

    events = [
        then(down_z, down_y, local[3]),
        nothing,
        nothing,
        then(out_y, out_x),
        nothing,
        nothing,
        nothing,
        then(up_z[0], up_y[0]),
        nothing,
        then(out_x, out_core),
        nothing,
        nothing,
        nothing,
        then(up_z[1], up_y[1]),
        nothing,
        then(down_y, down_core),
    ]

    def tile_body(slot, carry):
        turn, number = slot // 4, slot % 4
        rel = 3 - turn
        peer = h + (rel % 2) * (1 - 2 * x) + (rel // 2) * (2 - 4 * y)
        at = pl.ds(pl.multiple_of(peer * rows, rows), rows)
        at_slots(slot, events)
        queries = heads_ref[3 * number, at, :]
        keys = heads_ref[3 * number + 1]
        values = heads_ref[3 * number + 2]
        scores = lax.dot_general(keys, queries, (((1,), (1,)), ((), ())), preferred_element_type=jnp.float32)
        scores = jnp.where(key_live, scores * (scaling * LOG2E), -1e30)
        highest = jnp.max(scores, axis=0, keepdims=True)
        raw = jnp.exp2(scores - highest)
        totals = jnp.sum(raw, axis=0, keepdims=True)
        weights = (raw * (1.0 / totals)).astype(jnp.bfloat16)
        mixed = lax.dot_general(
            values, weights, (((0,), (0,)), ((), ())), preferred_element_type=jnp.float32
        )
        mixed = mixed.T.astype(jnp.bfloat16)
        for which in range(4):

            @pl.when(number == which)
            def _(which=which):
                staged[at, which * DH : (which + 1) * DH] = mixed

        logsum[number, :, at] = highest + jnp.log2(totals)

        @pl.when((number == 3) & (rel > 0))
        def _():
            back(rel).start()

        return carry

    lax.fori_loop(0, SLOTS, tile_body, 0)
    own = pltpu.make_async_copy(
        staged.at[pl.ds(pl.multiple_of(h * rows, rows), rows), :],
        attended.at[:, columns(h * narrow, narrow)],
        local_sem.at[6],
    )
    own.start()
    up_y[0].wait()
    up_core[0].start()
    for rel in (3, 2, 1):
        back(rel).wait()
    up_y[1].wait()
    up_core[1].start()
    for stage in (down_core, out_core, up_core[0], up_core[1]):
        stage.wait()
    own.wait()
    links.drain()


def front(live, normal, tile, w_qkv, w_out, w_up, w_down, scaling):
    rows, features = normal.shape
    vmem, hbm = pl.BlockSpec(memory_space=pltpu.VMEM), pl.BlockSpec(memory_space=pl.ANY)
    wide = w_qkv.shape[1] // 4
    heads = wide // (3 * DH)
    low = jnp.bfloat16

    def full(rows_of, columns_of):
        return jax.ShapeDtypeStruct((2, 2, 4, 2, rows_of, columns_of), low)

    return pl.pallas_call(
        partial(front_kernel, scaling),
        out_shape=[
            jax.ShapeDtypeStruct((rows, features), low),
            jax.ShapeDtypeStruct((3 * heads, 4 * rows, DH), low),
            jax.ShapeDtypeStruct((heads, 1, 4 * rows), jnp.float32),
            jax.ShapeDtypeStruct((4, rows, features), low),
            jax.ShapeDtypeStruct((8, features), jnp.float32),
            full(w_qkv.shape[0], wide),
            full(*w_out.shape),
            full(w_up.shape[0], w_up.shape[1] // 2),
            jax.ShapeDtypeStruct((2, 4, 2) + w_down.shape, low),
        ],
        in_specs=[pl.BlockSpec(memory_space=pltpu.SMEM), vmem, vmem] + [hbm] * 4,
        out_specs=[vmem] * 6 + [hbm] * 3,
        scratch_shapes=[
            pltpu.VMEM((2, 2, 4, 2) + tile.shape, low),
            pltpu.VMEM((4 * rows, wide // 3), low),
            pltpu.SemaphoreType.DMA((64,)),
            pltpu.SemaphoreType.DMA((64,)),
            pltpu.SemaphoreType.DMA((7,)),
        ],
        compiler_params=pltpu.CompilerParams(
            collective_id=1, has_side_effects=True, vmem_limit_bytes=40 * 2**20
        ),
        name="front",
    )(live, normal, tile, w_qkv, w_out, w_up, w_down)


class Sum:
    def __init__(self, links, partial_ref, total, sib, one, two, three, local, kind):
        y, x, z, c = links.y, links.x, links.z, links.c
        self.links, self.total, self.sib, self.one, self.two, self.three = links, total, sib, one, two, three
        self.kind = kind
        lead = (slice(None),) * (len(total.shape) - 2)
        self.local = pltpu.make_async_copy(partial_ref.at[(*lead, c)], total, local)
        self.core = Stage(links, [(partial_ref.at[(*lead, 1 - c)], sib, links.sibling)])
        if kind == "up":
            self.first = Stage(links, [(total.at[1 - y], one, links.along_y)])
            self.second = Stage(
                links,
                [(total.at[y, :, (z + k) % 4], two.at[k - 1], links.along_z[k - 1]) for k in (1, 2, 3)],
            )
            self.third = Stage(links, [(total.at[y, 1 - x, z], three, links.along_x)])
        elif kind == "down":
            self.first = Stage(links, [(total.at[1 - y], one, links.along_y)])
            self.second = Stage(
                links, [(total.at[y, (z + k) % 4], two.at[k - 1], links.along_z[k - 1]) for k in (1, 2, 3)]
            )
        elif kind == "all":
            self.first = Stage(links, [(total.at[:, 1 - x], one, links.along_x)])
            self.second = Stage(links, [(total.at[1 - y, x], two, links.along_y)])
            self.third = Stage(
                links,
                [(total.at[y, x, (z + k) % 4], three.at[k - 1], links.along_z[k - 1]) for k in (1, 2, 3)],
            )

    def begin(self):
        self.core.start()
        self.local.start()

    def add(self, pairs, count):
        total = self.total

        def body(i, carry):
            index, extra = pairs(i)
            total[index] = total[index] + extra
            return carry

        lax.fori_loop(0, count, body, 0)

    def run_first(self):
        self.local.wait()
        self.core.wait()
        sib = self.sib
        if self.kind == "down":
            self.add(lambda i: ((i // 4, i % 4), sib[i // 4, i % 4]), 8)
        else:
            self.add(lambda i: ((i // 8, i // 4 % 2, i % 4), sib[i // 8, i // 4 % 2, i % 4]), 16)
        self.first.start()

    def run_second(self):
        self.first.wait()
        y, x, one = self.links.y, self.links.x, self.one
        if self.kind == "up":
            self.add(lambda i: ((y, i // 4, i % 4), one[i // 4, i % 4]), 8)
        elif self.kind == "down":
            self.add(lambda i: ((y, i), one[i]), 4)
        else:
            self.add(lambda i: ((i // 4, x, i % 4), one[i // 4, i % 4]), 8)
        self.second.start()

    def run_third(self):
        self.second.wait()
        y, x, z, two = self.links.y, self.links.x, self.links.z, self.two
        if self.kind == "up":
            self.add(lambda i: ((y, i, z), two[0, i] + two[1, i] + two[2, i]), 2)
        else:
            self.add(lambda i: ((y, x, i), two[i]), 4)
        self.third.start()

    def finish(self, out):
        y, x, z = self.links.y, self.links.x, self.links.z
        if self.kind == "up":
            self.third.wait()
            half = self.total.shape[-1] // 2
            mine = self.total[y, x, z]
            theirs = self.three[...]
            for k in range(2):
                at = k * 2 * half
                for low, part in ((0, mine), (1, theirs)):
                    start = at + (x if low == 0 else 1 - x) * half
                    out[:, pl.ds(pl.multiple_of(start, 128), half)] = part[
                        :, k * half : (k + 1) * half
                    ].astype(jnp.float32)
            return
        stage, got = (self.second, self.two) if self.kind == "down" else (self.third, self.three)
        stage.wait()
        mine = self.total[y, z] if self.kind == "down" else self.total[y, x, z]
        value = mine.astype(jnp.float32)
        for k in range(3):
            value = value + got[k].astype(jnp.float32)
        out[...] = value


def rear_kernel(scaling, *refs):
    live_ref, d_rows, heads_ref, logsum, rows_ref, qkv, small_ref = refs[:7]
    partials = refs[7:12]
    d_normed, g_qkv, outs, small_out = refs[12], refs[13], refs[14:19], refs[19]
    at = 20
    d_out, d_heads, d_spread, grad_keys, grad_values = refs[at : at + 5]
    d_sent, d_got, q_part, q_sib, q_z, q_plane = refs[at + 5 : at + 11]
    small_own, small_got, send_sem, recv_sem, local_sem = refs[at + 11 : at + 16]
    scratch = refs[at + 16 :]
    links = Links(send_sem, recv_sem)
    y, x, z, c = links.y, links.x, links.z, links.c
    h = y * 2 + x
    rows, features = d_rows.shape
    slot_rows = rows * 4
    narrow = d_out.shape[1]
    heads = narrow // DH
    wide = 3 * narrow
    plane = [(links.across, 3 - h, 3), (links.along_x, y * 2 + 1 - x, 1), (links.along_y, (1 - y) * 2 + x, 2)]

    def columns(start, size):
        return pl.ds(pl.multiple_of(start, 128), size)

    def block(p):
        return pl.ds(pl.multiple_of(p * rows, rows), rows)

    spread_out = Stage(
        links, [(d_rows.at[:, columns(p * narrow, narrow)], d_out.at[block(h), :], peer) for peer, p, _ in plane]
    )
    own = pltpu.make_async_copy(d_rows.at[:, columns(h * narrow, narrow)], d_out.at[block(h), :], local_sem.at[0])
    kinds = ("up", "down", "all", "all", "all")
    sums = [
        Sum(links, partials[i], *scratch[5 * i : 5 * i + 5], local_sem.at[1 + i], kinds[i]) for i in range(5)
    ]
    back = [Stage(links, [(d_sent.at[rel - 1], d_got.at[rel - 1], peer)]) for peer, _, rel in plane]
    q_core = Stage(links, [(q_part.at[:, :, :, 1 - c], q_sib, links.sibling)])
    q_along = Stage(
        links,
        [(q_part.at[:, :, (z + k) % 4, c], q_z.at[k - 1], links.along_z[k - 1]) for k in (1, 2, 3)],
    )
    q_across = Stage(
        links, [(q_part.at[p // 2, p % 2, z, c], q_plane.at[h], peer) for peer, p, _ in plane]
    )
    small_core = Stage(links, [(small_own.at[0], small_got.at[0], links.sibling)])
    small_x = Stage(links, [(small_own.at[1], small_got.at[1], links.along_x)])
    small_y = Stage(links, [(small_own.at[2], small_got.at[2], links.along_y)])
    small_z = Stage(links, [(small_own.at[3], small_got.at[3 + z], peer) for peer in links.along_z])

    links.greet()
    spread_out.start()
    own.start()
    for entry in sums:
        entry.begin()
    small_own[0] = small_ref[...]
    small_core.start()
    own.wait()
    spread_out.wait()
    live = live_ref[0]
    key_live = lax.broadcasted_iota(jnp.int32, (slot_rows, 1), 0) < live
    up, down, out, patch, classes = sums

    def small_step(stage, number, following):
        def run():
            stage.wait()
            small_own[number + 1] = small_own[number] + small_got[number]
            if number == 2:
                small_got[3 + z] = small_own[3]
            following.start()

        return run

    def nothing():
        pass

    events = [
        up.run_first,
        patch.run_first,
        down.run_first,
        small_step(small_core, 0, small_x),
        classes.run_first,
        out.run_first,
        nothing,
        small_step(small_x, 1, small_y),
        patch.run_second,
        nothing,
        small_step(small_y, 2, small_z),
        nothing,
        up.run_second,
        nothing,
        classes.run_second,
        nothing,
    ]

    def tile_body(slot, carry):
        number, turn = slot // 4, slot % 4
        at_slots(slot, events)
        at = block(turn)

        @pl.when(turn == 0)
        def _():
            grad_keys[...] = jnp.zeros_like(grad_keys)
            grad_values[...] = jnp.zeros_like(grad_values)

        queries = heads_ref[3 * number, at, :]
        keys = heads_ref[3 * number + 1]
        values = heads_ref[3 * number + 2]
        grads = d_heads[number, at, :]
        scores = lax.dot_general(keys, queries, (((1,), (1,)), ((), ())), preferred_element_type=jnp.float32)
        powers = scores * (scaling * LOG2E) - logsum[number, :, at]
        weights = jnp.where(key_live, jnp.exp2(powers), 0.0)
        grad_values[...] += jnp.dot(weights.astype(jnp.bfloat16), grads, preferred_element_type=jnp.float32)
        grad_weights = lax.dot_general(
            values, grads, (((1,), (1,)), ((), ())), preferred_element_type=jnp.float32
        )
        deltas = jnp.sum(grad_weights * weights, axis=0, keepdims=True)
        grad_scores = (weights * (grad_weights - deltas)).astype(jnp.bfloat16)
        grad_keys[...] += jnp.dot(grad_scores, queries, preferred_element_type=jnp.float32)
        grad_queries = lax.dot_general(
            keys, grad_scores, (((0,), (0,)), ((), ())), preferred_element_type=jnp.float32
        )
        d_heads[4 + 3 * number, at, :] = (grad_queries.T * scaling).astype(jnp.bfloat16)

        @pl.when(turn == 3)
        def _():
            d_heads[5 + 3 * number] = (grad_keys[...] * scaling).astype(jnp.bfloat16)
            d_heads[6 + 3 * number] = grad_values[...].astype(jnp.bfloat16)

        return carry

    for number in range(heads):
        d_heads[number] = d_out[:, number * DH : (number + 1) * DH]
    lax.fori_loop(0, SLOTS, tile_body, 0)
    for number in range(3 * heads):
        d_spread[:, number * DH : (number + 1) * DH] = d_heads[4 + number]
    per = features // 4
    for j in range(4):
        left = jnp.concatenate([rows_ref[p, :, j * per : (j + 1) * per] for p in range(4)], axis=0)
        piece = lax.dot_general(
            left, d_spread[...], (((0,), (0,)), ((), ())), preferred_element_type=jnp.float32
        ).astype(jnp.bfloat16)
        q_part[j // 2, j % 2] = piece.reshape(4, 2, per // 8, wide)
    q_core.start()
    weight = qkv[...].reshape(features, wide)
    for (_, p, rel), stage in zip(plane, back):
        piece = lax.dot_general(
            d_spread[block(p), :], weight, (((1,), (1,)), ((), ())), preferred_element_type=jnp.float32
        )
        d_sent[rel - 1] = piece.astype(jnp.bfloat16)
        stage.start()
    q_core.wait()

    def add_sib(i, carry):
        index = (i // 8, i // 4 % 2, i % 4)
        q_part[(*index, c)] = q_part[(*index, c)] + q_sib[index]
        return carry

    lax.fori_loop(0, 16, add_sib, 0)
    q_along.start()
    d_normed[...] = lax.dot_general(
        d_spread[block(h), :], weight, (((1,), (1,)), ((), ())), preferred_element_type=jnp.float32
    )
    down.run_second()
    out.run_second()
    patch.run_third()
    up.run_third()
    classes.run_third()
    out.run_third()
    q_along.wait()

    def add_z(i, carry):
        index = (i // 2, i % 2)
        q_part[(*index, z, c)] = q_part[(*index, z, c)] + (q_z[(0, *index)] + q_z[(1, *index)] + q_z[(2, *index)])
        return carry

    lax.fori_loop(0, 4, add_z, 0)
    q_across.start()
    small_z.wait()
    small_out[...] = small_got[3] + small_got[4] + small_got[5] + small_got[6]
    patch.finish(outs[3])
    down.finish(outs[1])
    classes.finish(outs[4])
    out.finish(outs[2])
    up.finish(outs[0])
    q_across.wait()
    g_qkv[:, columns(h * wide, wide)] = q_part[y, x, z, c].astype(jnp.float32)
    for _, p, _ in plane:
        g_qkv[:, columns(p * wide, wide)] = q_plane[p].astype(jnp.float32)
    for stage in back:
        stage.wait()
    d_normed[...] = d_normed[...] + (
        d_got[0].astype(jnp.float32) + d_got[1].astype(jnp.float32) + d_got[2].astype(jnp.float32)
    )
    links.drain()


def rear(live, d_rows, heads_qkv, logsum, rows_all, qkv, small, partials, scaling):
    rows, features = d_rows.shape
    slot_rows = 4 * rows
    narrow = features // 4
    heads = narrow // DH
    wide = 3 * narrow
    vmem, hbm = pl.BlockSpec(memory_space=pltpu.VMEM), pl.BlockSpec(memory_space=pl.ANY)
    low = jnp.bfloat16
    up, down, *rest = [a.shape[-2:] for a in partials]
    shard = (features // 32, wide)
    buffers = [
        (2, 2, 4) + up,
        (2, 2, 4) + up,
        (2, 4) + up,
        (3, 2) + up,
        up,
        (2, 4) + down,
        (2, 4) + down,
        (4,) + down,
        (3,) + down,
        (8, 128),
    ]
    for shape in rest:
        buffers += [(2, 2, 4) + shape, (2, 2, 4) + shape, (2, 4) + shape, (4,) + shape, (3,) + shape]
    single = jnp.float32
    return pl.pallas_call(
        partial(rear_kernel, scaling),
        out_shape=[
            jax.ShapeDtypeStruct((rows, features), single),
            jax.ShapeDtypeStruct((features // 32, 4 * wide), single),
            jax.ShapeDtypeStruct((up[0], 2 * up[1]), single),
            jax.ShapeDtypeStruct(down, single),
        ]
        + [jax.ShapeDtypeStruct(shape, single) for shape in rest]
        + [jax.ShapeDtypeStruct(small.shape, single)],
        in_specs=[pl.BlockSpec(memory_space=pltpu.SMEM)] + [vmem] * 6 + [hbm] * 5,
        out_specs=[vmem] * 8,
        scratch_shapes=[
            pltpu.VMEM((slot_rows, narrow), low),
            pltpu.VMEM((4 * heads, slot_rows, DH), low),
            pltpu.VMEM((slot_rows, wide), low),
            pltpu.VMEM((slot_rows, DH), single),
            pltpu.VMEM((slot_rows, DH), single),
            pltpu.VMEM((3, rows, features), low),
            pltpu.VMEM((3, rows, features), low),
            pltpu.VMEM((2, 2, 4, 2) + shard, low),
            pltpu.VMEM((2, 2, 4) + shard, low),
            pltpu.VMEM((3, 2, 2) + shard, low),
            pltpu.VMEM((4,) + shard, low),
            pltpu.VMEM((4,) + small.shape, single),
            pltpu.VMEM((7,) + small.shape, single),
            pltpu.SemaphoreType.DMA((64,)),
            pltpu.SemaphoreType.DMA((64,)),
            pltpu.SemaphoreType.DMA((6,)),
        ]
        + [pltpu.VMEM(shape, low) for shape in buffers],
        compiler_params=pltpu.CompilerParams(
            collective_id=2, has_side_effects=True, vmem_limit_bytes=58 * 2**20
        ),
        name="rear",
    )(live, d_rows, heads_qkv, logsum, rows_all, qkv, small, *partials)


def hop(value, pairs):
    return lax.ppermute(value, "head", pairs)


def swap(value):
    return lax.ppermute(value, "head", [(0, 1), (1, 0), (2, 3), (3, 2)])


def matmul(left, right):
    return jnp.dot(left, right, preferred_element_type=jnp.float32)


def matmul_nt(left, right):
    return lax.dot_general(left, right, (((1,), (1,)), ((), ())), preferred_element_type=jnp.float32)


def matmul_tn(left, right):
    return lax.dot_general(left, right, (((0,), (0,)), ((), ())), preferred_element_type=jnp.float32)


def body_planned(
    tokens,
    patch_counts,
    w_qkv,
    w_out,
    w_up,
    w_down,
    w_patch,
    w_class,
    norm_gains,
    mask_norm,
    grad_masks,
):
    low = jnp.bfloat16
    h, s = lax.axis_index("head"), lax.axis_index("seq")
    tokens, grad_masks = tokens[0], grad_masks[0]
    row_count = tokens.shape[0]
    late = lax.all_gather(jnp.concatenate([w_patch, w_class], axis=1), ("head", "seq"), axis=0, tiled=True)
    full_patch, full_class = late[:, :1024], late[:, 1024:]
    tile = lax.dynamic_update_slice(jnp.zeros((16, 128), low), norm_gains, (0, (s % 4) * 32))
    position = h * row_count + jnp.arange(row_count, dtype=jnp.int32)
    live = CLS + patch_counts
    patch_rows = ((position >= CLS) & (position < live[0])).astype(jnp.float32)[:, None]
    root_flag = (h == 0).astype(jnp.float32)
    scaling = DH ** (-0.5)

    normal_one, inverse_one = standardize(tokens)
    attended, heads_qkv, logsum, rows_all, gains, qkv, full_out, half_up, half_down = front(
        live, normal_one, tile, w_qkv, w_out, w_up, w_down, scaling
    )
    full_out = full_out.reshape(1024, 1024)
    half_up = half_up.reshape(1024, -1)
    half_down = half_down.reshape(-1, 1024)
    gain_one, gain_two = gains[0], gains[1]
    second = tokens + matmul(attended, full_out)
    normal_two, inverse_two = standardize(second)
    normed_two = (normal_two * gain_two).astype(low)
    normed_beside = swap(normed_two)
    gelu_exact = partial(jax.nn.gelu, approximate=False)
    hidden = matmul(normed_two, half_up)
    active = gelu_exact(hidden).astype(low)
    hidden_beside = matmul(normed_beside, half_up)
    active_beside = gelu_exact(hidden_beside).astype(low)
    from_beside = swap(matmul(active_beside, half_down).astype(low))
    residual = second + (matmul(active, half_down) + from_beside.astype(jnp.float32))
    rounded = residual.astype(low)
    class_rows = rounded[:CLS]
    class_proj = matmul(class_rows, full_class)
    class_unit = (class_proj * unit_scale(class_proj)).astype(low)
    arrived = [hop(class_unit, [(0, rel)]) for rel in (1, 2, 3)]
    patch_proj = matmul(rounded, full_patch)
    patch_unit = (patch_proj * unit_scale(patch_proj)).astype(low)
    classes = jnp.where(h == 0, class_unit, arrived[0] + arrived[1] + arrived[2])
    products = matmul_nt(patch_unit, classes)
    normal_mask, inverse_mask = standardize(products)
    class_masks = (normal_mask * mask_norm[0] + mask_norm[1]) * patch_rows
    upstream = grad_masks * patch_rows
    mask_sums = jnp.stack([jnp.sum(upstream * normal_mask, axis=0), jnp.sum(upstream, axis=0)])
    d_products = standard_back(normal_mask, inverse_mask, upstream * mask_norm[0]).astype(low)
    class_part = matmul_tn(d_products, patch_unit)
    class_sent = class_part.astype(low)
    parts = [hop(class_sent, [(rel, 0)]) for rel in (1, 2, 3)]
    d_patch_unit = matmul(d_products, classes)
    d_patch_proj = unit_back(patch_proj, d_patch_unit).astype(low)
    d_class_unit = class_part + (
        parts[0].astype(jnp.float32) + parts[1].astype(jnp.float32) + parts[2].astype(jnp.float32)
    )
    d_class_proj = (unit_back(class_proj, d_class_unit) * root_flag).astype(low)
    grad_patch = matmul_tn(rounded, d_patch_proj).astype(low)
    grad_class = matmul_tn(class_rows, d_class_proj).astype(low)
    d_residual = matmul_nt(d_patch_proj, full_patch)
    d_residual = d_residual.at[:CLS].add(matmul_nt(d_class_proj, full_class))
    d_branch = d_residual.astype(low)
    branch_beside = swap(d_branch)
    d_active = matmul_nt(d_branch, half_down)
    d_hidden = jax.vjp(gelu_exact, hidden)[1](d_active)[0].astype(low)
    d_active_beside = matmul_nt(branch_beside, half_down)
    d_hidden_beside = jax.vjp(gelu_exact, hidden_beside)[1](d_active_beside)[0].astype(low)
    back_beside = swap(matmul_nt(d_hidden_beside, half_up).astype(low))
    d_normed_two = matmul_nt(d_hidden, half_up) + back_beside.astype(jnp.float32)
    grad_down = matmul_tn(
        jnp.concatenate([active, active_beside]), jnp.concatenate([d_branch, branch_beside])
    ).astype(low)
    grad_up = matmul_tn(
        jnp.concatenate([normed_two, normed_beside]), jnp.concatenate([d_hidden, d_hidden_beside])
    ).astype(low)
    d_second = d_residual + standard_back(normal_two, inverse_two, d_normed_two * gain_two)
    d_mix = d_second.astype(low)
    grad_out = matmul_tn(attended, d_mix).astype(low)
    d_attended = matmul_nt(d_mix, full_out).astype(low)

    def parted(value):
        return value.reshape(2, 2, 4, 2, value.shape[0] // 32, value.shape[1])

    partials = (
        parted(grad_up),
        grad_down.reshape(2, 4, 2, 128, 1024),
        parted(grad_out),
        parted(grad_patch),
        parted(grad_class),
    )
    small = jnp.pad(mask_sums, ((0, 6), (0, 256 - CLS)))
    d_normed_one, g_qkv, g_up, g_down, g_out, g_patch, g_class, sums = rear(
        live, d_attended, heads_qkv, logsum, rows_all, qkv, small, partials, scaling
    )
    grad_inputs = d_second + standard_back(normal_one, inverse_one, d_normed_one * gain_one)
    gain_sums = [
        jnp.sum(weight.astype(jnp.float32) * grad, axis=1) for weight, grad in ((w_qkv, g_qkv), (w_up, g_up))
    ]
    return (
        class_masks[None],
        grad_inputs[None],
        g_qkv,
        g_out,
        g_up,
        g_down,
        g_patch,
        g_class,
        jnp.stack(gain_sums) / norm_gains.astype(jnp.float32),
        sums[0:2, :CLS],
    )


def solution(mesh):
    planned = dict(mesh.shape) == {"head": 4, "seq": 8}
    return jax.shard_map(
        body_planned if planned else body_general,
        mesh=mesh,
        in_specs=(
            P("seq", "head", None),
            P("seq"),
            P(("head", "seq"), None),
            P(("head", "seq"), None),
            P(("head", "seq"), None),
            P(("head", "seq"), None),
            P(("head", "seq"), None),
            P(("head", "seq"), None),
            P(None, ("head", "seq")),
            P(),
            P("seq", "head", None),
        ),
        out_specs=(
            P("seq", "head", None),
            P("seq", "head", None),
            P(("head", "seq"), None),
            P(("head", "seq"), None),
            P(("head", "seq"), None),
            P(("head", "seq"), None),
            P(("head", "seq"), None),
            P(("head", "seq"), None),
            P(None, ("head", "seq")),
            P(),
        ),
        check_vma=False,
    )
```

```python
from functools import partial

import jax
import jax.numpy as jnp
from jax import lax
from jax.experimental import pallas as pl
from jax.experimental.pallas import tpu as pltpu
from jax.sharding import PartitionSpec as P

HEADS = 16
DH = 64
CLS = 150


def spread_2(value, axis, source):
    kept = jnp.where(lax.axis_index(axis) == source, value, 0).astype(value.dtype)
    return lax.psum(kept, axis)


def standardize(values):
    center = values - jnp.mean(values, axis=-1, keepdims=True)
    inverse = lax.rsqrt(jnp.mean(center * center, axis=-1, keepdims=True) + 1e-05)
    return (center * inverse, inverse)


def standard_back(normal, inverse, upstream):
    middle = jnp.mean(upstream, axis=-1, keepdims=True)
    along = jnp.mean(upstream * normal, axis=-1, keepdims=True)
    return inverse * (upstream - middle - normal * along)


def unit_scale(values):
    return lax.rsqrt(jnp.sum(values * values, axis=-1, keepdims=True) + 1e-06)


def unit_back(values, upstream):
    factor = unit_scale(values)
    direct = values * factor
    return factor * (upstream - direct * jnp.sum(upstream * direct, axis=-1, keepdims=True))


def block_scores(query_block, key_rows, key_live, scaling):
    scores = (
        jnp.einsum("qd,kd->qk", query_block, key_rows, preferred_element_type=jnp.float32) * scaling
    )
    return jnp.where(key_live, scores, -1e30)


def attend_head(queries, key_rows, values, key_live, scaling, blocks):
    head_width = queries.shape[-1]

    def single(query_block):
        scores = block_scores(query_block, key_rows, key_live, scaling)
        highest = jnp.max(scores, axis=-1, keepdims=True)
        weights_raw = jnp.exp(scores - highest)
        totals = jnp.sum(weights_raw, axis=-1, keepdims=True)
        weights = (weights_raw / totals).astype(jnp.bfloat16)
        output = jnp.einsum("qk,kd->qd", weights, values, preferred_element_type=jnp.float32)
        return (output.astype(jnp.bfloat16), (highest + jnp.log(totals))[:, 0])

    outputs, logsum = lax.map(single, queries.reshape(blocks, -1, head_width))
    return (outputs.reshape(-1, head_width), logsum.reshape(-1))


def attend_back(queries, key_rows, values, grad_out, logsum, key_live, scaling, blocks):
    head_width = queries.shape[-1]

    def single(running, pieces):
        grad_keys, grad_values = running
        query_block, grad_block, logsum_block = pieces
        scores = block_scores(query_block, key_rows, key_live, scaling)
        weights = jnp.exp(scores - logsum_block[:, None])
        grad_values = grad_values + jnp.einsum(
            "qk,qd->kd",
            weights.astype(jnp.bfloat16),
            grad_block,
            preferred_element_type=jnp.float32,
        )
        grad_weights = jnp.einsum(
            "qd,kd->qk", grad_block, values, preferred_element_type=jnp.float32
        )
        deltas = jnp.sum(grad_weights * weights, axis=-1, keepdims=True)
        grad_scores = (weights * (grad_weights - deltas)).astype(jnp.bfloat16)
        grad_query = (
            jnp.einsum("qk,kd->qd", grad_scores, key_rows, preferred_element_type=jnp.float32)
            * scaling
        )
        grad_keys = (
            grad_keys
            + jnp.einsum("qk,qd->kd", grad_scores, query_block, preferred_element_type=jnp.float32)
            * scaling
        )
        return ((grad_keys, grad_values), grad_query)

    zero_state = jnp.zeros(key_rows.shape, jnp.float32)
    pieces = (
        queries.reshape(blocks, -1, head_width),
        grad_out.reshape(blocks, -1, head_width),
        logsum.reshape(blocks, -1),
    )
    (grad_keys, grad_values), grad_queries = lax.scan(single, (zero_state, zero_state), pieces)
    return (grad_queries.reshape(-1, head_width), grad_keys, grad_values)


def body_general(
    tokens,
    patch_counts,
    w_qkv,
    w_out,
    w_up,
    w_down,
    w_patch,
    w_class,
    norm_gains,
    mask_norm,
    grad_masks,
):
    gains_rows = norm_gains.T
    gathered = (
        lax.all_gather(w_qkv, ("head", "seq"), axis=0, tiled=True),
        lax.all_gather(w_out, ("head", "seq"), axis=0, tiled=True),
        lax.all_gather(w_up, ("head", "seq"), axis=0, tiled=True),
        lax.all_gather(w_down, ("head", "seq"), axis=0, tiled=True),
        lax.all_gather(w_patch, ("head", "seq"), axis=0, tiled=True),
        lax.all_gather(w_class, ("head", "seq"), axis=0, tiled=True),
        lax.all_gather(gains_rows, ("head", "seq"), axis=0, tiled=True),
    )
    full_qkv, full_out, full_up, full_down, full_patch, full_class, full_gains = gathered
    gain_one = full_gains[:, 0].astype(jnp.float32)
    gain_two = full_gains[:, 1].astype(jnp.float32)
    image_count = tokens.shape[0]
    row_count = tokens.shape[1]
    groups = lax.axis_size("head")
    slot_rows = row_count * groups
    local_heads = HEADS // groups
    position = lax.axis_index("head") * row_count + jnp.arange(row_count, dtype=jnp.int32)
    live_limit = CLS + patch_counts
    patch_rows = ((position[None, :] >= CLS) & (position[None, :] < live_limit[:, None])).astype(
        jnp.float32
    )[:, :, None]
    key_live = (jnp.arange(slot_rows, dtype=jnp.int32)[None, :] < live_limit[:, None])[:, None, :]
    root_flag = (lax.axis_index("head") == 0).astype(jnp.float32)
    scaling = DH ** (-0.5)
    blocks = slot_rows // 512
    normal_one, inverse_one = standardize(tokens)
    normed_one = (normal_one * gain_one).astype(jnp.bfloat16)
    triple = jnp.einsum(
        "ird,dt->irt", normed_one, full_qkv, preferred_element_type=jnp.float32
    ).astype(jnp.bfloat16)
    spread = lax.all_to_all(triple, "head", split_axis=2, concat_axis=1, tiled=True).reshape(
        image_count, slot_rows, local_heads, 3, DH
    )
    image = 0
    outputs = []
    image_logsums = []
    for number in range(local_heads):
        output, logsum = attend_head(
            spread[image, :, number, 0],
            spread[image, :, number, 1],
            spread[image, :, number, 2],
            key_live[image],
            scaling,
            blocks,
        )
        outputs.append(output)
        image_logsums.append(logsum)
    image_outputs = [jnp.stack(outputs, axis=1).reshape(slot_rows, local_heads * DH)]
    logsums = [image_logsums]
    attended_heads = jnp.stack(image_outputs, axis=0)
    attended = lax.all_to_all(attended_heads, "head", split_axis=1, concat_axis=2, tiled=True)
    second = tokens + jnp.einsum(
        "ire,ed->ird", attended, full_out, preferred_element_type=jnp.float32
    )
    normal_two, inverse_two = standardize(second)
    normed_two = (normal_two * gain_two).astype(jnp.bfloat16)
    hidden = jnp.einsum("ird,df->irf", normed_two, full_up, preferred_element_type=jnp.float32)
    gelu_exact = partial(jax.nn.gelu, approximate=False)
    active = gelu_exact(hidden).astype(jnp.bfloat16)
    residual = second + jnp.einsum(
        "irf,fd->ird", active, full_down, preferred_element_type=jnp.float32
    )
    rounded = residual.astype(jnp.bfloat16)
    patch_proj = jnp.einsum("ird,de->ire", rounded, full_patch, preferred_element_type=jnp.float32)
    patch_unit = (patch_proj * unit_scale(patch_proj)).astype(jnp.bfloat16)
    class_proj = jnp.einsum(
        "ird,de->ire", rounded[:, :CLS], full_class, preferred_element_type=jnp.float32
    )
    class_unit = (class_proj * unit_scale(class_proj)).astype(jnp.bfloat16)
    classes = spread_2(class_unit, "head", 0)
    products = jnp.einsum("ird,icd->irc", patch_unit, classes, preferred_element_type=jnp.float32)
    normal_mask, inverse_mask = standardize(products)
    class_masks = (normal_mask * mask_norm[0] + mask_norm[1]) * patch_rows
    upstream = grad_masks * patch_rows
    norm_grads = lax.psum(
        jnp.stack([jnp.sum(upstream * normal_mask, axis=(0, 1)), jnp.sum(upstream, axis=(0, 1))]),
        ("head", "seq"),
    )
    d_products = standard_back(normal_mask, inverse_mask, upstream * mask_norm[0]).astype(
        jnp.bfloat16
    )
    d_patch_unit = jnp.einsum(
        "irc,icd->ird", d_products, classes, preferred_element_type=jnp.float32
    )
    class_part = jnp.einsum(
        "irc,ird->icd", d_products, patch_unit, preferred_element_type=jnp.float32
    )
    d_class_unit = lax.psum(class_part.astype(jnp.bfloat16), "head").astype(jnp.float32)
    d_patch_proj = unit_back(patch_proj, d_patch_unit).astype(jnp.bfloat16)
    d_class_proj = (unit_back(class_proj, d_class_unit) * root_flag).astype(jnp.bfloat16)
    regathered = (
        lax.all_gather(w_qkv, ("head", "seq"), axis=0, tiled=True),
        lax.all_gather(w_out, ("head", "seq"), axis=0, tiled=True),
        lax.all_gather(w_up, ("head", "seq"), axis=0, tiled=True),
        lax.all_gather(w_down, ("head", "seq"), axis=0, tiled=True),
        lax.all_gather(w_patch, ("head", "seq"), axis=0, tiled=True),
        lax.all_gather(w_class, ("head", "seq"), axis=0, tiled=True),
        lax.all_gather(gains_rows, ("head", "seq"), axis=0, tiled=True),
    )
    back_qkv, back_out, back_up, back_down, back_patch, back_class, back_gains = regathered
    back_one = back_gains[:, 0].astype(jnp.float32)
    back_two = back_gains[:, 1].astype(jnp.float32)
    grad_patch = jnp.einsum(
        "ird,ire->de", rounded, d_patch_proj, preferred_element_type=jnp.float32
    )
    grad_class = jnp.einsum(
        "ird,ire->de", rounded[:, :CLS], d_class_proj, preferred_element_type=jnp.float32
    )
    d_residual = jnp.einsum(
        "ire,de->ird", d_patch_proj, back_patch, preferred_element_type=jnp.float32
    )
    class_term = jnp.einsum(
        "ire,de->ird", d_class_proj, back_class, preferred_element_type=jnp.float32
    )
    d_residual = d_residual.at[:, :CLS].add(class_term)
    d_branch = d_residual.astype(jnp.bfloat16)
    grad_down = jnp.einsum("irf,ird->fd", active, d_branch, preferred_element_type=jnp.float32)
    d_active = jnp.einsum("ird,fd->irf", d_branch, back_down, preferred_element_type=jnp.float32)
    gelu_pull = jax.vjp(gelu_exact, hidden)[1]
    d_hidden = gelu_pull(d_active)[0].astype(jnp.bfloat16)
    grad_up = jnp.einsum("ird,irf->df", normed_two, d_hidden, preferred_element_type=jnp.float32)
    d_normed_two = jnp.einsum("irf,df->ird", d_hidden, back_up, preferred_element_type=jnp.float32)
    d_second = d_residual + standard_back(normal_two, inverse_two, d_normed_two * back_two)
    grad_gain_two = jnp.sum(d_normed_two * normal_two, axis=(0, 1))
    d_mix = d_second.astype(jnp.bfloat16)
    grad_out = jnp.einsum("ire,ird->ed", attended, d_mix, preferred_element_type=jnp.float32)
    d_attended = jnp.einsum(
        "ird,ed->ire", d_mix, back_out, preferred_element_type=jnp.float32
    ).astype(jnp.bfloat16)
    d_heads = lax.all_to_all(d_attended, "head", split_axis=2, concat_axis=1, tiled=True).reshape(
        image_count, slot_rows, local_heads, DH
    )
    image = 0
    head_grads = []
    for number in range(local_heads):
        grad_queries, grad_keys, grad_values = attend_back(
            spread[image, :, number, 0],
            spread[image, :, number, 1],
            spread[image, :, number, 2],
            d_heads[image, :, number],
            logsums[image][number],
            key_live[image],
            scaling,
            blocks,
        )
        head_grads.append(jnp.stack([grad_queries, grad_keys, grad_values], axis=1))
    image_grads = [jnp.stack(head_grads, axis=1).reshape(slot_rows, local_heads * 3 * DH)]
    d_spread = jnp.stack(image_grads, axis=0).astype(jnp.bfloat16)
    d_triple = lax.all_to_all(d_spread, "head", split_axis=1, concat_axis=2, tiled=True)
    grad_qkv = jnp.einsum("ird,irt->dt", normed_one, d_triple, preferred_element_type=jnp.float32)
    d_normed_one = jnp.einsum("irt,dt->ird", d_triple, back_qkv, preferred_element_type=jnp.float32)
    grad_inputs = d_second + standard_back(normal_one, inverse_one, d_normed_one * back_one)
    grad_gain_one = jnp.sum(d_normed_one * normal_one, axis=(0, 1))
    grad_gains = jnp.stack([grad_gain_one, grad_gain_two], axis=1)
    reduced = (
        lax.psum_scatter(grad_qkv, ("head", "seq"), scatter_dimension=0, tiled=True),
        lax.psum_scatter(grad_out, ("head", "seq"), scatter_dimension=0, tiled=True),
        lax.psum_scatter(grad_up, ("head", "seq"), scatter_dimension=0, tiled=True),
        lax.psum_scatter(grad_down, ("head", "seq"), scatter_dimension=0, tiled=True),
        lax.psum_scatter(grad_patch, ("head", "seq"), scatter_dimension=0, tiled=True),
        lax.psum_scatter(grad_class, ("head", "seq"), scatter_dimension=0, tiled=True),
        lax.psum_scatter(grad_gains, ("head", "seq"), scatter_dimension=0, tiled=True),
    )
    return (
        class_masks,
        grad_inputs,
        reduced[0],
        reduced[1],
        reduced[2],
        reduced[3],
        reduced[4],
        reduced[5],
        reduced[6].T,
        norm_grads,
    )


MESH = pl.DeviceIdType.MESH
LOG2E = 1.4426950408889634
SLOTS = 16
FRONT_COPIES = 88
REAR_COPIES = 88


def device(y, x, z, c):
    return (y * 2 + x, z * 2 + c)


class Links:
    def __init__(self, send_sem, recv_sem):
        head, seq = lax.axis_index("head"), lax.axis_index("seq")
        self.y, self.x, self.z, self.c = head // 2, head % 2, seq // 2, seq % 2
        y, x, z, c = self.y, self.x, self.z, self.c
        self.sibling = device(y, x, z, 1 - c)
        self.along_x = device(y, 1 - x, z, c)
        self.along_y = device(1 - y, x, z, c)
        self.across = device(1 - y, 1 - x, z, c)
        self.along_z = [device(y, x, (z + k) % 4, c) for k in (1, 2, 3)]
        self.send_sem, self.recv_sem, self.count, self.made, self.lines = send_sem, recv_sem, 0, [], []

    def greet(self):
        barrier = pltpu.get_barrier_semaphore()
        peers = [self.sibling, self.along_x, self.along_y, self.across] + self.along_z
        for peer in peers:
            pl.semaphore_signal(barrier, inc=1, device_id=peer, device_id_type=MESH)
        pl.semaphore_wait(barrier, len(peers))

    def plan(self, source, target, peer):
        number = self.count
        self.count += 1
        copy = pltpu.make_async_remote_copy(
            src_ref=source,
            dst_ref=target,
            send_sem=self.send_sem.at[number],
            recv_sem=self.recv_sem.at[number],
            device_id=peer,
            device_id_type=MESH,
        )
        self.made.append(copy)
        return copy

    def sent(self, stage):
        for copy in stage.copies:
            copy.wait_send()
        self.made = [copy for copy in self.made if all(copy is not other for other in stage.copies)]

    def drain(self):
        for copy in self.made:
            copy.wait_send()
        for line in self.lines:
            line.drain()


class Stage:
    def __init__(self, links, moves):
        self.copies = [links.plan(*move) for move in moves]

    def start(self):
        for copy in self.copies:
            copy.start()

    def wait(self):
        for copy in self.copies:
            copy.wait_recv()


class Line:
    def __init__(self, links, piece, source=None):
        self.links, self.piece = links, piece
        self.source = piece(links.z) if source is None else source
        self.base = links.count
        links.count += 5
        links.lines.append(self)

    def copy(self, source, target, sent, landed):
        links = self.links
        return pltpu.make_async_remote_copy(
            src_ref=source,
            dst_ref=self.piece(landed),
            send_sem=links.send_sem.at[self.base + sent],
            recv_sem=links.recv_sem.at[self.base + landed],
            device_id=device(links.y, links.x, target, links.c),
            device_id_type=MESH,
        )

    def direct(self, target):
        z = self.links.z
        return (z != target) if target in (1, 2) else (z != target) & (z != 3 - target)

    def start(self):
        for target in (1, 2, 0, 3):

            @pl.when(self.direct(target))
            def _(target=target):
                self.copy(self.source, target, target, self.links.z).start()

    def relay(self):
        for at, end in ((2, 0), (1, 3)):

            @pl.when(self.links.z == at)
            def _(end=end):
                self.copy(self.source, 3 - end, 4, end).wait_recv()
                self.copy(self.piece(end), 3 - end, 4, end).start()

    def wait(self):
        z = self.links.z
        for origin in range(4):
            pending = z != origin
            if origin in (0, 3):
                pending = pending & (z != (2 if origin == 0 else 1))

            @pl.when(pending)
            def _(origin=origin):
                self.copy(self.source, 0, 0, origin).wait_recv()

    def drain(self):
        for target in range(4):

            @pl.when(self.direct(target))
            def _(target=target):
                self.copy(self.source, target, target, self.links.z).wait_send()

        @pl.when((self.links.z == 1) | (self.links.z == 2))
        def _():
            self.copy(self.source, 0, 4, 0).wait_send()


def at_slots(slot, events):
    for number, event in events.items():
        pl.when(slot == number)(event)


def front_kernel(scaling, *refs):
    live_ref, normal, tile, qkv_shard, out_shard, up_shard, down_shard = refs[:7]
    attended, heads_ref, logsum, rows_ref, gains_ref, qkv, full_out, ups, downs = refs[7:16]
    tiles, staged, send_sem, recv_sem, local_sem = refs[16:]
    links = Links(send_sem, recv_sem)
    y, x, z, c = links.y, links.x, links.z, links.c
    h = y * 2 + x
    q = y * (1 - c) + x * c
    rows = normal.shape[0]
    wide = qkv.shape[-1]
    narrow = staged.shape[1]
    heads = narrow // DH
    block = ups.shape[-1]
    slot_rows = rows * 4
    plane = [(links.across, 3 - h, 3), (links.along_x, y * 2 + 1 - x, 1), (links.along_y, (1 - y) * 2 + x, 2)]
    at_x, at_y = plane[1][1], plane[2][1]

    def columns(start, size):
        return pl.ds(pl.multiple_of(start, 128), size)

    def up_block(number):
        return up_shard.at[:, columns(number * block, block)]

    local = [
        pltpu.make_async_copy(source, target, local_sem.at[number])
        for number, (source, target) in enumerate(
            [
                (tile, tiles.at[y, x, z, c]),
                (qkv_shard.at[:, columns(h * wide, wide)], qkv.at[y, x, z, c]),
                (out_shard, full_out.at[y, x, z, c]),
                (down_shard, downs.at[c, q, z]),
                (up_block(x), ups.at[0, y, x, z, c]),
                (up_block(2 + y), ups.at[1, y, x, z, c]),
            ]
        )
    ]
    gain_core = Stage(links, [(tile, tiles.at[y, x, z, c], links.sibling)])
    gain_z = Stage(links, [(tiles.at[y, x, z], tiles.at[y, x, z], peer) for peer in links.along_z])
    gain_plane = Stage(links, [(tiles.at[y, x], tiles.at[y, x], peer) for peer, _, _ in plane])
    qkv_plane = Stage(
        links, [(qkv_shard.at[:, columns(p * wide, wide)], qkv.at[y, x, z, c], peer) for peer, p, _ in plane]
    )
    part = qkv.shape[4] // 2
    qkv_z = [Line(links, lambda at, k=k: qkv.at[:, :, at, c, k * part : (k + 1) * part]) for k in range(2)]
    qkv_core = Stage(links, [(qkv.at[:, :, :, c], qkv.at[:, :, :, c], links.sibling)])
    up_split = [
        Stage(links, [(up_block(1 - x), ups.at[0, y, x, z, c], links.along_x)]),
        Stage(links, [(up_block(2 + 1 - y), ups.at[1, y, x, z, c], links.along_y)]),
    ]
    up_z = [
        Line(links, lambda at: ups.at[0, y, :, at, c]),
        Line(links, lambda at: ups.at[1, :, x, at, c]),
    ]
    up_on = [
        Stage(links, [(ups.at[0, y, :, :, c], ups.at[0, y, :, :, c], links.along_y)]),
        Stage(links, [(ups.at[1, :, x, :, c], ups.at[1, :, x, :, c], links.along_x)]),
    ]
    up_core = [
        Stage(links, [(ups.at[k, :, :, :, c], ups.at[k, :, :, :, c], links.sibling)]) for k in range(2)
    ]
    some = down_shard.shape[0] // 2
    turned = device(y + (1 - c) * (1 - 2 * y), x + c * (1 - 2 * x), z, c)
    spans = [slice(k * some, (k + 1) * some) for k in range(2)]
    down_z = [Line(links, lambda at, k=k: downs.at[c, q, at, spans[k]], down_shard.at[spans[k]]) for k in range(2)]
    down_on = [
        Stage(links, [(downs.at[c, q, :, spans[k]], downs.at[c, q, :, spans[k]], turned)]) for k in range(2)
    ]
    down_core = Stage(links, [(downs.at[c], downs.at[c], links.sibling)])
    part = out_shard.shape[0] // 2
    out_z = Line(links, lambda at: full_out.at[y, x, at, c], out_shard)
    piece_a, piece_b = full_out.at[y, x, :, c, 0:part], full_out.at[y, x, :, c, part:]
    out_one = Stage(links, [(piece_a, piece_a, links.along_y), (piece_b, piece_b, links.along_x)])
    piece_a, piece_b = full_out.at[:, x, :, c, 0:part], full_out.at[y, :, :, c, part:]
    out_two = Stage(links, [(piece_a, piece_a, links.along_x), (piece_b, piece_b, links.along_y)])
    out_core = Stage(links, [(full_out.at[:, :, :, c], full_out.at[:, :, :, c], links.sibling)])
    middle = rows // 2
    strips = [slice(0, middle), slice(middle, rows)]
    rows_x = [Stage(links, [(normal.at[strips[k]], rows_ref.at[h, strips[k]], links.along_x)]) for k in (0, 1)]
    rows_y = [Stage(links, [(normal.at[strips[k]], rows_ref.at[h, strips[k]], links.along_y)]) for k in (1, 0)]
    piece_a, piece_b = rows_ref.at[at_x, strips[0]], rows_ref.at[at_y, strips[1]]
    relay_y = Stage(links, [(piece_a, piece_a, links.along_y)])
    relay_x = Stage(links, [(piece_b, piece_b, links.along_x)])

    for copy in local:
        copy.start()
    links.greet()
    for stage in (qkv_plane, gain_core, *up_split, rows_x[0], rows_y[0], rows_x[1], rows_y[1], out_z):
        stage.start()
    local[0].wait()
    gain_core.wait()
    gain_z.start()
    local[1].wait()
    qkv_plane.wait()
    for line in qkv_z:
        line.start()
    gain_z.wait()
    gain_plane.start()
    rows_x[0].wait()
    relay_y.start()
    rows_y[0].wait()
    relay_x.start()
    out_z.relay()
    for line in qkv_z:
        line.relay()
    gain_plane.wait()
    for j in range(8):
        piece = tiles[j // 4, j // 2 % 2, (j % 2) * 2, 0].astype(jnp.float32)
        for i in range(1, 4):
            piece = piece + tiles[j // 4, j // 2 % 2, (j % 2) * 2 + i // 2, i % 2].astype(jnp.float32)
        gains_ref[:, j * 128 : (j + 1) * 128] = piece[0:8]
    for line in qkv_z:
        line.wait()
    qkv_core.start()
    for k in range(2):
        local[4 + k].wait()
        up_split[k].wait()
        up_z[k].start()
    out_z.wait()
    local[2].wait()

    def scale(p):
        rows_ref[p] = (rows_ref[p].astype(jnp.float32) * gains_ref[0:1, :]).astype(jnp.bfloat16)

    def project(p):
        weight = qkv[...].reshape(rows * 4, wide)
        piece = jnp.dot(rows_ref[p], weight, preferred_element_type=jnp.float32).astype(jnp.bfloat16)
        at = pl.ds(pl.multiple_of(p * rows, rows), rows)
        for number in range(3 * heads):
            heads_ref[number, at, :] = piece[:, number * DH : (number + 1) * DH]

    rows_ref[h] = (normal[...].astype(jnp.float32) * gains_ref[0:1, :]).astype(jnp.bfloat16)
    qkv_core.wait()
    project(h)
    rows_x[1].wait()
    rows_y[1].wait()
    links.sent(relay_x)
    links.sent(relay_y)
    out_one.start()
    for p in (at_x, at_y):
        scale(p)
        project(p)
    relay_y.wait()
    relay_x.wait()
    scale(3 - h)
    project(3 - h)

    live = live_ref[0]
    key_live = lax.broadcasted_iota(jnp.int32, (slot_rows, 1), 0) < live
    returned = links.count - 1
    assert returned + 4 <= FRONT_COPIES

    def back(rel):
        peer = h + (rel % 2) * (1 - 2 * x) + (rel // 2) * (2 - 4 * y)
        return pltpu.make_async_remote_copy(
            src_ref=staged.at[pl.ds(pl.multiple_of(peer * rows, rows), rows), :],
            dst_ref=attended.at[:, columns(h * narrow, narrow)],
            send_sem=send_sem.at[returned + rel],
            recv_sem=recv_sem.at[returned + rel],
            device_id=(peer, z * 2 + c),
            device_id_type=MESH,
        )

    def up_next(k):
        up_z[k].wait()
        up_on[k].start()

    def up_end(k):
        up_on[k].wait()
        up_core[k].start()

    def out_next():
        out_one.wait()
        out_two.start()

    def out_end():
        out_two.wait()
        out_core.start()

    def down_next(k):
        down_z[k].wait()
        down_on[k].start()

    def last_up():
        up_next(1)
        down_z[1].start()

    def first_down():
        up_z[1].relay()
        local[3].wait()
        down_z[0].start()

    events = {
        0: up_z[0].relay,
        2: partial(up_next, 0),
        6: first_down,
        8: out_next,
        11: last_up,
        15: out_end,
    }

    def tile_body(slot, carry):
        turn, number = slot // 4, slot % 4
        rel = 3 - turn
        peer = h + (rel % 2) * (1 - 2 * x) + (rel // 2) * (2 - 4 * y)
        at = pl.ds(pl.multiple_of(peer * rows, rows), rows)
        at_slots(slot, events)
        queries = heads_ref[3 * number, at, :]
        keys = heads_ref[3 * number + 1]
        values = heads_ref[3 * number + 2]
        scores = lax.dot_general(keys, queries, (((1,), (1,)), ((), ())), preferred_element_type=jnp.float32)
        scores = jnp.where(key_live, scores * (scaling * LOG2E), -1e30)
        highest = jnp.max(scores, axis=0, keepdims=True)
        raw = jnp.exp2(scores - highest)
        totals = jnp.sum(raw, axis=0, keepdims=True)
        weights = (raw * (1.0 / totals)).astype(jnp.bfloat16)
        mixed = lax.dot_general(
            values, weights, (((0,), (0,)), ((), ())), preferred_element_type=jnp.float32
        )
        mixed = mixed.T.astype(jnp.bfloat16)
        for which in range(4):

            @pl.when(number == which)
            def _(which=which):
                staged[at, which * DH : (which + 1) * DH] = mixed

        logsum[number, :, at] = highest + jnp.log2(totals)

        @pl.when((number == 3) & (rel > 0))
        def _():
            back(rel).start()

        return carry

    lax.fori_loop(0, SLOTS, tile_body, 0)
    own = pltpu.make_async_copy(
        staged.at[pl.ds(pl.multiple_of(h * rows, rows), rows), :],
        attended.at[:, columns(h * narrow, narrow)],
        local_sem.at[6],
    )
    own.start()
    down_z[0].relay()
    up_end(0)
    down_next(0)
    down_z[1].relay()
    for rel in (3, 2, 1):
        back(rel).wait()
    up_end(1)
    down_next(1)
    for stage in down_on:
        stage.wait()
    down_core.start()
    for stage in (out_core, *up_core, down_core):
        stage.wait()
    own.wait()
    links.drain()


def front(live, normal, tile, w_qkv, w_out, w_up, w_down, scaling):
    rows, features = normal.shape
    vmem, hbm = pl.BlockSpec(memory_space=pltpu.VMEM), pl.BlockSpec(memory_space=pl.ANY)
    wide = w_qkv.shape[1] // 4
    heads = wide // (3 * DH)
    low = jnp.bfloat16
    return pl.pallas_call(
        partial(front_kernel, scaling),
        out_shape=[
            jax.ShapeDtypeStruct((rows, features), low),
            jax.ShapeDtypeStruct((3 * heads, 4 * rows, DH), low),
            jax.ShapeDtypeStruct((heads, 1, 4 * rows), jnp.float32),
            jax.ShapeDtypeStruct((4, rows, features), low),
            jax.ShapeDtypeStruct((8, features), jnp.float32),
            jax.ShapeDtypeStruct((2, 2, 4, 2, w_qkv.shape[0], wide), low),
            jax.ShapeDtypeStruct((2, 2, 4, 2) + w_out.shape, low),
            jax.ShapeDtypeStruct((2, 2, 2, 4, 2, w_up.shape[0], w_up.shape[1] // 4), low),
            jax.ShapeDtypeStruct((2, 2, 4) + w_down.shape, low),
        ],
        in_specs=[pl.BlockSpec(memory_space=pltpu.SMEM), vmem, vmem] + [hbm] * 4,
        out_specs=[vmem] * 6 + [hbm] * 3,
        scratch_shapes=[
            pltpu.VMEM((2, 2, 4, 2) + tile.shape, low),
            pltpu.VMEM((4 * rows, wide // 3), low),
            pltpu.SemaphoreType.DMA((FRONT_COPIES,)),
            pltpu.SemaphoreType.DMA((FRONT_COPIES,)),
            pltpu.SemaphoreType.DMA((7,)),
        ],
        compiler_params=pltpu.CompilerParams(
            collective_id=1, has_side_effects=True, vmem_limit_bytes=40 * 2**20
        ),
        name="front",
    )(live, normal, tile, w_qkv, w_out, w_up, w_down)


class LineSum:
    def __init__(self, links, piece, got):
        self.links, self.piece, self.got = links, piece, got
        self.base = links.count
        links.count += 5
        links.lines.append(self)

    def copy(self, piece, target, slot, sent):
        links = self.links
        return pltpu.make_async_remote_copy(
            src_ref=self.piece(piece),
            dst_ref=self.got.at[slot],
            send_sem=links.send_sem.at[self.base + sent],
            recv_sem=links.recv_sem.at[self.base + slot],
            device_id=device(links.y, links.x, target, links.c),
            device_id_type=MESH,
        )

    def start(self):
        z = self.links.z
        for target, end, middle in ((3, 0, 1), (0, 3, 2)):

            @pl.when(z == end)
            def _(target=target, middle=middle):
                self.copy(target, middle, 4, target).start()

        for target in range(4):
            direct = z != target
            if target in (0, 3):
                direct = z == (1 if target == 0 else 2)

            @pl.when(direct)
            def _(target=target):
                self.copy(target, target, z, target).start()

    def relay(self):
        z = self.links.z
        for target, middle in ((3, 1), (0, 2)):

            @pl.when(z == middle)
            def _(target=target, middle=middle):
                self.copy(target, target, 4, target).wait_recv()
                own = self.piece(target)
                own[...] = own[...] + self.got[4]
                self.copy(target, target, middle, target).start()

    def collect(self, add):
        z = self.links.z
        for origin in range(4):
            comes = z != origin
            if origin in (0, 3):
                comes = comes & (z != 3 - origin)

            @pl.when(comes)
            def _(origin=origin):
                self.copy(0, 0, origin, 0).wait_recv()
                add(origin)

    def drain(self):
        for target in range(4):

            @pl.when(self.links.z != target)
            def _(target=target):
                self.copy(target, target, 0, target).wait_send()


class Sum:
    def __init__(self, links, partial_ref, total, sib, one, two, three, local, kind):
        y, x, z, c = links.y, links.x, links.z, links.c
        self.links, self.total, self.sib, self.one, self.two, self.three = links, total, sib, one, two, three
        self.kind = kind
        self.q = y * (1 - c) + x * c
        lead = () if kind == "down" else (slice(None),) * (len(total.shape) - 2)
        self.local = pltpu.make_async_copy(partial_ref.at[(*lead, c)], total, local)
        self.core = Stage(links, [(partial_ref.at[(*lead, 1 - c)], sib, links.sibling)])
        if kind in ("up_y", "all_y"):
            self.first = Stage(links, [(total.at[1 - y], one, links.along_y)])
            self.kept = lambda i, j: (y, i, j)
        elif kind in ("up_x", "all_x"):
            self.first = Stage(links, [(total.at[:, 1 - x], one, links.along_x)])
            self.kept = lambda i, j: (i, x, j)
        else:
            turned = device(y + (1 - c) * (1 - 2 * y), x + c * (1 - 2 * x), z, c)
            self.first = Stage(links, [(total.at[1 - self.q], one, turned)])
            self.line = LineSum(links, lambda at: total.at[self.q, at], three)
        if kind == "up_y":
            self.line = LineSum(links, lambda at: total.at[y, :, at], three)
            self.last = Stage(links, [(total.at[y, 1 - x, z], two, links.along_x)])
        elif kind == "up_x":
            self.line = LineSum(links, lambda at: total.at[:, x, at], three)
            self.last = Stage(links, [(total.at[1 - y, x, z], two, links.along_y)])
        elif kind == "all_x":
            self.second = Stage(links, [(total.at[1 - y, x], two, links.along_y)])
        elif kind == "all_y":
            self.second = Stage(links, [(total.at[y, 1 - x], two, links.along_x)])
        if kind in ("all_x", "all_y"):
            self.line = LineSum(links, lambda at: total.at[y, x, at], three)

    def begin(self):
        self.core.start()
        self.local.start()

    def add(self, pairs, count):
        total = self.total

        def body(i, carry):
            index, extra = pairs(i)
            total[index] = total[index] + extra
            return carry

        lax.fori_loop(0, count, body, 0)

    def run_first(self):
        self.local.wait()
        self.core.wait()
        sib = self.sib
        if self.kind == "down":
            self.add(lambda i: ((i // 4, i % 4), sib[i // 4, i % 4]), 8)
        else:
            self.add(lambda i: ((i // 8, i // 4 % 2, i % 4), sib[i // 8, i // 4 % 2, i % 4]), 16)
        self.first.start()

    def run_second(self):
        self.first.wait()
        one = self.one
        if self.kind == "down":
            self.add(lambda i: ((self.q, i), one[i]), 4)
        else:
            self.add(lambda i: (self.kept(i // 4, i % 4), one[i // 4, i % 4]), 8)
        if self.kind in ("all_x", "all_y"):
            self.second.start()
        else:
            self.line.start()

    def run_third(self):
        self.second.wait()
        y, x, two = self.links.y, self.links.x, self.two
        self.add(lambda i: ((y, x, i), two[i]), 4)
        self.line.start()

    def run_last(self):
        z, total, got = self.links.z, self.total, self.three

        def add(slot):
            for i in range(2):
                index = self.kept(i, z)
                total[index] = total[index] + got[slot, i]

        self.line.collect(add)
        self.last.start()

    def finish(self, out):
        y, x, z = self.links.y, self.links.x, self.links.z
        if self.kind in ("up_y", "up_x"):
            self.last.wait()
            block = self.total.shape[-1]
            base, mine = (0, x) if self.kind == "up_y" else (2, y)
            for number, part in ((mine, self.total[y, x, z]), (1 - mine, self.two[...])):
                at = pl.ds(pl.multiple_of((base + number) * block, 128), block)
                out[:, at] = part.astype(jnp.float32)
            return
        out[...] = (self.total[self.q, z] if self.kind == "down" else self.total[y, x, z]).astype(jnp.float32)

        def add(slot):
            out[...] = out[...] + self.three[slot].astype(jnp.float32)

        self.line.collect(add)


def rear_kernel(scaling, *refs):
    live_ref, d_rows, heads_ref, logsum, rows_ref, qkv, small_ref = refs[:7]
    up_ref, down_ref = refs[7:9]
    partials = (up_ref.at[0], up_ref.at[1], down_ref) + tuple(refs[9:12])
    d_normed, g_qkv, g_up, g_down, g_out, g_patch, g_class, small_out = refs[12:20]
    at = 20
    d_out, d_heads, d_spread, grad_keys, grad_values = refs[at : at + 5]
    d_sent, d_got, q_part, q_sib, q_z, q_plane = refs[at + 5 : at + 11]
    small_own, small_got, send_sem, recv_sem, local_sem = refs[at + 11 : at + 16]
    scratch = refs[at + 16 :]
    links = Links(send_sem, recv_sem)
    y, x, z, c = links.y, links.x, links.z, links.c
    h = y * 2 + x
    rows, features = d_rows.shape
    slot_rows = rows * 4
    narrow = d_out.shape[1]
    heads = narrow // DH
    wide = 3 * narrow
    plane = [(links.across, 3 - h, 3), (links.along_x, y * 2 + 1 - x, 1), (links.along_y, (1 - y) * 2 + x, 2)]

    def columns(start, size):
        return pl.ds(pl.multiple_of(start, 128), size)

    def block(p):
        return pl.ds(pl.multiple_of(p * rows, rows), rows)

    spread_out = Stage(
        links, [(d_rows.at[:, columns(p * narrow, narrow)], d_out.at[block(h), :], peer) for peer, p, _ in plane]
    )
    own = pltpu.make_async_copy(d_rows.at[:, columns(h * narrow, narrow)], d_out.at[block(h), :], local_sem.at[0])
    kinds = ("up_y", "up_x", "down", "all_x", "all_x", "all_y")
    sums = [
        Sum(links, partials[i], *scratch[5 * i : 5 * i + 5], local_sem.at[1 + i], kinds[i]) for i in range(6)
    ]
    back = [Stage(links, [(d_sent.at[rel - 1], d_got.at[rel - 1], peer)]) for peer, _, rel in plane]
    q_core = Stage(links, [(q_part.at[:, :, :, 1 - c], q_sib, links.sibling)])
    q_line = LineSum(links, lambda at: q_part.at[:, :, at, c], q_z)
    q_across = Stage(
        links, [(q_part.at[p // 2, p % 2, z, c], q_plane.at[h], peer) for peer, p, _ in plane]
    )
    small_core = Stage(links, [(small_own.at[0], small_got.at[0], links.sibling)])
    small_x = Stage(links, [(small_own.at[1], small_got.at[1], links.along_x)])
    small_y = Stage(links, [(small_own.at[2], small_got.at[2], links.along_y)])
    small_z = Stage(links, [(small_own.at[3], small_got.at[3 + z], peer) for peer in links.along_z])

    links.greet()
    spread_out.start()
    own.start()
    for entry in sums:
        entry.begin()
    small_own[0] = small_ref[...]
    small_core.start()
    own.wait()
    spread_out.wait()
    live = live_ref[0]
    key_live = lax.broadcasted_iota(jnp.int32, (slot_rows, 1), 0) < live
    up_y, up_x, down, out, patch, classes = sums
    assert links.count <= REAR_COPIES

    def small_step(stage, number, following):
        def run():
            stage.wait()
            small_own[number + 1] = small_own[number] + small_got[number]
            if number == 2:
                small_got[3 + z] = small_own[3]
            following.start()

        return run

    def both(*steps):
        def run():
            for step in steps:
                step()

        return run

    events = {
        0: up_y.run_first,
        1: up_x.run_first,
        2: down.run_first,
        3: small_step(small_core, 0, small_x),
        4: patch.run_first,
        5: classes.run_first,
        6: out.run_first,
        7: small_step(small_x, 1, small_y),
        8: both(up_y.run_second, up_x.run_second),
        9: small_step(small_y, 2, small_z),
        11: both(up_y.line.relay, up_x.line.relay),
        13: down.run_second,
        14: patch.run_second,
        15: both(up_y.run_last, up_x.run_last),
    }

    def tile_body(slot, carry):
        number, turn = slot // 4, slot % 4
        at_slots(slot, events)
        at = block(turn)

        @pl.when(turn == 0)
        def _():
            grad_keys[...] = jnp.zeros_like(grad_keys)
            grad_values[...] = jnp.zeros_like(grad_values)

        queries = heads_ref[3 * number, at, :]
        keys = heads_ref[3 * number + 1]
        values = heads_ref[3 * number + 2]
        grads = d_heads[number, at, :]
        scores = lax.dot_general(keys, queries, (((1,), (1,)), ((), ())), preferred_element_type=jnp.float32)
        powers = scores * (scaling * LOG2E) - logsum[number, :, at]
        weights = jnp.where(key_live, jnp.exp2(powers), 0.0)
        grad_values[...] += jnp.dot(weights.astype(jnp.bfloat16), grads, preferred_element_type=jnp.float32)
        grad_weights = lax.dot_general(
            values, grads, (((1,), (1,)), ((), ())), preferred_element_type=jnp.float32
        )
        deltas = jnp.sum(grad_weights * weights, axis=0, keepdims=True)
        grad_scores = (weights * (grad_weights - deltas)).astype(jnp.bfloat16)
        grad_keys[...] += jnp.dot(grad_scores, queries, preferred_element_type=jnp.float32)
        grad_queries = lax.dot_general(
            keys, grad_scores, (((0,), (0,)), ((), ())), preferred_element_type=jnp.float32
        )
        d_heads[4 + 3 * number, at, :] = (grad_queries.T * scaling).astype(jnp.bfloat16)

        @pl.when(turn == 3)
        def _():
            d_heads[5 + 3 * number] = (grad_keys[...] * scaling).astype(jnp.bfloat16)
            d_heads[6 + 3 * number] = grad_values[...].astype(jnp.bfloat16)

        return carry

    for number in range(heads):
        d_heads[number] = d_out[:, number * DH : (number + 1) * DH]
    lax.fori_loop(0, SLOTS, tile_body, 0)
    for number in range(3 * heads):
        d_spread[:, number * DH : (number + 1) * DH] = d_heads[4 + number]
    per = features // 4
    for j in range(4):
        left = jnp.concatenate([rows_ref[p, :, j * per : (j + 1) * per] for p in range(4)], axis=0)
        piece = lax.dot_general(
            left, d_spread[...], (((0,), (0,)), ((), ())), preferred_element_type=jnp.float32
        ).astype(jnp.bfloat16)
        q_part[j // 2, j % 2] = piece.reshape(4, 2, per // 8, wide)
    q_core.start()
    weight = qkv[...].reshape(features, wide)
    for (_, p, rel), stage in zip(plane, back):
        piece = lax.dot_general(
            d_spread[block(p), :], weight, (((1,), (1,)), ((), ())), preferred_element_type=jnp.float32
        )
        d_sent[rel - 1] = piece.astype(jnp.bfloat16)
        stage.start()
    q_core.wait()

    def add_sib(i, carry):
        index = (i // 8, i // 4 % 2, i % 4)
        q_part[(*index, c)] = q_part[(*index, c)] + q_sib[index]
        return carry

    lax.fori_loop(0, 16, add_sib, 0)
    q_line.start()
    d_normed[...] = lax.dot_general(
        d_spread[block(h), :], weight, (((1,), (1,)), ((), ())), preferred_element_type=jnp.float32
    )
    down.line.relay()
    q_line.relay()
    patch.run_third()
    classes.run_second()
    out.run_second()
    patch.line.relay()
    classes.run_third()
    out.run_third()
    classes.line.relay()

    def add_line(slot):
        for i in range(4):
            index = (i // 2, i % 2)
            q_part[(*index, z, c)] = q_part[(*index, z, c)] + q_z[(slot, *index)]

    q_line.collect(add_line)
    q_across.start()
    out.line.relay()
    small_z.wait()
    small_out[...] = small_got[3] + small_got[4] + small_got[5] + small_got[6]
    down.finish(g_down)
    up_y.finish(g_up)
    up_x.finish(g_up)
    patch.finish(g_patch)
    classes.finish(g_class)
    out.finish(g_out)
    q_across.wait()
    g_qkv[:, columns(h * wide, wide)] = q_part[y, x, z, c].astype(jnp.float32)
    for _, p, _ in plane:
        g_qkv[:, columns(p * wide, wide)] = q_plane[p].astype(jnp.float32)
    for stage in back:
        stage.wait()
    d_normed[...] = d_normed[...] + (
        d_got[0].astype(jnp.float32) + d_got[1].astype(jnp.float32) + d_got[2].astype(jnp.float32)
    )
    links.drain()


def rear(live, d_rows, heads_qkv, logsum, rows_all, qkv, small, partials, scaling):
    rows, features = d_rows.shape
    slot_rows = 4 * rows
    narrow = features // 4
    heads = narrow // DH
    wide = 3 * narrow
    vmem, hbm = pl.BlockSpec(memory_space=pltpu.VMEM), pl.BlockSpec(memory_space=pl.ANY)
    low = jnp.bfloat16
    up, down, *rest = [a.shape[-2:] for a in partials]
    shard = (features // 32, wide)
    buffers = []
    for _ in range(2):
        buffers += [(2, 2, 4) + up, (2, 2, 4) + up, (2, 4) + up, up, (5, 2) + up]
    buffers += [(2, 4) + down, (2, 4) + down, (4,) + down, (8, 128), (5,) + down]
    for shape in rest:
        buffers += [(2, 2, 4) + shape, (2, 2, 4) + shape, (2, 4) + shape, (4,) + shape, (5,) + shape]
    single = jnp.float32
    return pl.pallas_call(
        partial(rear_kernel, scaling),
        out_shape=[
            jax.ShapeDtypeStruct((rows, features), single),
            jax.ShapeDtypeStruct((features // 32, 4 * wide), single),
            jax.ShapeDtypeStruct((up[0], 4 * up[1]), single),
            jax.ShapeDtypeStruct(down, single),
        ]
        + [jax.ShapeDtypeStruct(shape, single) for shape in rest]
        + [jax.ShapeDtypeStruct(small.shape, single)],
        in_specs=[pl.BlockSpec(memory_space=pltpu.SMEM)] + [vmem] * 6 + [hbm] * 5,
        out_specs=[vmem] * 8,
        scratch_shapes=[
            pltpu.VMEM((slot_rows, narrow), low),
            pltpu.VMEM((4 * heads, slot_rows, DH), low),
            pltpu.VMEM((slot_rows, wide), low),
            pltpu.VMEM((slot_rows, DH), single),
            pltpu.VMEM((slot_rows, DH), single),
            pltpu.VMEM((3, rows, features), low),
            pltpu.VMEM((3, rows, features), low),
            pltpu.VMEM((2, 2, 4, 2) + shard, low),
            pltpu.VMEM((2, 2, 4) + shard, low),
            pltpu.VMEM((5, 2, 2) + shard, low),
            pltpu.VMEM((4,) + shard, low),
            pltpu.VMEM((4,) + small.shape, single),
            pltpu.VMEM((7,) + small.shape, single),
            pltpu.SemaphoreType.DMA((REAR_COPIES,)),
            pltpu.SemaphoreType.DMA((REAR_COPIES,)),
            pltpu.SemaphoreType.DMA((7,)),
        ]
        + [pltpu.VMEM(shape, low) for shape in buffers],
        compiler_params=pltpu.CompilerParams(
            collective_id=2, has_side_effects=True, vmem_limit_bytes=58 * 2**20
        ),
        name="rear",
    )(live, d_rows, heads_qkv, logsum, rows_all, qkv, small, *partials)


def hop(value, pairs):
    return lax.ppermute(value, "head", pairs)


def swap_x(value):
    return lax.ppermute(value, "head", [(0, 1), (1, 0), (2, 3), (3, 2)])


def swap_y(value):
    return lax.ppermute(value, "head", [(0, 2), (2, 0), (1, 3), (3, 1)])


def matmul(left, right):
    return jnp.dot(left, right, preferred_element_type=jnp.float32)


def matmul_nt(left, right):
    return lax.dot_general(left, right, (((1,), (1,)), ((), ())), preferred_element_type=jnp.float32)


def matmul_tn(left, right):
    return lax.dot_general(left, right, (((0,), (0,)), ((), ())), preferred_element_type=jnp.float32)


def body_planned(
    tokens,
    patch_counts,
    w_qkv,
    w_out,
    w_up,
    w_down,
    w_patch,
    w_class,
    norm_gains,
    mask_norm,
    grad_masks,
):
    low = jnp.bfloat16
    h, s = lax.axis_index("head"), lax.axis_index("seq")
    tokens, grad_masks = tokens[0], grad_masks[0]
    row_count = tokens.shape[0]
    late = lax.all_gather(jnp.concatenate([w_patch, w_class], axis=1), ("head", "seq"), axis=0, tiled=True)
    full_patch, full_class = late[:, :1024], late[:, 1024:]
    tile = lax.dynamic_update_slice(jnp.zeros((16, 128), low), norm_gains, (0, (s % 4) * 32))
    position = h * row_count + jnp.arange(row_count, dtype=jnp.int32)
    live = CLS + patch_counts
    patch_rows = ((position >= CLS) & (position < live[0])).astype(jnp.float32)[:, None]
    root_flag = (h == 0).astype(jnp.float32)
    scaling = DH ** (-0.5)

    normal_one, inverse_one = standardize(tokens)
    sets = w_up.reshape(32, 2, 2, 4, 2, 128)
    up_blocks = jnp.concatenate(
        [sets[:, :, 0, :, 0], sets[:, :, 1, :, 0], sets[:, 0, :, :, 1], sets[:, 1, :, :, 1]], axis=1
    ).reshape(32, 4096)
    attended, heads_qkv, logsum, rows_all, gains, qkv, full_out, ups, downs = front(
        live, normal_one.astype(low), tile, w_qkv, w_out, up_blocks, w_down, scaling
    )
    full_out = full_out.reshape(1024, 1024)
    ups = ups.reshape(2, 1024, 1024)
    downs = downs.reshape(2, 1024, 1024)
    gain_one, gain_two = gains[0], gains[1]
    second = tokens + matmul(attended, full_out)
    normal_two, inverse_two = standardize(second)
    normed_two = (normal_two * gain_two).astype(low)
    swaps = (swap_x, swap_y)
    gelu_exact = partial(jax.nn.gelu, approximate=False)
    normed_beside = [swap(normed_two) for swap in swaps]
    hidden = [matmul(normed_two, ups[k]) for k in range(2)]
    active = [gelu_exact(value).astype(low) for value in hidden]
    hidden_beside = [matmul(normed_beside[k], ups[k]) for k in range(2)]
    active_beside = [gelu_exact(value).astype(low) for value in hidden_beside]
    from_beside = [swaps[k](matmul(active_beside[k], downs[k]).astype(low)) for k in range(2)]
    residual = second + (matmul(active[0], downs[0]) + matmul(active[1], downs[1]))
    residual = residual + (from_beside[0].astype(jnp.float32) + from_beside[1].astype(jnp.float32))
    rounded = residual.astype(low)
    class_rows = rounded[:CLS]
    class_proj = matmul(class_rows, full_class)
    class_unit = (class_proj * unit_scale(class_proj)).astype(low)
    arrived = [hop(class_unit, [(0, rel)]) for rel in (1, 2, 3)]
    patch_proj = matmul(rounded, full_patch)
    patch_unit = (patch_proj * unit_scale(patch_proj)).astype(low)
    classes = jnp.where(h == 0, class_unit, arrived[0] + arrived[1] + arrived[2])
    products = matmul_nt(patch_unit, classes)
    normal_mask, inverse_mask = standardize(products)
    class_masks = (normal_mask * mask_norm[0] + mask_norm[1]) * patch_rows
    upstream = grad_masks * patch_rows
    mask_sums = jnp.stack([jnp.sum(upstream * normal_mask, axis=0), jnp.sum(upstream, axis=0)])
    d_products = standard_back(normal_mask, inverse_mask, upstream * mask_norm[0]).astype(low)
    class_part = matmul_tn(d_products, patch_unit)
    class_sent = class_part.astype(low)
    parts = [hop(class_sent, [(rel, 0)]) for rel in (1, 2, 3)]
    d_patch_unit = matmul(d_products, classes)
    d_patch_proj = unit_back(patch_proj, d_patch_unit).astype(low)
    d_class_unit = class_part + (
        parts[0].astype(jnp.float32) + parts[1].astype(jnp.float32) + parts[2].astype(jnp.float32)
    )
    d_class_proj = (unit_back(class_proj, d_class_unit) * root_flag).astype(low)
    grad_patch = matmul_tn(rounded, d_patch_proj).astype(low)
    grad_class = matmul_tn(class_rows, d_class_proj).astype(low)
    d_residual = matmul_nt(d_patch_proj, full_patch)
    d_residual = d_residual.at[:CLS].add(matmul_nt(d_class_proj, full_class))
    d_branch = d_residual.astype(low)
    branch_beside = [swap(d_branch) for swap in swaps]

    def gelu_back(value, upstream):
        return jax.vjp(gelu_exact, value)[1](upstream)[0].astype(low)

    d_hidden = [gelu_back(hidden[k], matmul_nt(d_branch, downs[k])) for k in range(2)]
    d_hidden_beside = [gelu_back(hidden_beside[k], matmul_nt(branch_beside[k], downs[k])) for k in range(2)]
    back_beside = [swaps[k](matmul_nt(d_hidden_beside[k], ups[k]).astype(low)) for k in range(2)]
    d_normed_two = matmul_nt(d_hidden[0], ups[0]) + matmul_nt(d_hidden[1], ups[1])
    d_normed_two = d_normed_two + (back_beside[0].astype(jnp.float32) + back_beside[1].astype(jnp.float32))
    grad_down = jnp.stack(
        [
            matmul_tn(
                jnp.concatenate([active[k], active_beside[k]]), jnp.concatenate([d_branch, branch_beside[k]])
            ).astype(low)
            for k in range(2)
        ]
    )
    grad_up = jnp.stack(
        [
            matmul_tn(
                jnp.concatenate([normed_two, normed_beside[k]]), jnp.concatenate([d_hidden[k], d_hidden_beside[k]])
            ).astype(low)
            for k in range(2)
        ]
    )
    d_second = d_residual + standard_back(normal_two, inverse_two, d_normed_two * gain_two)
    d_mix = d_second.astype(low)
    grad_out = matmul_tn(attended, d_mix).astype(low)
    d_attended = matmul_nt(d_mix, full_out).astype(low)

    def parted(value):
        return value.reshape(2, 2, 4, 2, value.shape[0] // 32, value.shape[1])

    partials = (
        grad_up.reshape(2, 2, 2, 4, 2, 32, 1024),
        grad_down.reshape(2, 2, 4, 128, 1024),
        parted(grad_out),
        parted(grad_patch),
        parted(grad_class),
    )
    small = jnp.pad(mask_sums, ((0, 6), (0, 256 - CLS)))
    d_normed_one, g_qkv, g_up, g_down, g_out, g_patch, g_class, sums = rear(
        live, d_attended, heads_qkv, logsum, rows_all, qkv, small, partials, scaling
    )
    grad_inputs = d_second + standard_back(normal_one, inverse_one, d_normed_one * gain_one)
    gain_sums = [
        jnp.sum(weight.astype(jnp.float32) * grad, axis=1) for weight, grad in ((w_qkv, g_qkv), (up_blocks, g_up))
    ]
    at_x, at_y = (g_up[:, k * 2048 : (k + 1) * 2048].reshape(32, 2, 2, 4, 1, 128) for k in range(2))
    g_up = jnp.concatenate([at_x.transpose(0, 2, 1, 3, 4, 5), at_y], axis=4).reshape(32, 4096)
    return (
        class_masks[None],
        grad_inputs[None],
        g_qkv,
        g_out,
        g_up,
        g_down,
        g_patch,
        g_class,
        jnp.stack(gain_sums) / norm_gains.astype(jnp.float32),
        sums[0:2, :CLS],
    )


def solution(mesh):
    planned = dict(mesh.shape) == {"head": 4, "seq": 8}
    return jax.shard_map(
        body_planned if planned else body_general,
        mesh=mesh,
        in_specs=(
            P("seq", "head", None),
            P("seq"),
            P(("head", "seq"), None),
            P(("head", "seq"), None),
            P(("head", "seq"), None),
            P(("head", "seq"), None),
            P(("head", "seq"), None),
            P(("head", "seq"), None),
            P(None, ("head", "seq")),
            P(),
            P("seq", "head", None),
        ),
        out_specs=(
            P("seq", "head", None),
            P("seq", "head", None),
            P(("head", "seq"), None),
            P(("head", "seq"), None),
            P(("head", "seq"), None),
            P(("head", "seq"), None),
            P(("head", "seq"), None),
            P(("head", "seq"), None),
            P(None, ("head", "seq")),
            P(),
        ),
        check_vma=False,
    )
```

```python
from functools import partial

import jax
import jax.numpy as jnp
from jax import lax
from jax.experimental import pallas as pl
from jax.experimental.pallas import tpu as pltpu
from jax.sharding import PartitionSpec as P

HEADS = 16
DH = 64
CLS = 150


def spread_2(value, axis, source):
    kept = jnp.where(lax.axis_index(axis) == source, value, 0).astype(value.dtype)
    return lax.psum(kept, axis)


def standardize(values):
    center = values - jnp.mean(values, axis=-1, keepdims=True)
    inverse = lax.rsqrt(jnp.mean(center * center, axis=-1, keepdims=True) + 1e-05)
    return (center * inverse, inverse)


def standard_back(normal, inverse, upstream):
    middle = jnp.mean(upstream, axis=-1, keepdims=True)
    along = jnp.mean(upstream * normal, axis=-1, keepdims=True)
    return inverse * (upstream - middle - normal * along)


def unit_scale(values):
    return lax.rsqrt(jnp.sum(values * values, axis=-1, keepdims=True) + 1e-06)


def unit_back(values, upstream):
    factor = unit_scale(values)
    direct = values * factor
    return factor * (upstream - direct * jnp.sum(upstream * direct, axis=-1, keepdims=True))


def block_scores(query_block, key_rows, key_live, scaling):
    scores = (
        jnp.einsum("qd,kd->qk", query_block, key_rows, preferred_element_type=jnp.float32) * scaling
    )
    return jnp.where(key_live, scores, -1e30)


def attend_head(queries, key_rows, values, key_live, scaling, blocks):
    head_width = queries.shape[-1]

    def single(query_block):
        scores = block_scores(query_block, key_rows, key_live, scaling)
        highest = jnp.max(scores, axis=-1, keepdims=True)
        weights_raw = jnp.exp(scores - highest)
        totals = jnp.sum(weights_raw, axis=-1, keepdims=True)
        weights = (weights_raw / totals).astype(jnp.bfloat16)
        output = jnp.einsum("qk,kd->qd", weights, values, preferred_element_type=jnp.float32)
        return (output.astype(jnp.bfloat16), (highest + jnp.log(totals))[:, 0])

    outputs, logsum = lax.map(single, queries.reshape(blocks, -1, head_width))
    return (outputs.reshape(-1, head_width), logsum.reshape(-1))


def attend_back(queries, key_rows, values, grad_out, logsum, key_live, scaling, blocks):
    head_width = queries.shape[-1]

    def single(running, pieces):
        grad_keys, grad_values = running
        query_block, grad_block, logsum_block = pieces
        scores = block_scores(query_block, key_rows, key_live, scaling)
        weights = jnp.exp(scores - logsum_block[:, None])
        grad_values = grad_values + jnp.einsum(
            "qk,qd->kd",
            weights.astype(jnp.bfloat16),
            grad_block,
            preferred_element_type=jnp.float32,
        )
        grad_weights = jnp.einsum(
            "qd,kd->qk", grad_block, values, preferred_element_type=jnp.float32
        )
        deltas = jnp.sum(grad_weights * weights, axis=-1, keepdims=True)
        grad_scores = (weights * (grad_weights - deltas)).astype(jnp.bfloat16)
        grad_query = (
            jnp.einsum("qk,kd->qd", grad_scores, key_rows, preferred_element_type=jnp.float32)
            * scaling
        )
        grad_keys = (
            grad_keys
            + jnp.einsum("qk,qd->kd", grad_scores, query_block, preferred_element_type=jnp.float32)
            * scaling
        )
        return ((grad_keys, grad_values), grad_query)

    zero_state = jnp.zeros(key_rows.shape, jnp.float32)
    pieces = (
        queries.reshape(blocks, -1, head_width),
        grad_out.reshape(blocks, -1, head_width),
        logsum.reshape(blocks, -1),
    )
    (grad_keys, grad_values), grad_queries = lax.scan(single, (zero_state, zero_state), pieces)
    return (grad_queries.reshape(-1, head_width), grad_keys, grad_values)


def body_general(
    tokens,
    patch_counts,
    w_qkv,
    w_out,
    w_up,
    w_down,
    w_patch,
    w_class,
    norm_gains,
    mask_norm,
    grad_masks,
):
    gains_rows = norm_gains.T
    gathered = (
        lax.all_gather(w_qkv, ("head", "seq"), axis=0, tiled=True),
        lax.all_gather(w_out, ("head", "seq"), axis=0, tiled=True),
        lax.all_gather(w_up, ("head", "seq"), axis=0, tiled=True),
        lax.all_gather(w_down, ("head", "seq"), axis=0, tiled=True),
        lax.all_gather(w_patch, ("head", "seq"), axis=0, tiled=True),
        lax.all_gather(w_class, ("head", "seq"), axis=0, tiled=True),
        lax.all_gather(gains_rows, ("head", "seq"), axis=0, tiled=True),
    )
    full_qkv, full_out, full_up, full_down, full_patch, full_class, full_gains = gathered
    gain_one = full_gains[:, 0].astype(jnp.float32)
    gain_two = full_gains[:, 1].astype(jnp.float32)
    image_count = tokens.shape[0]
    row_count = tokens.shape[1]
    groups = lax.axis_size("head")
    slot_rows = row_count * groups
    local_heads = HEADS // groups
    position = lax.axis_index("head") * row_count + jnp.arange(row_count, dtype=jnp.int32)
    live_limit = CLS + patch_counts
    patch_rows = ((position[None, :] >= CLS) & (position[None, :] < live_limit[:, None])).astype(
        jnp.float32
    )[:, :, None]
    key_live = (jnp.arange(slot_rows, dtype=jnp.int32)[None, :] < live_limit[:, None])[:, None, :]
    root_flag = (lax.axis_index("head") == 0).astype(jnp.float32)
    scaling = DH ** (-0.5)
    blocks = slot_rows // 512
    normal_one, inverse_one = standardize(tokens)
    normed_one = (normal_one * gain_one).astype(jnp.bfloat16)
    triple = jnp.einsum(
        "ird,dt->irt", normed_one, full_qkv, preferred_element_type=jnp.float32
    ).astype(jnp.bfloat16)
    spread = lax.all_to_all(triple, "head", split_axis=2, concat_axis=1, tiled=True).reshape(
        image_count, slot_rows, local_heads, 3, DH
    )
    image = 0
    outputs = []
    image_logsums = []
    for number in range(local_heads):
        output, logsum = attend_head(
            spread[image, :, number, 0],
            spread[image, :, number, 1],
            spread[image, :, number, 2],
            key_live[image],
            scaling,
            blocks,
        )
        outputs.append(output)
        image_logsums.append(logsum)
    image_outputs = [jnp.stack(outputs, axis=1).reshape(slot_rows, local_heads * DH)]
    logsums = [image_logsums]
    attended_heads = jnp.stack(image_outputs, axis=0)
    attended = lax.all_to_all(attended_heads, "head", split_axis=1, concat_axis=2, tiled=True)
    second = tokens + jnp.einsum(
        "ire,ed->ird", attended, full_out, preferred_element_type=jnp.float32
    )
    normal_two, inverse_two = standardize(second)
    normed_two = (normal_two * gain_two).astype(jnp.bfloat16)
    hidden = jnp.einsum("ird,df->irf", normed_two, full_up, preferred_element_type=jnp.float32)
    gelu_exact = partial(jax.nn.gelu, approximate=False)
    active = gelu_exact(hidden).astype(jnp.bfloat16)
    residual = second + jnp.einsum(
        "irf,fd->ird", active, full_down, preferred_element_type=jnp.float32
    )
    rounded = residual.astype(jnp.bfloat16)
    patch_proj = jnp.einsum("ird,de->ire", rounded, full_patch, preferred_element_type=jnp.float32)
    patch_unit = (patch_proj * unit_scale(patch_proj)).astype(jnp.bfloat16)
    class_proj = jnp.einsum(
        "ird,de->ire", rounded[:, :CLS], full_class, preferred_element_type=jnp.float32
    )
    class_unit = (class_proj * unit_scale(class_proj)).astype(jnp.bfloat16)
    classes = spread_2(class_unit, "head", 0)
    products = jnp.einsum("ird,icd->irc", patch_unit, classes, preferred_element_type=jnp.float32)
    normal_mask, inverse_mask = standardize(products)
    class_masks = (normal_mask * mask_norm[0] + mask_norm[1]) * patch_rows
    upstream = grad_masks * patch_rows
    norm_grads = lax.psum(
        jnp.stack([jnp.sum(upstream * normal_mask, axis=(0, 1)), jnp.sum(upstream, axis=(0, 1))]),
        ("head", "seq"),
    )
    d_products = standard_back(normal_mask, inverse_mask, upstream * mask_norm[0]).astype(
        jnp.bfloat16
    )
    d_patch_unit = jnp.einsum(
        "irc,icd->ird", d_products, classes, preferred_element_type=jnp.float32
    )
    class_part = jnp.einsum(
        "irc,ird->icd", d_products, patch_unit, preferred_element_type=jnp.float32
    )
    d_class_unit = lax.psum(class_part.astype(jnp.bfloat16), "head").astype(jnp.float32)
    d_patch_proj = unit_back(patch_proj, d_patch_unit).astype(jnp.bfloat16)
    d_class_proj = (unit_back(class_proj, d_class_unit) * root_flag).astype(jnp.bfloat16)
    regathered = (
        lax.all_gather(w_qkv, ("head", "seq"), axis=0, tiled=True),
        lax.all_gather(w_out, ("head", "seq"), axis=0, tiled=True),
        lax.all_gather(w_up, ("head", "seq"), axis=0, tiled=True),
        lax.all_gather(w_down, ("head", "seq"), axis=0, tiled=True),
        lax.all_gather(w_patch, ("head", "seq"), axis=0, tiled=True),
        lax.all_gather(w_class, ("head", "seq"), axis=0, tiled=True),
        lax.all_gather(gains_rows, ("head", "seq"), axis=0, tiled=True),
    )
    back_qkv, back_out, back_up, back_down, back_patch, back_class, back_gains = regathered
    back_one = back_gains[:, 0].astype(jnp.float32)
    back_two = back_gains[:, 1].astype(jnp.float32)
    grad_patch = jnp.einsum(
        "ird,ire->de", rounded, d_patch_proj, preferred_element_type=jnp.float32
    )
    grad_class = jnp.einsum(
        "ird,ire->de", rounded[:, :CLS], d_class_proj, preferred_element_type=jnp.float32
    )
    d_residual = jnp.einsum(
        "ire,de->ird", d_patch_proj, back_patch, preferred_element_type=jnp.float32
    )
    class_term = jnp.einsum(
        "ire,de->ird", d_class_proj, back_class, preferred_element_type=jnp.float32
    )
    d_residual = d_residual.at[:, :CLS].add(class_term)
    d_branch = d_residual.astype(jnp.bfloat16)
    grad_down = jnp.einsum("irf,ird->fd", active, d_branch, preferred_element_type=jnp.float32)
    d_active = jnp.einsum("ird,fd->irf", d_branch, back_down, preferred_element_type=jnp.float32)
    gelu_pull = jax.vjp(gelu_exact, hidden)[1]
    d_hidden = gelu_pull(d_active)[0].astype(jnp.bfloat16)
    grad_up = jnp.einsum("ird,irf->df", normed_two, d_hidden, preferred_element_type=jnp.float32)
    d_normed_two = jnp.einsum("irf,df->ird", d_hidden, back_up, preferred_element_type=jnp.float32)
    d_second = d_residual + standard_back(normal_two, inverse_two, d_normed_two * back_two)
    grad_gain_two = jnp.sum(d_normed_two * normal_two, axis=(0, 1))
    d_mix = d_second.astype(jnp.bfloat16)
    grad_out = jnp.einsum("ire,ird->ed", attended, d_mix, preferred_element_type=jnp.float32)
    d_attended = jnp.einsum(
        "ird,ed->ire", d_mix, back_out, preferred_element_type=jnp.float32
    ).astype(jnp.bfloat16)
    d_heads = lax.all_to_all(d_attended, "head", split_axis=2, concat_axis=1, tiled=True).reshape(
        image_count, slot_rows, local_heads, DH
    )
    image = 0
    head_grads = []
    for number in range(local_heads):
        grad_queries, grad_keys, grad_values = attend_back(
            spread[image, :, number, 0],
            spread[image, :, number, 1],
            spread[image, :, number, 2],
            d_heads[image, :, number],
            logsums[image][number],
            key_live[image],
            scaling,
            blocks,
        )
        head_grads.append(jnp.stack([grad_queries, grad_keys, grad_values], axis=1))
    image_grads = [jnp.stack(head_grads, axis=1).reshape(slot_rows, local_heads * 3 * DH)]
    d_spread = jnp.stack(image_grads, axis=0).astype(jnp.bfloat16)
    d_triple = lax.all_to_all(d_spread, "head", split_axis=1, concat_axis=2, tiled=True)
    grad_qkv = jnp.einsum("ird,irt->dt", normed_one, d_triple, preferred_element_type=jnp.float32)
    d_normed_one = jnp.einsum("irt,dt->ird", d_triple, back_qkv, preferred_element_type=jnp.float32)
    grad_inputs = d_second + standard_back(normal_one, inverse_one, d_normed_one * back_one)
    grad_gain_one = jnp.sum(d_normed_one * normal_one, axis=(0, 1))
    grad_gains = jnp.stack([grad_gain_one, grad_gain_two], axis=1)
    reduced = (
        lax.psum_scatter(grad_qkv, ("head", "seq"), scatter_dimension=0, tiled=True),
        lax.psum_scatter(grad_out, ("head", "seq"), scatter_dimension=0, tiled=True),
        lax.psum_scatter(grad_up, ("head", "seq"), scatter_dimension=0, tiled=True),
        lax.psum_scatter(grad_down, ("head", "seq"), scatter_dimension=0, tiled=True),
        lax.psum_scatter(grad_patch, ("head", "seq"), scatter_dimension=0, tiled=True),
        lax.psum_scatter(grad_class, ("head", "seq"), scatter_dimension=0, tiled=True),
        lax.psum_scatter(grad_gains, ("head", "seq"), scatter_dimension=0, tiled=True),
    )
    return (
        class_masks,
        grad_inputs,
        reduced[0],
        reduced[1],
        reduced[2],
        reduced[3],
        reduced[4],
        reduced[5],
        reduced[6].T,
        norm_grads,
    )


MESH = pl.DeviceIdType.MESH
LOG2E = 1.4426950408889634
SLOTS = 16
FRONT_COPIES = 160
REAR_COPIES = 88


def matmul(left, right):
    return jnp.dot(left, right, preferred_element_type=jnp.float32)


def matmul_nt(left, right):
    return lax.dot_general(left, right, (((1,), (1,)), ((), ())), preferred_element_type=jnp.float32)


def matmul_tn(left, right):
    return lax.dot_general(left, right, (((0,), (0,)), ((), ())), preferred_element_type=jnp.float32)


def device(y, x, z, c):
    return (y * 2 + x, z * 2 + c)


class Links:
    def __init__(self, send_sem, recv_sem):
        head, seq = lax.axis_index("head"), lax.axis_index("seq")
        self.y, self.x, self.z, self.c = head // 2, head % 2, seq // 2, seq % 2
        y, x, z, c = self.y, self.x, self.z, self.c
        self.sibling = device(y, x, z, 1 - c)
        self.along_x = device(y, 1 - x, z, c)
        self.along_y = device(1 - y, x, z, c)
        self.across = device(1 - y, 1 - x, z, c)
        self.along_z = [device(y, x, (z + k) % 4, c) for k in (1, 2, 3)]
        self.send_sem, self.recv_sem, self.count, self.made, self.lines = send_sem, recv_sem, 0, [], []

    def greet(self):
        barrier = pltpu.get_barrier_semaphore()
        peers = [self.sibling, self.along_x, self.along_y, self.across] + self.along_z
        for peer in peers:
            pl.semaphore_signal(barrier, inc=1, device_id=peer, device_id_type=MESH)
        pl.semaphore_wait(barrier, len(peers))

    def plan(self, source, target, peer, sends=None, again=False):
        number = self.count - again
        self.count = number + 1
        copy = pltpu.make_async_remote_copy(
            src_ref=source,
            dst_ref=target,
            send_sem=self.send_sem.at[number],
            recv_sem=self.recv_sem.at[number],
            device_id=peer,
            device_id_type=MESH,
        )
        if not again:
            self.made.append((copy, sends))
        return copy

    def drain(self):
        for copy, sends in self.made:
            if sends is None:
                copy.wait_send()
            else:
                pl.when(sends)(copy.wait_send)
        for line in self.lines:
            line.drain()


class Stage:
    def __init__(self, links, moves, again=False):
        self.copies = [links.plan(*move, again=again) for move in moves]

    def start(self):
        for copy in self.copies:
            copy.start()

    def wait(self):
        for copy in self.copies:
            copy.wait_recv()


class Line:
    def __init__(self, links, piece, source=None):
        self.links, self.piece = links, piece
        self.source = piece(links.z) if source is None else source
        self.base = links.count
        links.count += 5
        links.lines.append(self)

    def copy(self, source, target, sent, landed):
        links = self.links
        return pltpu.make_async_remote_copy(
            src_ref=source,
            dst_ref=self.piece(landed),
            send_sem=links.send_sem.at[self.base + sent],
            recv_sem=links.recv_sem.at[self.base + landed],
            device_id=device(links.y, links.x, target, links.c),
            device_id_type=MESH,
        )

    def direct(self, target):
        z = self.links.z
        return (z != target) if target in (1, 2) else (z != target) & (z != 3 - target)

    def start(self):
        for target in (1, 2, 0, 3):

            @pl.when(self.direct(target))
            def _(target=target):
                self.copy(self.source, target, target, self.links.z).start()

    def relay(self):
        for at, end in ((2, 0), (1, 3)):

            @pl.when(self.links.z == at)
            def _(end=end):
                self.copy(self.source, 3 - end, 4, end).wait_recv()
                self.copy(self.piece(end), 3 - end, 4, end).start()

    def wait(self):
        z = self.links.z
        for origin in range(4):
            pending = z != origin
            if origin in (0, 3):
                pending = pending & (z != (2 if origin == 0 else 1))

            @pl.when(pending)
            def _(origin=origin):
                self.copy(self.source, 0, 0, origin).wait_recv()

    def drain(self):
        for target in range(4):

            @pl.when(self.direct(target))
            def _(target=target):
                self.copy(self.source, target, target, self.links.z).wait_send()

        @pl.when((self.links.z == 1) | (self.links.z == 2))
        def _():
            self.copy(self.source, 0, 4, 0).wait_send()


def at_slots(slot, events):
    for number, event in events.items():
        pl.when(slot == number)(event)


def front_kernel(scaling, *refs):
    live_ref, tokens, normal, tile, grad_masks, mask_norm = refs[:6]
    qkv_shard, out_shard, up_shard, down_shard, patch_shard, class_shard = refs[6:12]
    attended, heads_ref, logsum, rows_ref, gains_ref, qkv, class_masks, mask_sums = refs[12:20]
    normed_two, active, d_branch, d_hidden, rounded, d_patch, d_class, d_mix, d_second, d_attended = refs[20:30]
    full_out, ups, downs, full_patch, full_class, tiles, staged = refs[30:37]
    slope, second, normal_two, inverse_two, residual, patch_proj, class_proj, classes = refs[37:45]
    part_sent, part_got, back_sent, back_got, class_sent, class_got, d_residual = refs[45:52]
    send_sem, recv_sem, local_sem = refs[52:]
    links = Links(send_sem, recv_sem)
    y, x, z, c = links.y, links.x, links.z, links.c
    h = y * 2 + x
    q = y * (1 - c) + x * c
    rows = normal.shape[0]
    wide = qkv.shape[-1]
    narrow = staged.shape[1]
    heads = narrow // DH
    block = ups.shape[-1]
    slot_rows = rows * 4
    plane = [(links.across, 3 - h, 3), (links.along_x, y * 2 + 1 - x, 1), (links.along_y, (1 - y) * 2 + x, 2)]
    at_x, at_y = plane[1][1], plane[2][1]

    def columns(start, size):
        return pl.ds(pl.multiple_of(start, 128), size)

    def up_block(number):
        return up_shard.at[:, columns(number * block, block)]

    local = [
        pltpu.make_async_copy(source, target, local_sem.at[number])
        for number, (source, target) in zip(
            (0, 1, 2, 3, 4, 5, 7, 8),
            [
                (tile, tiles.at[y, x, z, c]),
                (qkv_shard.at[:, columns(h * wide, wide)], qkv.at[y, x, z, c]),
                (out_shard, full_out.at[y, x, z, c]),
                (down_shard, downs.at[c, q, z]),
                (up_block(x), ups.at[0, y, x, z, c]),
                (up_block(2 + y), ups.at[1, y, x, z, c]),
                (patch_shard, full_patch.at[y, x, z, c]),
                (class_shard, full_class.at[y, x, z, c]),
            ]
        )
    ]
    gain_core = Stage(links, [(tile, tiles.at[y, x, z, c], links.sibling)])
    gain_z = Stage(links, [(tiles.at[y, x, z], tiles.at[y, x, z], peer) for peer in links.along_z])
    gain_plane = Stage(links, [(tiles.at[y, x], tiles.at[y, x], peer) for peer, _, _ in plane])
    qkv_plane = Stage(
        links, [(qkv_shard.at[:, columns(p * wide, wide)], qkv.at[y, x, z, c], peer) for peer, p, _ in plane]
    )
    part = qkv.shape[4] // 2
    qkv_z = [Line(links, lambda at, k=k: qkv.at[:, :, at, c, k * part : (k + 1) * part]) for k in range(2)]
    qkv_core = Stage(links, [(qkv.at[:, :, :, c], qkv.at[:, :, :, c], links.sibling)])
    up_split = [
        Stage(links, [(up_block(1 - x), ups.at[0, y, x, z, c], links.along_x)]),
        Stage(links, [(up_block(2 + 1 - y), ups.at[1, y, x, z, c], links.along_y)]),
    ]
    up_z = [
        Line(links, lambda at: ups.at[0, y, :, at, c]),
        Line(links, lambda at: ups.at[1, :, x, at, c]),
    ]
    up_on = [
        Stage(links, [(ups.at[0, y, :, :, c], ups.at[0, y, :, :, c], links.along_y)]),
        Stage(links, [(ups.at[1, :, x, :, c], ups.at[1, :, x, :, c], links.along_x)]),
    ]
    up_core = [
        Stage(links, [(ups.at[k, :, :, :, c], ups.at[k, :, :, :, c], links.sibling)]) for k in range(2)
    ]
    some = down_shard.shape[0] // 4
    turned = device(y + (1 - c) * (1 - 2 * y), x + c * (1 - 2 * x), z, c)
    spans = [slice(k * some, (k + 1) * some) for k in range(4)]
    down_z = [Line(links, lambda at, k=k: downs.at[c, q, at, spans[k]], down_shard.at[spans[k]]) for k in range(4)]
    down_on = [
        Stage(links, [(downs.at[c, q, :, spans[k]], downs.at[c, q, :, spans[k]], turned)]) for k in range(4)
    ]
    down_core = [
        Stage(links, [(downs.at[c, :, :, span], downs.at[c, :, :, span], links.sibling)])
        for span in (slice(0, 2 * some), slice(2 * some, 4 * some))
    ]
    part = out_shard.shape[0] // 2
    out_z = Line(links, lambda at: full_out.at[y, x, at, c], out_shard)
    piece_a, piece_b = full_out.at[y, x, :, c, 0:part], full_out.at[y, x, :, c, part:]
    out_one = Stage(links, [(piece_a, piece_a, links.along_y), (piece_b, piece_b, links.along_x)])
    piece_a, piece_b = full_out.at[:, x, :, c, 0:part], full_out.at[y, :, :, c, part:]
    out_two = Stage(links, [(piece_a, piece_a, links.along_x), (piece_b, piece_b, links.along_y)])
    out_core = Stage(links, [(full_out.at[:, :, :, c], full_out.at[:, :, :, c], links.sibling)])
    patch_x = Stage(links, [(patch_shard, full_patch.at[y, x, z, c], links.along_x)])
    patch_y = Stage(links, [(full_patch.at[y, :, z, c],) * 2 + (links.along_y,)])
    class_y = Stage(links, [(class_shard, full_class.at[y, x, z, c], links.along_y)])
    class_x = Stage(links, [(full_class.at[:, x, z, c],) * 2 + (links.along_x,)])
    halves = [slice(k * part, (k + 1) * part) for k in range(2)]
    patch_z = [Line(links, lambda at, k=k: full_patch.at[:, :, at, c, halves[k]]) for k in range(2)]
    class_z = [Line(links, lambda at, k=k: full_class.at[:, :, at, c, halves[k]]) for k in range(2)]
    patch_core = Stage(links, [(full_patch.at[:, :, :, c],) * 2 + (links.sibling,)])
    class_core = Stage(links, [(full_class.at[:, :, :, c],) * 2 + (links.sibling,)])
    beside = (links.along_x, links.along_y)
    here, there = slice(0, rows), slice(rows, 2 * rows)
    normed_out = [Stage(links, [(normed_two.at[k, here], normed_two.at[k, there], beside[k])]) for k in range(2)]
    branch_out = [Stage(links, [(d_branch.at[k, here], d_branch.at[k, there], beside[k])]) for k in range(2)]
    halved = [slice(0, rows // 2), slice(rows // 2, rows)]
    part_back = [
        [Stage(links, [(part_sent.at[k, at], part_got.at[k, at], beside[k])]) for at in halved] for k in range(2)
    ]
    grad_back = [
        [Stage(links, [(back_sent.at[k, at], back_got.at[k, at], beside[k])]) for at in halved] for k in range(2)
    ]
    tall = class_proj.shape[0]
    unit_out = [links.plan(classes.at[0:tall], classes.at[0:tall], peer, h == 0) for peer, _, _ in plane]
    class_back = [
        links.plan(class_sent, class_got.at[rel - 1], peer, h == rel) for peer, _, rel in plane
    ]
    middle = rows // 2
    strips = [slice(0, middle), slice(middle, rows)]
    rows_x = [Stage(links, [(rows_ref.at[h, strips[k]],) * 2 + (links.along_x,)]) for k in (0, 1)]
    rows_y = [Stage(links, [(rows_ref.at[h, strips[k]],) * 2 + (links.along_y,)]) for k in (1, 0)]
    piece_a, piece_b = rows_ref.at[at_x, strips[0]], rows_ref.at[at_y, strips[1]]
    relay_y = Stage(links, [(piece_a, piece_a, links.along_y)])
    relay_x = Stage(links, [(piece_b, piece_b, links.along_x)])

    for copy in local:
        copy.start()
    links.greet()
    for stage in (gain_core, qkv_plane, *up_split, out_z, patch_x, class_y):
        stage.start()
    local[0].wait()
    gain_core.wait()
    gain_z.start()
    gain_z.wait()
    gain_plane.start()
    local[1].wait()
    qkv_plane.wait()
    for line in qkv_z:
        line.start()
    gain_plane.wait()
    for j in range(8):
        piece = tiles[j // 4, j // 2 % 2, (j % 2) * 2, 0].astype(jnp.float32)
        for i in range(1, 4):
            piece = piece + tiles[j // 4, j // 2 % 2, (j % 2) * 2 + i // 2, i % 2].astype(jnp.float32)
        gains_ref[:, j * 128 : (j + 1) * 128] = piece[0:8]
    rows_ref[h] = (normal[...] * gains_ref[0:1, :]).astype(jnp.bfloat16)
    for stage in (rows_x[0], rows_y[0], rows_x[1], rows_y[1]):
        stage.start()
    for line in (out_z, *qkv_z):
        line.relay()
    rows_x[0].wait()
    relay_y.start()
    rows_y[0].wait()
    relay_x.start()
    local[6].wait()
    patch_x.wait()
    patch_y.start()
    local[7].wait()
    class_y.wait()
    class_x.start()
    for line in qkv_z:
        line.wait()
    qkv_core.start()
    for k in range(2):
        local[4 + k].wait()
        up_split[k].wait()
        up_z[k].start()
    out_z.wait()
    local[2].wait()

    def project(p):
        weight = qkv[...].reshape(rows * 4, wide)
        piece = jnp.dot(rows_ref[p], weight, preferred_element_type=jnp.float32).astype(jnp.bfloat16)
        at = pl.ds(pl.multiple_of(p * rows, rows), rows)
        for number in range(3 * heads):
            heads_ref[number, at, :] = piece[:, number * DH : (number + 1) * DH]

    qkv_core.wait()
    project(h)
    rows_x[1].wait()
    project(at_x)
    rows_y[1].wait()
    project(at_y)
    out_one.start()
    relay_y.wait()
    relay_x.wait()
    project(3 - h)

    live = live_ref[0]
    key_live = lax.broadcasted_iota(jnp.int32, (slot_rows, 1), 0) < live
    returned = links.count - 1
    assert returned + 4 <= FRONT_COPIES

    def back(rel):
        peer = h + (rel % 2) * (1 - 2 * x) + (rel // 2) * (2 - 4 * y)
        return pltpu.make_async_remote_copy(
            src_ref=staged.at[pl.ds(pl.multiple_of(peer * rows, rows), rows), :],
            dst_ref=attended.at[:, columns(h * narrow, narrow)],
            send_sem=send_sem.at[returned + rel],
            recv_sem=recv_sem.at[returned + rel],
            device_id=(peer, z * 2 + c),
            device_id_type=MESH,
        )

    def up_next(k):
        up_z[k].wait()
        up_on[k].start()

    def up_end(k):
        up_on[k].wait()
        up_core[k].start()

    def out_next():
        out_one.wait()
        out_two.start()

    def out_end():
        out_two.wait()
        out_core.start()

    def down_begin(k):
        if k == 0:
            local[3].wait()
        down_z[k].start()
        down_z[k + 1].start()

    def down_next(k):
        down_z[k].wait()
        down_on[k].start()

    def down_half(k):
        down_on[2 * k].wait()
        down_on[2 * k + 1].wait()
        down_core[k].start()

    events = {
        0: up_z[0].relay,
        2: partial(up_next, 0),
        7: up_z[1].relay,
        8: partial(down_begin, 0),
        9: out_next,
        12: partial(up_next, 1),
        13: partial(down_begin, 2),
        15: out_end,
    }

    def tile_body(slot, carry):
        turn, number = slot // 4, slot % 4
        rel = 3 - turn
        peer = h + (rel % 2) * (1 - 2 * x) + (rel // 2) * (2 - 4 * y)
        at = pl.ds(pl.multiple_of(peer * rows, rows), rows)
        at_slots(slot, events)
        queries = heads_ref[3 * number, at, :]
        keys = heads_ref[3 * number + 1]
        values = heads_ref[3 * number + 2]
        scores = lax.dot_general(keys, queries, (((1,), (1,)), ((), ())), preferred_element_type=jnp.float32)
        scores = jnp.where(key_live, scores * (scaling * LOG2E), -1e30)
        highest = jnp.max(scores, axis=0, keepdims=True)
        raw = jnp.exp2(scores - highest)
        totals = jnp.sum(raw, axis=0, keepdims=True)
        weights = (raw * (1.0 / totals)).astype(jnp.bfloat16)
        mixed = lax.dot_general(
            values, weights, (((0,), (0,)), ((), ())), preferred_element_type=jnp.float32
        )
        mixed = mixed.T.astype(jnp.bfloat16)
        for which in range(4):

            @pl.when(number == which)
            def _(which=which):
                staged[at, which * DH : (which + 1) * DH] = mixed

        logsum[number, :, at] = highest + jnp.log2(totals)

        @pl.when((number == 3) & (rel > 0))
        def _():
            back(rel).start()

        return carry

    lax.fori_loop(0, SLOTS, tile_body, 0)
    own = pltpu.make_async_copy(
        staged.at[pl.ds(pl.multiple_of(h * rows, rows), rows), :],
        attended.at[:, columns(h * narrow, narrow)],
        local_sem.at[6],
    )
    own.start()
    patch_y.wait()
    class_x.wait()
    for line in patch_z:
        line.start()
    down_z[0].relay()
    down_z[1].relay()
    up_end(0)
    down_next(0)
    down_next(1)
    for rel in (3, 2, 1):
        back(rel).wait()
    own.wait()
    out_core.wait()

    def whole(weight):
        return weight[...].reshape(-1, weight.shape[-1])

    def norm(values):
        center = values - jnp.mean(values, axis=-1, keepdims=True)
        inverse = lax.rsqrt(jnp.mean(center * center, axis=-1, keepdims=True) + 1e-05)
        return center * inverse, inverse

    features = tokens.shape[1]
    second[...] = tokens[...] + matmul(attended[...], whole(full_out))
    value, inverse = norm(second[...])
    normal_two[...] = value
    inverse_two[...] = jnp.broadcast_to(inverse, inverse_two.shape)
    value = (value * gains_ref[1:2, :]).astype(jnp.bfloat16)
    for k in range(2):
        normed_two[k, here] = value
        normed_out[k].start()
    down_z[2].relay()
    down_z[3].relay()
    for line in class_z:
        line.start()
    up_end(1)
    down_half(0)
    down_next(2)
    down_next(3)
    for k in range(2):
        up_core[k].wait()
    wide_step = 256

    def forward(k, at, size):
        def step(j, carry):
            span = pl.ds(pl.multiple_of(j * wide_step, wide_step), wide_step)
            weight = ups[k, :, :, :, :, :, span].reshape(features, wide_step)
            hidden = matmul(normed_two[k, at], weight)
            spread = 0.5 + 0.5 * lax.erf(hidden * 0.7071067811865476)
            density = jnp.exp(hidden * hidden * -0.5) * 0.3989422804014327
            active[k, at, span] = (hidden * spread).astype(jnp.bfloat16)
            slope[k, at, span] = spread + hidden * density
            return carry

        lax.fori_loop(0, block // wide_step, step, 0)

    forward(0, here, rows)
    patch_z[0].relay()
    forward(1, here, rows)
    patch_z[1].relay()
    down_half(1)
    for stage in down_core:
        stage.wait()
    for k in range(2):
        normed_out[k].wait()
        for half, at in enumerate(halved):
            low = slice(rows + at.start, rows + at.stop)
            forward(k, low, rows // 2)
            part_sent[k, at] = matmul(active[k, low], whole(downs.at[k])).astype(jnp.bfloat16)
            part_back[k][half].start()
    for line in class_z:
        line.relay()
    residual[...] = second[...] + (
        matmul(active[0, here], whole(downs.at[0])) + matmul(active[1, here], whole(downs.at[1]))
    )
    for line in patch_z:
        line.wait()
    patch_core.start()
    for line in class_z:
        line.wait()
    class_core.start()
    for k in range(2):
        for stage in part_back[k]:
            stage.wait()
    residual[...] = residual[...] + (part_got[0].astype(jnp.float32) + part_got[1].astype(jnp.float32))
    rounded[...] = residual[...].astype(jnp.bfloat16)
    patch_core.wait()
    class_core.wait()

    class_proj[...] = matmul(rounded[0:tall, :], whole(full_class))

    @pl.when(h == 0)
    def _():
        value = class_proj[...]
        row = lax.broadcasted_iota(jnp.int32, (tall, 1), 0)
        classes[0:tall] = jnp.where(row < CLS, value * unit_scale(value), 0.0).astype(jnp.bfloat16)
        for copy in unit_out:
            copy.start()

    classes[tall:] = jnp.zeros((classes.shape[0] - tall, features), jnp.bfloat16)
    patch_proj[...] = matmul(rounded[...], whole(full_patch))
    factor = unit_scale(patch_proj[...])
    patch_unit = (patch_proj[...] * factor).astype(jnp.bfloat16)
    for copy, (_, _, rel) in zip(unit_out, plane):
        pl.when(h == rel)(copy.wait_recv)
    products = matmul_nt(patch_unit, classes[...])
    lane = lax.broadcasted_iota(jnp.int32, products.shape, 1)
    position = h * rows + lax.broadcasted_iota(jnp.int32, (rows, 1), 0)
    patch_rows = ((position >= CLS) & (position < live)).astype(jnp.float32)

    def class_mean(values):
        return jnp.sum(values, axis=-1, keepdims=True) * (1.0 / CLS)

    center = jnp.where(lane < CLS, products - class_mean(products), 0.0)
    inverse = lax.rsqrt(class_mean(center * center) + 1e-05)
    mask_normal = center * inverse
    class_masks[...] = (mask_normal * mask_norm[0:1, :] + mask_norm[1:2, :]) * patch_rows
    upstream = grad_masks[...] * patch_rows
    mask_sums[...] = jnp.zeros_like(mask_sums)
    mask_sums[0:1, :] = jnp.sum(upstream * mask_normal, axis=0, keepdims=True)
    mask_sums[1:2, :] = jnp.sum(upstream, axis=0, keepdims=True)
    upstream = upstream * mask_norm[0:1, :]
    upstream = inverse * (upstream - class_mean(upstream) - mask_normal * class_mean(upstream * mask_normal))
    d_products = jnp.where(lane < CLS, upstream, 0.0).astype(jnp.bfloat16)
    class_part = matmul_tn(d_products, patch_unit)[0:tall]
    class_sent[...] = class_part.astype(jnp.bfloat16)
    for copy, (_, _, rel) in zip(class_back, plane):
        pl.when(h == rel)(copy.start)
    upstream = matmul(d_products, classes[...])
    direct = patch_proj[...] * factor
    upstream = factor * (upstream - direct * jnp.sum(upstream * direct, axis=-1, keepdims=True))
    d_patch[...] = upstream.astype(jnp.bfloat16)
    d_residual[...] = matmul_nt(d_patch[...], whole(full_patch))
    d_class[...] = jnp.zeros_like(d_class)

    @pl.when(h == 0)
    def _():
        for copy in class_back:
            copy.wait_recv()
        upstream = class_part + (
            class_got[0].astype(jnp.float32) + class_got[1].astype(jnp.float32) + class_got[2].astype(jnp.float32)
        )
        row = lax.broadcasted_iota(jnp.int32, (tall, 1), 0)
        d_class[...] = jnp.where(row < CLS, unit_back(class_proj[...], upstream), 0.0).astype(jnp.bfloat16)
        d_residual[0:tall] = d_residual[0:tall] + matmul_nt(d_class[...], whole(full_class))

    value = d_residual[...].astype(jnp.bfloat16)
    for k in range(2):
        d_branch[k, here] = value
        branch_out[k].start()

    def backward(k, at):
        for j in range(block // wide_step):
            weight = downs[k, j // 2, 2 * (j % 2) : 2 * (j % 2) + 2].reshape(wide_step, features)
            span = slice(j * wide_step, (j + 1) * wide_step)
            d_hidden[k, at, span] = (matmul_nt(d_branch[k, at], weight) * slope[k, at, span]).astype(jnp.bfloat16)

    backward(0, here)
    backward(1, here)
    for k in range(2):
        branch_out[k].wait()
        for half, at in enumerate(halved):
            low = slice(rows + at.start, rows + at.stop)
            backward(k, low)
            back_sent[k, at] = matmul_nt(d_hidden[k, low], whole(ups.at[k])).astype(jnp.bfloat16)
            grad_back[k][half].start()
    upstream = matmul_nt(d_hidden[0, here], whole(ups.at[0])) + matmul_nt(d_hidden[1, here], whole(ups.at[1]))
    for k in range(2):
        for stage in grad_back[k]:
            stage.wait()
    upstream = upstream + (back_got[0].astype(jnp.float32) + back_got[1].astype(jnp.float32))
    upstream = upstream * gains_ref[1:2, :]
    value = normal_two[...]
    middle = jnp.mean(upstream, axis=-1, keepdims=True)
    along = jnp.mean(upstream * value, axis=-1, keepdims=True)
    d_second[...] = d_residual[...] + inverse_two[:, 0:1] * (upstream - middle - value * along)
    d_mix[...] = d_second[...].astype(jnp.bfloat16)
    d_attended[...] = matmul_nt(d_mix[...], whole(full_out)).astype(jnp.bfloat16)
    links.drain()


def front(live, tokens, normal, tile, grad_masks, mask_norm, shards, scaling):
    rows, features = normal.shape
    vmem, hbm = pl.BlockSpec(memory_space=pltpu.VMEM), pl.BlockSpec(memory_space=pl.ANY)
    w_qkv, w_out, w_up, w_down, w_patch, w_class = shards
    wide = w_qkv.shape[1] // 4
    heads = wide // (3 * DH)
    block = w_up.shape[1] // 4
    lanes = grad_masks.shape[1]
    tall = -(-CLS // 16) * 16
    low, single = jnp.bfloat16, jnp.float32
    outs = [
        ((rows, features), low),
        ((3 * heads, 4 * rows, DH), low),
        ((heads, 1, 4 * rows), single),
        ((4, rows, features), low),
        ((8, features), single),
        ((2, 2, 4, 2, w_qkv.shape[0], wide), low),
        ((rows, lanes), single),
        ((8, lanes), single),
        ((2, 2 * rows, features), low),
        ((2, 2 * rows, block), low),
        ((2, 2 * rows, features), low),
        ((2, 2 * rows, block), low),
        ((rows, features), low),
        ((rows, features), low),
        ((tall, features), low),
        ((rows, features), low),
        ((rows, features), single),
        ((rows, features), low),
    ]
    scratch = [
        ((2, 2, 4, 2) + w_out.shape, low),
        ((2, 2, 2, 4, 2, w_up.shape[0], block), low),
        ((2, 2, 4) + w_down.shape, low),
        ((2, 2, 4, 2) + w_patch.shape, low),
        ((2, 2, 4, 2) + w_class.shape, low),
        ((2, 2, 4, 2) + tile.shape, low),
        ((4 * rows, wide // 3), low),
        ((2, 2 * rows, block), single),
        ((rows, features), single),
        ((rows, features), single),
        ((rows, 128), single),
        ((rows, features), single),
        ((rows, features), single),
        ((tall, features), single),
        ((lanes, features), low),
        ((2, rows, features), low),
        ((2, rows, features), low),
        ((2, rows, features), low),
        ((2, rows, features), low),
        ((tall, features), low),
        ((3, tall, features), low),
        ((rows, features), single),
    ]
    return pl.pallas_call(
        partial(front_kernel, scaling),
        out_shape=[jax.ShapeDtypeStruct(*out) for out in outs],
        in_specs=[pl.BlockSpec(memory_space=pltpu.SMEM)] + [vmem] * 5 + [hbm] * 6,
        out_specs=[vmem] * len(outs),
        scratch_shapes=[pltpu.VMEM(*shape) for shape in scratch]
        + [
            pltpu.SemaphoreType.DMA((FRONT_COPIES,)),
            pltpu.SemaphoreType.DMA((FRONT_COPIES,)),
            pltpu.SemaphoreType.DMA((9,)),
        ],
        compiler_params=pltpu.CompilerParams(
            collective_id=1, has_side_effects=True, vmem_limit_bytes=60 * 2**20
        ),
        name="front",
    )(live, tokens, normal, tile, grad_masks, mask_norm, *shards)


class LineSum:
    def __init__(self, links, piece, got):
        self.links, self.piece, self.got = links, piece, got
        self.base = links.count
        links.count += 5
        links.lines.append(self)

    def copy(self, piece, target, slot, sent):
        links = self.links
        return pltpu.make_async_remote_copy(
            src_ref=self.piece(piece),
            dst_ref=self.got.at[slot],
            send_sem=links.send_sem.at[self.base + sent],
            recv_sem=links.recv_sem.at[self.base + slot],
            device_id=device(links.y, links.x, target, links.c),
            device_id_type=MESH,
        )

    def start(self):
        z = self.links.z
        for target, end, middle in ((3, 0, 1), (0, 3, 2)):

            @pl.when(z == end)
            def _(target=target, middle=middle):
                self.copy(target, middle, 4, target).start()

        for target in range(4):
            direct = z != target
            if target in (0, 3):
                direct = z == (1 if target == 0 else 2)

            @pl.when(direct)
            def _(target=target):
                self.copy(target, target, z, target).start()

    def relay(self):
        z = self.links.z
        for target, middle in ((3, 1), (0, 2)):

            @pl.when(z == middle)
            def _(target=target, middle=middle):
                self.copy(target, target, 4, target).wait_recv()
                own = self.piece(target)
                own[...] = own[...] + self.got[4]
                self.copy(target, target, middle, target).start()

    def collect(self, add):
        z = self.links.z
        for origin in range(4):
            comes = z != origin
            if origin in (0, 3):
                comes = comes & (z != 3 - origin)

            @pl.when(comes)
            def _(origin=origin):
                self.copy(0, 0, origin, 0).wait_recv()
                add(origin)

    def drain(self):
        for target in range(4):

            @pl.when(self.links.z != target)
            def _(target=target):
                self.copy(target, target, 0, target).wait_send()


class Sum:
    def __init__(self, links, partial_ref, total, sib, one, two, three, local, kind):
        y, x, z, c = links.y, links.x, links.z, links.c
        self.links, self.total, self.sib, self.one, self.two, self.three = links, total, sib, one, two, three
        self.kind = kind
        self.q = y * (1 - c) + x * c
        if kind == "down":
            self.choices = [
                (
                    c == k,
                    pltpu.make_async_copy(partial_ref[k], total, local),
                    Stage(links, [(partial_ref[1 - k], sib, links.sibling)], again=k == 1),
                )
                for k in range(2)
            ]
            self.local, self.core = self.choices[0][1:]
        else:
            self.choices = None
            self.local = pltpu.make_async_copy(partial_ref.at[:, :, :, c], total, local)
            self.core = Stage(links, [(partial_ref.at[:, :, :, 1 - c], sib, links.sibling)])
        if kind in ("up_y", "all_y"):
            self.first = Stage(links, [(total.at[1 - y], one, links.along_y)])
            self.kept = lambda i, j: (y, i, j)
        elif kind in ("up_x", "all_x"):
            self.first = Stage(links, [(total.at[:, 1 - x], one, links.along_x)])
            self.kept = lambda i, j: (i, x, j)
        else:
            turned = device(y + (1 - c) * (1 - 2 * y), x + c * (1 - 2 * x), z, c)
            self.first = Stage(links, [(total.at[1 - self.q], one, turned)])
            self.line = LineSum(links, lambda at: total.at[self.q, at], three)
        if kind == "up_y":
            self.line = LineSum(links, lambda at: total.at[y, :, at], three)
            self.last = Stage(links, [(total.at[y, 1 - x, z], two, links.along_x)])
        elif kind == "up_x":
            self.line = LineSum(links, lambda at: total.at[:, x, at], three)
            self.last = Stage(links, [(total.at[1 - y, x, z], two, links.along_y)])
        elif kind == "all_x":
            self.second = Stage(links, [(total.at[1 - y, x], two, links.along_y)])
        elif kind == "all_y":
            self.second = Stage(links, [(total.at[y, 1 - x], two, links.along_x)])
        if kind in ("all_x", "all_y"):
            self.line = LineSum(links, lambda at: total.at[y, x, at], three)

    def begin(self):
        if self.choices is None:
            self.core.start()
            self.local.start()
            return
        for taken, local, core in self.choices:

            @pl.when(taken)
            def _(local=local, core=core):
                core.start()
                local.start()

    def add(self, pairs, count):
        total = self.total

        def body(i, carry):
            index, extra = pairs(i)
            total[index] = total[index] + extra
            return carry

        lax.fori_loop(0, count, body, 0)

    def run_first(self):
        self.local.wait()
        self.core.wait()
        sib = self.sib
        if self.kind == "down":
            self.add(lambda i: ((i // 4, i % 4), sib[i // 4, i % 4]), 8)
        else:
            self.add(lambda i: ((i // 8, i // 4 % 2, i % 4), sib[i // 8, i // 4 % 2, i % 4]), 16)
        self.first.start()

    def run_second(self):
        self.first.wait()
        one = self.one
        if self.kind == "down":
            self.add(lambda i: ((self.q, i), one[i]), 4)
        else:
            self.add(lambda i: (self.kept(i // 4, i % 4), one[i // 4, i % 4]), 8)
        if self.kind in ("all_x", "all_y"):
            self.second.start()
        else:
            self.line.start()

    def run_third(self):
        self.second.wait()
        y, x, two = self.links.y, self.links.x, self.two
        self.add(lambda i: ((y, x, i), two[i]), 4)
        self.line.start()

    def run_last(self):
        z, total, got = self.links.z, self.total, self.three

        def add(slot):
            for i in range(2):
                index = self.kept(i, z)
                total[index] = total[index] + got[slot, i]

        self.line.collect(add)
        self.last.start()

    def finish(self, out):
        y, x, z = self.links.y, self.links.x, self.links.z
        if self.kind in ("up_y", "up_x"):
            self.last.wait()
            along_x = self.kind == "up_y"
            mine = x if along_x else y
            for number, part in ((mine, self.total[y, x, z]), (1 - mine, self.two[...])):
                for j in range(8):
                    place = (j // 4 * 2 + number) if along_x else (number * 2 + j // 4)
                    start = (place * 4 + j % 4) * 256 + (0 if along_x else 128)
                    at = pl.ds(pl.multiple_of(start, 128), 128)
                    out[:, at] = part[:, j * 128 : (j + 1) * 128].astype(jnp.float32)
            return
        out[...] = (self.total[self.q, z] if self.kind == "down" else self.total[y, x, z]).astype(jnp.float32)

        def add(slot):
            out[...] = out[...] + self.three[slot].astype(jnp.float32)

        self.line.collect(add)


def rear_kernel(scaling, *refs):
    live_ref, d_rows, heads_ref, logsum, rows_ref, qkv, small_ref = refs[:7]
    partials = (refs[7], refs[8], refs[9:11]) + tuple(refs[11:14])
    d_normed, g_qkv, g_up, g_down, g_out, g_patch, g_class, small_out = refs[14:22]
    at = 22
    d_out, d_heads, d_spread, grad_keys, grad_values = refs[at : at + 5]
    d_sent, d_got, q_part, q_sib, q_z, q_plane = refs[at + 5 : at + 11]
    small_own, small_got, send_sem, recv_sem, local_sem = refs[at + 11 : at + 16]
    scratch = refs[at + 16 :]
    links = Links(send_sem, recv_sem)
    y, x, z, c = links.y, links.x, links.z, links.c
    h = y * 2 + x
    rows, features = d_rows.shape
    slot_rows = rows * 4
    narrow = d_out.shape[1]
    heads = narrow // DH
    wide = 3 * narrow
    plane = [(links.across, 3 - h, 3), (links.along_x, y * 2 + 1 - x, 1), (links.along_y, (1 - y) * 2 + x, 2)]

    def columns(start, size):
        return pl.ds(pl.multiple_of(start, 128), size)

    def block(p):
        return pl.ds(pl.multiple_of(p * rows, rows), rows)

    spread_out = Stage(
        links, [(d_rows.at[:, columns(p * narrow, narrow)], d_out.at[block(h), :], peer) for peer, p, _ in plane]
    )
    own = pltpu.make_async_copy(d_rows.at[:, columns(h * narrow, narrow)], d_out.at[block(h), :], local_sem.at[0])
    kinds = ("up_y", "up_x", "down", "all_x", "all_x", "all_y")
    sums = [
        Sum(links, partials[i], *scratch[5 * i : 5 * i + 5], local_sem.at[1 + i], kinds[i]) for i in range(6)
    ]
    back = [Stage(links, [(d_sent.at[rel - 1], d_got.at[rel - 1], peer)]) for peer, _, rel in plane]
    q_core = Stage(links, [(q_part.at[:, :, :, 1 - c], q_sib, links.sibling)])
    q_line = LineSum(links, lambda at: q_part.at[:, :, at, c], q_z)
    q_across = Stage(
        links, [(q_part.at[p // 2, p % 2, z, c], q_plane.at[h], peer) for peer, p, _ in plane]
    )
    small_core = Stage(links, [(small_own.at[0], small_got.at[0], links.sibling)])
    small_x = Stage(links, [(small_own.at[1], small_got.at[1], links.along_x)])
    small_y = Stage(links, [(small_own.at[2], small_got.at[2], links.along_y)])
    small_z = Stage(links, [(small_own.at[3], small_got.at[3 + z], peer) for peer in links.along_z])

    links.greet()
    spread_out.start()
    own.start()
    for entry in sums:
        entry.begin()
    small_own[0] = small_ref[...]
    small_core.start()
    own.wait()
    spread_out.wait()
    live = live_ref[0]
    key_live = lax.broadcasted_iota(jnp.int32, (slot_rows, 1), 0) < live
    up_y, up_x, down, out, patch, classes = sums
    assert links.count <= REAR_COPIES

    def small_step(stage, number, following):
        def run():
            stage.wait()
            small_own[number + 1] = small_own[number] + small_got[number]
            if number == 2:
                small_got[3 + z] = small_own[3]
            following.start()

        return run

    def both(*steps):
        def run():
            for step in steps:
                step()

        return run

    events = {
        0: up_y.run_first,
        1: up_x.run_first,
        2: down.run_first,
        3: small_step(small_core, 0, small_x),
        4: patch.run_first,
        5: classes.run_first,
        6: out.run_first,
        7: small_step(small_x, 1, small_y),
        8: both(up_y.run_second, up_x.run_second),
        9: small_step(small_y, 2, small_z),
        11: both(up_y.line.relay, up_x.line.relay),
        13: down.run_second,
        14: patch.run_second,
        15: both(up_y.run_last, up_x.run_last),
    }

    def tile_body(slot, carry):
        number, turn = slot // 4, slot % 4
        at_slots(slot, events)
        at = block(turn)

        @pl.when(turn == 0)
        def _():
            grad_keys[...] = jnp.zeros_like(grad_keys)
            grad_values[...] = jnp.zeros_like(grad_values)

        queries = heads_ref[3 * number, at, :]
        keys = heads_ref[3 * number + 1]
        values = heads_ref[3 * number + 2]
        grads = d_heads[number, at, :]
        scores = lax.dot_general(keys, queries, (((1,), (1,)), ((), ())), preferred_element_type=jnp.float32)
        powers = scores * (scaling * LOG2E) - logsum[number, :, at]
        weights = jnp.where(key_live, jnp.exp2(powers), 0.0)
        grad_values[...] += jnp.dot(weights.astype(jnp.bfloat16), grads, preferred_element_type=jnp.float32)
        grad_weights = lax.dot_general(
            values, grads, (((1,), (1,)), ((), ())), preferred_element_type=jnp.float32
        )
        deltas = jnp.sum(grad_weights * weights, axis=0, keepdims=True)
        grad_scores = (weights * (grad_weights - deltas)).astype(jnp.bfloat16)
        grad_keys[...] += jnp.dot(grad_scores, queries, preferred_element_type=jnp.float32)
        grad_queries = lax.dot_general(
            keys, grad_scores, (((0,), (0,)), ((), ())), preferred_element_type=jnp.float32
        )
        d_heads[4 + 3 * number, at, :] = (grad_queries.T * scaling).astype(jnp.bfloat16)

        @pl.when(turn == 3)
        def _():
            d_heads[5 + 3 * number] = (grad_keys[...] * scaling).astype(jnp.bfloat16)
            d_heads[6 + 3 * number] = grad_values[...].astype(jnp.bfloat16)

        return carry

    for number in range(heads):
        d_heads[number] = d_out[:, number * DH : (number + 1) * DH]
    lax.fori_loop(0, SLOTS, tile_body, 0)
    for number in range(3 * heads):
        d_spread[:, number * DH : (number + 1) * DH] = d_heads[4 + number]
    per = features // 4
    for j in range(4):
        left = jnp.concatenate([rows_ref[p, :, j * per : (j + 1) * per] for p in range(4)], axis=0)
        piece = lax.dot_general(
            left, d_spread[...], (((0,), (0,)), ((), ())), preferred_element_type=jnp.float32
        ).astype(jnp.bfloat16)
        q_part[j // 2, j % 2] = piece.reshape(4, 2, per // 8, wide)
    q_core.start()
    weight = qkv[...].reshape(features, wide)
    for (_, p, rel), stage in zip(plane, back):
        piece = lax.dot_general(
            d_spread[block(p), :], weight, (((1,), (1,)), ((), ())), preferred_element_type=jnp.float32
        )
        d_sent[rel - 1] = piece.astype(jnp.bfloat16)
        stage.start()
    q_core.wait()

    def add_sib(i, carry):
        index = (i // 8, i // 4 % 2, i % 4)
        q_part[(*index, c)] = q_part[(*index, c)] + q_sib[index]
        return carry

    lax.fori_loop(0, 16, add_sib, 0)
    q_line.start()
    d_normed[...] = lax.dot_general(
        d_spread[block(h), :], weight, (((1,), (1,)), ((), ())), preferred_element_type=jnp.float32
    )
    down.line.relay()
    q_line.relay()
    patch.run_third()
    classes.run_second()
    out.run_second()
    patch.line.relay()
    classes.run_third()
    out.run_third()
    classes.line.relay()

    def add_line(slot):
        for i in range(4):
            index = (i // 2, i % 2)
            q_part[(*index, z, c)] = q_part[(*index, z, c)] + q_z[(slot, *index)]

    q_line.collect(add_line)
    q_across.start()
    out.line.relay()
    small_z.wait()
    small_out[...] = small_got[3] + small_got[4] + small_got[5] + small_got[6]
    down.finish(g_down)
    up_y.finish(g_up)
    up_x.finish(g_up)
    patch.finish(g_patch)
    classes.finish(g_class)
    out.finish(g_out)
    q_across.wait()
    g_qkv[:, columns(h * wide, wide)] = q_part[y, x, z, c].astype(jnp.float32)
    for _, p, _ in plane:
        g_qkv[:, columns(p * wide, wide)] = q_plane[p].astype(jnp.float32)
    for stage in back:
        stage.wait()
    d_normed[...] = d_normed[...] + (
        d_got[0].astype(jnp.float32) + d_got[1].astype(jnp.float32) + d_got[2].astype(jnp.float32)
    )
    links.drain()


def rear(live, d_rows, heads_qkv, logsum, rows_all, qkv, small, partials, scaling):
    rows, features = d_rows.shape
    slot_rows = 4 * rows
    narrow = features // 4
    heads = narrow // DH
    wide = 3 * narrow
    vmem, hbm = pl.BlockSpec(memory_space=pltpu.VMEM), pl.BlockSpec(memory_space=pl.ANY)
    low = jnp.bfloat16
    up, _, down, _, *rest = [a.shape[-2:] for a in partials]
    shard = (features // 32, wide)
    buffers = []
    for _ in range(2):
        buffers += [(2, 2, 4) + up, (2, 2, 4) + up, (2, 4) + up, up, (5, 2) + up]
    buffers += [(2, 4) + down, (2, 4) + down, (4,) + down, (8, 128), (5,) + down]
    for shape in rest:
        buffers += [(2, 2, 4) + shape, (2, 2, 4) + shape, (2, 4) + shape, (4,) + shape, (5,) + shape]
    single = jnp.float32
    return pl.pallas_call(
        partial(rear_kernel, scaling),
        out_shape=[
            jax.ShapeDtypeStruct((rows, features), single),
            jax.ShapeDtypeStruct((features // 32, 4 * wide), single),
            jax.ShapeDtypeStruct((up[0], 4 * up[1]), single),
            jax.ShapeDtypeStruct(down, single),
        ]
        + [jax.ShapeDtypeStruct(shape, single) for shape in rest]
        + [jax.ShapeDtypeStruct(small.shape, single)],
        in_specs=[pl.BlockSpec(memory_space=pltpu.SMEM)] + [vmem] * 6 + [hbm] * 7,
        out_specs=[vmem] * 8,
        scratch_shapes=[
            pltpu.VMEM((slot_rows, narrow), low),
            pltpu.VMEM((4 * heads, slot_rows, DH), low),
            pltpu.VMEM((slot_rows, wide), low),
            pltpu.VMEM((slot_rows, DH), single),
            pltpu.VMEM((slot_rows, DH), single),
            pltpu.VMEM((3, rows, features), low),
            pltpu.VMEM((3, rows, features), low),
            pltpu.VMEM((2, 2, 4, 2) + shard, low),
            pltpu.VMEM((2, 2, 4) + shard, low),
            pltpu.VMEM((5, 2, 2) + shard, low),
            pltpu.VMEM((4,) + shard, low),
            pltpu.VMEM((4,) + small.shape, single),
            pltpu.VMEM((7,) + small.shape, single),
            pltpu.SemaphoreType.DMA((REAR_COPIES,)),
            pltpu.SemaphoreType.DMA((REAR_COPIES,)),
            pltpu.SemaphoreType.DMA((7,)),
        ]
        + [pltpu.VMEM(shape, low) for shape in buffers],
        compiler_params=pltpu.CompilerParams(
            collective_id=2, has_side_effects=True, vmem_limit_bytes=58 * 2**20
        ),
        name="rear",
    )(live, d_rows, heads_qkv, logsum, rows_all, qkv, small, *partials)


def body_planned(
    tokens,
    patch_counts,
    w_qkv,
    w_out,
    w_up,
    w_down,
    w_patch,
    w_class,
    norm_gains,
    mask_norm,
    grad_masks,
):
    low = jnp.bfloat16
    h, s = lax.axis_index("head"), lax.axis_index("seq")
    tokens, grad_masks = tokens[0], grad_masks[0]
    row_count = tokens.shape[0]
    tile = lax.dynamic_update_slice(jnp.zeros((16, 128), low), norm_gains, (0, (s % 4) * 32))
    live = CLS + patch_counts
    scaling = DH ** (-0.5)

    normal_one, inverse_one = standardize(tokens)
    sets = w_up.reshape(32, 2, 2, 4, 2, 128)
    up_blocks = jnp.concatenate(
        [sets[:, :, 0, :, 0], sets[:, :, 1, :, 0], sets[:, 0, :, :, 1], sets[:, 1, :, :, 1]], axis=1
    ).reshape(32, 4096)
    lanes = ((0, 0), (0, 256 - CLS))
    outs = front(
        live,
        tokens,
        normal_one,
        tile,
        jnp.pad(grad_masks, lanes),
        jnp.pad(mask_norm, ((0, 6), lanes[1])),
        (w_qkv, w_out, up_blocks, w_down, w_patch, w_class),
        scaling,
    )
    attended, heads_qkv, logsum, rows_all, gains, qkv, class_masks, mask_sums = outs[:8]
    normed_two, active, d_branch, d_hidden, rounded, d_patch, d_class, d_mix, d_second, d_attended = outs[8:]
    grad_down = [matmul_tn(active[k], d_branch[k]).astype(low) for k in range(2)]
    grad_up = [matmul_tn(normed_two[k], d_hidden[k]).astype(low) for k in range(2)]
    grad_out = matmul_tn(attended, d_mix).astype(low)
    grad_patch = matmul_tn(rounded, d_patch).astype(low)
    grad_class = matmul_tn(rounded[: d_class.shape[0]], d_class).astype(low)

    def parted(value):
        return value.reshape(2, 2, 4, 2, value.shape[0] // 32, value.shape[1])

    partials = (
        parted(grad_up[0]),
        parted(grad_up[1]),
        grad_down[0].reshape(2, 4, 128, 1024),
        grad_down[1].reshape(2, 4, 128, 1024),
        parted(grad_out),
        parted(grad_patch),
        parted(grad_class),
    )
    d_normed_one, g_qkv, g_up, g_down, g_out, g_patch, g_class, sums = rear(
        live, d_attended, heads_qkv, logsum, rows_all, qkv, mask_sums, partials, scaling
    )
    grad_inputs = d_second + standard_back(normal_one, inverse_one, d_normed_one * gains[0])
    gain_sums = [
        jnp.sum(weight.astype(jnp.float32) * grad, axis=1) for weight, grad in ((w_qkv, g_qkv), (w_up, g_up))
    ]
    return (
        class_masks[None, :, :CLS],
        grad_inputs[None],
        g_qkv,
        g_out,
        g_up,
        g_down,
        g_patch,
        g_class,
        jnp.stack(gain_sums) / norm_gains.astype(jnp.float32),
        sums[0:2, :CLS],
    )


def solution(mesh):
    planned = dict(mesh.shape) == {"head": 4, "seq": 8}
    return jax.shard_map(
        body_planned if planned else body_general,
        mesh=mesh,
        in_specs=(
            P("seq", "head", None),
            P("seq"),
            P(("head", "seq"), None),
            P(("head", "seq"), None),
            P(("head", "seq"), None),
            P(("head", "seq"), None),
            P(("head", "seq"), None),
            P(("head", "seq"), None),
            P(None, ("head", "seq")),
            P(),
            P("seq", "head", None),
        ),
        out_specs=(
            P("seq", "head", None),
            P("seq", "head", None),
            P(("head", "seq"), None),
            P(("head", "seq"), None),
            P(("head", "seq"), None),
            P(("head", "seq"), None),
            P(("head", "seq"), None),
            P(("head", "seq"), None),
            P(None, ("head", "seq")),
            P(),
        ),
        check_vma=False,
    )
```

```python
from functools import partial

import jax
import jax.numpy as jnp
from jax import lax
from jax.experimental import pallas as pl
from jax.experimental.pallas import tpu as pltpu
from jax.sharding import PartitionSpec as P

HEADS = 16
DH = 64
CLS = 150


def spread_2(value, axis, source):
    kept = jnp.where(lax.axis_index(axis) == source, value, 0).astype(value.dtype)
    return lax.psum(kept, axis)


def standardize(values):
    center = values - jnp.mean(values, axis=-1, keepdims=True)
    inverse = lax.rsqrt(jnp.mean(center * center, axis=-1, keepdims=True) + 1e-05)
    return (center * inverse, inverse)


def standard_back(normal, inverse, upstream):
    middle = jnp.mean(upstream, axis=-1, keepdims=True)
    along = jnp.mean(upstream * normal, axis=-1, keepdims=True)
    return inverse * (upstream - middle - normal * along)


def unit_scale(values):
    return lax.rsqrt(jnp.sum(values * values, axis=-1, keepdims=True) + 1e-06)


def unit_back(values, upstream):
    factor = unit_scale(values)
    direct = values * factor
    return factor * (upstream - direct * jnp.sum(upstream * direct, axis=-1, keepdims=True))


def block_scores(query_block, key_rows, key_live, scaling):
    scores = (
        jnp.einsum("qd,kd->qk", query_block, key_rows, preferred_element_type=jnp.float32) * scaling
    )
    return jnp.where(key_live, scores, -1e30)


def attend_head(queries, key_rows, values, key_live, scaling, blocks):
    head_width = queries.shape[-1]

    def single(query_block):
        scores = block_scores(query_block, key_rows, key_live, scaling)
        highest = jnp.max(scores, axis=-1, keepdims=True)
        weights_raw = jnp.exp(scores - highest)
        totals = jnp.sum(weights_raw, axis=-1, keepdims=True)
        weights = (weights_raw / totals).astype(jnp.bfloat16)
        output = jnp.einsum("qk,kd->qd", weights, values, preferred_element_type=jnp.float32)
        return (output.astype(jnp.bfloat16), (highest + jnp.log(totals))[:, 0])

    outputs, logsum = lax.map(single, queries.reshape(blocks, -1, head_width))
    return (outputs.reshape(-1, head_width), logsum.reshape(-1))


def attend_back(queries, key_rows, values, grad_out, logsum, key_live, scaling, blocks):
    head_width = queries.shape[-1]

    def single(running, pieces):
        grad_keys, grad_values = running
        query_block, grad_block, logsum_block = pieces
        scores = block_scores(query_block, key_rows, key_live, scaling)
        weights = jnp.exp(scores - logsum_block[:, None])
        grad_values = grad_values + jnp.einsum(
            "qk,qd->kd",
            weights.astype(jnp.bfloat16),
            grad_block,
            preferred_element_type=jnp.float32,
        )
        grad_weights = jnp.einsum(
            "qd,kd->qk", grad_block, values, preferred_element_type=jnp.float32
        )
        deltas = jnp.sum(grad_weights * weights, axis=-1, keepdims=True)
        grad_scores = (weights * (grad_weights - deltas)).astype(jnp.bfloat16)
        grad_query = (
            jnp.einsum("qk,kd->qd", grad_scores, key_rows, preferred_element_type=jnp.float32)
            * scaling
        )
        grad_keys = (
            grad_keys
            + jnp.einsum("qk,qd->kd", grad_scores, query_block, preferred_element_type=jnp.float32)
            * scaling
        )
        return ((grad_keys, grad_values), grad_query)

    zero_state = jnp.zeros(key_rows.shape, jnp.float32)
    pieces = (
        queries.reshape(blocks, -1, head_width),
        grad_out.reshape(blocks, -1, head_width),
        logsum.reshape(blocks, -1),
    )
    (grad_keys, grad_values), grad_queries = lax.scan(single, (zero_state, zero_state), pieces)
    return (grad_queries.reshape(-1, head_width), grad_keys, grad_values)


def body_general(
    tokens,
    patch_counts,
    w_qkv,
    w_out,
    w_up,
    w_down,
    w_patch,
    w_class,
    norm_gains,
    mask_norm,
    grad_masks,
):
    gains_rows = norm_gains.T
    gathered = (
        lax.all_gather(w_qkv, ("head", "seq"), axis=0, tiled=True),
        lax.all_gather(w_out, ("head", "seq"), axis=0, tiled=True),
        lax.all_gather(w_up, ("head", "seq"), axis=0, tiled=True),
        lax.all_gather(w_down, ("head", "seq"), axis=0, tiled=True),
        lax.all_gather(w_patch, ("head", "seq"), axis=0, tiled=True),
        lax.all_gather(w_class, ("head", "seq"), axis=0, tiled=True),
        lax.all_gather(gains_rows, ("head", "seq"), axis=0, tiled=True),
    )
    full_qkv, full_out, full_up, full_down, full_patch, full_class, full_gains = gathered
    gain_one = full_gains[:, 0].astype(jnp.float32)
    gain_two = full_gains[:, 1].astype(jnp.float32)
    image_count = tokens.shape[0]
    row_count = tokens.shape[1]
    groups = lax.axis_size("head")
    slot_rows = row_count * groups
    local_heads = HEADS // groups
    position = lax.axis_index("head") * row_count + jnp.arange(row_count, dtype=jnp.int32)
    live_limit = CLS + patch_counts
    patch_rows = ((position[None, :] >= CLS) & (position[None, :] < live_limit[:, None])).astype(
        jnp.float32
    )[:, :, None]
    key_live = (jnp.arange(slot_rows, dtype=jnp.int32)[None, :] < live_limit[:, None])[:, None, :]
    root_flag = (lax.axis_index("head") == 0).astype(jnp.float32)
    scaling = DH ** (-0.5)
    blocks = slot_rows // 512
    normal_one, inverse_one = standardize(tokens)
    normed_one = (normal_one * gain_one).astype(jnp.bfloat16)
    triple = jnp.einsum(
        "ird,dt->irt", normed_one, full_qkv, preferred_element_type=jnp.float32
    ).astype(jnp.bfloat16)
    spread = lax.all_to_all(triple, "head", split_axis=2, concat_axis=1, tiled=True).reshape(
        image_count, slot_rows, local_heads, 3, DH
    )
    image = 0
    outputs = []
    image_logsums = []
    for number in range(local_heads):
        output, logsum = attend_head(
            spread[image, :, number, 0],
            spread[image, :, number, 1],
            spread[image, :, number, 2],
            key_live[image],
            scaling,
            blocks,
        )
        outputs.append(output)
        image_logsums.append(logsum)
    image_outputs = [jnp.stack(outputs, axis=1).reshape(slot_rows, local_heads * DH)]
    logsums = [image_logsums]
    attended_heads = jnp.stack(image_outputs, axis=0)
    attended = lax.all_to_all(attended_heads, "head", split_axis=1, concat_axis=2, tiled=True)
    second = tokens + jnp.einsum(
        "ire,ed->ird", attended, full_out, preferred_element_type=jnp.float32
    )
    normal_two, inverse_two = standardize(second)
    normed_two = (normal_two * gain_two).astype(jnp.bfloat16)
    hidden = jnp.einsum("ird,df->irf", normed_two, full_up, preferred_element_type=jnp.float32)
    gelu_exact = partial(jax.nn.gelu, approximate=False)
    active = gelu_exact(hidden).astype(jnp.bfloat16)
    residual = second + jnp.einsum(
        "irf,fd->ird", active, full_down, preferred_element_type=jnp.float32
    )
    rounded = residual.astype(jnp.bfloat16)
    patch_proj = jnp.einsum("ird,de->ire", rounded, full_patch, preferred_element_type=jnp.float32)
    patch_unit = (patch_proj * unit_scale(patch_proj)).astype(jnp.bfloat16)
    class_proj = jnp.einsum(
        "ird,de->ire", rounded[:, :CLS], full_class, preferred_element_type=jnp.float32
    )
    class_unit = (class_proj * unit_scale(class_proj)).astype(jnp.bfloat16)
    classes = spread_2(class_unit, "head", 0)
    products = jnp.einsum("ird,icd->irc", patch_unit, classes, preferred_element_type=jnp.float32)
    normal_mask, inverse_mask = standardize(products)
    class_masks = (normal_mask * mask_norm[0] + mask_norm[1]) * patch_rows
    upstream = grad_masks * patch_rows
    norm_grads = lax.psum(
        jnp.stack([jnp.sum(upstream * normal_mask, axis=(0, 1)), jnp.sum(upstream, axis=(0, 1))]),
        ("head", "seq"),
    )
    d_products = standard_back(normal_mask, inverse_mask, upstream * mask_norm[0]).astype(
        jnp.bfloat16
    )
    d_patch_unit = jnp.einsum(
        "irc,icd->ird", d_products, classes, preferred_element_type=jnp.float32
    )
    class_part = jnp.einsum(
        "irc,ird->icd", d_products, patch_unit, preferred_element_type=jnp.float32
    )
    d_class_unit = lax.psum(class_part.astype(jnp.bfloat16), "head").astype(jnp.float32)
    d_patch_proj = unit_back(patch_proj, d_patch_unit).astype(jnp.bfloat16)
    d_class_proj = (unit_back(class_proj, d_class_unit) * root_flag).astype(jnp.bfloat16)
    regathered = (
        lax.all_gather(w_qkv, ("head", "seq"), axis=0, tiled=True),
        lax.all_gather(w_out, ("head", "seq"), axis=0, tiled=True),
        lax.all_gather(w_up, ("head", "seq"), axis=0, tiled=True),
        lax.all_gather(w_down, ("head", "seq"), axis=0, tiled=True),
        lax.all_gather(w_patch, ("head", "seq"), axis=0, tiled=True),
        lax.all_gather(w_class, ("head", "seq"), axis=0, tiled=True),
        lax.all_gather(gains_rows, ("head", "seq"), axis=0, tiled=True),
    )
    back_qkv, back_out, back_up, back_down, back_patch, back_class, back_gains = regathered
    back_one = back_gains[:, 0].astype(jnp.float32)
    back_two = back_gains[:, 1].astype(jnp.float32)
    grad_patch = jnp.einsum(
        "ird,ire->de", rounded, d_patch_proj, preferred_element_type=jnp.float32
    )
    grad_class = jnp.einsum(
        "ird,ire->de", rounded[:, :CLS], d_class_proj, preferred_element_type=jnp.float32
    )
    d_residual = jnp.einsum(
        "ire,de->ird", d_patch_proj, back_patch, preferred_element_type=jnp.float32
    )
    class_term = jnp.einsum(
        "ire,de->ird", d_class_proj, back_class, preferred_element_type=jnp.float32
    )
    d_residual = d_residual.at[:, :CLS].add(class_term)
    d_branch = d_residual.astype(jnp.bfloat16)
    grad_down = jnp.einsum("irf,ird->fd", active, d_branch, preferred_element_type=jnp.float32)
    d_active = jnp.einsum("ird,fd->irf", d_branch, back_down, preferred_element_type=jnp.float32)
    gelu_pull = jax.vjp(gelu_exact, hidden)[1]
    d_hidden = gelu_pull(d_active)[0].astype(jnp.bfloat16)
    grad_up = jnp.einsum("ird,irf->df", normed_two, d_hidden, preferred_element_type=jnp.float32)
    d_normed_two = jnp.einsum("irf,df->ird", d_hidden, back_up, preferred_element_type=jnp.float32)
    d_second = d_residual + standard_back(normal_two, inverse_two, d_normed_two * back_two)
    grad_gain_two = jnp.sum(d_normed_two * normal_two, axis=(0, 1))
    d_mix = d_second.astype(jnp.bfloat16)
    grad_out = jnp.einsum("ire,ird->ed", attended, d_mix, preferred_element_type=jnp.float32)
    d_attended = jnp.einsum(
        "ird,ed->ire", d_mix, back_out, preferred_element_type=jnp.float32
    ).astype(jnp.bfloat16)
    d_heads = lax.all_to_all(d_attended, "head", split_axis=2, concat_axis=1, tiled=True).reshape(
        image_count, slot_rows, local_heads, DH
    )
    image = 0
    head_grads = []
    for number in range(local_heads):
        grad_queries, grad_keys, grad_values = attend_back(
            spread[image, :, number, 0],
            spread[image, :, number, 1],
            spread[image, :, number, 2],
            d_heads[image, :, number],
            logsums[image][number],
            key_live[image],
            scaling,
            blocks,
        )
        head_grads.append(jnp.stack([grad_queries, grad_keys, grad_values], axis=1))
    image_grads = [jnp.stack(head_grads, axis=1).reshape(slot_rows, local_heads * 3 * DH)]
    d_spread = jnp.stack(image_grads, axis=0).astype(jnp.bfloat16)
    d_triple = lax.all_to_all(d_spread, "head", split_axis=1, concat_axis=2, tiled=True)
    grad_qkv = jnp.einsum("ird,irt->dt", normed_one, d_triple, preferred_element_type=jnp.float32)
    d_normed_one = jnp.einsum("irt,dt->ird", d_triple, back_qkv, preferred_element_type=jnp.float32)
    grad_inputs = d_second + standard_back(normal_one, inverse_one, d_normed_one * back_one)
    grad_gain_one = jnp.sum(d_normed_one * normal_one, axis=(0, 1))
    grad_gains = jnp.stack([grad_gain_one, grad_gain_two], axis=1)
    reduced = (
        lax.psum_scatter(grad_qkv, ("head", "seq"), scatter_dimension=0, tiled=True),
        lax.psum_scatter(grad_out, ("head", "seq"), scatter_dimension=0, tiled=True),
        lax.psum_scatter(grad_up, ("head", "seq"), scatter_dimension=0, tiled=True),
        lax.psum_scatter(grad_down, ("head", "seq"), scatter_dimension=0, tiled=True),
        lax.psum_scatter(grad_patch, ("head", "seq"), scatter_dimension=0, tiled=True),
        lax.psum_scatter(grad_class, ("head", "seq"), scatter_dimension=0, tiled=True),
        lax.psum_scatter(grad_gains, ("head", "seq"), scatter_dimension=0, tiled=True),
    )
    return (
        class_masks,
        grad_inputs,
        reduced[0],
        reduced[1],
        reduced[2],
        reduced[3],
        reduced[4],
        reduced[5],
        reduced[6].T,
        norm_grads,
    )


MESH = pl.DeviceIdType.MESH
LOG2E = 1.4426950408889634
SLOTS = 16
FRONT_COPIES = 160
REAR_COPIES = 88


def matmul(left, right):
    return jnp.dot(left, right, preferred_element_type=jnp.float32)


def matmul_nt(left, right):
    return lax.dot_general(left, right, (((1,), (1,)), ((), ())), preferred_element_type=jnp.float32)


def matmul_tn(left, right):
    return lax.dot_general(left, right, (((0,), (0,)), ((), ())), preferred_element_type=jnp.float32)


def norm(values):
    center = values - jnp.mean(values, axis=-1, keepdims=True)
    inverse = lax.rsqrt(jnp.mean(center * center, axis=-1, keepdims=True) + 1e-05)
    return center * inverse, inverse


def device(y, x, z, c):
    return (y * 2 + x, z * 2 + c)


class Links:
    def __init__(self, send_sem, recv_sem):
        head, seq = lax.axis_index("head"), lax.axis_index("seq")
        self.y, self.x, self.z, self.c = head // 2, head % 2, seq // 2, seq % 2
        y, x, z, c = self.y, self.x, self.z, self.c
        self.sibling = device(y, x, z, 1 - c)
        self.along_x = device(y, 1 - x, z, c)
        self.along_y = device(1 - y, x, z, c)
        self.across = device(1 - y, 1 - x, z, c)
        self.along_z = [device(y, x, (z + k) % 4, c) for k in (1, 2, 3)]
        self.send_sem, self.recv_sem, self.count, self.made, self.lines = send_sem, recv_sem, 0, [], []

    def greet(self):
        barrier = pltpu.get_barrier_semaphore()
        peers = [self.sibling, self.along_x, self.along_y, self.across] + self.along_z
        for peer in peers:
            pl.semaphore_signal(barrier, inc=1, device_id=peer, device_id_type=MESH)
        pl.semaphore_wait(barrier, len(peers))

    def plan(self, source, target, peer, sends=None, again=False):
        number = self.count - again
        self.count = number + 1
        copy = pltpu.make_async_remote_copy(
            src_ref=source,
            dst_ref=target,
            send_sem=self.send_sem.at[number],
            recv_sem=self.recv_sem.at[number],
            device_id=peer,
            device_id_type=MESH,
        )
        if not again:
            self.made.append((copy, sends))
        return copy

    def drain(self):
        for copy, sends in self.made:
            if sends is None:
                copy.wait_send()
            else:
                pl.when(sends)(copy.wait_send)
        for line in self.lines:
            line.drain()


class Stage:
    def __init__(self, links, moves, again=False):
        self.copies = [links.plan(*move, again=again) for move in moves]

    def start(self):
        for copy in self.copies:
            copy.start()

    def wait(self):
        for copy in self.copies:
            copy.wait_recv()


class Line:
    def __init__(self, links, piece, source=None):
        self.links, self.piece = links, piece
        self.source = piece(links.z) if source is None else source
        self.base = links.count
        links.count += 5
        links.lines.append(self)

    def copy(self, source, target, sent, landed):
        links = self.links
        return pltpu.make_async_remote_copy(
            src_ref=source,
            dst_ref=self.piece(landed),
            send_sem=links.send_sem.at[self.base + sent],
            recv_sem=links.recv_sem.at[self.base + landed],
            device_id=device(links.y, links.x, target, links.c),
            device_id_type=MESH,
        )

    def direct(self, target):
        z = self.links.z
        return (z != target) if target in (1, 2) else (z != target) & (z != 3 - target)

    def start(self):
        for target in (1, 2, 0, 3):

            @pl.when(self.direct(target))
            def _(target=target):
                self.copy(self.source, target, target, self.links.z).start()

    def relay(self):
        for at, end in ((2, 0), (1, 3)):

            @pl.when(self.links.z == at)
            def _(end=end):
                self.copy(self.source, 3 - end, 4, end).wait_recv()
                self.copy(self.piece(end), 3 - end, 4, end).start()

    def wait(self):
        z = self.links.z
        for origin in range(4):
            pending = z != origin
            if origin in (0, 3):
                pending = pending & (z != (2 if origin == 0 else 1))

            @pl.when(pending)
            def _(origin=origin):
                self.copy(self.source, 0, 0, origin).wait_recv()

    def drain(self):
        for target in range(4):

            @pl.when(self.direct(target))
            def _(target=target):
                self.copy(self.source, target, target, self.links.z).wait_send()

        @pl.when((self.links.z == 1) | (self.links.z == 2))
        def _():
            self.copy(self.source, 0, 4, 0).wait_send()


def at_slots(slot, events):
    for number, event in events.items():
        pl.when(slot == number)(event)


def front_kernel(scaling, *refs):
    live_ref, tokens, tile, grad_masks, mask_norm = refs[:5]
    qkv_shard, out_shard, up_shard, down_shard, patch_shard, class_shard = refs[5:11]
    attended, heads_ref, logsum, rows_ref, gains_ref, qkv, class_masks, mask_sums = refs[11:19]
    normal_one, inverse_one, normed_two, active, d_branch, d_hidden, rounded, d_patch = refs[19:27]
    class_rows, d_class, d_mix, d_second, d_attended = refs[27:32]
    full_out, ups, downs, full_patch, full_class, tiles, staged = refs[32:39]
    slope, second, normal_two, inverse_two, residual, patch_proj, class_proj, classes = refs[39:47]
    part_sent, part_got, back_sent, back_got, class_sent, class_got = refs[47:53]
    term_sent, term_got, d_residual, mask_in = refs[53:57]
    send_sem, recv_sem, local_sem = refs[57:]
    links = Links(send_sem, recv_sem)
    y, x, z, c = links.y, links.x, links.z, links.c
    h = y * 2 + x
    q = y * (1 - c) + x * c
    rows, features = tokens.shape
    wide = qkv.shape[-1]
    narrow = staged.shape[1]
    heads = narrow // DH
    block = ups.shape[-1]
    slot_rows = rows * 4
    plane = [(links.across, 3 - h, 3), (links.along_x, y * 2 + 1 - x, 1), (links.along_y, (1 - y) * 2 + x, 2)]
    at_x, at_y = plane[1][1], plane[2][1]

    def columns(start, size):
        return pl.ds(pl.multiple_of(start, 128), size)

    def up_block(number):
        return up_shard.at[:, columns(number * block, block)]

    local = [
        pltpu.make_async_copy(source, target, local_sem.at[number])
        for number, (source, target) in zip(
            (0, 1, 2, 3, 4, 5, 7, 8),
            [
                (tile, tiles.at[y, x, z, c]),
                (qkv_shard.at[:, columns(h * wide, wide)], qkv.at[y, x, z, c]),
                (out_shard, full_out.at[y, x, z, c]),
                (down_shard, downs.at[c, q, z]),
                (up_block(x), ups.at[0, y, x, z, c]),
                (up_block(2 + y), ups.at[1, y, x, z, c]),
                (patch_shard, full_patch.at[y, x, z, c]),
                (class_shard, full_class.at[y, x, z, c]),
            ]
        )
    ]
    gain_core = Stage(links, [(tile, tiles.at[y, x, z, c], links.sibling)])
    gain_z = Stage(links, [(tiles.at[y, x, z], tiles.at[y, x, z], peer) for peer in links.along_z])
    gain_plane = Stage(links, [(tiles.at[y, x], tiles.at[y, x], peer) for peer, _, _ in plane])
    qkv_plane = Stage(
        links, [(qkv_shard.at[:, columns(p * wide, wide)], qkv.at[y, x, z, c], peer) for peer, p, _ in plane]
    )
    part = qkv.shape[4] // 2
    qkv_z = [Line(links, lambda at, k=k: qkv.at[:, :, at, c, k * part : (k + 1) * part]) for k in range(2)]
    qkv_core = Stage(links, [(qkv.at[:, :, :, c], qkv.at[:, :, :, c], links.sibling)])
    up_split = [
        Stage(links, [(up_block(1 - x), ups.at[0, y, x, z, c], links.along_x)]),
        Stage(links, [(up_block(2 + 1 - y), ups.at[1, y, x, z, c], links.along_y)]),
    ]
    up_z = [
        Line(links, lambda at: ups.at[0, y, :, at, c]),
        Line(links, lambda at: ups.at[1, :, x, at, c]),
    ]
    up_on = [
        Stage(links, [(ups.at[0, y, :, :, c], ups.at[0, y, :, :, c], links.along_y)]),
        Stage(links, [(ups.at[1, :, x, :, c], ups.at[1, :, x, :, c], links.along_x)]),
    ]
    up_core = [
        Stage(links, [(ups.at[k, :, :, :, c], ups.at[k, :, :, :, c], links.sibling)]) for k in range(2)
    ]
    some = down_shard.shape[0] // 4
    turned = device(y + (1 - c) * (1 - 2 * y), x + c * (1 - 2 * x), z, c)
    spans = [slice(k * some, (k + 1) * some) for k in range(4)]
    down_turn = [Stage(links, [(down_shard.at[spans[k]], downs.at[c, q, z, spans[k]], turned)]) for k in (0, 1)]
    down_z = [Line(links, lambda at, k=k: downs.at[c, :, at, spans[k]]) for k in (0, 1)] + [
        Line(links, lambda at, k=k: downs.at[c, q, at, spans[k]], down_shard.at[spans[k]]) for k in (2, 3)
    ]
    down_on = [Stage(links, [(downs.at[c, q, :, spans[k]],) * 2 + (turned,)]) for k in (2, 3)]
    down_core = [
        Stage(links, [(downs.at[c, :, :, span], downs.at[c, :, :, span], links.sibling)])
        for span in (slice(0, 2 * some), slice(2 * some, 4 * some))
    ]
    part = out_shard.shape[0] // 2

    def square(full, shard):
        first = [full.at[y, x, :, c, 0:part], full.at[y, x, :, c, part:]]
        second = [full.at[:, x, :, c, 0:part], full.at[y, :, :, c, part:]]
        return (
            Line(links, lambda at: full.at[y, x, at, c], shard),
            Stage(links, [(first[0], first[0], links.along_y), (first[1], first[1], links.along_x)]),
            Stage(links, [(second[0], second[0], links.along_x), (second[1], second[1], links.along_y)]),
            Stage(links, [(full.at[:, :, :, c],) * 2 + (links.sibling,)]),
        )

    out_z, out_one, out_two, out_core = square(full_out, out_shard)
    near, far = slice(0, part), slice(part, 2 * part)
    patch_x = Stage(links, [(patch_shard.at[far], full_patch.at[y, x, z, c, far], links.along_x)])
    patch_y = Stage(links, [(full_patch.at[y, :, z, c, far],) * 2 + (links.along_y,)])
    patch_first = Line(links, lambda at: full_patch.at[y, x, at, c, near], patch_shard.at[near])
    patch_one = Stage(links, [(full_patch.at[y, x, :, c, near],) * 2 + (links.along_y,)])
    patch_two = Stage(links, [(full_patch.at[:, x, :, c, near],) * 2 + (links.along_x,)])
    class_y = Stage(links, [(class_shard, full_class.at[y, x, z, c], links.along_y)])
    class_x = Stage(links, [(full_class.at[:, x, z, c],) * 2 + (links.along_x,)])
    halves = [slice(k * part, (k + 1) * part) for k in range(2)]
    class_z = [Line(links, lambda at, k=k: full_class.at[:, :, at, c, k * part : (k + 1) * part]) for k in range(2)]
    halves = [slice(part + k * part // 2, part + (k + 1) * part // 2) for k in range(2)]
    patch_z = [Line(links, lambda at, k=k: full_patch.at[:, :, at, c, halves[k]]) for k in range(2)]
    patch_core = Stage(links, [(full_patch.at[:, :, :, c],) * 2 + (links.sibling,)])
    class_core = Stage(links, [(full_class.at[:, :, :, c],) * 2 + (links.sibling,)])
    beside = (links.along_x, links.along_y)
    here = slice(0, rows)
    few = class_proj.shape[0]
    tall = -(-CLS // 16) * 16
    parts = (slice(0, tall), slice(tall, rows))
    theirs = [slice(rows + at.start, rows + at.stop) for at in parts]

    def exchange(sent, got, sent_at, got_at):
        return [
            [Stage(links, [(sent.at[k, sent_at[i]], got.at[k, got_at[i]], beside[k])]) for i in range(2)]
            for k in range(2)
        ]

    normed_out = exchange(normed_two, normed_two, parts, theirs)
    branch_out = exchange(d_branch, d_branch, parts, theirs)
    part_back = exchange(part_sent, part_got, parts, parts)
    grad_back = exchange(back_sent, back_got, parts, parts)
    sizes = {1: few, 2: few, 3: tall - 3 * few}
    class_out = [
        links.plan(
            rounded.at[few * rel : few * rel + sizes[rel]], class_rows.at[0 : sizes[rel]], peer, h == 0
        )
        for peer, _, rel in plane
    ]
    mine = pl.ds(pl.multiple_of(h * few, few), few)
    unit_out = Stage(links, [(classes.at[mine], classes.at[mine], peer) for peer, _, _ in plane])
    class_back = Stage(links, [(class_sent.at[p], class_got.at[rel - 1], peer) for peer, p, rel in plane])
    term_back = [
        links.plan(term_sent.at[0 : sizes[rel]], term_got.at[rel - 1, 0 : sizes[rel]], peer, h == rel)
        for peer, _, rel in plane
    ]
    middle = rows // 2
    strips = [slice(0, middle), slice(middle, rows)]
    rows_x = [Stage(links, [(rows_ref.at[h, strips[k]],) * 2 + (links.along_x,)]) for k in (0, 1)]
    rows_y = [Stage(links, [(rows_ref.at[h, strips[k]],) * 2 + (links.along_y,)]) for k in (1, 0)]
    piece_a, piece_b = rows_ref.at[at_x, strips[0]], rows_ref.at[at_y, strips[1]]
    relay_y = Stage(links, [(piece_a, piece_a, links.along_y)])
    relay_x = Stage(links, [(piece_b, piece_b, links.along_x)])

    for copy in local:
        copy.start()
    class_rows[...] = jnp.zeros_like(class_rows)
    links.greet()
    for stage in (gain_core, qkv_plane, *up_split, *down_turn, class_y, patch_x, out_z, patch_first):
        stage.start()
    value, inverse = norm(tokens[...])
    normal_one[...] = value
    inverse_one[...] = jnp.broadcast_to(inverse, inverse_one.shape)
    local[0].wait()
    gain_core.wait()
    gain_z.start()
    gain_z.wait()
    gain_plane.start()
    local[1].wait()
    qkv_plane.wait()
    for line in qkv_z:
        line.start()
    gain_plane.wait()
    for j in range(8):
        piece = tiles[j // 4, j // 2 % 2, (j % 2) * 2, 0].astype(jnp.float32)
        for i in range(1, 4):
            piece = piece + tiles[j // 4, j // 2 % 2, (j % 2) * 2 + i // 2, i % 2].astype(jnp.float32)
        gains_ref[:, j * 128 : (j + 1) * 128] = piece[0:8]
    rows_ref[h] = (normal_one[...] * gains_ref[0:1, :]).astype(jnp.bfloat16)
    for stage in (rows_x[0], rows_y[0], rows_x[1], rows_y[1]):
        stage.start()
    for line in (out_z, patch_first, *qkv_z):
        line.relay()
    rows_x[0].wait()
    relay_y.start()
    rows_y[0].wait()
    relay_x.start()
    local[6].wait()
    patch_x.wait()
    patch_y.start()
    local[7].wait()
    class_y.wait()
    class_x.start()
    for line in qkv_z:
        line.wait()
    qkv_core.start()
    for k in range(2):
        local[4 + k].wait()
        up_split[k].wait()
        up_z[k].start()
    out_z.wait()
    patch_first.wait()
    for number in (2, 3):
        local[number].wait()

    def project(p):
        weight = qkv[...].reshape(rows * 4, wide)
        piece = jnp.dot(rows_ref[p], weight, preferred_element_type=jnp.float32).astype(jnp.bfloat16)
        at = pl.ds(pl.multiple_of(p * rows, rows), rows)
        for number in range(3 * heads):
            heads_ref[number, at, :] = piece[:, number * DH : (number + 1) * DH]

    qkv_core.wait()
    project(h)
    rows_x[1].wait()
    project(at_x)
    rows_y[1].wait()
    project(at_y)
    out_one.start()
    patch_one.start()
    relay_y.wait()
    relay_x.wait()
    project(3 - h)

    live = live_ref[0]
    key_live = lax.broadcasted_iota(jnp.int32, (slot_rows, 1), 0) < live
    returned = links.count - 1
    assert returned + 4 <= FRONT_COPIES

    def back(rel):
        peer = h + (rel % 2) * (1 - 2 * x) + (rel // 2) * (2 - 4 * y)
        return pltpu.make_async_remote_copy(
            src_ref=staged.at[pl.ds(pl.multiple_of(peer * rows, rows), rows), :],
            dst_ref=attended.at[:, columns(h * narrow, narrow)],
            send_sem=send_sem.at[returned + rel],
            recv_sem=recv_sem.at[returned + rel],
            device_id=(peer, z * 2 + c),
            device_id_type=MESH,
        )

    def up_next(k):
        up_z[k].wait()
        up_on[k].start()

    def up_end(k):
        up_on[k].wait()
        up_core[k].start()

    def out_next():
        out_one.wait()
        out_two.start()

    def out_end():
        out_two.wait()
        out_core.start()

    def patch_next():
        patch_one.wait()
        patch_two.start()

    def down_late():
        down_z[2].start()
        down_z[3].start()

    def down_early():
        for stage in down_turn:
            stage.wait()
        down_z[0].start()
        down_z[1].start()

    def down_relays():
        down_z[2].relay()
        down_z[3].relay()

    events = {
        0: up_z[0].relay,
        3: out_next,
        5: up_z[1].relay,
        6: down_late,
        11: down_early,
        12: out_end,
        14: down_relays,
    }

    def tile_body(slot, carry):
        turn, number = slot // 4, slot % 4
        rel = 3 - turn
        peer = h + (rel % 2) * (1 - 2 * x) + (rel // 2) * (2 - 4 * y)
        at = pl.ds(pl.multiple_of(peer * rows, rows), rows)
        at_slots(slot, events)
        queries = heads_ref[3 * number, at, :]
        keys = heads_ref[3 * number + 1]
        values = heads_ref[3 * number + 2]
        scores = lax.dot_general(keys, queries, (((1,), (1,)), ((), ())), preferred_element_type=jnp.float32)
        scores = jnp.where(key_live, scores * (scaling * LOG2E), -1e30)
        highest = jnp.max(scores, axis=0, keepdims=True)
        raw = jnp.exp2(scores - highest)
        totals = jnp.sum(raw, axis=0, keepdims=True)
        weights = (raw * (1.0 / totals)).astype(jnp.bfloat16)
        mixed = lax.dot_general(
            values, weights, (((0,), (0,)), ((), ())), preferred_element_type=jnp.float32
        )
        mixed = mixed.T.astype(jnp.bfloat16)
        for which in range(4):

            @pl.when(number == which)
            def _(which=which):
                staged[at, which * DH : (which + 1) * DH] = mixed

        logsum[number, :, at] = highest + jnp.log2(totals)

        @pl.when((number == 3) & (rel > 0))
        def _():
            back(rel).start()

        return carry

    lax.fori_loop(0, SLOTS, tile_body, 0)
    own = pltpu.make_async_copy(
        staged.at[pl.ds(pl.multiple_of(h * rows, rows), rows), :],
        attended.at[:, columns(h * narrow, narrow)],
        local_sem.at[6],
    )
    own.start()
    class_x.wait()
    patch_y.wait()
    for line in (*class_z, *patch_z):
        line.start()
    up_next(0)
    up_next(1)
    for k in range(2):
        down_z[2 + k].wait()
        down_on[k].start()
    for rel in (3, 2, 1):
        back(rel).wait()
    own.wait()
    out_core.wait()
    down_z[0].relay()

    def whole(weight):
        return weight[...].reshape(-1, weight.shape[-1])

    second[...] = tokens[...] + matmul(attended[...], whole(full_out))
    value, inverse = norm(second[...])
    normal_two[...] = value
    inverse_two[...] = jnp.broadcast_to(inverse, inverse_two.shape)
    value = (value * gains_ref[1:2, :]).astype(jnp.bfloat16)
    for k in range(2):
        normed_two[k, here] = value
    for i in range(2):
        for k in range(2):
            normed_out[k][i].start()
    down_z[1].relay()
    patch_next()
    up_end(0)
    up_end(1)
    for k in range(2):
        up_core[k].wait()
    wide_step = 256

    def forward(k, at, size):
        def step(j, carry):
            span = pl.ds(pl.multiple_of(j * wide_step, wide_step), wide_step)
            weight = ups[k, :, :, :, :, :, span].reshape(features, wide_step)
            hidden = matmul(normed_two[k, at], weight)
            spread = 0.5 + 0.5 * lax.erf(hidden * 0.7071067811865476)
            density = jnp.exp(hidden * hidden * -0.5) * 0.3989422804014327
            active[k, at, span] = (hidden * spread).astype(jnp.bfloat16)
            slope[k, at, span] = spread + hidden * density
            return carry

        lax.fori_loop(0, block // wide_step, step, 0)

    forward(0, here, rows)
    for stage in down_on:
        stage.wait()
    down_core[1].start()
    forward(1, here, rows)
    for line in down_z[:2]:
        line.wait()
    down_core[0].start()
    for stage in down_core:
        stage.wait()
    for i in range(2):
        for k in range(2):
            normed_out[k][i].wait()
            forward(k, theirs[i], parts[i].stop - parts[i].start)
            part_sent[k, parts[i]] = matmul(active[k, theirs[i]], whole(downs.at[k])).astype(jnp.bfloat16)
            part_back[k][i].start()
        if i == 0:
            for line in class_z:
                line.relay()
    residual[...] = second[...] + (
        matmul(active[0, here], whole(downs.at[0])) + matmul(active[1, here], whole(downs.at[1]))
    )
    for line in patch_z:
        line.relay()

    def complete(at):
        for k in range(2):
            part_back[k][0 if at.start == 0 else 1].wait()
        value = residual[at] + (part_got[0, at].astype(jnp.float32) + part_got[1, at].astype(jnp.float32))
        rounded[at] = value.astype(jnp.bfloat16)

    complete(parts[0])

    @pl.when(h == 0)
    def _():
        for copy in class_out:
            copy.start()
        class_rows[...] = rounded[0:few]

    for line in class_z:
        line.wait()
    class_core.start()
    complete(parts[1])
    for line in patch_z:
        line.wait()
    patch_two.wait()
    patch_core.start()
    patch_core.wait()

    patch_proj[...] = matmul(rounded[...], whole(full_patch))
    factor = unit_scale(patch_proj[...])
    patch_unit = (patch_proj[...] * factor).astype(jnp.bfloat16)
    classes[4 * few :] = jnp.zeros((classes.shape[0] - 4 * few, features), jnp.bfloat16)
    for copy, (_, _, rel) in zip(class_out, plane):
        pl.when(h == rel)(copy.wait_recv)
    class_core.wait()
    class_live = h * few + lax.broadcasted_iota(jnp.int32, (few, 1), 0) < CLS
    value = matmul(class_rows[...], whole(full_class))
    class_proj[...] = value
    classes[mine] = jnp.where(class_live, value * unit_scale(value), 0.0).astype(jnp.bfloat16)
    unit_out.start()
    mask_in[...] = jnp.zeros_like(mask_in)
    mask_in[0:rows, 0:CLS] = grad_masks[...]
    mask_in[rows : rows + 2, 0:CLS] = mask_norm[...]
    mask_gain, mask_bias = mask_in[rows : rows + 1, :], mask_in[rows + 1 : rows + 2, :]
    unit_out.wait()
    products = matmul_nt(patch_unit, classes[...])
    lane = lax.broadcasted_iota(jnp.int32, products.shape, 1)
    position = h * rows + lax.broadcasted_iota(jnp.int32, (rows, 1), 0)
    patch_rows = ((position >= CLS) & (position < live)).astype(jnp.float32)

    def class_mean(values):
        return jnp.sum(values, axis=-1, keepdims=True) * (1.0 / CLS)

    center = jnp.where(lane < CLS, products - class_mean(products), 0.0)
    inverse = lax.rsqrt(class_mean(center * center) + 1e-05)
    mask_normal = center * inverse
    class_masks[...] = ((mask_normal * mask_gain + mask_bias) * patch_rows)[:, 0:CLS]
    upstream = mask_in[0:rows, :] * patch_rows
    mask_sums[...] = jnp.zeros_like(mask_sums)
    mask_sums[0:1, :] = jnp.sum(upstream * mask_normal, axis=0, keepdims=True)
    mask_sums[1:2, :] = jnp.sum(upstream, axis=0, keepdims=True)
    upstream = upstream * mask_gain
    upstream = inverse * (upstream - class_mean(upstream) - mask_normal * class_mean(upstream * mask_normal))
    d_products = jnp.where(lane < CLS, upstream, 0.0).astype(jnp.bfloat16)
    class_part = matmul_tn(d_products, patch_unit)
    for p in range(4):
        class_sent[p] = class_part[few * p : few * (p + 1)].astype(jnp.bfloat16)
    class_back.start()
    upstream = matmul(d_products, classes[...])
    direct = patch_proj[...] * factor
    upstream = factor * (upstream - direct * jnp.sum(upstream * direct, axis=-1, keepdims=True))
    d_patch[...] = upstream.astype(jnp.bfloat16)
    d_residual[...] = matmul_nt(d_patch[...], whole(full_patch))

    def branch(i):
        value = d_residual[parts[i]].astype(jnp.bfloat16)
        for k in range(2):
            d_branch[k, parts[i]] = value
            branch_out[k][i].start()

    branch(1)
    class_back.wait()
    upstream = class_sent[h].astype(jnp.float32)
    for number in range(3):
        upstream = upstream + class_got[number].astype(jnp.float32)
    d_class[...] = jnp.where(class_live, unit_back(class_proj[...], upstream), 0.0).astype(jnp.bfloat16)
    term = matmul_nt(d_class[...], whole(full_class))
    term_sent[...] = term.astype(jnp.bfloat16)
    for copy, (_, _, rel) in zip(term_back, plane):
        pl.when(h == rel)(copy.start)

    def backward(k, at):
        for j in range(block // wide_step):
            weight = downs[k, j // 2, 2 * (j % 2) : 2 * (j % 2) + 2].reshape(wide_step, features)
            span = slice(j * wide_step, (j + 1) * wide_step)
            d_hidden[k, at, span] = (matmul_nt(d_branch[k, at], weight) * slope[k, at, span]).astype(jnp.bfloat16)


    def returned_rows(i):
        for k in range(2):
            branch_out[k][i].wait()
            backward(k, theirs[i])
            back_sent[k, parts[i]] = matmul_nt(d_hidden[k, theirs[i]], whole(ups.at[k])).astype(jnp.bfloat16)
            grad_back[k][i].start()

    for k in range(2):
        backward(k, parts[1])
    returned_rows(1)

    @pl.when(h == 0)
    def _():
        d_residual[0:few] = d_residual[0:few] + term_sent[...].astype(jnp.float32)
        for copy, (_, _, rel) in zip(term_back, plane):
            copy.wait_recv()
            at = slice(few * rel, few * rel + sizes[rel])
            d_residual[at] = d_residual[at] + term_got[rel - 1, 0 : sizes[rel]].astype(jnp.float32)

    branch(0)
    for k in range(2):
        backward(k, parts[0])
    returned_rows(0)
    upstream = matmul_nt(d_hidden[0, here], whole(ups.at[0])) + matmul_nt(d_hidden[1, here], whole(ups.at[1]))
    for k in range(2):
        for stage in grad_back[k]:
            stage.wait()
    upstream = upstream + (back_got[0].astype(jnp.float32) + back_got[1].astype(jnp.float32))
    upstream = upstream * gains_ref[1:2, :]
    value = normal_two[...]
    middle = jnp.mean(upstream, axis=-1, keepdims=True)
    along = jnp.mean(upstream * value, axis=-1, keepdims=True)
    d_second[...] = d_residual[...] + inverse_two[:, 0:1] * (upstream - middle - value * along)
    d_mix[...] = d_second[...].astype(jnp.bfloat16)
    d_attended[...] = matmul_nt(d_mix[...], whole(full_out)).astype(jnp.bfloat16)
    links.drain()


def front(live, tokens, tile, grad_masks, mask_norm, shards, scaling):
    rows, features = tokens.shape
    vmem, hbm = pl.BlockSpec(memory_space=pltpu.VMEM), pl.BlockSpec(memory_space=pl.ANY)
    w_qkv, w_out, w_up, w_down, w_patch, w_class = shards
    wide = w_qkv.shape[1] // 4
    heads = wide // (3 * DH)
    block = w_up.shape[1] // 4
    lanes = 256
    few = -(-CLS // 64) * 16
    low, single = jnp.bfloat16, jnp.float32
    outs = [
        ((rows, features), low),
        ((3 * heads, 4 * rows, DH), low),
        ((heads, 1, 4 * rows), single),
        ((4, rows, features), low),
        ((8, features), single),
        ((2, 2, 4, 2, w_qkv.shape[0], wide), low),
        (grad_masks.shape, single),
        ((8, lanes), single),
        ((rows, features), single),
        ((rows, 128), single),
        ((2, 2 * rows, features), low),
        ((2, 2 * rows, block), low),
        ((2, 2 * rows, features), low),
        ((2, 2 * rows, block), low),
        ((rows, features), low),
        ((rows, features), low),
        ((few, features), low),
        ((few, features), low),
        ((rows, features), low),
        ((rows, features), single),
        ((rows, features), low),
    ]
    scratch = [
        ((2, 2, 4, 2) + w_out.shape, low),
        ((2, 2, 2, 4, 2, w_up.shape[0], block), low),
        ((2, 2, 4) + w_down.shape, low),
        ((2, 2, 4, 2) + w_patch.shape, low),
        ((2, 2, 4, 2) + w_class.shape, low),
        ((2, 2, 4, 2) + tile.shape, low),
        ((4 * rows, wide // 3), low),
        ((2, 2 * rows, block), single),
        ((rows, features), single),
        ((rows, features), single),
        ((rows, 128), single),
        ((rows, features), single),
        ((rows, features), single),
        ((few, features), single),
        ((lanes, features), low),
        ((2, rows, features), low),
        ((2, rows, features), low),
        ((2, rows, features), low),
        ((2, rows, features), low),
        ((4, few, features), low),
        ((3, few, features), low),
        ((few, features), low),
        ((3, few, features), low),
        ((rows, features), single),
        ((rows + 8, lanes), single),
    ]
    return pl.pallas_call(
        partial(front_kernel, scaling),
        out_shape=[jax.ShapeDtypeStruct(*out) for out in outs],
        in_specs=[pl.BlockSpec(memory_space=pltpu.SMEM)] + [vmem] * 4 + [hbm] * 6,
        out_specs=[vmem] * len(outs),
        scratch_shapes=[pltpu.VMEM(*shape) for shape in scratch]
        + [
            pltpu.SemaphoreType.DMA((FRONT_COPIES,)),
            pltpu.SemaphoreType.DMA((FRONT_COPIES,)),
            pltpu.SemaphoreType.DMA((9,)),
        ],
        compiler_params=pltpu.CompilerParams(
            collective_id=1, has_side_effects=True, vmem_limit_bytes=60 * 2**20
        ),
        name="front",
    )(live, tokens, tile, grad_masks, mask_norm, *shards)


class LineSum:
    def __init__(self, links, piece, got):
        self.links, self.piece, self.got = links, piece, got
        self.base = links.count
        links.count += 5
        links.lines.append(self)

    def copy(self, piece, target, slot, sent):
        links = self.links
        return pltpu.make_async_remote_copy(
            src_ref=self.piece(piece),
            dst_ref=self.got.at[slot],
            send_sem=links.send_sem.at[self.base + sent],
            recv_sem=links.recv_sem.at[self.base + slot],
            device_id=device(links.y, links.x, target, links.c),
            device_id_type=MESH,
        )

    def start(self):
        z = self.links.z
        for target, end, middle in ((3, 0, 1), (0, 3, 2)):

            @pl.when(z == end)
            def _(target=target, middle=middle):
                self.copy(target, middle, 4, target).start()

        for target in range(4):
            direct = z != target
            if target in (0, 3):
                direct = z == (1 if target == 0 else 2)

            @pl.when(direct)
            def _(target=target):
                self.copy(target, target, z, target).start()

    def relay(self):
        z = self.links.z
        for target, middle in ((3, 1), (0, 2)):

            @pl.when(z == middle)
            def _(target=target, middle=middle):
                self.copy(target, target, 4, target).wait_recv()
                own = self.piece(target)
                own[...] = own[...] + self.got[4]
                self.copy(target, target, middle, target).start()

    def collect(self, add):
        z = self.links.z
        for origin in range(4):
            comes = z != origin
            if origin in (0, 3):
                comes = comes & (z != 3 - origin)

            @pl.when(comes)
            def _(origin=origin):
                self.copy(0, 0, origin, 0).wait_recv()
                add(origin)

    def drain(self):
        for target in range(4):

            @pl.when(self.links.z != target)
            def _(target=target):
                self.copy(target, target, 0, target).wait_send()


class Sum:
    def __init__(self, links, partial_ref, total, sib, one, two, three, local, kind):
        y, x, z, c = links.y, links.x, links.z, links.c
        self.links, self.total, self.sib, self.one, self.two, self.three = links, total, sib, one, two, three
        self.kind = kind
        self.q = y * (1 - c) + x * c
        if kind == "down":
            self.choices = [
                (
                    c == k,
                    pltpu.make_async_copy(partial_ref[k], total, local),
                    Stage(links, [(partial_ref[1 - k], sib, links.sibling)], again=k == 1),
                )
                for k in range(2)
            ]
            self.local, self.core = self.choices[0][1:]
        else:
            self.choices = None
            self.local = pltpu.make_async_copy(partial_ref.at[:, :, :, c], total, local)
            self.core = Stage(links, [(partial_ref.at[:, :, :, 1 - c], sib, links.sibling)])
        if kind in ("up_y", "all_y"):
            self.first = Stage(links, [(total.at[1 - y], one, links.along_y)])
            self.kept = lambda i, j: (y, i, j)
        elif kind in ("up_x", "all_x"):
            self.first = Stage(links, [(total.at[:, 1 - x], one, links.along_x)])
            self.kept = lambda i, j: (i, x, j)
        else:
            turned = device(y + (1 - c) * (1 - 2 * y), x + c * (1 - 2 * x), z, c)
            self.first = Stage(links, [(total.at[1 - self.q], one, turned)])
            self.line = LineSum(links, lambda at: total.at[self.q, at], three)
        if kind == "up_y":
            self.line = LineSum(links, lambda at: total.at[y, :, at], three)
            self.last = Stage(links, [(total.at[y, 1 - x, z], two, links.along_x)])
        elif kind == "up_x":
            self.line = LineSum(links, lambda at: total.at[:, x, at], three)
            self.last = Stage(links, [(total.at[1 - y, x, z], two, links.along_y)])
        elif kind == "all_x":
            self.second = Stage(links, [(total.at[1 - y, x], two, links.along_y)])
        elif kind == "all_y":
            self.second = Stage(links, [(total.at[y, 1 - x], two, links.along_x)])
        if kind in ("all_x", "all_y"):
            self.line = LineSum(links, lambda at: total.at[y, x, at], three)

    def begin(self):
        if self.choices is None:
            self.core.start()
            self.local.start()
            return
        for taken, local, core in self.choices:

            @pl.when(taken)
            def _(local=local, core=core):
                core.start()
                local.start()

    def add(self, pairs, count):
        total = self.total

        def body(i, carry):
            index, extra = pairs(i)
            total[index] = total[index] + extra
            return carry

        lax.fori_loop(0, count, body, 0)

    def run_first(self):
        self.local.wait()
        self.core.wait()
        sib = self.sib
        if self.kind == "down":
            self.add(lambda i: ((i // 4, i % 4), sib[i // 4, i % 4]), 8)
        else:
            self.add(lambda i: ((i // 8, i // 4 % 2, i % 4), sib[i // 8, i // 4 % 2, i % 4]), 16)
        self.first.start()

    def run_second(self):
        self.first.wait()
        one = self.one
        if self.kind == "down":
            self.add(lambda i: ((self.q, i), one[i]), 4)
        else:
            self.add(lambda i: (self.kept(i // 4, i % 4), one[i // 4, i % 4]), 8)
        if self.kind in ("all_x", "all_y"):
            self.second.start()
        else:
            self.line.start()

    def run_third(self):
        self.second.wait()
        y, x, two = self.links.y, self.links.x, self.two
        self.add(lambda i: ((y, x, i), two[i]), 4)
        self.line.start()

    def run_last(self):
        z, total, got = self.links.z, self.total, self.three

        def add(slot):
            for i in range(2):
                index = self.kept(i, z)
                total[index] = total[index] + got[slot, i]

        self.line.collect(add)
        self.last.start()

    def finish(self, out):
        y, x, z = self.links.y, self.links.x, self.links.z
        if self.kind in ("up_y", "up_x"):
            self.last.wait()
            along_x = self.kind == "up_y"
            mine = x if along_x else y
            for number, part in ((mine, self.total[y, x, z]), (1 - mine, self.two[...])):
                for j in range(8):
                    place = (j // 4 * 2 + number) if along_x else (number * 2 + j // 4)
                    start = (place * 4 + j % 4) * 256 + (0 if along_x else 128)
                    at = pl.ds(pl.multiple_of(start, 128), 128)
                    out[:, at] = part[:, j * 128 : (j + 1) * 128].astype(jnp.float32)
            return
        out[...] = (self.total[self.q, z] if self.kind == "down" else self.total[y, x, z]).astype(jnp.float32)

        def add(slot):
            out[...] = out[...] + self.three[slot].astype(jnp.float32)

        self.line.collect(add)


def rear_kernel(scaling, *refs):
    live_ref, d_rows, heads_ref, logsum, rows_ref, qkv, small_ref = refs[:7]
    normal_one, inverse_one, d_second, gains_ref = refs[7:11]
    refs = refs[:7] + refs[11:]
    partials = (refs[7], refs[8], refs[9:11]) + tuple(refs[11:14])
    d_normed, g_qkv, g_up, g_down, g_out, g_patch, g_class, small_out = refs[14:22]
    at = 22
    d_out, d_heads, d_spread, grad_keys, grad_values = refs[at : at + 5]
    d_sent, d_got, q_part, q_sib, q_z, q_plane = refs[at + 5 : at + 11]
    small_own, small_got, send_sem, recv_sem, local_sem = refs[at + 11 : at + 16]
    scratch = refs[at + 16 :]
    links = Links(send_sem, recv_sem)
    y, x, z, c = links.y, links.x, links.z, links.c
    h = y * 2 + x
    rows, features = d_rows.shape
    slot_rows = rows * 4
    narrow = d_out.shape[1]
    heads = narrow // DH
    wide = 3 * narrow
    plane = [(links.across, 3 - h, 3), (links.along_x, y * 2 + 1 - x, 1), (links.along_y, (1 - y) * 2 + x, 2)]

    def columns(start, size):
        return pl.ds(pl.multiple_of(start, 128), size)

    def block(p):
        return pl.ds(pl.multiple_of(p * rows, rows), rows)

    spread_out = Stage(
        links, [(d_rows.at[:, columns(p * narrow, narrow)], d_out.at[block(h), :], peer) for peer, p, _ in plane]
    )
    own = pltpu.make_async_copy(d_rows.at[:, columns(h * narrow, narrow)], d_out.at[block(h), :], local_sem.at[0])
    kinds = ("up_y", "up_x", "down", "all_x", "all_x", "all_y")
    sums = [
        Sum(links, partials[i], *scratch[5 * i : 5 * i + 5], local_sem.at[1 + i], kinds[i]) for i in range(6)
    ]
    back = [Stage(links, [(d_sent.at[rel - 1], d_got.at[rel - 1], peer)]) for peer, _, rel in plane]
    q_core = Stage(links, [(q_part.at[:, :, :, 1 - c], q_sib, links.sibling)])
    q_line = LineSum(links, lambda at: q_part.at[:, :, at, c], q_z)
    q_across = Stage(
        links, [(q_part.at[p // 2, p % 2, z, c], q_plane.at[h], peer) for peer, p, _ in plane]
    )
    small_core = Stage(links, [(small_own.at[0], small_got.at[0], links.sibling)])
    small_x = Stage(links, [(small_own.at[1], small_got.at[1], links.along_x)])
    small_y = Stage(links, [(small_own.at[2], small_got.at[2], links.along_y)])
    small_z = Stage(links, [(small_own.at[3], small_got.at[3 + z], peer) for peer in links.along_z])

    links.greet()
    spread_out.start()
    own.start()
    for entry in sums:
        entry.begin()
    small_own[0] = small_ref[...]
    small_core.start()
    own.wait()
    spread_out.wait()
    live = live_ref[0]
    key_live = lax.broadcasted_iota(jnp.int32, (slot_rows, 1), 0) < live
    up_y, up_x, down, out, patch, classes = sums
    assert links.count <= REAR_COPIES

    def small_step(stage, number, following):
        def run():
            stage.wait()
            small_own[number + 1] = small_own[number] + small_got[number]
            if number == 2:
                small_got[3 + z] = small_own[3]
            following.start()

        return run

    def both(*steps):
        def run():
            for step in steps:
                step()

        return run

    events = {
        0: up_y.run_first,
        1: up_x.run_first,
        2: down.run_first,
        3: small_step(small_core, 0, small_x),
        4: patch.run_first,
        5: classes.run_first,
        6: out.run_first,
        7: small_step(small_x, 1, small_y),
        8: both(up_y.run_second, up_x.run_second),
        9: small_step(small_y, 2, small_z),
        11: both(up_y.line.relay, up_x.line.relay),
        13: down.run_second,
        14: patch.run_second,
        15: both(up_y.run_last, up_x.run_last),
    }

    def tile_body(slot, carry):
        number, turn = slot // 4, slot % 4
        at_slots(slot, events)
        at = block(turn)

        @pl.when(turn == 0)
        def _():
            grad_keys[...] = jnp.zeros_like(grad_keys)
            grad_values[...] = jnp.zeros_like(grad_values)

        queries = heads_ref[3 * number, at, :]
        keys = heads_ref[3 * number + 1]
        values = heads_ref[3 * number + 2]
        grads = d_heads[number, at, :]
        scores = lax.dot_general(keys, queries, (((1,), (1,)), ((), ())), preferred_element_type=jnp.float32)
        powers = scores * (scaling * LOG2E) - logsum[number, :, at]
        weights = jnp.where(key_live, jnp.exp2(powers), 0.0)
        grad_values[...] += jnp.dot(weights.astype(jnp.bfloat16), grads, preferred_element_type=jnp.float32)
        grad_weights = lax.dot_general(
            values, grads, (((1,), (1,)), ((), ())), preferred_element_type=jnp.float32
        )
        deltas = jnp.sum(grad_weights * weights, axis=0, keepdims=True)
        grad_scores = (weights * (grad_weights - deltas)).astype(jnp.bfloat16)
        grad_keys[...] += jnp.dot(grad_scores, queries, preferred_element_type=jnp.float32)
        grad_queries = lax.dot_general(
            keys, grad_scores, (((0,), (0,)), ((), ())), preferred_element_type=jnp.float32
        )
        d_heads[4 + 3 * number, at, :] = (grad_queries.T * scaling).astype(jnp.bfloat16)

        @pl.when(turn == 3)
        def _():
            d_heads[5 + 3 * number] = (grad_keys[...] * scaling).astype(jnp.bfloat16)
            d_heads[6 + 3 * number] = grad_values[...].astype(jnp.bfloat16)

        return carry

    for number in range(heads):
        d_heads[number] = d_out[:, number * DH : (number + 1) * DH]
    lax.fori_loop(0, SLOTS, tile_body, 0)
    for number in range(3 * heads):
        d_spread[:, number * DH : (number + 1) * DH] = d_heads[4 + number]
    per = features // 4
    for j in range(4):
        left = jnp.concatenate([rows_ref[p, :, j * per : (j + 1) * per] for p in range(4)], axis=0)
        piece = lax.dot_general(
            left, d_spread[...], (((0,), (0,)), ((), ())), preferred_element_type=jnp.float32
        ).astype(jnp.bfloat16)
        q_part[j // 2, j % 2] = piece.reshape(4, 2, per // 8, wide)
    q_core.start()
    weight = qkv[...].reshape(features, wide)
    for (_, p, rel), stage in zip(plane, back):
        piece = lax.dot_general(
            d_spread[block(p), :], weight, (((1,), (1,)), ((), ())), preferred_element_type=jnp.float32
        )
        d_sent[rel - 1] = piece.astype(jnp.bfloat16)
        stage.start()
    q_core.wait()

    def add_sib(i, carry):
        index = (i // 8, i // 4 % 2, i % 4)
        q_part[(*index, c)] = q_part[(*index, c)] + q_sib[index]
        return carry

    lax.fori_loop(0, 16, add_sib, 0)
    q_line.start()
    d_normed[...] = lax.dot_general(
        d_spread[block(h), :], weight, (((1,), (1,)), ((), ())), preferred_element_type=jnp.float32
    )
    down.line.relay()
    q_line.relay()
    patch.run_third()
    classes.run_second()
    out.run_second()
    patch.line.relay()
    classes.run_third()
    out.run_third()
    classes.line.relay()

    def add_line(slot):
        for i in range(4):
            index = (i // 2, i % 2)
            q_part[(*index, z, c)] = q_part[(*index, z, c)] + q_z[(slot, *index)]

    q_line.collect(add_line)
    q_across.start()
    out.line.relay()
    small_z.wait()
    small_out[...] = (small_got[3] + small_got[4] + small_got[5] + small_got[6])[0:2, 0:CLS]
    down.finish(g_down)
    up_y.finish(g_up)
    up_x.finish(g_up)
    patch.finish(g_patch)
    classes.finish(g_class)
    out.finish(g_out)
    q_across.wait()
    g_qkv[:, columns(h * wide, wide)] = q_part[y, x, z, c].astype(jnp.float32)
    for _, p, _ in plane:
        g_qkv[:, columns(p * wide, wide)] = q_plane[p].astype(jnp.float32)
    for stage in back:
        stage.wait()
    upstream = d_normed[...] + (
        d_got[0].astype(jnp.float32) + d_got[1].astype(jnp.float32) + d_got[2].astype(jnp.float32)
    )
    upstream = upstream * gains_ref[0:1, :]
    value = normal_one[...]
    middle = jnp.mean(upstream, axis=-1, keepdims=True)
    along = jnp.mean(upstream * value, axis=-1, keepdims=True)
    d_normed[...] = d_second[...] + inverse_one[:, 0:1] * (upstream - middle - value * along)
    links.drain()


def rear(live, d_rows, heads_qkv, logsum, rows_all, qkv, small, ending, partials, scaling):
    rows, features = d_rows.shape
    slot_rows = 4 * rows
    narrow = features // 4
    heads = narrow // DH
    wide = 3 * narrow
    vmem, hbm = pl.BlockSpec(memory_space=pltpu.VMEM), pl.BlockSpec(memory_space=pl.ANY)
    low = jnp.bfloat16
    up, _, down, _, *rest = [a.shape[-2:] for a in partials]
    shard = (features // 32, wide)
    buffers = []
    for _ in range(2):
        buffers += [(2, 2, 4) + up, (2, 2, 4) + up, (2, 4) + up, up, (5, 2) + up]
    buffers += [(2, 4) + down, (2, 4) + down, (4,) + down, (8, 128), (5,) + down]
    for shape in rest:
        buffers += [(2, 2, 4) + shape, (2, 2, 4) + shape, (2, 4) + shape, (4,) + shape, (5,) + shape]
    single = jnp.float32
    return pl.pallas_call(
        partial(rear_kernel, scaling),
        out_shape=[
            jax.ShapeDtypeStruct((rows, features), single),
            jax.ShapeDtypeStruct((features // 32, 4 * wide), single),
            jax.ShapeDtypeStruct((up[0], 4 * up[1]), single),
            jax.ShapeDtypeStruct(down, single),
        ]
        + [jax.ShapeDtypeStruct(shape, single) for shape in rest]
        + [jax.ShapeDtypeStruct((2, CLS), single)],
        in_specs=[pl.BlockSpec(memory_space=pltpu.SMEM)] + [vmem] * 10 + [hbm] * 7,
        out_specs=[vmem] * 8,
        scratch_shapes=[
            pltpu.VMEM((slot_rows, narrow), low),
            pltpu.VMEM((4 * heads, slot_rows, DH), low),
            pltpu.VMEM((slot_rows, wide), low),
            pltpu.VMEM((slot_rows, DH), single),
            pltpu.VMEM((slot_rows, DH), single),
            pltpu.VMEM((3, rows, features), low),
            pltpu.VMEM((3, rows, features), low),
            pltpu.VMEM((2, 2, 4, 2) + shard, low),
            pltpu.VMEM((2, 2, 4) + shard, low),
            pltpu.VMEM((5, 2, 2) + shard, low),
            pltpu.VMEM((4,) + shard, low),
            pltpu.VMEM((4,) + small.shape, single),
            pltpu.VMEM((7,) + small.shape, single),
            pltpu.SemaphoreType.DMA((REAR_COPIES,)),
            pltpu.SemaphoreType.DMA((REAR_COPIES,)),
            pltpu.SemaphoreType.DMA((7,)),
        ]
        + [pltpu.VMEM(shape, low) for shape in buffers],
        compiler_params=pltpu.CompilerParams(
            collective_id=2, has_side_effects=True, vmem_limit_bytes=58 * 2**20
        ),
        name="rear",
    )(live, d_rows, heads_qkv, logsum, rows_all, qkv, small, *ending, *partials)


def body_planned(
    tokens,
    patch_counts,
    w_qkv,
    w_out,
    w_up,
    w_down,
    w_patch,
    w_class,
    norm_gains,
    mask_norm,
    grad_masks,
):
    low = jnp.bfloat16
    h, s = lax.axis_index("head"), lax.axis_index("seq")
    tokens, grad_masks = tokens[0], grad_masks[0]
    row_count = tokens.shape[0]
    tile = lax.dynamic_update_slice(jnp.zeros((16, 128), low), norm_gains, (0, (s % 4) * 32))
    live = CLS + patch_counts
    scaling = DH ** (-0.5)

    sets = w_up.reshape(32, 2, 2, 4, 2, 128)
    up_blocks = jnp.concatenate(
        [sets[:, :, 0, :, 0], sets[:, :, 1, :, 0], sets[:, 0, :, :, 1], sets[:, 1, :, :, 1]], axis=1
    ).reshape(32, 4096)
    outs = front(
        live,
        tokens,
        tile,
        grad_masks,
        mask_norm,
        (w_qkv, w_out, up_blocks, w_down, w_patch, w_class),
        scaling,
    )
    attended, heads_qkv, logsum, rows_all, gains, qkv, class_masks, mask_sums = outs[:8]
    normal_one, inverse_one, normed_two, active, d_branch, d_hidden, rounded, d_patch = outs[8:16]
    class_rows, d_class, d_mix, d_second, d_attended = outs[16:]
    grad_down = [matmul_tn(active[k], d_branch[k]).astype(low) for k in range(2)]
    grad_up = [matmul_tn(normed_two[k], d_hidden[k]).astype(low) for k in range(2)]
    grad_out = matmul_tn(attended, d_mix).astype(low)
    grad_patch = matmul_tn(rounded, d_patch).astype(low)
    grad_class = matmul_tn(class_rows, d_class).astype(low)

    def parted(value):
        return value.reshape(2, 2, 4, 2, value.shape[0] // 32, value.shape[1])

    partials = (
        parted(grad_up[0]),
        parted(grad_up[1]),
        grad_down[0].reshape(2, 4, 128, 1024),
        grad_down[1].reshape(2, 4, 128, 1024),
        parted(grad_out),
        parted(grad_patch),
        parted(grad_class),
    )
    ending = (normal_one, inverse_one, d_second, gains)
    grad_inputs, g_qkv, g_up, g_down, g_out, g_patch, g_class, sums = rear(
        live, d_attended, heads_qkv, logsum, rows_all, qkv, mask_sums, ending, partials, scaling
    )
    gain_sums = [
        jnp.sum(weight.astype(jnp.float32) * grad, axis=1) for weight, grad in ((w_qkv, g_qkv), (w_up, g_up))
    ]
    return (
        class_masks[None],
        grad_inputs[None],
        g_qkv,
        g_out,
        g_up,
        g_down,
        g_patch,
        g_class,
        jnp.stack(gain_sums) / norm_gains.astype(jnp.float32),
        sums,
    )


def solution(mesh):
    planned = dict(mesh.shape) == {"head": 4, "seq": 8}
    return jax.shard_map(
        body_planned if planned else body_general,
        mesh=mesh,
        in_specs=(
            P("seq", "head", None),
            P("seq"),
            P(("head", "seq"), None),
            P(("head", "seq"), None),
            P(("head", "seq"), None),
            P(("head", "seq"), None),
            P(("head", "seq"), None),
            P(("head", "seq"), None),
            P(None, ("head", "seq")),
            P(),
            P("seq", "head", None),
        ),
        out_specs=(
            P("seq", "head", None),
            P("seq", "head", None),
            P(("head", "seq"), None),
            P(("head", "seq"), None),
            P(("head", "seq"), None),
            P(("head", "seq"), None),
            P(("head", "seq"), None),
            P(("head", "seq"), None),
            P(None, ("head", "seq")),
            P(),
        ),
        check_vma=False,
    )
```

```python
from functools import partial

import jax
import jax.numpy as jnp
from jax import lax
from jax.experimental import pallas as pl
from jax.experimental.pallas import tpu as pltpu
from jax.sharding import PartitionSpec as P

HEADS = 16
DH = 64
CLS = 150


def spread_2(value, axis, source):
    kept = jnp.where(lax.axis_index(axis) == source, value, 0).astype(value.dtype)
    return lax.psum(kept, axis)


def standardize(values):
    center = values - jnp.mean(values, axis=-1, keepdims=True)
    inverse = lax.rsqrt(jnp.mean(center * center, axis=-1, keepdims=True) + 1e-05)
    return (center * inverse, inverse)


def standard_back(normal, inverse, upstream):
    middle = jnp.mean(upstream, axis=-1, keepdims=True)
    along = jnp.mean(upstream * normal, axis=-1, keepdims=True)
    return inverse * (upstream - middle - normal * along)


def unit_scale(values):
    return lax.rsqrt(jnp.sum(values * values, axis=-1, keepdims=True) + 1e-06)


def unit_back(values, upstream):
    factor = unit_scale(values)
    direct = values * factor
    return factor * (upstream - direct * jnp.sum(upstream * direct, axis=-1, keepdims=True))


def block_scores(query_block, key_rows, key_live, scaling):
    scores = (
        jnp.einsum("qd,kd->qk", query_block, key_rows, preferred_element_type=jnp.float32) * scaling
    )
    return jnp.where(key_live, scores, -1e30)


def attend_head(queries, key_rows, values, key_live, scaling, blocks):
    head_width = queries.shape[-1]

    def single(query_block):
        scores = block_scores(query_block, key_rows, key_live, scaling)
        highest = jnp.max(scores, axis=-1, keepdims=True)
        weights_raw = jnp.exp(scores - highest)
        totals = jnp.sum(weights_raw, axis=-1, keepdims=True)
        weights = (weights_raw / totals).astype(jnp.bfloat16)
        output = jnp.einsum("qk,kd->qd", weights, values, preferred_element_type=jnp.float32)
        return (output.astype(jnp.bfloat16), (highest + jnp.log(totals))[:, 0])

    outputs, logsum = lax.map(single, queries.reshape(blocks, -1, head_width))
    return (outputs.reshape(-1, head_width), logsum.reshape(-1))


def attend_back(queries, key_rows, values, grad_out, logsum, key_live, scaling, blocks):
    head_width = queries.shape[-1]

    def single(running, pieces):
        grad_keys, grad_values = running
        query_block, grad_block, logsum_block = pieces
        scores = block_scores(query_block, key_rows, key_live, scaling)
        weights = jnp.exp(scores - logsum_block[:, None])
        grad_values = grad_values + jnp.einsum(
            "qk,qd->kd",
            weights.astype(jnp.bfloat16),
            grad_block,
            preferred_element_type=jnp.float32,
        )
        grad_weights = jnp.einsum(
            "qd,kd->qk", grad_block, values, preferred_element_type=jnp.float32
        )
        deltas = jnp.sum(grad_weights * weights, axis=-1, keepdims=True)
        grad_scores = (weights * (grad_weights - deltas)).astype(jnp.bfloat16)
        grad_query = (
            jnp.einsum("qk,kd->qd", grad_scores, key_rows, preferred_element_type=jnp.float32)
            * scaling
        )
        grad_keys = (
            grad_keys
            + jnp.einsum("qk,qd->kd", grad_scores, query_block, preferred_element_type=jnp.float32)
            * scaling
        )
        return ((grad_keys, grad_values), grad_query)

    zero_state = jnp.zeros(key_rows.shape, jnp.float32)
    pieces = (
        queries.reshape(blocks, -1, head_width),
        grad_out.reshape(blocks, -1, head_width),
        logsum.reshape(blocks, -1),
    )
    (grad_keys, grad_values), grad_queries = lax.scan(single, (zero_state, zero_state), pieces)
    return (grad_queries.reshape(-1, head_width), grad_keys, grad_values)


def body_general(
    tokens,
    patch_counts,
    w_qkv,
    w_out,
    w_up,
    w_down,
    w_patch,
    w_class,
    norm_gains,
    mask_norm,
    grad_masks,
):
    gains_rows = norm_gains.T
    gathered = (
        lax.all_gather(w_qkv, ("head", "seq"), axis=0, tiled=True),
        lax.all_gather(w_out, ("head", "seq"), axis=0, tiled=True),
        lax.all_gather(w_up, ("head", "seq"), axis=0, tiled=True),
        lax.all_gather(w_down, ("head", "seq"), axis=0, tiled=True),
        lax.all_gather(w_patch, ("head", "seq"), axis=0, tiled=True),
        lax.all_gather(w_class, ("head", "seq"), axis=0, tiled=True),
        lax.all_gather(gains_rows, ("head", "seq"), axis=0, tiled=True),
    )
    full_qkv, full_out, full_up, full_down, full_patch, full_class, full_gains = gathered
    gain_one = full_gains[:, 0].astype(jnp.float32)
    gain_two = full_gains[:, 1].astype(jnp.float32)
    image_count = tokens.shape[0]
    row_count = tokens.shape[1]
    groups = lax.axis_size("head")
    slot_rows = row_count * groups
    local_heads = HEADS // groups
    position = lax.axis_index("head") * row_count + jnp.arange(row_count, dtype=jnp.int32)
    live_limit = CLS + patch_counts
    patch_rows = ((position[None, :] >= CLS) & (position[None, :] < live_limit[:, None])).astype(
        jnp.float32
    )[:, :, None]
    key_live = (jnp.arange(slot_rows, dtype=jnp.int32)[None, :] < live_limit[:, None])[:, None, :]
    root_flag = (lax.axis_index("head") == 0).astype(jnp.float32)
    scaling = DH ** (-0.5)
    blocks = slot_rows // 512
    normal_one, inverse_one = standardize(tokens)
    normed_one = (normal_one * gain_one).astype(jnp.bfloat16)
    triple = jnp.einsum(
        "ird,dt->irt", normed_one, full_qkv, preferred_element_type=jnp.float32
    ).astype(jnp.bfloat16)
    spread = lax.all_to_all(triple, "head", split_axis=2, concat_axis=1, tiled=True).reshape(
        image_count, slot_rows, local_heads, 3, DH
    )
    image = 0
    outputs = []
    image_logsums = []
    for number in range(local_heads):
        output, logsum = attend_head(
            spread[image, :, number, 0],
            spread[image, :, number, 1],
            spread[image, :, number, 2],
            key_live[image],
            scaling,
            blocks,
        )
        outputs.append(output)
        image_logsums.append(logsum)
    image_outputs = [jnp.stack(outputs, axis=1).reshape(slot_rows, local_heads * DH)]
    logsums = [image_logsums]
    attended_heads = jnp.stack(image_outputs, axis=0)
    attended = lax.all_to_all(attended_heads, "head", split_axis=1, concat_axis=2, tiled=True)
    second = tokens + jnp.einsum(
        "ire,ed->ird", attended, full_out, preferred_element_type=jnp.float32
    )
    normal_two, inverse_two = standardize(second)
    normed_two = (normal_two * gain_two).astype(jnp.bfloat16)
    hidden = jnp.einsum("ird,df->irf", normed_two, full_up, preferred_element_type=jnp.float32)
    gelu_exact = partial(jax.nn.gelu, approximate=False)
    active = gelu_exact(hidden).astype(jnp.bfloat16)
    residual = second + jnp.einsum(
        "irf,fd->ird", active, full_down, preferred_element_type=jnp.float32
    )
    rounded = residual.astype(jnp.bfloat16)
    patch_proj = jnp.einsum("ird,de->ire", rounded, full_patch, preferred_element_type=jnp.float32)
    patch_unit = (patch_proj * unit_scale(patch_proj)).astype(jnp.bfloat16)
    class_proj = jnp.einsum(
        "ird,de->ire", rounded[:, :CLS], full_class, preferred_element_type=jnp.float32
    )
    class_unit = (class_proj * unit_scale(class_proj)).astype(jnp.bfloat16)
    classes = spread_2(class_unit, "head", 0)
    products = jnp.einsum("ird,icd->irc", patch_unit, classes, preferred_element_type=jnp.float32)
    normal_mask, inverse_mask = standardize(products)
    class_masks = (normal_mask * mask_norm[0] + mask_norm[1]) * patch_rows
    upstream = grad_masks * patch_rows
    norm_grads = lax.psum(
        jnp.stack([jnp.sum(upstream * normal_mask, axis=(0, 1)), jnp.sum(upstream, axis=(0, 1))]),
        ("head", "seq"),
    )
    d_products = standard_back(normal_mask, inverse_mask, upstream * mask_norm[0]).astype(
        jnp.bfloat16
    )
    d_patch_unit = jnp.einsum(
        "irc,icd->ird", d_products, classes, preferred_element_type=jnp.float32
    )
    class_part = jnp.einsum(
        "irc,ird->icd", d_products, patch_unit, preferred_element_type=jnp.float32
    )
    d_class_unit = lax.psum(class_part.astype(jnp.bfloat16), "head").astype(jnp.float32)
    d_patch_proj = unit_back(patch_proj, d_patch_unit).astype(jnp.bfloat16)
    d_class_proj = (unit_back(class_proj, d_class_unit) * root_flag).astype(jnp.bfloat16)
    regathered = (
        lax.all_gather(w_qkv, ("head", "seq"), axis=0, tiled=True),
        lax.all_gather(w_out, ("head", "seq"), axis=0, tiled=True),
        lax.all_gather(w_up, ("head", "seq"), axis=0, tiled=True),
        lax.all_gather(w_down, ("head", "seq"), axis=0, tiled=True),
        lax.all_gather(w_patch, ("head", "seq"), axis=0, tiled=True),
        lax.all_gather(w_class, ("head", "seq"), axis=0, tiled=True),
        lax.all_gather(gains_rows, ("head", "seq"), axis=0, tiled=True),
    )
    back_qkv, back_out, back_up, back_down, back_patch, back_class, back_gains = regathered
    back_one = back_gains[:, 0].astype(jnp.float32)
    back_two = back_gains[:, 1].astype(jnp.float32)
    grad_patch = jnp.einsum(
        "ird,ire->de", rounded, d_patch_proj, preferred_element_type=jnp.float32
    )
    grad_class = jnp.einsum(
        "ird,ire->de", rounded[:, :CLS], d_class_proj, preferred_element_type=jnp.float32
    )
    d_residual = jnp.einsum(
        "ire,de->ird", d_patch_proj, back_patch, preferred_element_type=jnp.float32
    )
    class_term = jnp.einsum(
        "ire,de->ird", d_class_proj, back_class, preferred_element_type=jnp.float32
    )
    d_residual = d_residual.at[:, :CLS].add(class_term)
    d_branch = d_residual.astype(jnp.bfloat16)
    grad_down = jnp.einsum("irf,ird->fd", active, d_branch, preferred_element_type=jnp.float32)
    d_active = jnp.einsum("ird,fd->irf", d_branch, back_down, preferred_element_type=jnp.float32)
    gelu_pull = jax.vjp(gelu_exact, hidden)[1]
    d_hidden = gelu_pull(d_active)[0].astype(jnp.bfloat16)
    grad_up = jnp.einsum("ird,irf->df", normed_two, d_hidden, preferred_element_type=jnp.float32)
    d_normed_two = jnp.einsum("irf,df->ird", d_hidden, back_up, preferred_element_type=jnp.float32)
    d_second = d_residual + standard_back(normal_two, inverse_two, d_normed_two * back_two)
    grad_gain_two = jnp.sum(d_normed_two * normal_two, axis=(0, 1))
    d_mix = d_second.astype(jnp.bfloat16)
    grad_out = jnp.einsum("ire,ird->ed", attended, d_mix, preferred_element_type=jnp.float32)
    d_attended = jnp.einsum(
        "ird,ed->ire", d_mix, back_out, preferred_element_type=jnp.float32
    ).astype(jnp.bfloat16)
    d_heads = lax.all_to_all(d_attended, "head", split_axis=2, concat_axis=1, tiled=True).reshape(
        image_count, slot_rows, local_heads, DH
    )
    image = 0
    head_grads = []
    for number in range(local_heads):
        grad_queries, grad_keys, grad_values = attend_back(
            spread[image, :, number, 0],
            spread[image, :, number, 1],
            spread[image, :, number, 2],
            d_heads[image, :, number],
            logsums[image][number],
            key_live[image],
            scaling,
            blocks,
        )
        head_grads.append(jnp.stack([grad_queries, grad_keys, grad_values], axis=1))
    image_grads = [jnp.stack(head_grads, axis=1).reshape(slot_rows, local_heads * 3 * DH)]
    d_spread = jnp.stack(image_grads, axis=0).astype(jnp.bfloat16)
    d_triple = lax.all_to_all(d_spread, "head", split_axis=1, concat_axis=2, tiled=True)
    grad_qkv = jnp.einsum("ird,irt->dt", normed_one, d_triple, preferred_element_type=jnp.float32)
    d_normed_one = jnp.einsum("irt,dt->ird", d_triple, back_qkv, preferred_element_type=jnp.float32)
    grad_inputs = d_second + standard_back(normal_one, inverse_one, d_normed_one * back_one)
    grad_gain_one = jnp.sum(d_normed_one * normal_one, axis=(0, 1))
    grad_gains = jnp.stack([grad_gain_one, grad_gain_two], axis=1)
    reduced = (
        lax.psum_scatter(grad_qkv, ("head", "seq"), scatter_dimension=0, tiled=True),
        lax.psum_scatter(grad_out, ("head", "seq"), scatter_dimension=0, tiled=True),
        lax.psum_scatter(grad_up, ("head", "seq"), scatter_dimension=0, tiled=True),
        lax.psum_scatter(grad_down, ("head", "seq"), scatter_dimension=0, tiled=True),
        lax.psum_scatter(grad_patch, ("head", "seq"), scatter_dimension=0, tiled=True),
        lax.psum_scatter(grad_class, ("head", "seq"), scatter_dimension=0, tiled=True),
        lax.psum_scatter(grad_gains, ("head", "seq"), scatter_dimension=0, tiled=True),
    )
    return (
        class_masks,
        grad_inputs,
        reduced[0],
        reduced[1],
        reduced[2],
        reduced[3],
        reduced[4],
        reduced[5],
        reduced[6].T,
        norm_grads,
    )


MESH = pl.DeviceIdType.MESH
LOG2E = 1.4426950408889634
SLOTS = 16
FRONT_COPIES = 160
REAR_COPIES = 88


def matmul(left, right):
    return jnp.dot(left, right, preferred_element_type=jnp.float32)


def matmul_nt(left, right):
    return lax.dot_general(left, right, (((1,), (1,)), ((), ())), preferred_element_type=jnp.float32)


def matmul_tn(left, right):
    return lax.dot_general(left, right, (((0,), (0,)), ((), ())), preferred_element_type=jnp.float32)


def norm(values):
    center = values - jnp.mean(values, axis=-1, keepdims=True)
    inverse = lax.rsqrt(jnp.mean(center * center, axis=-1, keepdims=True) + 1e-05)
    return center * inverse, inverse


def device(y, x, z, c):
    return (y * 2 + x, z * 2 + c)


class Links:
    def __init__(self, send_sem, recv_sem):
        head, seq = lax.axis_index("head"), lax.axis_index("seq")
        self.y, self.x, self.z, self.c = head // 2, head % 2, seq // 2, seq % 2
        y, x, z, c = self.y, self.x, self.z, self.c
        self.sibling = device(y, x, z, 1 - c)
        self.along_x = device(y, 1 - x, z, c)
        self.along_y = device(1 - y, x, z, c)
        self.across = device(1 - y, 1 - x, z, c)
        self.along_z = [device(y, x, (z + k) % 4, c) for k in (1, 2, 3)]
        self.send_sem, self.recv_sem, self.count, self.made, self.lines = send_sem, recv_sem, 0, [], []

    def greet(self):
        barrier = pltpu.get_barrier_semaphore()
        peers = [self.sibling, self.along_x, self.along_y, self.across] + self.along_z
        for peer in peers:
            pl.semaphore_signal(barrier, inc=1, device_id=peer, device_id_type=MESH)
        pl.semaphore_wait(barrier, len(peers))

    def plan(self, source, target, peer, sends=None, again=False):
        number = self.count - again
        self.count = number + 1
        copy = pltpu.make_async_remote_copy(
            src_ref=source,
            dst_ref=target,
            send_sem=self.send_sem.at[number],
            recv_sem=self.recv_sem.at[number],
            device_id=peer,
            device_id_type=MESH,
        )
        if not again:
            self.made.append((copy, sends))
        return copy

    def drain(self):
        for copy, sends in self.made:
            if sends is None:
                copy.wait_send()
            else:
                pl.when(sends)(copy.wait_send)
        for line in self.lines:
            line.drain()


class Stage:
    def __init__(self, links, moves, again=False):
        self.copies = [links.plan(*move, again=again) for move in moves]

    def start(self):
        for copy in self.copies:
            copy.start()

    def wait(self):
        for copy in self.copies:
            copy.wait_recv()


class Line:
    def __init__(self, links, piece, source=None):
        self.links, self.piece = links, piece
        self.source = piece(links.z) if source is None else source
        self.base = links.count
        links.count += 5
        links.lines.append(self)

    def copy(self, source, target, sent, landed):
        links = self.links
        return pltpu.make_async_remote_copy(
            src_ref=source,
            dst_ref=self.piece(landed),
            send_sem=links.send_sem.at[self.base + sent],
            recv_sem=links.recv_sem.at[self.base + landed],
            device_id=device(links.y, links.x, target, links.c),
            device_id_type=MESH,
        )

    def direct(self, target):
        z = self.links.z
        return (z != target) if target in (1, 2) else (z != target) & (z != 3 - target)

    def start(self):
        for target in (1, 2, 0, 3):

            @pl.when(self.direct(target))
            def _(target=target):
                self.copy(self.source, target, target, self.links.z).start()

    def relay(self):
        for at, end in ((2, 0), (1, 3)):

            @pl.when(self.links.z == at)
            def _(end=end):
                self.copy(self.source, 3 - end, 4, end).wait_recv()
                self.copy(self.piece(end), 3 - end, 4, end).start()

    def wait(self):
        z = self.links.z
        for origin in range(4):
            pending = z != origin
            if origin in (0, 3):
                pending = pending & (z != (2 if origin == 0 else 1))

            @pl.when(pending)
            def _(origin=origin):
                self.copy(self.source, 0, 0, origin).wait_recv()

    def drain(self):
        for target in range(4):

            @pl.when(self.direct(target))
            def _(target=target):
                self.copy(self.source, target, target, self.links.z).wait_send()

        @pl.when((self.links.z == 1) | (self.links.z == 2))
        def _():
            self.copy(self.source, 0, 4, 0).wait_send()


def at_slots(slot, events):
    for number, event in events.items():
        pl.when(slot == number)(event)


def front_kernel(scaling, *refs):
    live_ref, tokens, norm_gains, grad_masks, mask_norm = refs[:5]
    qkv_shard, out_shard, up_given, down_shard, patch_shard, class_shard = refs[5:11]
    attended, heads_ref, logsum, rows_ref, gains_ref, qkv, class_masks, mask_sums = refs[11:19]
    normal_one, inverse_one, normed_two, active, d_branch, d_hidden, rounded, d_patch = refs[19:27]
    class_rows, d_class, d_mix, d_second, d_attended = refs[27:32]
    full_out, ups, downs, full_patch, full_class, tiles, staged = refs[32:39]
    slope, second, normal_two, inverse_two, residual, patch_proj, class_proj, classes = refs[39:47]
    part_sent, part_got, back_sent, back_got, class_sent, class_got = refs[47:53]
    term_sent, term_got, d_residual, mask_in, tile, up_shard = refs[53:59]
    send_sem, recv_sem, local_sem = refs[59:]
    links = Links(send_sem, recv_sem)
    y, x, z, c = links.y, links.x, links.z, links.c
    h = y * 2 + x
    q = y * (1 - c) + x * c
    rows, features = tokens.shape
    wide = qkv.shape[-1]
    narrow = staged.shape[1]
    heads = narrow // DH
    block = ups.shape[-1]
    slot_rows = rows * 4
    plane = [(links.across, 3 - h, 3), (links.along_x, y * 2 + 1 - x, 1), (links.along_y, (1 - y) * 2 + x, 2)]
    at_x, at_y = plane[1][1], plane[2][1]

    def columns(start, size):
        return pl.ds(pl.multiple_of(start, 128), size)

    def up_block(number):
        return up_shard.at[:, columns(number * block, block)]

    local = [
        pltpu.make_async_copy(source, target, local_sem.at[number])
        for number, (source, target) in zip(
            (0, 1, 2, 3, 4, 5, 7, 8),
            [
                (tile, tiles.at[y, x, z, c]),
                (qkv_shard.at[:, columns(h * wide, wide)], qkv.at[y, x, z, c]),
                (out_shard, full_out.at[y, x, z, c]),
                (down_shard, downs.at[c, q, z]),
                (up_block(x), ups.at[0, y, x, z, c]),
                (up_block(2 + y), ups.at[1, y, x, z, c]),
                (patch_shard, full_patch.at[y, x, z, c]),
                (class_shard, full_class.at[y, x, z, c]),
            ]
        )
    ]
    gain_core = Stage(links, [(tile, tiles.at[y, x, z, c], links.sibling)])
    gain_z = Stage(links, [(tiles.at[y, x, z], tiles.at[y, x, z], peer) for peer in links.along_z])
    gain_plane = Stage(links, [(tiles.at[y, x], tiles.at[y, x], peer) for peer, _, _ in plane])
    qkv_plane = Stage(
        links, [(qkv_shard.at[:, columns(p * wide, wide)], qkv.at[y, x, z, c], peer) for peer, p, _ in plane]
    )
    part = qkv.shape[4] // 2
    qkv_z = [Line(links, lambda at, k=k: qkv.at[:, :, at, c, k * part : (k + 1) * part]) for k in range(2)]
    qkv_core = Stage(links, [(qkv.at[:, :, :, c], qkv.at[:, :, :, c], links.sibling)])
    up_split = [
        Stage(links, [(up_block(1 - x), ups.at[0, y, x, z, c], links.along_x)]),
        Stage(links, [(up_block(2 + 1 - y), ups.at[1, y, x, z, c], links.along_y)]),
    ]
    up_z = [
        Line(links, lambda at: ups.at[0, y, :, at, c]),
        Line(links, lambda at: ups.at[1, :, x, at, c]),
    ]
    up_on = [
        Stage(links, [(ups.at[0, y, :, :, c], ups.at[0, y, :, :, c], links.along_y)]),
        Stage(links, [(ups.at[1, :, x, :, c], ups.at[1, :, x, :, c], links.along_x)]),
    ]
    up_core = [
        Stage(links, [(ups.at[k, :, :, :, c], ups.at[k, :, :, :, c], links.sibling)]) for k in range(2)
    ]
    some = down_shard.shape[0] // 4
    turned = device(y + (1 - c) * (1 - 2 * y), x + c * (1 - 2 * x), z, c)
    spans = [slice(k * some, (k + 1) * some) for k in range(4)]
    down_turn = [Stage(links, [(down_shard.at[spans[k]], downs.at[c, q, z, spans[k]], turned)]) for k in (0, 1)]
    down_z = [Line(links, lambda at, k=k: downs.at[c, :, at, spans[k]]) for k in (0, 1)] + [
        Line(links, lambda at, k=k: downs.at[c, q, at, spans[k]], down_shard.at[spans[k]]) for k in (2, 3)
    ]
    down_on = [Stage(links, [(downs.at[c, q, :, spans[k]],) * 2 + (turned,)]) for k in (2, 3)]
    down_core = [
        Stage(links, [(downs.at[c, :, :, span], downs.at[c, :, :, span], links.sibling)])
        for span in (slice(0, 2 * some), slice(2 * some, 4 * some))
    ]
    part = out_shard.shape[0] // 2

    def square(full, shard):
        first = [full.at[y, x, :, c, 0:part], full.at[y, x, :, c, part:]]
        second = [full.at[:, x, :, c, 0:part], full.at[y, :, :, c, part:]]
        return (
            Line(links, lambda at: full.at[y, x, at, c], shard),
            Stage(links, [(first[0], first[0], links.along_y), (first[1], first[1], links.along_x)]),
            Stage(links, [(second[0], second[0], links.along_x), (second[1], second[1], links.along_y)]),
            Stage(links, [(full.at[:, :, :, c],) * 2 + (links.sibling,)]),
        )

    out_z, out_one, out_two, out_core = square(full_out, out_shard)
    near, far = slice(0, part), slice(part, 2 * part)
    patch_x = Stage(links, [(patch_shard.at[far], full_patch.at[y, x, z, c, far], links.along_x)])
    patch_y = Stage(links, [(full_patch.at[y, :, z, c, far],) * 2 + (links.along_y,)])
    patch_first = Line(links, lambda at: full_patch.at[y, x, at, c, near], patch_shard.at[near])
    patch_one = Stage(links, [(full_patch.at[y, x, :, c, near],) * 2 + (links.along_y,)])
    patch_two = Stage(links, [(full_patch.at[:, x, :, c, near],) * 2 + (links.along_x,)])
    class_y = Stage(links, [(class_shard, full_class.at[y, x, z, c], links.along_y)])
    class_x = Stage(links, [(full_class.at[:, x, z, c],) * 2 + (links.along_x,)])
    halves = [slice(k * part, (k + 1) * part) for k in range(2)]
    class_z = [Line(links, lambda at, k=k: full_class.at[:, :, at, c, k * part : (k + 1) * part]) for k in range(2)]
    halves = [slice(part + k * part // 2, part + (k + 1) * part // 2) for k in range(2)]
    patch_z = [Line(links, lambda at, k=k: full_patch.at[:, :, at, c, halves[k]]) for k in range(2)]
    patch_core = Stage(links, [(full_patch.at[:, :, :, c],) * 2 + (links.sibling,)])
    class_core = Stage(links, [(full_class.at[:, :, :, c],) * 2 + (links.sibling,)])
    beside = (links.along_x, links.along_y)
    here = slice(0, rows)
    few = class_proj.shape[0]
    tall = -(-CLS // 16) * 16
    parts = (slice(0, tall), slice(tall, rows))
    theirs = [slice(rows + at.start, rows + at.stop) for at in parts]

    def exchange(sent, got, sent_at, got_at):
        return [
            [Stage(links, [(sent.at[k, sent_at[i]], got.at[k, got_at[i]], beside[k])]) for i in range(2)]
            for k in range(2)
        ]

    normed_out = exchange(normed_two, normed_two, parts, theirs)
    branch_out = exchange(d_branch, d_branch, parts, theirs)
    part_back = exchange(part_sent, part_got, parts, parts)
    grad_back = exchange(back_sent, back_got, parts, parts)
    sizes = {1: few, 2: few, 3: tall - 3 * few}
    class_out = [
        links.plan(
            rounded.at[few * rel : few * rel + sizes[rel]], class_rows.at[0 : sizes[rel]], peer, h == 0
        )
        for peer, _, rel in plane
    ]
    mine = pl.ds(pl.multiple_of(h * few, few), few)
    unit_out = Stage(links, [(classes.at[mine], classes.at[mine], peer) for peer, _, _ in plane])
    class_back = Stage(links, [(class_sent.at[p], class_got.at[rel - 1], peer) for peer, p, rel in plane])
    term_back = [
        links.plan(term_sent.at[0 : sizes[rel]], term_got.at[rel - 1, 0 : sizes[rel]], peer, h == rel)
        for peer, _, rel in plane
    ]
    middle = rows // 2
    strips = [slice(0, middle), slice(middle, rows)]
    rows_x = [Stage(links, [(rows_ref.at[h, strips[k]],) * 2 + (links.along_x,)]) for k in (0, 1)]
    rows_y = [Stage(links, [(rows_ref.at[h, strips[k]],) * 2 + (links.along_y,)]) for k in (1, 0)]
    piece_a, piece_b = rows_ref.at[at_x, strips[0]], rows_ref.at[at_y, strips[1]]
    relay_y = Stage(links, [(piece_a, piece_a, links.along_y)])
    relay_x = Stage(links, [(piece_b, piece_b, links.along_x)])

    share = norm_gains.shape[1]
    tile[...] = jnp.zeros_like(tile)
    for i in range(4):

        @pl.when((z * 2 + c) % 4 == i)
        def _(i=i):
            tile[0:2, i * share : (i + 1) * share] = norm_gains[...].astype(jnp.float32)

    for number in range(4):
        for j in range(8):
            at = (j // 4 * 2 + number) if number < 2 else ((number - 2) * 2 + j // 4)
            at = (at * 4 + j % 4) * 256 + (0 if number < 2 else 128)
            up_shard[:, number * block + j * 128 : number * block + (j + 1) * 128] = up_given[:, at : at + 128]
    for copy in local:
        copy.start()
    class_rows[...] = jnp.zeros_like(class_rows)
    links.greet()
    for stage in (gain_core, qkv_plane, *up_split, *down_turn, class_y, patch_x, out_z, patch_first):
        stage.start()
    value, inverse = norm(tokens[...])
    normal_one[...] = value
    inverse_one[...] = jnp.broadcast_to(inverse, inverse_one.shape)
    local[0].wait()
    gain_core.wait()
    gain_z.start()
    gain_z.wait()
    gain_plane.start()
    local[1].wait()
    qkv_plane.wait()
    for line in qkv_z:
        line.start()
    gain_plane.wait()
    for j in range(8):
        piece = tiles[j // 4, j // 2 % 2, (j % 2) * 2, 0].astype(jnp.float32)
        for i in range(1, 4):
            piece = piece + tiles[j // 4, j // 2 % 2, (j % 2) * 2 + i // 2, i % 2].astype(jnp.float32)
        gains_ref[:, j * 128 : (j + 1) * 128] = piece[0:8]
    rows_ref[h] = (normal_one[...] * gains_ref[0:1, :]).astype(jnp.bfloat16)
    for stage in (rows_x[0], rows_y[0], rows_x[1], rows_y[1]):
        stage.start()
    for line in (out_z, patch_first, *qkv_z):
        line.relay()
    rows_x[0].wait()
    relay_y.start()
    rows_y[0].wait()
    relay_x.start()
    local[6].wait()
    patch_x.wait()
    patch_y.start()
    local[7].wait()
    class_y.wait()
    class_x.start()
    for line in qkv_z:
        line.wait()
    qkv_core.start()
    for k in range(2):
        local[4 + k].wait()
        up_split[k].wait()
        up_z[k].start()
    out_z.wait()
    patch_first.wait()
    for number in (2, 3):
        local[number].wait()

    def project(p):
        weight = qkv[...].reshape(rows * 4, wide)
        piece = jnp.dot(rows_ref[p], weight, preferred_element_type=jnp.float32).astype(jnp.bfloat16)
        at = pl.ds(pl.multiple_of(p * rows, rows), rows)
        for number in range(3 * heads):
            heads_ref[number, at, :] = piece[:, number * DH : (number + 1) * DH]

    qkv_core.wait()
    project(h)
    rows_x[1].wait()
    project(at_x)
    rows_y[1].wait()
    project(at_y)
    out_one.start()
    patch_one.start()
    relay_y.wait()
    relay_x.wait()
    project(3 - h)

    live = live_ref[0]
    key_live = lax.broadcasted_iota(jnp.int32, (slot_rows, 1), 0) < live
    returned = links.count - 1
    assert returned + 4 <= FRONT_COPIES

    def back(rel):
        peer = h + (rel % 2) * (1 - 2 * x) + (rel // 2) * (2 - 4 * y)
        return pltpu.make_async_remote_copy(
            src_ref=staged.at[pl.ds(pl.multiple_of(peer * rows, rows), rows), :],
            dst_ref=attended.at[:, columns(h * narrow, narrow)],
            send_sem=send_sem.at[returned + rel],
            recv_sem=recv_sem.at[returned + rel],
            device_id=(peer, z * 2 + c),
            device_id_type=MESH,
        )

    def up_next(k):
        up_z[k].wait()
        up_on[k].start()

    def up_end(k):
        up_on[k].wait()
        up_core[k].start()

    def out_next():
        out_one.wait()
        out_two.start()

    def out_end():
        out_two.wait()
        out_core.start()

    def patch_next():
        patch_one.wait()
        patch_two.start()

    def down_late():
        down_z[2].start()
        down_z[3].start()

    def down_early():
        for stage in down_turn:
            stage.wait()
        down_z[0].start()
        down_z[1].start()

    def down_relays():
        down_z[2].relay()
        down_z[3].relay()

    events = {
        0: up_z[0].relay,
        3: out_next,
        5: up_z[1].relay,
        6: down_late,
        11: down_early,
        12: out_end,
        14: down_relays,
    }

    def tile_body(slot, carry):
        turn, number = slot // 4, slot % 4
        rel = 3 - turn
        peer = h + (rel % 2) * (1 - 2 * x) + (rel // 2) * (2 - 4 * y)
        at = pl.ds(pl.multiple_of(peer * rows, rows), rows)
        at_slots(slot, events)
        queries = heads_ref[3 * number, at, :]
        keys = heads_ref[3 * number + 1]
        values = heads_ref[3 * number + 2]
        scores = lax.dot_general(keys, queries, (((1,), (1,)), ((), ())), preferred_element_type=jnp.float32)
        scores = jnp.where(key_live, scores * (scaling * LOG2E), -1e30)
        highest = jnp.max(scores, axis=0, keepdims=True)
        raw = jnp.exp2(scores - highest)
        totals = jnp.sum(raw, axis=0, keepdims=True)
        weights = (raw * (1.0 / totals)).astype(jnp.bfloat16)
        mixed = lax.dot_general(
            values, weights, (((0,), (0,)), ((), ())), preferred_element_type=jnp.float32
        )
        mixed = mixed.T.astype(jnp.bfloat16)
        for which in range(4):

            @pl.when(number == which)
            def _(which=which):
                staged[at, which * DH : (which + 1) * DH] = mixed

        logsum[number, :, at] = highest + jnp.log2(totals)

        @pl.when((number == 3) & (rel > 0))
        def _():
            back(rel).start()

        return carry

    lax.fori_loop(0, SLOTS, tile_body, 0)
    own = pltpu.make_async_copy(
        staged.at[pl.ds(pl.multiple_of(h * rows, rows), rows), :],
        attended.at[:, columns(h * narrow, narrow)],
        local_sem.at[6],
    )
    own.start()
    class_x.wait()
    patch_y.wait()
    for line in (*class_z, *patch_z):
        line.start()
    up_next(0)
    up_next(1)
    for k in range(2):
        down_z[2 + k].wait()
        down_on[k].start()
    for rel in (3, 2, 1):
        back(rel).wait()
    own.wait()
    out_core.wait()
    down_z[0].relay()

    def whole(weight):
        return weight[...].reshape(-1, weight.shape[-1])

    second[...] = tokens[...] + matmul(attended[...], whole(full_out))
    value, inverse = norm(second[...])
    normal_two[...] = value
    inverse_two[...] = jnp.broadcast_to(inverse, inverse_two.shape)
    value = (value * gains_ref[1:2, :]).astype(jnp.bfloat16)
    for k in range(2):
        normed_two[k, here] = value
    for i in range(2):
        for k in range(2):
            normed_out[k][i].start()
    down_z[1].relay()
    patch_next()
    up_end(0)
    up_end(1)
    for k in range(2):
        up_core[k].wait()
    wide_step = 256

    def forward(k, at, size):
        def step(j, carry):
            span = pl.ds(pl.multiple_of(j * wide_step, wide_step), wide_step)
            weight = ups[k, :, :, :, :, :, span].reshape(features, wide_step)
            hidden = matmul(normed_two[k, at], weight)
            spread = 0.5 + 0.5 * lax.erf(hidden * 0.7071067811865476)
            density = jnp.exp(hidden * hidden * -0.5) * 0.3989422804014327
            active[k, at, span] = (hidden * spread).astype(jnp.bfloat16)
            slope[k, at, span] = spread + hidden * density
            return carry

        lax.fori_loop(0, block // wide_step, step, 0)

    forward(0, here, rows)
    for stage in down_on:
        stage.wait()
    down_core[1].start()
    forward(1, here, rows)
    for line in down_z[:2]:
        line.wait()
    down_core[0].start()
    for stage in down_core:
        stage.wait()
    for i in range(2):
        for k in range(2):
            normed_out[k][i].wait()
            forward(k, theirs[i], parts[i].stop - parts[i].start)
            part_sent[k, parts[i]] = matmul(active[k, theirs[i]], whole(downs.at[k])).astype(jnp.bfloat16)
            part_back[k][i].start()
        if i == 0:
            for line in class_z:
                line.relay()
    residual[...] = second[...] + (
        matmul(active[0, here], whole(downs.at[0])) + matmul(active[1, here], whole(downs.at[1]))
    )
    for line in patch_z:
        line.relay()

    def complete(at):
        for k in range(2):
            part_back[k][0 if at.start == 0 else 1].wait()
        value = residual[at] + (part_got[0, at].astype(jnp.float32) + part_got[1, at].astype(jnp.float32))
        rounded[at] = value.astype(jnp.bfloat16)

    complete(parts[0])

    @pl.when(h == 0)
    def _():
        for copy in class_out:
            copy.start()
        class_rows[...] = rounded[0:few]

    for line in class_z:
        line.wait()
    class_core.start()
    complete(parts[1])
    for line in patch_z:
        line.wait()
    patch_two.wait()
    patch_core.start()
    patch_core.wait()

    patch_proj[...] = matmul(rounded[...], whole(full_patch))
    factor = unit_scale(patch_proj[...])
    patch_unit = (patch_proj[...] * factor).astype(jnp.bfloat16)
    classes[4 * few :] = jnp.zeros((classes.shape[0] - 4 * few, features), jnp.bfloat16)
    for copy, (_, _, rel) in zip(class_out, plane):
        pl.when(h == rel)(copy.wait_recv)
    class_core.wait()
    class_live = h * few + lax.broadcasted_iota(jnp.int32, (few, 1), 0) < CLS
    value = matmul(class_rows[...], whole(full_class))
    class_proj[...] = value
    classes[mine] = jnp.where(class_live, value * unit_scale(value), 0.0).astype(jnp.bfloat16)
    unit_out.start()
    mask_in[...] = jnp.zeros_like(mask_in)
    mask_in[0:rows, 0:CLS] = grad_masks[...]
    mask_in[rows : rows + 2, 0:CLS] = mask_norm[...]
    mask_gain, mask_bias = mask_in[rows : rows + 1, :], mask_in[rows + 1 : rows + 2, :]
    unit_out.wait()
    products = matmul_nt(patch_unit, classes[...])
    lane = lax.broadcasted_iota(jnp.int32, products.shape, 1)
    position = h * rows + lax.broadcasted_iota(jnp.int32, (rows, 1), 0)
    patch_rows = ((position >= CLS) & (position < live)).astype(jnp.float32)

    def class_mean(values):
        return jnp.sum(values, axis=-1, keepdims=True) * (1.0 / CLS)

    center = jnp.where(lane < CLS, products - class_mean(products), 0.0)
    inverse = lax.rsqrt(class_mean(center * center) + 1e-05)
    mask_normal = center * inverse
    class_masks[...] = ((mask_normal * mask_gain + mask_bias) * patch_rows)[:, 0:CLS]
    upstream = mask_in[0:rows, :] * patch_rows
    mask_sums[...] = jnp.zeros_like(mask_sums)
    mask_sums[0:1, :] = jnp.sum(upstream * mask_normal, axis=0, keepdims=True)
    mask_sums[1:2, :] = jnp.sum(upstream, axis=0, keepdims=True)
    upstream = upstream * mask_gain
    upstream = inverse * (upstream - class_mean(upstream) - mask_normal * class_mean(upstream * mask_normal))
    d_products = jnp.where(lane < CLS, upstream, 0.0).astype(jnp.bfloat16)
    class_part = matmul_tn(d_products, patch_unit)
    for p in range(4):
        class_sent[p] = class_part[few * p : few * (p + 1)].astype(jnp.bfloat16)
    class_back.start()
    upstream = matmul(d_products, classes[...])
    direct = patch_proj[...] * factor
    upstream = factor * (upstream - direct * jnp.sum(upstream * direct, axis=-1, keepdims=True))
    d_patch[...] = upstream.astype(jnp.bfloat16)
    d_residual[...] = matmul_nt(d_patch[...], whole(full_patch))

    def branch(i):
        value = d_residual[parts[i]].astype(jnp.bfloat16)
        for k in range(2):
            d_branch[k, parts[i]] = value
            branch_out[k][i].start()

    branch(1)
    class_back.wait()
    upstream = class_sent[h].astype(jnp.float32)
    for number in range(3):
        upstream = upstream + class_got[number].astype(jnp.float32)
    d_class[...] = jnp.where(class_live, unit_back(class_proj[...], upstream), 0.0).astype(jnp.bfloat16)
    term = matmul_nt(d_class[...], whole(full_class))
    term_sent[...] = term.astype(jnp.bfloat16)
    for copy, (_, _, rel) in zip(term_back, plane):
        pl.when(h == rel)(copy.start)

    def backward(k, at):
        for j in range(block // wide_step):
            weight = downs[k, j // 2, 2 * (j % 2) : 2 * (j % 2) + 2].reshape(wide_step, features)
            span = slice(j * wide_step, (j + 1) * wide_step)
            d_hidden[k, at, span] = (matmul_nt(d_branch[k, at], weight) * slope[k, at, span]).astype(jnp.bfloat16)


    def returned_rows(i):
        for k in range(2):
            branch_out[k][i].wait()
            backward(k, theirs[i])
            back_sent[k, parts[i]] = matmul_nt(d_hidden[k, theirs[i]], whole(ups.at[k])).astype(jnp.bfloat16)
            grad_back[k][i].start()

    for k in range(2):
        backward(k, parts[1])
    returned_rows(1)

    @pl.when(h == 0)
    def _():
        d_residual[0:few] = d_residual[0:few] + term_sent[...].astype(jnp.float32)
        for copy, (_, _, rel) in zip(term_back, plane):
            copy.wait_recv()
            at = slice(few * rel, few * rel + sizes[rel])
            d_residual[at] = d_residual[at] + term_got[rel - 1, 0 : sizes[rel]].astype(jnp.float32)

    branch(0)
    for k in range(2):
        backward(k, parts[0])
    returned_rows(0)
    upstream = matmul_nt(d_hidden[0, here], whole(ups.at[0])) + matmul_nt(d_hidden[1, here], whole(ups.at[1]))
    for k in range(2):
        for stage in grad_back[k]:
            stage.wait()
    upstream = upstream + (back_got[0].astype(jnp.float32) + back_got[1].astype(jnp.float32))
    upstream = upstream * gains_ref[1:2, :]
    value = normal_two[...]
    middle = jnp.mean(upstream, axis=-1, keepdims=True)
    along = jnp.mean(upstream * value, axis=-1, keepdims=True)
    d_second[...] = d_residual[...] + inverse_two[:, 0:1] * (upstream - middle - value * along)
    d_mix[...] = d_second[...].astype(jnp.bfloat16)
    d_attended[...] = matmul_nt(d_mix[...], whole(full_out)).astype(jnp.bfloat16)
    links.drain()


def front(live, tokens, norm_gains, grad_masks, mask_norm, shards, scaling):
    rows, features = tokens.shape
    vmem, hbm = pl.BlockSpec(memory_space=pltpu.VMEM), pl.BlockSpec(memory_space=pl.ANY)
    w_qkv, w_out, w_up, w_down, w_patch, w_class = shards
    wide = w_qkv.shape[1] // 4
    heads = wide // (3 * DH)
    block = w_up.shape[1] // 4
    lanes = 256
    few = -(-CLS // 64) * 16
    low, single = jnp.bfloat16, jnp.float32
    outs = [
        ((rows, features), low),
        ((3 * heads, 4 * rows, DH), low),
        ((heads, 1, 4 * rows), single),
        ((4, rows, features), low),
        ((8, features), single),
        ((2, 2, 4, 2, w_qkv.shape[0], wide), low),
        (grad_masks.shape, single),
        ((8, lanes), single),
        ((rows, features), single),
        ((rows, 128), single),
        ((2, 2 * rows, features), low),
        ((2, 2 * rows, block), low),
        ((2, 2 * rows, features), low),
        ((2, 2 * rows, block), low),
        ((rows, features), low),
        ((rows, features), low),
        ((few, features), low),
        ((few, features), low),
        ((rows, features), low),
        ((rows, features), single),
        ((rows, features), low),
    ]
    scratch = [
        ((2, 2, 4, 2) + w_out.shape, low),
        ((2, 2, 2, 4, 2, w_up.shape[0], block), low),
        ((2, 2, 4) + w_down.shape, low),
        ((2, 2, 4, 2) + w_patch.shape, low),
        ((2, 2, 4, 2) + w_class.shape, low),
        ((2, 2, 4, 2, 8, 128), single),
        ((4 * rows, wide // 3), low),
        ((2, 2 * rows, block), single),
        ((rows, features), single),
        ((rows, features), single),
        ((rows, 128), single),
        ((rows, features), single),
        ((rows, features), single),
        ((few, features), single),
        ((lanes, features), low),
        ((2, rows, features), low),
        ((2, rows, features), low),
        ((2, rows, features), low),
        ((2, rows, features), low),
        ((4, few, features), low),
        ((3, few, features), low),
        ((few, features), low),
        ((3, few, features), low),
        ((rows, features), single),
        ((rows + 8, lanes), single),
        ((8, 128), single),
        (w_up.shape, low),
    ]
    return pl.pallas_call(
        partial(front_kernel, scaling),
        out_shape=[jax.ShapeDtypeStruct(*out) for out in outs],
        in_specs=[pl.BlockSpec(memory_space=pltpu.SMEM)] + [vmem] * 4 + [hbm] * 2 + [vmem] + [hbm] * 3,
        out_specs=[vmem] * len(outs),
        scratch_shapes=[pltpu.VMEM(*shape) for shape in scratch]
        + [
            pltpu.SemaphoreType.DMA((FRONT_COPIES,)),
            pltpu.SemaphoreType.DMA((FRONT_COPIES,)),
            pltpu.SemaphoreType.DMA((9,)),
        ],
        compiler_params=pltpu.CompilerParams(
            collective_id=1, has_side_effects=True, vmem_limit_bytes=60 * 2**20
        ),
        name="front",
    )(live, tokens, norm_gains, grad_masks, mask_norm, *shards)


class LineSum:
    def __init__(self, links, piece, got):
        self.links, self.piece, self.got = links, piece, got
        self.base = links.count
        links.count += 5
        links.lines.append(self)

    def copy(self, piece, target, slot, sent):
        links = self.links
        return pltpu.make_async_remote_copy(
            src_ref=self.piece(piece),
            dst_ref=self.got.at[slot],
            send_sem=links.send_sem.at[self.base + sent],
            recv_sem=links.recv_sem.at[self.base + slot],
            device_id=device(links.y, links.x, target, links.c),
            device_id_type=MESH,
        )

    def start(self):
        z = self.links.z
        for target, end, middle in ((3, 0, 1), (0, 3, 2)):

            @pl.when(z == end)
            def _(target=target, middle=middle):
                self.copy(target, middle, 4, target).start()

        for target in range(4):
            direct = z != target
            if target in (0, 3):
                direct = z == (1 if target == 0 else 2)

            @pl.when(direct)
            def _(target=target):
                self.copy(target, target, z, target).start()

    def relay(self):
        z = self.links.z
        for target, middle in ((3, 1), (0, 2)):

            @pl.when(z == middle)
            def _(target=target, middle=middle):
                self.copy(target, target, 4, target).wait_recv()
                own = self.piece(target)
                own[...] = own[...] + self.got[4]
                self.copy(target, target, middle, target).start()

    def collect(self, add):
        z = self.links.z
        for origin in range(4):
            comes = z != origin
            if origin in (0, 3):
                comes = comes & (z != 3 - origin)

            @pl.when(comes)
            def _(origin=origin):
                self.copy(0, 0, origin, 0).wait_recv()
                add(origin)

    def drain(self):
        for target in range(4):

            @pl.when(self.links.z != target)
            def _(target=target):
                self.copy(target, target, 0, target).wait_send()


class Sum:
    def __init__(self, links, partial_ref, total, sib, one, two, three, local, kind):
        y, x, z, c = links.y, links.x, links.z, links.c
        self.links, self.total, self.sib, self.one, self.two, self.three = links, total, sib, one, two, three
        self.kind = kind
        self.q = y * (1 - c) + x * c
        if kind == "down":
            self.choices = [
                (
                    c == k,
                    pltpu.make_async_copy(partial_ref[k], total, local),
                    Stage(links, [(partial_ref[1 - k], sib, links.sibling)], again=k == 1),
                )
                for k in range(2)
            ]
            self.local, self.core = self.choices[0][1:]
        else:
            self.choices = None
            self.local = pltpu.make_async_copy(partial_ref.at[:, :, :, c], total, local)
            self.core = Stage(links, [(partial_ref.at[:, :, :, 1 - c], sib, links.sibling)])
        if kind in ("up_y", "all_y"):
            self.first = Stage(links, [(total.at[1 - y], one, links.along_y)])
            self.kept = lambda i, j: (y, i, j)
        elif kind in ("up_x", "all_x"):
            self.first = Stage(links, [(total.at[:, 1 - x], one, links.along_x)])
            self.kept = lambda i, j: (i, x, j)
        else:
            turned = device(y + (1 - c) * (1 - 2 * y), x + c * (1 - 2 * x), z, c)
            self.first = Stage(links, [(total.at[1 - self.q], one, turned)])
            self.line = LineSum(links, lambda at: total.at[self.q, at], three)
        if kind == "up_y":
            self.line = LineSum(links, lambda at: total.at[y, :, at], three)
            self.last = Stage(links, [(total.at[y, 1 - x, z], two, links.along_x)])
        elif kind == "up_x":
            self.line = LineSum(links, lambda at: total.at[:, x, at], three)
            self.last = Stage(links, [(total.at[1 - y, x, z], two, links.along_y)])
        elif kind == "all_x":
            self.second = Stage(links, [(total.at[1 - y, x], two, links.along_y)])
        elif kind == "all_y":
            self.second = Stage(links, [(total.at[y, 1 - x], two, links.along_x)])
        if kind in ("all_x", "all_y"):
            self.line = LineSum(links, lambda at: total.at[y, x, at], three)

    def begin(self):
        if self.choices is None:
            self.core.start()
            self.local.start()
            return
        for taken, local, core in self.choices:

            @pl.when(taken)
            def _(local=local, core=core):
                core.start()
                local.start()

    def add(self, pairs, count):
        total = self.total

        def body(i, carry):
            index, extra = pairs(i)
            total[index] = total[index] + extra
            return carry

        lax.fori_loop(0, count, body, 0)

    def run_first(self):
        self.local.wait()
        self.core.wait()
        sib = self.sib
        if self.kind == "down":
            self.add(lambda i: ((i // 4, i % 4), sib[i // 4, i % 4]), 8)
        else:
            self.add(lambda i: ((i // 8, i // 4 % 2, i % 4), sib[i // 8, i // 4 % 2, i % 4]), 16)
        self.first.start()

    def run_second(self):
        self.first.wait()
        one = self.one
        if self.kind == "down":
            self.add(lambda i: ((self.q, i), one[i]), 4)
        else:
            self.add(lambda i: (self.kept(i // 4, i % 4), one[i // 4, i % 4]), 8)
        if self.kind in ("all_x", "all_y"):
            self.second.start()
        else:
            self.line.start()

    def run_third(self):
        self.second.wait()
        y, x, two = self.links.y, self.links.x, self.two
        self.add(lambda i: ((y, x, i), two[i]), 4)
        self.line.start()

    def run_last(self):
        z, total, got = self.links.z, self.total, self.three

        def add(slot):
            for i in range(2):
                index = self.kept(i, z)
                total[index] = total[index] + got[slot, i]

        self.line.collect(add)
        self.last.start()

    def finish(self, out):
        y, x, z = self.links.y, self.links.x, self.links.z
        if self.kind in ("up_y", "up_x"):
            self.last.wait()
            along_x = self.kind == "up_y"
            mine = x if along_x else y
            for number, part in ((mine, self.total[y, x, z]), (1 - mine, self.two[...])):
                for j in range(8):
                    place = (j // 4 * 2 + number) if along_x else (number * 2 + j // 4)
                    start = (place * 4 + j % 4) * 256 + (0 if along_x else 128)
                    at = pl.ds(pl.multiple_of(start, 128), 128)
                    out[:, at] = part[:, j * 128 : (j + 1) * 128].astype(jnp.float32)
            return
        out[...] = (self.total[self.q, z] if self.kind == "down" else self.total[y, x, z]).astype(jnp.float32)

        def add(slot):
            out[...] = out[...] + self.three[slot].astype(jnp.float32)

        self.line.collect(add)


def rear_kernel(scaling, *refs):
    live_ref, d_rows, heads_ref, logsum, rows_ref, qkv, small_ref = refs[:7]
    normal_one, inverse_one, d_second, gains_ref = refs[7:11]
    refs = refs[:7] + refs[11:]
    partials = (refs[7], refs[8], refs[9:11]) + tuple(refs[11:14])
    d_normed, g_qkv, g_up, g_down, g_out, g_patch, g_class, small_out = refs[14:22]
    at = 22
    d_out, d_heads, d_spread, grad_keys, grad_values = refs[at : at + 5]
    d_sent, d_got, q_part, q_sib, q_z, q_plane = refs[at + 5 : at + 11]
    small_own, small_got, send_sem, recv_sem, local_sem = refs[at + 11 : at + 16]
    scratch = refs[at + 16 :]
    links = Links(send_sem, recv_sem)
    y, x, z, c = links.y, links.x, links.z, links.c
    h = y * 2 + x
    rows, features = d_rows.shape
    slot_rows = rows * 4
    narrow = d_out.shape[1]
    heads = narrow // DH
    wide = 3 * narrow
    plane = [(links.across, 3 - h, 3), (links.along_x, y * 2 + 1 - x, 1), (links.along_y, (1 - y) * 2 + x, 2)]

    def columns(start, size):
        return pl.ds(pl.multiple_of(start, 128), size)

    def block(p):
        return pl.ds(pl.multiple_of(p * rows, rows), rows)

    spread_out = Stage(
        links, [(d_rows.at[:, columns(p * narrow, narrow)], d_out.at[block(h), :], peer) for peer, p, _ in plane]
    )
    own = pltpu.make_async_copy(d_rows.at[:, columns(h * narrow, narrow)], d_out.at[block(h), :], local_sem.at[0])
    kinds = ("up_y", "up_x", "down", "all_x", "all_x", "all_y")
    sums = [
        Sum(links, partials[i], *scratch[5 * i : 5 * i + 5], local_sem.at[1 + i], kinds[i]) for i in range(6)
    ]
    back = [Stage(links, [(d_sent.at[rel - 1], d_got.at[rel - 1], peer)]) for peer, _, rel in plane]
    q_core = Stage(links, [(q_part.at[:, :, :, 1 - c], q_sib, links.sibling)])
    q_line = LineSum(links, lambda at: q_part.at[:, :, at, c], q_z)
    q_across = Stage(
        links, [(q_part.at[p // 2, p % 2, z, c], q_plane.at[h], peer) for peer, p, _ in plane]
    )
    small_core = Stage(links, [(small_own.at[0], small_got.at[0], links.sibling)])
    small_x = Stage(links, [(small_own.at[1], small_got.at[1], links.along_x)])
    small_y = Stage(links, [(small_own.at[2], small_got.at[2], links.along_y)])
    small_z = Stage(links, [(small_own.at[3], small_got.at[3 + z], peer) for peer in links.along_z])

    links.greet()
    spread_out.start()
    own.start()
    for entry in sums:
        entry.begin()
    small_own[0] = small_ref[...]
    small_core.start()
    own.wait()
    spread_out.wait()
    live = live_ref[0]
    key_live = lax.broadcasted_iota(jnp.int32, (slot_rows, 1), 0) < live
    up_y, up_x, down, out, patch, classes = sums
    assert links.count <= REAR_COPIES

    def small_step(stage, number, following):
        def run():
            stage.wait()
            small_own[number + 1] = small_own[number] + small_got[number]
            if number == 2:
                small_got[3 + z] = small_own[3]
            following.start()

        return run

    def both(*steps):
        def run():
            for step in steps:
                step()

        return run

    events = {
        0: up_y.run_first,
        1: up_x.run_first,
        2: down.run_first,
        3: small_step(small_core, 0, small_x),
        4: patch.run_first,
        5: classes.run_first,
        6: out.run_first,
        7: small_step(small_x, 1, small_y),
        8: both(up_y.run_second, up_x.run_second),
        9: small_step(small_y, 2, small_z),
        11: both(up_y.line.relay, up_x.line.relay),
        13: down.run_second,
        14: patch.run_second,
        15: both(up_y.run_last, up_x.run_last),
    }

    def tile_body(slot, carry):
        number, turn = slot // 4, slot % 4
        at_slots(slot, events)
        at = block(turn)

        @pl.when(turn == 0)
        def _():
            grad_keys[...] = jnp.zeros_like(grad_keys)
            grad_values[...] = jnp.zeros_like(grad_values)

        queries = heads_ref[3 * number, at, :]
        keys = heads_ref[3 * number + 1]
        values = heads_ref[3 * number + 2]
        grads = d_heads[number, at, :]
        scores = lax.dot_general(keys, queries, (((1,), (1,)), ((), ())), preferred_element_type=jnp.float32)
        powers = scores * (scaling * LOG2E) - logsum[number, :, at]
        weights = jnp.where(key_live, jnp.exp2(powers), 0.0)
        grad_values[...] += jnp.dot(weights.astype(jnp.bfloat16), grads, preferred_element_type=jnp.float32)
        grad_weights = lax.dot_general(
            values, grads, (((1,), (1,)), ((), ())), preferred_element_type=jnp.float32
        )
        deltas = jnp.sum(grad_weights * weights, axis=0, keepdims=True)
        grad_scores = (weights * (grad_weights - deltas)).astype(jnp.bfloat16)
        grad_keys[...] += jnp.dot(grad_scores, queries, preferred_element_type=jnp.float32)
        grad_queries = lax.dot_general(
            keys, grad_scores, (((0,), (0,)), ((), ())), preferred_element_type=jnp.float32
        )
        d_heads[4 + 3 * number, at, :] = (grad_queries.T * scaling).astype(jnp.bfloat16)

        @pl.when(turn == 3)
        def _():
            d_heads[5 + 3 * number] = (grad_keys[...] * scaling).astype(jnp.bfloat16)
            d_heads[6 + 3 * number] = grad_values[...].astype(jnp.bfloat16)

        return carry

    for number in range(heads):
        d_heads[number] = d_out[:, number * DH : (number + 1) * DH]
    lax.fori_loop(0, SLOTS, tile_body, 0)
    for number in range(3 * heads):
        d_spread[:, number * DH : (number + 1) * DH] = d_heads[4 + number]
    per = features // 4
    for j in range(4):
        left = jnp.concatenate([rows_ref[p, :, j * per : (j + 1) * per] for p in range(4)], axis=0)
        piece = lax.dot_general(
            left, d_spread[...], (((0,), (0,)), ((), ())), preferred_element_type=jnp.float32
        ).astype(jnp.bfloat16)
        q_part[j // 2, j % 2] = piece.reshape(4, 2, per // 8, wide)
    q_core.start()
    weight = qkv[...].reshape(features, wide)
    for (_, p, rel), stage in zip(plane, back):
        piece = lax.dot_general(
            d_spread[block(p), :], weight, (((1,), (1,)), ((), ())), preferred_element_type=jnp.float32
        )
        d_sent[rel - 1] = piece.astype(jnp.bfloat16)
        stage.start()
    q_core.wait()

    def add_sib(i, carry):
        index = (i // 8, i // 4 % 2, i % 4)
        q_part[(*index, c)] = q_part[(*index, c)] + q_sib[index]
        return carry

    lax.fori_loop(0, 16, add_sib, 0)
    q_line.start()
    d_normed[...] = lax.dot_general(
        d_spread[block(h), :], weight, (((1,), (1,)), ((), ())), preferred_element_type=jnp.float32
    )
    down.line.relay()
    q_line.relay()
    patch.run_third()
    classes.run_second()
    out.run_second()
    patch.line.relay()
    classes.run_third()
    out.run_third()
    classes.line.relay()

    def add_line(slot):
        for i in range(4):
            index = (i // 2, i % 2)
            q_part[(*index, z, c)] = q_part[(*index, z, c)] + q_z[(slot, *index)]

    q_line.collect(add_line)
    q_across.start()
    out.line.relay()
    small_z.wait()
    small_out[...] = (small_got[3] + small_got[4] + small_got[5] + small_got[6])[0:2, 0:CLS]
    down.finish(g_down)
    up_y.finish(g_up)
    up_x.finish(g_up)
    patch.finish(g_patch)
    classes.finish(g_class)
    out.finish(g_out)
    q_across.wait()
    g_qkv[:, columns(h * wide, wide)] = q_part[y, x, z, c].astype(jnp.float32)
    for _, p, _ in plane:
        g_qkv[:, columns(p * wide, wide)] = q_plane[p].astype(jnp.float32)
    for stage in back:
        stage.wait()
    upstream = d_normed[...] + (
        d_got[0].astype(jnp.float32) + d_got[1].astype(jnp.float32) + d_got[2].astype(jnp.float32)
    )
    upstream = upstream * gains_ref[0:1, :]
    value = normal_one[...]
    middle = jnp.mean(upstream, axis=-1, keepdims=True)
    along = jnp.mean(upstream * value, axis=-1, keepdims=True)
    d_normed[...] = d_second[...] + inverse_one[:, 0:1] * (upstream - middle - value * along)
    links.drain()


def rear(live, d_rows, heads_qkv, logsum, rows_all, qkv, small, ending, partials, scaling):
    rows, features = d_rows.shape
    slot_rows = 4 * rows
    narrow = features // 4
    heads = narrow // DH
    wide = 3 * narrow
    vmem, hbm = pl.BlockSpec(memory_space=pltpu.VMEM), pl.BlockSpec(memory_space=pl.ANY)
    low = jnp.bfloat16
    up, _, down, _, *rest = [a.shape[-2:] for a in partials]
    shard = (features // 32, wide)
    buffers = []
    for _ in range(2):
        buffers += [(2, 2, 4) + up, (2, 2, 4) + up, (2, 4) + up, up, (5, 2) + up]
    buffers += [(2, 4) + down, (2, 4) + down, (4,) + down, (8, 128), (5,) + down]
    for shape in rest:
        buffers += [(2, 2, 4) + shape, (2, 2, 4) + shape, (2, 4) + shape, (4,) + shape, (5,) + shape]
    single = jnp.float32
    return pl.pallas_call(
        partial(rear_kernel, scaling),
        out_shape=[
            jax.ShapeDtypeStruct((rows, features), single),
            jax.ShapeDtypeStruct((features // 32, 4 * wide), single),
            jax.ShapeDtypeStruct((up[0], 4 * up[1]), single),
            jax.ShapeDtypeStruct(down, single),
        ]
        + [jax.ShapeDtypeStruct(shape, single) for shape in rest]
        + [jax.ShapeDtypeStruct((2, CLS), single)],
        in_specs=[pl.BlockSpec(memory_space=pltpu.SMEM)] + [vmem] * 10 + [hbm] * 7,
        out_specs=[vmem] * 8,
        scratch_shapes=[
            pltpu.VMEM((slot_rows, narrow), low),
            pltpu.VMEM((4 * heads, slot_rows, DH), low),
            pltpu.VMEM((slot_rows, wide), low),
            pltpu.VMEM((slot_rows, DH), single),
            pltpu.VMEM((slot_rows, DH), single),
            pltpu.VMEM((3, rows, features), low),
            pltpu.VMEM((3, rows, features), low),
            pltpu.VMEM((2, 2, 4, 2) + shard, low),
            pltpu.VMEM((2, 2, 4) + shard, low),
            pltpu.VMEM((5, 2, 2) + shard, low),
            pltpu.VMEM((4,) + shard, low),
            pltpu.VMEM((4,) + small.shape, single),
            pltpu.VMEM((7,) + small.shape, single),
            pltpu.SemaphoreType.DMA((REAR_COPIES,)),
            pltpu.SemaphoreType.DMA((REAR_COPIES,)),
            pltpu.SemaphoreType.DMA((7,)),
        ]
        + [pltpu.VMEM(shape, low) for shape in buffers],
        compiler_params=pltpu.CompilerParams(
            collective_id=2, has_side_effects=True, vmem_limit_bytes=58 * 2**20
        ),
        name="rear",
    )(live, d_rows, heads_qkv, logsum, rows_all, qkv, small, *ending, *partials)


def ending_kernel(*refs):
    count = (len(refs) - 6) // 2
    results, (w_qkv, w_up, gains) = refs[:count], refs[count : count + 3]
    outs, gain_out, gain_sums, sems = refs[count + 3 : 2 * count + 3], *refs[2 * count + 3 :]
    copies = [pltpu.make_async_copy(results[i], outs[i], sems.at[i]) for i in range(count)]
    for copy in copies:
        copy.start()
    for number, (weight, grad) in enumerate(((w_qkv, results[2]), (w_up, results[4]))):
        total = jnp.sum(weight[...].astype(jnp.float32) * grad[...], axis=1, keepdims=True)
        total = jnp.broadcast_to(total, (total.shape[0], 128)).T[0:1, :]
        gain_sums[number : number + 1, :] = total / gains[number : number + 1, :].astype(jnp.float32)
    last = pltpu.make_async_copy(gain_sums, gain_out, sems.at[count])
    last.start()
    for copy in copies:
        copy.wait()
    last.wait()


def ending_copies(results, w_qkv, w_up, gains):
    vmem, hbm = pl.BlockSpec(memory_space=pltpu.VMEM), pl.BlockSpec(memory_space=pl.ANY)
    count = len(results)
    shapes = [jax.ShapeDtypeStruct(a.shape, a.dtype) for a in results]
    return pl.pallas_call(
        ending_kernel,
        out_shape=shapes + [jax.ShapeDtypeStruct(gains.shape, jnp.float32)],
        in_specs=[vmem] * (count + 3),
        out_specs=[hbm] * (count + 1),
        scratch_shapes=[pltpu.VMEM(gains.shape, jnp.float32), pltpu.SemaphoreType.DMA((count + 1,))],
        name="ending",
    )(*results, w_qkv, w_up, gains)


def body_planned(
    tokens,
    patch_counts,
    w_qkv,
    w_out,
    w_up,
    w_down,
    w_patch,
    w_class,
    norm_gains,
    mask_norm,
    grad_masks,
):
    low = jnp.bfloat16
    h, s = lax.axis_index("head"), lax.axis_index("seq")
    tokens, grad_masks = tokens[0], grad_masks[0]
    row_count = tokens.shape[0]
    live = CLS + patch_counts
    scaling = DH ** (-0.5)

    outs = front(
        live,
        tokens,
        norm_gains,
        grad_masks,
        mask_norm,
        (w_qkv, w_out, w_up, w_down, w_patch, w_class),
        scaling,
    )
    attended, heads_qkv, logsum, rows_all, gains, qkv, class_masks, mask_sums = outs[:8]
    normal_one, inverse_one, normed_two, active, d_branch, d_hidden, rounded, d_patch = outs[8:16]
    class_rows, d_class, d_mix, d_second, d_attended = outs[16:]
    grad_down = [matmul_tn(active[k], d_branch[k]).astype(low) for k in range(2)]
    grad_up = [matmul_tn(normed_two[k], d_hidden[k]).astype(low) for k in range(2)]
    grad_out = matmul_tn(attended, d_mix).astype(low)
    grad_patch = matmul_tn(rounded, d_patch).astype(low)
    grad_class = matmul_tn(class_rows, d_class).astype(low)

    def parted(value):
        return value.reshape(2, 2, 4, 2, value.shape[0] // 32, value.shape[1])

    partials = (
        parted(grad_up[0]),
        parted(grad_up[1]),
        grad_down[0].reshape(2, 4, 128, 1024),
        grad_down[1].reshape(2, 4, 128, 1024),
        parted(grad_out),
        parted(grad_patch),
        parted(grad_class),
    )
    ending = (normal_one, inverse_one, d_second, gains)
    grad_inputs, g_qkv, g_up, g_down, g_out, g_patch, g_class, sums = rear(
        live, d_attended, heads_qkv, logsum, rows_all, qkv, mask_sums, ending, partials, scaling
    )
    results = ending_copies(
        (class_masks, grad_inputs, g_qkv, g_out, g_up, g_down, g_patch, g_class, sums), w_qkv, w_up, norm_gains
    )
    return (results[0][None], results[1][None], *results[2:8], results[9], results[8])


def solution(mesh):
    planned = dict(mesh.shape) == {"head": 4, "seq": 8}
    return jax.shard_map(
        body_planned if planned else body_general,
        mesh=mesh,
        in_specs=(
            P("seq", "head", None),
            P("seq"),
            P(("head", "seq"), None),
            P(("head", "seq"), None),
            P(("head", "seq"), None),
            P(("head", "seq"), None),
            P(("head", "seq"), None),
            P(("head", "seq"), None),
            P(None, ("head", "seq")),
            P(),
            P("seq", "head", None),
        ),
        out_specs=(
            P("seq", "head", None),
            P("seq", "head", None),
            P(("head", "seq"), None),
            P(("head", "seq"), None),
            P(("head", "seq"), None),
            P(("head", "seq"), None),
            P(("head", "seq"), None),
            P(("head", "seq"), None),
            P(None, ("head", "seq")),
            P(),
        ),
        check_vma=False,
    )
```

```python
from functools import partial

import jax
import jax.numpy as jnp
from jax import lax
from jax.experimental import pallas as pl
from jax.experimental.pallas import tpu as pltpu
from jax.sharding import PartitionSpec as P

HEADS = 16
DH = 64
CLS = 150


def spread_2(value, axis, source):
    kept = jnp.where(lax.axis_index(axis) == source, value, 0).astype(value.dtype)
    return lax.psum(kept, axis)


def standardize(values):
    center = values - jnp.mean(values, axis=-1, keepdims=True)
    inverse = lax.rsqrt(jnp.mean(center * center, axis=-1, keepdims=True) + 1e-05)
    return (center * inverse, inverse)


def standard_back(normal, inverse, upstream):
    middle = jnp.mean(upstream, axis=-1, keepdims=True)
    along = jnp.mean(upstream * normal, axis=-1, keepdims=True)
    return inverse * (upstream - middle - normal * along)


def unit_scale(values):
    return lax.rsqrt(jnp.sum(values * values, axis=-1, keepdims=True) + 1e-06)


def unit_back(values, upstream):
    factor = unit_scale(values)
    direct = values * factor
    return factor * (upstream - direct * jnp.sum(upstream * direct, axis=-1, keepdims=True))


def block_scores(query_block, key_rows, key_live, scaling):
    scores = (
        jnp.einsum("qd,kd->qk", query_block, key_rows, preferred_element_type=jnp.float32) * scaling
    )
    return jnp.where(key_live, scores, -1e30)


def attend_head(queries, key_rows, values, key_live, scaling, blocks):
    head_width = queries.shape[-1]

    def single(query_block):
        scores = block_scores(query_block, key_rows, key_live, scaling)
        highest = jnp.max(scores, axis=-1, keepdims=True)
        weights_raw = jnp.exp(scores - highest)
        totals = jnp.sum(weights_raw, axis=-1, keepdims=True)
        weights = (weights_raw / totals).astype(jnp.bfloat16)
        output = jnp.einsum("qk,kd->qd", weights, values, preferred_element_type=jnp.float32)
        return (output.astype(jnp.bfloat16), (highest + jnp.log(totals))[:, 0])

    outputs, logsum = lax.map(single, queries.reshape(blocks, -1, head_width))
    return (outputs.reshape(-1, head_width), logsum.reshape(-1))


def attend_back(queries, key_rows, values, grad_out, logsum, key_live, scaling, blocks):
    head_width = queries.shape[-1]

    def single(running, pieces):
        grad_keys, grad_values = running
        query_block, grad_block, logsum_block = pieces
        scores = block_scores(query_block, key_rows, key_live, scaling)
        weights = jnp.exp(scores - logsum_block[:, None])
        grad_values = grad_values + jnp.einsum(
            "qk,qd->kd",
            weights.astype(jnp.bfloat16),
            grad_block,
            preferred_element_type=jnp.float32,
        )
        grad_weights = jnp.einsum(
            "qd,kd->qk", grad_block, values, preferred_element_type=jnp.float32
        )
        deltas = jnp.sum(grad_weights * weights, axis=-1, keepdims=True)
        grad_scores = (weights * (grad_weights - deltas)).astype(jnp.bfloat16)
        grad_query = (
            jnp.einsum("qk,kd->qd", grad_scores, key_rows, preferred_element_type=jnp.float32)
            * scaling
        )
        grad_keys = (
            grad_keys
            + jnp.einsum("qk,qd->kd", grad_scores, query_block, preferred_element_type=jnp.float32)
            * scaling
        )
        return ((grad_keys, grad_values), grad_query)

    zero_state = jnp.zeros(key_rows.shape, jnp.float32)
    pieces = (
        queries.reshape(blocks, -1, head_width),
        grad_out.reshape(blocks, -1, head_width),
        logsum.reshape(blocks, -1),
    )
    (grad_keys, grad_values), grad_queries = lax.scan(single, (zero_state, zero_state), pieces)
    return (grad_queries.reshape(-1, head_width), grad_keys, grad_values)


def body_general(
    tokens,
    patch_counts,
    w_qkv,
    w_out,
    w_up,
    w_down,
    w_patch,
    w_class,
    norm_gains,
    mask_norm,
    grad_masks,
):
    gains_rows = norm_gains.T
    gathered = (
        lax.all_gather(w_qkv, ("head", "seq"), axis=0, tiled=True),
        lax.all_gather(w_out, ("head", "seq"), axis=0, tiled=True),
        lax.all_gather(w_up, ("head", "seq"), axis=0, tiled=True),
        lax.all_gather(w_down, ("head", "seq"), axis=0, tiled=True),
        lax.all_gather(w_patch, ("head", "seq"), axis=0, tiled=True),
        lax.all_gather(w_class, ("head", "seq"), axis=0, tiled=True),
        lax.all_gather(gains_rows, ("head", "seq"), axis=0, tiled=True),
    )
    full_qkv, full_out, full_up, full_down, full_patch, full_class, full_gains = gathered
    gain_one = full_gains[:, 0].astype(jnp.float32)
    gain_two = full_gains[:, 1].astype(jnp.float32)
    image_count = tokens.shape[0]
    row_count = tokens.shape[1]
    groups = lax.axis_size("head")
    slot_rows = row_count * groups
    local_heads = HEADS // groups
    position = lax.axis_index("head") * row_count + jnp.arange(row_count, dtype=jnp.int32)
    live_limit = CLS + patch_counts
    patch_rows = ((position[None, :] >= CLS) & (position[None, :] < live_limit[:, None])).astype(
        jnp.float32
    )[:, :, None]
    key_live = (jnp.arange(slot_rows, dtype=jnp.int32)[None, :] < live_limit[:, None])[:, None, :]
    root_flag = (lax.axis_index("head") == 0).astype(jnp.float32)
    scaling = DH ** (-0.5)
    blocks = slot_rows // 512
    normal_one, inverse_one = standardize(tokens)
    normed_one = (normal_one * gain_one).astype(jnp.bfloat16)
    triple = jnp.einsum(
        "ird,dt->irt", normed_one, full_qkv, preferred_element_type=jnp.float32
    ).astype(jnp.bfloat16)
    spread = lax.all_to_all(triple, "head", split_axis=2, concat_axis=1, tiled=True).reshape(
        image_count, slot_rows, local_heads, 3, DH
    )
    image = 0
    outputs = []
    image_logsums = []
    for number in range(local_heads):
        output, logsum = attend_head(
            spread[image, :, number, 0],
            spread[image, :, number, 1],
            spread[image, :, number, 2],
            key_live[image],
            scaling,
            blocks,
        )
        outputs.append(output)
        image_logsums.append(logsum)
    image_outputs = [jnp.stack(outputs, axis=1).reshape(slot_rows, local_heads * DH)]
    logsums = [image_logsums]
    attended_heads = jnp.stack(image_outputs, axis=0)
    attended = lax.all_to_all(attended_heads, "head", split_axis=1, concat_axis=2, tiled=True)
    second = tokens + jnp.einsum(
        "ire,ed->ird", attended, full_out, preferred_element_type=jnp.float32
    )
    normal_two, inverse_two = standardize(second)
    normed_two = (normal_two * gain_two).astype(jnp.bfloat16)
    hidden = jnp.einsum("ird,df->irf", normed_two, full_up, preferred_element_type=jnp.float32)
    gelu_exact = partial(jax.nn.gelu, approximate=False)
    active = gelu_exact(hidden).astype(jnp.bfloat16)
    residual = second + jnp.einsum(
        "irf,fd->ird", active, full_down, preferred_element_type=jnp.float32
    )
    rounded = residual.astype(jnp.bfloat16)
    patch_proj = jnp.einsum("ird,de->ire", rounded, full_patch, preferred_element_type=jnp.float32)
    patch_unit = (patch_proj * unit_scale(patch_proj)).astype(jnp.bfloat16)
    class_proj = jnp.einsum(
        "ird,de->ire", rounded[:, :CLS], full_class, preferred_element_type=jnp.float32
    )
    class_unit = (class_proj * unit_scale(class_proj)).astype(jnp.bfloat16)
    classes = spread_2(class_unit, "head", 0)
    products = jnp.einsum("ird,icd->irc", patch_unit, classes, preferred_element_type=jnp.float32)
    normal_mask, inverse_mask = standardize(products)
    class_masks = (normal_mask * mask_norm[0] + mask_norm[1]) * patch_rows
    upstream = grad_masks * patch_rows
    norm_grads = lax.psum(
        jnp.stack([jnp.sum(upstream * normal_mask, axis=(0, 1)), jnp.sum(upstream, axis=(0, 1))]),
        ("head", "seq"),
    )
    d_products = standard_back(normal_mask, inverse_mask, upstream * mask_norm[0]).astype(
        jnp.bfloat16
    )
    d_patch_unit = jnp.einsum(
        "irc,icd->ird", d_products, classes, preferred_element_type=jnp.float32
    )
    class_part = jnp.einsum(
        "irc,ird->icd", d_products, patch_unit, preferred_element_type=jnp.float32
    )
    d_class_unit = lax.psum(class_part.astype(jnp.bfloat16), "head").astype(jnp.float32)
    d_patch_proj = unit_back(patch_proj, d_patch_unit).astype(jnp.bfloat16)
    d_class_proj = (unit_back(class_proj, d_class_unit) * root_flag).astype(jnp.bfloat16)
    regathered = (
        lax.all_gather(w_qkv, ("head", "seq"), axis=0, tiled=True),
        lax.all_gather(w_out, ("head", "seq"), axis=0, tiled=True),
        lax.all_gather(w_up, ("head", "seq"), axis=0, tiled=True),
        lax.all_gather(w_down, ("head", "seq"), axis=0, tiled=True),
        lax.all_gather(w_patch, ("head", "seq"), axis=0, tiled=True),
        lax.all_gather(w_class, ("head", "seq"), axis=0, tiled=True),
        lax.all_gather(gains_rows, ("head", "seq"), axis=0, tiled=True),
    )
    back_qkv, back_out, back_up, back_down, back_patch, back_class, back_gains = regathered
    back_one = back_gains[:, 0].astype(jnp.float32)
    back_two = back_gains[:, 1].astype(jnp.float32)
    grad_patch = jnp.einsum(
        "ird,ire->de", rounded, d_patch_proj, preferred_element_type=jnp.float32
    )
    grad_class = jnp.einsum(
        "ird,ire->de", rounded[:, :CLS], d_class_proj, preferred_element_type=jnp.float32
    )
    d_residual = jnp.einsum(
        "ire,de->ird", d_patch_proj, back_patch, preferred_element_type=jnp.float32
    )
    class_term = jnp.einsum(
        "ire,de->ird", d_class_proj, back_class, preferred_element_type=jnp.float32
    )
    d_residual = d_residual.at[:, :CLS].add(class_term)
    d_branch = d_residual.astype(jnp.bfloat16)
    grad_down = jnp.einsum("irf,ird->fd", active, d_branch, preferred_element_type=jnp.float32)
    d_active = jnp.einsum("ird,fd->irf", d_branch, back_down, preferred_element_type=jnp.float32)
    gelu_pull = jax.vjp(gelu_exact, hidden)[1]
    d_hidden = gelu_pull(d_active)[0].astype(jnp.bfloat16)
    grad_up = jnp.einsum("ird,irf->df", normed_two, d_hidden, preferred_element_type=jnp.float32)
    d_normed_two = jnp.einsum("irf,df->ird", d_hidden, back_up, preferred_element_type=jnp.float32)
    d_second = d_residual + standard_back(normal_two, inverse_two, d_normed_two * back_two)
    grad_gain_two = jnp.sum(d_normed_two * normal_two, axis=(0, 1))
    d_mix = d_second.astype(jnp.bfloat16)
    grad_out = jnp.einsum("ire,ird->ed", attended, d_mix, preferred_element_type=jnp.float32)
    d_attended = jnp.einsum(
        "ird,ed->ire", d_mix, back_out, preferred_element_type=jnp.float32
    ).astype(jnp.bfloat16)
    d_heads = lax.all_to_all(d_attended, "head", split_axis=2, concat_axis=1, tiled=True).reshape(
        image_count, slot_rows, local_heads, DH
    )
    image = 0
    head_grads = []
    for number in range(local_heads):
        grad_queries, grad_keys, grad_values = attend_back(
            spread[image, :, number, 0],
            spread[image, :, number, 1],
            spread[image, :, number, 2],
            d_heads[image, :, number],
            logsums[image][number],
            key_live[image],
            scaling,
            blocks,
        )
        head_grads.append(jnp.stack([grad_queries, grad_keys, grad_values], axis=1))
    image_grads = [jnp.stack(head_grads, axis=1).reshape(slot_rows, local_heads * 3 * DH)]
    d_spread = jnp.stack(image_grads, axis=0).astype(jnp.bfloat16)
    d_triple = lax.all_to_all(d_spread, "head", split_axis=1, concat_axis=2, tiled=True)
    grad_qkv = jnp.einsum("ird,irt->dt", normed_one, d_triple, preferred_element_type=jnp.float32)
    d_normed_one = jnp.einsum("irt,dt->ird", d_triple, back_qkv, preferred_element_type=jnp.float32)
    grad_inputs = d_second + standard_back(normal_one, inverse_one, d_normed_one * back_one)
    grad_gain_one = jnp.sum(d_normed_one * normal_one, axis=(0, 1))
    grad_gains = jnp.stack([grad_gain_one, grad_gain_two], axis=1)
    reduced = (
        lax.psum_scatter(grad_qkv, ("head", "seq"), scatter_dimension=0, tiled=True),
        lax.psum_scatter(grad_out, ("head", "seq"), scatter_dimension=0, tiled=True),
        lax.psum_scatter(grad_up, ("head", "seq"), scatter_dimension=0, tiled=True),
        lax.psum_scatter(grad_down, ("head", "seq"), scatter_dimension=0, tiled=True),
        lax.psum_scatter(grad_patch, ("head", "seq"), scatter_dimension=0, tiled=True),
        lax.psum_scatter(grad_class, ("head", "seq"), scatter_dimension=0, tiled=True),
        lax.psum_scatter(grad_gains, ("head", "seq"), scatter_dimension=0, tiled=True),
    )
    return (
        class_masks,
        grad_inputs,
        reduced[0],
        reduced[1],
        reduced[2],
        reduced[3],
        reduced[4],
        reduced[5],
        reduced[6].T,
        norm_grads,
    )


MESH = pl.DeviceIdType.MESH
LOG2E = 1.4426950408889634
SLOTS = 16
FRONT_COPIES = 160
REAR_COPIES = 88


def matmul(left, right):
    return jnp.dot(left, right, preferred_element_type=jnp.float32)


def matmul_nt(left, right):
    return lax.dot_general(left, right, (((1,), (1,)), ((), ())), preferred_element_type=jnp.float32)


def matmul_tn(left, right):
    return lax.dot_general(left, right, (((0,), (0,)), ((), ())), preferred_element_type=jnp.float32)


def norm(values):
    center = values - jnp.mean(values, axis=-1, keepdims=True)
    inverse = lax.rsqrt(jnp.mean(center * center, axis=-1, keepdims=True) + 1e-05)
    return center * inverse, inverse


def device(y, x, z, c):
    return (y * 2 + x, z * 2 + c)


class Links:
    def __init__(self, send_sem, recv_sem):
        head, seq = lax.axis_index("head"), lax.axis_index("seq")
        self.y, self.x, self.z, self.c = head // 2, head % 2, seq // 2, seq % 2
        y, x, z, c = self.y, self.x, self.z, self.c
        self.sibling = device(y, x, z, 1 - c)
        self.along_x = device(y, 1 - x, z, c)
        self.along_y = device(1 - y, x, z, c)
        self.across = device(1 - y, 1 - x, z, c)
        self.along_z = [device(y, x, (z + k) % 4, c) for k in (1, 2, 3)]
        self.send_sem, self.recv_sem, self.count, self.made, self.lines = send_sem, recv_sem, 0, [], []

    def greet(self):
        barrier = pltpu.get_barrier_semaphore()
        peers = [self.sibling, self.along_x, self.along_y, self.across] + self.along_z
        for peer in peers:
            pl.semaphore_signal(barrier, inc=1, device_id=peer, device_id_type=MESH)
        pl.semaphore_wait(barrier, len(peers))

    def plan(self, source, target, peer, sends=None, again=False):
        number = self.count - again
        self.count = number + 1
        copy = pltpu.make_async_remote_copy(
            src_ref=source,
            dst_ref=target,
            send_sem=self.send_sem.at[number],
            recv_sem=self.recv_sem.at[number],
            device_id=peer,
            device_id_type=MESH,
        )
        if not again:
            self.made.append((copy, sends))
        return copy

    def drain(self):
        for copy, sends in self.made:
            if sends is None:
                copy.wait_send()
            else:
                pl.when(sends)(copy.wait_send)
        for line in self.lines:
            line.drain()


class Stage:
    def __init__(self, links, moves, again=False):
        self.copies = [links.plan(*move, again=again) for move in moves]

    def start(self):
        for copy in self.copies:
            copy.start()

    def wait(self):
        for copy in self.copies:
            copy.wait_recv()


class Line:
    def __init__(self, links, piece, source=None):
        self.links, self.piece = links, piece
        self.source = piece(links.z) if source is None else source
        self.base = links.count
        links.count += 5
        links.lines.append(self)

    def copy(self, source, target, sent, landed):
        links = self.links
        return pltpu.make_async_remote_copy(
            src_ref=source,
            dst_ref=self.piece(landed),
            send_sem=links.send_sem.at[self.base + sent],
            recv_sem=links.recv_sem.at[self.base + landed],
            device_id=device(links.y, links.x, target, links.c),
            device_id_type=MESH,
        )

    def direct(self, target):
        z = self.links.z
        return (z != target) if target in (1, 2) else (z != target) & (z != 3 - target)

    def start(self):
        for target in (1, 2, 0, 3):

            @pl.when(self.direct(target))
            def _(target=target):
                self.copy(self.source, target, target, self.links.z).start()

    def relay(self):
        for at, end in ((2, 0), (1, 3)):

            @pl.when(self.links.z == at)
            def _(end=end):
                self.copy(self.source, 3 - end, 4, end).wait_recv()
                self.copy(self.piece(end), 3 - end, 4, end).start()

    def wait(self):
        z = self.links.z
        for origin in range(4):
            pending = z != origin
            if origin in (0, 3):
                pending = pending & (z != (2 if origin == 0 else 1))

            @pl.when(pending)
            def _(origin=origin):
                self.copy(self.source, 0, 0, origin).wait_recv()

    def drain(self):
        for target in range(4):

            @pl.when(self.direct(target))
            def _(target=target):
                self.copy(self.source, target, target, self.links.z).wait_send()

        @pl.when((self.links.z == 1) | (self.links.z == 2))
        def _():
            self.copy(self.source, 0, 4, 0).wait_send()


def at_slots(slot, events):
    for number, event in events.items():
        pl.when(slot == number)(event)


class LineSum:
    def __init__(self, links, piece, got):
        self.links, self.piece, self.got = links, piece, got
        self.base = links.count
        links.count += 5
        links.lines.append(self)

    def copy(self, piece, target, slot, sent):
        links = self.links
        return pltpu.make_async_remote_copy(
            src_ref=self.piece(piece),
            dst_ref=self.got.at[slot],
            send_sem=links.send_sem.at[self.base + sent],
            recv_sem=links.recv_sem.at[self.base + slot],
            device_id=device(links.y, links.x, target, links.c),
            device_id_type=MESH,
        )

    def start(self):
        z = self.links.z
        for target, end, middle in ((3, 0, 1), (0, 3, 2)):

            @pl.when(z == end)
            def _(target=target, middle=middle):
                self.copy(target, middle, 4, target).start()

        for target in range(4):
            direct = z != target
            if target in (0, 3):
                direct = z == (1 if target == 0 else 2)

            @pl.when(direct)
            def _(target=target):
                self.copy(target, target, z, target).start()

    def relay(self):
        z = self.links.z
        for target, middle in ((3, 1), (0, 2)):

            @pl.when(z == middle)
            def _(target=target, middle=middle):
                self.copy(target, target, 4, target).wait_recv()
                own = self.piece(target)
                own[...] = own[...] + self.got[4]
                self.copy(target, target, middle, target).start()

    def collect(self, add):
        z = self.links.z
        for origin in range(4):
            comes = z != origin
            if origin in (0, 3):
                comes = comes & (z != 3 - origin)

            @pl.when(comes)
            def _(origin=origin):
                self.copy(0, 0, origin, 0).wait_recv()
                add(origin)

    def drain(self):
        for target in range(4):

            @pl.when(self.links.z != target)
            def _(target=target):
                self.copy(target, target, 0, target).wait_send()


class Sum:
    def __init__(self, links, partial_ref, total, sib, one, two, three, local, kind):
        y, x, z, c = links.y, links.x, links.z, links.c
        self.links, self.total, self.sib, self.one, self.two, self.three = links, total, sib, one, two, three
        self.kind = kind
        self.q = y * (1 - c) + x * c
        if kind == "down":
            self.choices = [
                (
                    c == k,
                    pltpu.make_async_copy(partial_ref[k], total, local),
                    Stage(links, [(partial_ref[1 - k], sib, links.sibling)], again=k == 1),
                )
                for k in range(2)
            ]
            self.local, self.core = self.choices[0][1:]
        else:
            self.choices = None
            self.local = None
            if total is None:
                total = self.total = partial_ref.at[:, :, :, c]
            else:
                self.local = pltpu.make_async_copy(partial_ref.at[:, :, :, c], total, local)
            self.core = Stage(links, [(partial_ref.at[:, :, :, 1 - c], sib, links.sibling)])
        if kind in ("up_y", "all_y"):
            self.first = Stage(links, [(total.at[1 - y], one, links.along_y)])
            self.kept = lambda i, j: (y, i, j)
        elif kind in ("up_x", "all_x"):
            self.first = Stage(links, [(total.at[:, 1 - x], one, links.along_x)])
            self.kept = lambda i, j: (i, x, j)
        else:
            turned = device(y + (1 - c) * (1 - 2 * y), x + c * (1 - 2 * x), z, c)
            self.first = Stage(links, [(total.at[1 - self.q], one, turned)])
            self.line = LineSum(links, lambda at: total.at[self.q, at], three)
        if kind == "up_y":
            self.line = LineSum(links, lambda at: total.at[y, :, at], three)
            self.last = Stage(links, [(total.at[y, 1 - x, z], two, links.along_x)])
        elif kind == "up_x":
            self.line = LineSum(links, lambda at: total.at[:, x, at], three)
            self.last = Stage(links, [(total.at[1 - y, x, z], two, links.along_y)])
        elif kind == "all_x":
            self.second = Stage(links, [(total.at[1 - y, x], two, links.along_y)])
        elif kind == "all_y":
            self.second = Stage(links, [(total.at[y, 1 - x], two, links.along_x)])
        if kind in ("all_x", "all_y"):
            self.line = LineSum(links, lambda at: total.at[y, x, at], three)

    def begin(self):
        if self.choices is None:
            self.core.start()
            if self.local is not None:
                self.local.start()
            return
        for taken, local, core in self.choices:

            @pl.when(taken)
            def _(local=local, core=core):
                core.start()
                local.start()

    def add(self, pairs, count):
        total = self.total

        def body(i, carry):
            index, extra = pairs(i)
            total[index] = total[index] + extra
            return carry

        lax.fori_loop(0, count, body, 0)

    def run_first(self):
        if self.local is not None:
            self.local.wait()
        self.core.wait()
        sib = self.sib
        if self.kind == "down":
            self.add(lambda i: ((i // 4, i % 4), sib[i // 4, i % 4]), 8)
        else:
            self.add(lambda i: ((i // 8, i // 4 % 2, i % 4), sib[i // 8, i // 4 % 2, i % 4]), 16)
        self.first.start()

    def run_second(self):
        self.first.wait()
        one = self.one
        if self.kind == "down":
            self.add(lambda i: ((self.q, i), one[i]), 4)
        else:
            self.add(lambda i: (self.kept(i // 4, i % 4), one[i // 4, i % 4]), 8)
        if self.kind in ("all_x", "all_y"):
            self.second.start()
        else:
            self.line.start()

    def run_third(self):
        self.second.wait()
        y, x, two = self.links.y, self.links.x, self.two
        self.add(lambda i: ((y, x, i), two[i]), 4)
        self.line.start()

    def run_last(self):
        z, total, got = self.links.z, self.total, self.three

        def add(slot):
            for i in range(2):
                index = self.kept(i, z)
                total[index] = total[index] + got[slot, i]

        self.line.collect(add)
        self.last.start()

    def finish(self, out):
        y, x, z = self.links.y, self.links.x, self.links.z
        if self.kind in ("up_y", "up_x"):
            self.last.wait()
            along_x = self.kind == "up_y"
            mine = x if along_x else y
            for number, part in ((mine, self.total[y, x, z]), (1 - mine, self.two[...])):
                for j in range(8):
                    place = (j // 4 * 2 + number) if along_x else (number * 2 + j // 4)
                    start = (place * 4 + j % 4) * 256 + (0 if along_x else 128)
                    at = pl.ds(pl.multiple_of(start, 128), 128)
                    out[:, at] = part[:, j * 128 : (j + 1) * 128].astype(jnp.float32)
            return
        out[...] = (self.total[self.q, z] if self.kind == "down" else self.total[y, x, z]).astype(jnp.float32)

        def add(slot):
            out[...] = out[...] + self.three[slot].astype(jnp.float32)

        self.line.collect(add)


def front_kernel(scaling, *refs):
    live_ref, tokens, norm_gains, grad_masks, mask_norm = refs[:5]
    qkv_shard, out_shard, up_given, down_shard, patch_shard, class_shard = refs[5:11]
    attended, heads_ref, logsum, rows_ref, gains_ref, qkv, class_masks, mask_sums = refs[11:19]
    normal_one, inverse_one, normed_two, active, d_branch, d_hidden = refs[19:25]
    d_mix, d_second, d_attended, g_patch, g_class = refs[25:30]
    refs = refs[30:]
    full_out, ups, downs, full_patch, full_class, tiles, staged = refs[:7]
    slope, stream, normal_two, inverse_two, patch_proj, class_proj, classes = refs[7:14]
    part_sent, part_got, back_sent, back_got, class_sent, class_got = refs[14:20]
    term_sent, term_got, mask_in, tile, up_shard = refs[20:25]
    rounded, d_patch, class_rows, d_class = refs[25:29]
    patch_parts, class_parts = refs[29:34], refs[34:39]
    send_sem, recv_sem, local_sem = refs[39:]
    second = residual = d_residual = stream
    links = Links(send_sem, recv_sem)
    y, x, z, c = links.y, links.x, links.z, links.c
    h = y * 2 + x
    q = y * (1 - c) + x * c
    rows, features = tokens.shape
    wide = qkv.shape[-1]
    narrow = staged.shape[1]
    heads = narrow // DH
    block = ups.shape[-1]
    slot_rows = rows * 4
    plane = [(links.across, 3 - h, 3), (links.along_x, y * 2 + 1 - x, 1), (links.along_y, (1 - y) * 2 + x, 2)]
    at_x, at_y = plane[1][1], plane[2][1]

    def columns(start, size):
        return pl.ds(pl.multiple_of(start, 128), size)

    def up_block(number):
        return up_shard.at[:, columns(number * block, block)]

    local = [
        pltpu.make_async_copy(source, target, local_sem.at[number])
        for number, (source, target) in zip(
            (0, 1, 2, 3, 4, 5, 7, 8),
            [
                (tile, tiles.at[y, x, z, c]),
                (qkv_shard.at[:, columns(h * wide, wide)], qkv.at[y, x, z, c]),
                (out_shard, full_out.at[y, x, z, c]),
                (down_shard, downs.at[c, q, z]),
                (up_block(x), ups.at[0, y, x, z, c]),
                (up_block(2 + y), ups.at[1, y, x, z, c]),
                (patch_shard, full_patch.at[y, x, z, c]),
                (class_shard, full_class.at[y, x, z, c]),
            ]
        )
    ]
    gain_core = Stage(links, [(tile, tiles.at[y, x, z, c], links.sibling)])
    gain_z = Stage(links, [(tiles.at[y, x, z], tiles.at[y, x, z], peer) for peer in links.along_z])
    gain_plane = Stage(links, [(tiles.at[y, x], tiles.at[y, x], peer) for peer, _, _ in plane])
    qkv_plane = Stage(
        links, [(qkv_shard.at[:, columns(p * wide, wide)], qkv.at[y, x, z, c], peer) for peer, p, _ in plane]
    )
    part = qkv.shape[4] // 2
    qkv_z = [Line(links, lambda at, k=k: qkv.at[:, :, at, c, k * part : (k + 1) * part]) for k in range(2)]
    qkv_core = Stage(links, [(qkv.at[:, :, :, c], qkv.at[:, :, :, c], links.sibling)])
    up_split = [
        Stage(links, [(up_block(1 - x), ups.at[0, y, x, z, c], links.along_x)]),
        Stage(links, [(up_block(2 + 1 - y), ups.at[1, y, x, z, c], links.along_y)]),
    ]
    up_z = [
        Line(links, lambda at: ups.at[0, y, :, at, c]),
        Line(links, lambda at: ups.at[1, :, x, at, c]),
    ]
    up_on = [
        Stage(links, [(ups.at[0, y, :, :, c], ups.at[0, y, :, :, c], links.along_y)]),
        Stage(links, [(ups.at[1, :, x, :, c], ups.at[1, :, x, :, c], links.along_x)]),
    ]
    up_core = [
        Stage(links, [(ups.at[k, :, :, :, c], ups.at[k, :, :, :, c], links.sibling)]) for k in range(2)
    ]
    some = down_shard.shape[0] // 4
    turned = device(y + (1 - c) * (1 - 2 * y), x + c * (1 - 2 * x), z, c)
    spans = [slice(k * some, (k + 1) * some) for k in range(4)]
    down_turn = [Stage(links, [(down_shard.at[spans[k]], downs.at[c, q, z, spans[k]], turned)]) for k in (0, 1)]
    down_z = [Line(links, lambda at, k=k: downs.at[c, :, at, spans[k]]) for k in (0, 1)] + [
        Line(links, lambda at, k=k: downs.at[c, q, at, spans[k]], down_shard.at[spans[k]]) for k in (2, 3)
    ]
    down_on = [Stage(links, [(downs.at[c, q, :, spans[k]],) * 2 + (turned,)]) for k in (2, 3)]
    down_core = [
        Stage(links, [(downs.at[c, :, :, span], downs.at[c, :, :, span], links.sibling)])
        for span in (slice(0, 2 * some), slice(2 * some, 4 * some))
    ]
    patch_sum = Sum(links, patch_parts[0], None, *patch_parts[1:], None, "all_x")
    class_sum = Sum(links, class_parts[0], None, *class_parts[1:], None, "all_y")
    part = out_shard.shape[0] // 2

    def square(full, shard):
        first = [full.at[y, x, :, c, 0:part], full.at[y, x, :, c, part:]]
        second = [full.at[:, x, :, c, 0:part], full.at[y, :, :, c, part:]]
        return (
            Line(links, lambda at: full.at[y, x, at, c], shard),
            Stage(links, [(first[0], first[0], links.along_y), (first[1], first[1], links.along_x)]),
            Stage(links, [(second[0], second[0], links.along_x), (second[1], second[1], links.along_y)]),
            Stage(links, [(full.at[:, :, :, c],) * 2 + (links.sibling,)]),
        )

    out_z, out_one, out_two, out_core = square(full_out, out_shard)
    near, far = slice(0, part), slice(part, 2 * part)
    patch_x = Stage(links, [(patch_shard.at[far], full_patch.at[y, x, z, c, far], links.along_x)])
    patch_y = Stage(links, [(full_patch.at[y, :, z, c, far],) * 2 + (links.along_y,)])
    patch_first = Line(links, lambda at: full_patch.at[y, x, at, c, near], patch_shard.at[near])
    patch_one = Stage(links, [(full_patch.at[y, x, :, c, near],) * 2 + (links.along_y,)])
    patch_two = Stage(links, [(full_patch.at[:, x, :, c, near],) * 2 + (links.along_x,)])
    class_y = Stage(links, [(class_shard, full_class.at[y, x, z, c], links.along_y)])
    class_x = Stage(links, [(full_class.at[:, x, z, c],) * 2 + (links.along_x,)])
    halves = [slice(k * part, (k + 1) * part) for k in range(2)]
    class_z = [Line(links, lambda at, k=k: full_class.at[:, :, at, c, k * part : (k + 1) * part]) for k in range(2)]
    halves = [slice(part + k * part // 2, part + (k + 1) * part // 2) for k in range(2)]
    patch_z = [Line(links, lambda at, k=k: full_patch.at[:, :, at, c, halves[k]]) for k in range(2)]
    patch_core = Stage(links, [(full_patch.at[:, :, :, c],) * 2 + (links.sibling,)])
    class_core = Stage(links, [(full_class.at[:, :, :, c],) * 2 + (links.sibling,)])
    beside = (links.along_x, links.along_y)
    here = slice(0, rows)
    few = class_proj.shape[0]
    tall = -(-CLS // 16) * 16
    parts = (slice(0, tall), slice(tall, rows))
    theirs = [slice(rows + at.start, rows + at.stop) for at in parts]

    def exchange(sent, got, sent_at, got_at):
        return [
            [Stage(links, [(sent.at[k, sent_at[i]], got.at[k, got_at[i]], beside[k])]) for i in range(2)]
            for k in range(2)
        ]

    normed_out = exchange(normed_two, normed_two, parts, theirs)
    branch_out = exchange(d_branch, d_branch, parts, theirs)
    part_back = exchange(part_sent, part_got, parts, parts)
    grad_back = exchange(back_sent, back_got, parts, parts)
    sizes = {1: few, 2: few, 3: tall - 3 * few}
    class_out = [
        links.plan(
            rounded.at[few * rel : few * rel + sizes[rel]], class_rows.at[0 : sizes[rel]], peer, h == 0
        )
        for peer, _, rel in plane
    ]
    mine = pl.ds(pl.multiple_of(h * few, few), few)
    unit_out = Stage(links, [(classes.at[mine], classes.at[mine], peer) for peer, _, _ in plane])
    class_back = Stage(links, [(class_sent.at[p], class_got.at[rel - 1], peer) for peer, p, rel in plane])
    term_back = [
        links.plan(term_sent.at[0 : sizes[rel]], term_got.at[rel - 1, 0 : sizes[rel]], peer, h == rel)
        for peer, _, rel in plane
    ]
    middle = rows // 2
    strips = [slice(0, middle), slice(middle, rows)]
    rows_x = [Stage(links, [(rows_ref.at[h, strips[k]],) * 2 + (links.along_x,)]) for k in (0, 1)]
    rows_y = [Stage(links, [(rows_ref.at[h, strips[k]],) * 2 + (links.along_y,)]) for k in (1, 0)]
    piece_a, piece_b = rows_ref.at[at_x, strips[0]], rows_ref.at[at_y, strips[1]]
    relay_y = Stage(links, [(piece_a, piece_a, links.along_y)])
    relay_x = Stage(links, [(piece_b, piece_b, links.along_x)])

    share = norm_gains.shape[1]
    tile[...] = jnp.zeros_like(tile)
    for i in range(4):

        @pl.when((z * 2 + c) % 4 == i)
        def _(i=i):
            tile[0:2, i * share : (i + 1) * share] = norm_gains[...].astype(jnp.float32)

    for number in range(4):
        for j in range(8):
            at = (j // 4 * 2 + number) if number < 2 else ((number - 2) * 2 + j // 4)
            at = (at * 4 + j % 4) * 256 + (0 if number < 2 else 128)
            up_shard[:, number * block + j * 128 : number * block + (j + 1) * 128] = up_given[:, at : at + 128]
    for copy in local:
        copy.start()
    class_rows[...] = jnp.zeros_like(class_rows)
    links.greet()
    for stage in (gain_core, qkv_plane, *up_split, *down_turn, class_y, patch_x, out_z, patch_first):
        stage.start()
    value, inverse = norm(tokens[...])
    normal_one[...] = value
    inverse_one[...] = jnp.broadcast_to(inverse, inverse_one.shape)
    local[0].wait()
    gain_core.wait()
    gain_z.start()
    gain_z.wait()
    gain_plane.start()
    local[1].wait()
    qkv_plane.wait()
    for line in qkv_z:
        line.start()
    gain_plane.wait()
    for j in range(8):
        piece = tiles[j // 4, j // 2 % 2, (j % 2) * 2, 0].astype(jnp.float32)
        for i in range(1, 4):
            piece = piece + tiles[j // 4, j // 2 % 2, (j % 2) * 2 + i // 2, i % 2].astype(jnp.float32)
        gains_ref[:, j * 128 : (j + 1) * 128] = piece[0:8]
    rows_ref[h] = (normal_one[...] * gains_ref[0:1, :]).astype(jnp.bfloat16)
    for stage in (rows_x[0], rows_y[0], rows_x[1], rows_y[1]):
        stage.start()
    for line in (out_z, patch_first, *qkv_z):
        line.relay()
    rows_x[0].wait()
    relay_y.start()
    rows_y[0].wait()
    relay_x.start()
    local[6].wait()
    patch_x.wait()
    patch_y.start()
    local[7].wait()
    class_y.wait()
    class_x.start()
    for line in qkv_z:
        line.wait()
    qkv_core.start()
    for k in range(2):
        local[4 + k].wait()
        up_split[k].wait()
        up_z[k].start()
    out_z.wait()
    patch_first.wait()
    for number in (2, 3):
        local[number].wait()

    def project(p):
        weight = qkv[...].reshape(rows * 4, wide)
        piece = jnp.dot(rows_ref[p], weight, preferred_element_type=jnp.float32).astype(jnp.bfloat16)
        at = pl.ds(pl.multiple_of(p * rows, rows), rows)
        for number in range(3 * heads):
            heads_ref[number, at, :] = piece[:, number * DH : (number + 1) * DH]

    qkv_core.wait()
    project(h)
    rows_x[1].wait()
    project(at_x)
    rows_y[1].wait()
    project(at_y)
    out_one.start()
    patch_one.start()
    relay_y.wait()
    relay_x.wait()
    project(3 - h)

    live = live_ref[0]
    key_live = lax.broadcasted_iota(jnp.int32, (slot_rows, 1), 0) < live
    returned = links.count - 1
    assert returned + 4 <= FRONT_COPIES

    def back(rel):
        peer = h + (rel % 2) * (1 - 2 * x) + (rel // 2) * (2 - 4 * y)
        return pltpu.make_async_remote_copy(
            src_ref=staged.at[pl.ds(pl.multiple_of(peer * rows, rows), rows), :],
            dst_ref=attended.at[:, columns(h * narrow, narrow)],
            send_sem=send_sem.at[returned + rel],
            recv_sem=recv_sem.at[returned + rel],
            device_id=(peer, z * 2 + c),
            device_id_type=MESH,
        )

    def up_next(k):
        up_z[k].wait()
        up_on[k].start()

    def up_end(k):
        up_on[k].wait()
        up_core[k].start()

    def out_next():
        out_one.wait()
        out_two.start()

    def out_end():
        out_two.wait()
        out_core.start()

    def patch_next():
        patch_one.wait()
        patch_two.start()

    def down_late():
        down_z[2].start()
        down_z[3].start()

    def down_early():
        for stage in down_turn:
            stage.wait()
        down_z[0].start()
        down_z[1].start()

    def down_relays():
        down_z[2].relay()
        down_z[3].relay()

    events = {
        0: up_z[0].relay,
        3: out_next,
        5: up_z[1].relay,
        6: down_late,
        11: down_early,
        12: out_end,
        14: down_relays,
    }

    def tile_body(slot, carry):
        turn, number = slot // 4, slot % 4
        rel = 3 - turn
        peer = h + (rel % 2) * (1 - 2 * x) + (rel // 2) * (2 - 4 * y)
        at = pl.ds(pl.multiple_of(peer * rows, rows), rows)
        at_slots(slot, events)
        queries = heads_ref[3 * number, at, :]
        keys = heads_ref[3 * number + 1]
        values = heads_ref[3 * number + 2]
        scores = lax.dot_general(keys, queries, (((1,), (1,)), ((), ())), preferred_element_type=jnp.float32)
        scores = jnp.where(key_live, scores * (scaling * LOG2E), -1e30)
        highest = jnp.max(scores, axis=0, keepdims=True)
        raw = jnp.exp2(scores - highest)
        totals = jnp.sum(raw, axis=0, keepdims=True)
        weights = (raw * (1.0 / totals)).astype(jnp.bfloat16)
        mixed = lax.dot_general(
            values, weights, (((0,), (0,)), ((), ())), preferred_element_type=jnp.float32
        )
        mixed = mixed.T.astype(jnp.bfloat16)
        for which in range(4):

            @pl.when(number == which)
            def _(which=which):
                staged[at, which * DH : (which + 1) * DH] = mixed

        logsum[number, :, at] = highest + jnp.log2(totals)

        @pl.when((number == 3) & (rel > 0))
        def _():
            back(rel).start()

        return carry

    lax.fori_loop(0, SLOTS, tile_body, 0)
    own = pltpu.make_async_copy(
        staged.at[pl.ds(pl.multiple_of(h * rows, rows), rows), :],
        attended.at[:, columns(h * narrow, narrow)],
        local_sem.at[6],
    )
    own.start()
    class_x.wait()
    patch_y.wait()
    for line in (*class_z, *patch_z):
        line.start()
    up_next(0)
    up_next(1)
    for k in range(2):
        down_z[2 + k].wait()
        down_on[k].start()
    for rel in (3, 2, 1):
        back(rel).wait()
    own.wait()
    out_core.wait()
    down_z[0].relay()

    def whole(weight):
        return weight[...].reshape(-1, weight.shape[-1])

    second[...] = tokens[...] + matmul(attended[...], whole(full_out))
    value, inverse = norm(second[...])
    normal_two[...] = value
    inverse_two[...] = jnp.broadcast_to(inverse, inverse_two.shape)
    value = (value * gains_ref[1:2, :]).astype(jnp.bfloat16)
    for k in range(2):
        normed_two[k, here] = value
    for i in range(2):
        for k in range(2):
            normed_out[k][i].start()
    down_z[1].relay()
    patch_next()
    up_end(0)
    up_end(1)
    for k in range(2):
        up_core[k].wait()
    wide_step = 256

    def forward(k, at, size):
        def step(j, carry):
            span = pl.ds(pl.multiple_of(j * wide_step, wide_step), wide_step)
            weight = ups[k, :, :, :, :, :, span].reshape(features, wide_step)
            hidden = matmul(normed_two[k, at], weight)
            spread = 0.5 + 0.5 * lax.erf(hidden * 0.7071067811865476)
            density = jnp.exp(hidden * hidden * -0.5) * 0.3989422804014327
            active[k, at, span] = (hidden * spread).astype(jnp.bfloat16)
            slope[k, at, span] = spread + hidden * density
            return carry

        lax.fori_loop(0, block // wide_step, step, 0)

    forward(0, here, rows)
    for stage in down_on:
        stage.wait()
    down_core[1].start()
    forward(1, here, rows)
    for line in down_z[:2]:
        line.wait()
    down_core[0].start()
    for stage in down_core:
        stage.wait()
    for i in range(2):
        for k in range(2):
            normed_out[k][i].wait()
            forward(k, theirs[i], parts[i].stop - parts[i].start)
            part_sent[k, parts[i]] = matmul(active[k, theirs[i]], whole(downs.at[k])).astype(jnp.bfloat16)
            part_back[k][i].start()
        if i == 0:
            for line in class_z:
                line.relay()
    residual[...] = second[...] + (
        matmul(active[0, here], whole(downs.at[0])) + matmul(active[1, here], whole(downs.at[1]))
    )
    for line in patch_z:
        line.relay()

    def complete(at):
        for k in range(2):
            part_back[k][0 if at.start == 0 else 1].wait()
        value = residual[at] + (part_got[0, at].astype(jnp.float32) + part_got[1, at].astype(jnp.float32))
        rounded[at] = value.astype(jnp.bfloat16)

    complete(parts[0])

    @pl.when(h == 0)
    def _():
        for copy in class_out:
            copy.start()
        class_rows[...] = rounded[0:few]

    for line in class_z:
        line.wait()
    class_core.start()
    complete(parts[1])
    for line in patch_z:
        line.wait()
    patch_two.wait()
    patch_core.start()
    patch_core.wait()

    patch_proj[...] = matmul(rounded[...], whole(full_patch))
    factor = unit_scale(patch_proj[...])
    patch_unit = (patch_proj[...] * factor).astype(jnp.bfloat16)
    classes[4 * few :] = jnp.zeros((classes.shape[0] - 4 * few, features), jnp.bfloat16)
    for copy, (_, _, rel) in zip(class_out, plane):
        pl.when(h == rel)(copy.wait_recv)
    class_core.wait()
    class_live = h * few + lax.broadcasted_iota(jnp.int32, (few, 1), 0) < CLS
    value = matmul(class_rows[...], whole(full_class))
    class_proj[...] = value
    classes[mine] = jnp.where(class_live, value * unit_scale(value), 0.0).astype(jnp.bfloat16)
    unit_out.start()
    mask_in[...] = jnp.zeros_like(mask_in)
    mask_in[0:rows, 0:CLS] = grad_masks[...]
    mask_in[rows : rows + 2, 0:CLS] = mask_norm[...]
    mask_gain, mask_bias = mask_in[rows : rows + 1, :], mask_in[rows + 1 : rows + 2, :]
    unit_out.wait()
    products = matmul_nt(patch_unit, classes[...])
    lane = lax.broadcasted_iota(jnp.int32, products.shape, 1)
    position = h * rows + lax.broadcasted_iota(jnp.int32, (rows, 1), 0)
    patch_rows = ((position >= CLS) & (position < live)).astype(jnp.float32)

    def class_mean(values):
        return jnp.sum(values, axis=-1, keepdims=True) * (1.0 / CLS)

    center = jnp.where(lane < CLS, products - class_mean(products), 0.0)
    inverse = lax.rsqrt(class_mean(center * center) + 1e-05)
    mask_normal = center * inverse
    class_masks[...] = ((mask_normal * mask_gain + mask_bias) * patch_rows)[:, 0:CLS]
    upstream = mask_in[0:rows, :] * patch_rows
    mask_sums[...] = jnp.zeros_like(mask_sums)
    mask_sums[0:1, :] = jnp.sum(upstream * mask_normal, axis=0, keepdims=True)
    mask_sums[1:2, :] = jnp.sum(upstream, axis=0, keepdims=True)
    upstream = upstream * mask_gain
    upstream = inverse * (upstream - class_mean(upstream) - mask_normal * class_mean(upstream * mask_normal))
    d_products = jnp.where(lane < CLS, upstream, 0.0).astype(jnp.bfloat16)
    class_part = matmul_tn(d_products, patch_unit)
    for p in range(4):
        class_sent[p] = class_part[few * p : few * (p + 1)].astype(jnp.bfloat16)
    class_back.start()
    upstream = matmul(d_products, classes[...])
    direct = patch_proj[...] * factor
    upstream = factor * (upstream - direct * jnp.sum(upstream * direct, axis=-1, keepdims=True))
    d_patch[...] = upstream.astype(jnp.bfloat16)
    d_residual[...] = matmul_nt(d_patch[...], whole(full_patch))

    def branch(i):
        value = d_residual[parts[i]].astype(jnp.bfloat16)
        for k in range(2):
            d_branch[k, parts[i]] = value
            branch_out[k][i].start()

    branch(1)

    def weight_gradient(target, left, right):
        per = features // 4
        for j in range(4):
            piece = matmul_tn(left[:, j * per : (j + 1) * per], right[...]).astype(jnp.bfloat16)
            target[j // 2, j % 2] = piece.reshape(4, 2, per // 8, features)

    weight_gradient(patch_parts[0], rounded, d_patch)
    patch_sum.begin()
    class_back.wait()
    upstream = class_sent[h].astype(jnp.float32)
    for number in range(3):
        upstream = upstream + class_got[number].astype(jnp.float32)
    d_class[...] = jnp.where(class_live, unit_back(class_proj[...], upstream), 0.0).astype(jnp.bfloat16)
    term = matmul_nt(d_class[...], whole(full_class))
    term_sent[...] = term.astype(jnp.bfloat16)
    for copy, (_, _, rel) in zip(term_back, plane):
        pl.when(h == rel)(copy.start)
    weight_gradient(class_parts[0], class_rows, d_class)
    class_sum.begin()

    def backward(k, at):
        for j in range(block // wide_step):
            weight = downs[k, j // 2, 2 * (j % 2) : 2 * (j % 2) + 2].reshape(wide_step, features)
            span = slice(j * wide_step, (j + 1) * wide_step)
            d_hidden[k, at, span] = (matmul_nt(d_branch[k, at], weight) * slope[k, at, span]).astype(jnp.bfloat16)


    def returned_rows(i):
        for k in range(2):
            branch_out[k][i].wait()
            backward(k, theirs[i])
            back_sent[k, parts[i]] = matmul_nt(d_hidden[k, theirs[i]], whole(ups.at[k])).astype(jnp.bfloat16)
            grad_back[k][i].start()

    for k in range(2):
        backward(k, parts[1])
    returned_rows(1)

    @pl.when(h == 0)
    def _():
        d_residual[0:few] = d_residual[0:few] + term_sent[...].astype(jnp.float32)
        for copy, (_, _, rel) in zip(term_back, plane):
            copy.wait_recv()
            at = slice(few * rel, few * rel + sizes[rel])
            d_residual[at] = d_residual[at] + term_got[rel - 1, 0 : sizes[rel]].astype(jnp.float32)

    branch(0)
    patch_sum.run_first()
    class_sum.run_first()
    for k in range(2):
        backward(k, parts[0])
    returned_rows(0)
    upstream = matmul_nt(d_hidden[0, here], whole(ups.at[0])) + matmul_nt(d_hidden[1, here], whole(ups.at[1]))
    patch_sum.run_second()
    class_sum.run_second()
    for k in range(2):
        for stage in grad_back[k]:
            stage.wait()
    upstream = upstream + (back_got[0].astype(jnp.float32) + back_got[1].astype(jnp.float32))
    upstream = upstream * gains_ref[1:2, :]
    value = normal_two[...]
    middle = jnp.mean(upstream, axis=-1, keepdims=True)
    along = jnp.mean(upstream * value, axis=-1, keepdims=True)
    d_second[...] = d_residual[...] + inverse_two[:, 0:1] * (upstream - middle - value * along)
    patch_sum.run_third()
    class_sum.run_third()
    d_mix[...] = d_second[...].astype(jnp.bfloat16)
    d_attended[...] = matmul_nt(d_mix[...], whole(full_out)).astype(jnp.bfloat16)
    patch_sum.line.relay()
    class_sum.line.relay()
    patch_sum.finish(g_patch)
    class_sum.finish(g_class)
    links.drain()


def front(live, tokens, norm_gains, grad_masks, mask_norm, shards, scaling):
    rows, features = tokens.shape
    vmem, hbm = pl.BlockSpec(memory_space=pltpu.VMEM), pl.BlockSpec(memory_space=pl.ANY)
    w_qkv, w_out, w_up, w_down, w_patch, w_class = shards
    wide = w_qkv.shape[1] // 4
    heads = wide // (3 * DH)
    block = w_up.shape[1] // 4
    lanes = 256
    few = -(-CLS // 64) * 16
    low, single = jnp.bfloat16, jnp.float32
    outs = [
        ((rows, features), low),
        ((3 * heads, 4 * rows, DH), low),
        ((heads, 1, 4 * rows), single),
        ((4, rows, features), low),
        ((8, features), single),
        ((2, 2, 4, 2, w_qkv.shape[0], wide), low),
        (grad_masks.shape, single),
        ((8, lanes), single),
        ((rows, features), single),
        ((rows, 128), single),
        ((2, 2 * rows, features), low),
        ((2, 2 * rows, block), low),
        ((2, 2 * rows, features), low),
        ((2, 2 * rows, block), low),
        ((rows, features), low),
        ((rows, features), single),
        ((rows, features), low),
        (w_patch.shape, single),
        (w_class.shape, single),
    ]
    scratch = [
        ((2, 2, 4, 2) + w_out.shape, low),
        ((2, 2, 2, 4, 2, w_up.shape[0], block), low),
        ((2, 2, 4) + w_down.shape, low),
        ((2, 2, 4, 2) + w_patch.shape, low),
        ((2, 2, 4, 2) + w_class.shape, low),
        ((2, 2, 4, 2, 8, 128), single),
        ((4 * rows, wide // 3), low),
        ((2, 2 * rows, block), single),
        ((rows, features), single),
        ((rows, features), single),
        ((rows, 128), single),
        ((rows, features), single),
        ((few, features), single),
        ((lanes, features), low),
        ((2, rows, features), low),
        ((2, rows, features), low),
        ((2, rows, features), low),
        ((2, rows, features), low),
        ((4, few, features), low),
        ((3, few, features), low),
        ((few, features), low),
        ((3, few, features), low),
        ((rows + 8, lanes), single),
        ((8, 128), single),
        (w_up.shape, low),
        ((rows, features), low),
        ((rows, features), low),
        ((few, features), low),
        ((few, features), low),
    ]
    for shape in (w_patch.shape, w_class.shape):
        for lead in ((2, 2, 4, 2), (2, 2, 4), (2, 4), (4,), (5,)):
            scratch.append((lead + shape, low))
    return pl.pallas_call(
        partial(front_kernel, scaling),
        out_shape=[jax.ShapeDtypeStruct(*out) for out in outs],
        in_specs=[pl.BlockSpec(memory_space=pltpu.SMEM)] + [vmem] * 4 + [hbm] * 2 + [vmem] + [hbm] * 3,
        out_specs=[vmem] * len(outs),
        scratch_shapes=[pltpu.VMEM(*shape) for shape in scratch]
        + [
            pltpu.SemaphoreType.DMA((FRONT_COPIES,)),
            pltpu.SemaphoreType.DMA((FRONT_COPIES,)),
            pltpu.SemaphoreType.DMA((9,)),
        ],
        compiler_params=pltpu.CompilerParams(
            collective_id=1, has_side_effects=True, vmem_limit_bytes=121 * 2**19
        ),
        name="front",
    )(live, tokens, norm_gains, grad_masks, mask_norm, *shards)


def rear_kernel(scaling, *refs):
    live_ref, d_rows, heads_ref, logsum, rows_ref, qkv, small_ref = refs[:7]
    normal_one, inverse_one, d_second, gains_ref = refs[7:11]
    refs = refs[:7] + refs[11:]
    partials = (refs[7], refs[8], refs[9:11], refs[11])
    d_normed, g_qkv, g_up, g_down, g_out, small_out = refs[12:18]
    at = 18
    d_out, d_heads, d_spread, grad_keys, grad_values = refs[at : at + 5]
    d_sent, d_got, q_part, q_sib, q_z, q_plane = refs[at + 5 : at + 11]
    small_own, small_got, send_sem, recv_sem, local_sem = refs[at + 11 : at + 16]
    scratch = refs[at + 16 :]
    links = Links(send_sem, recv_sem)
    y, x, z, c = links.y, links.x, links.z, links.c
    h = y * 2 + x
    rows, features = d_rows.shape
    slot_rows = rows * 4
    narrow = d_out.shape[1]
    heads = narrow // DH
    wide = 3 * narrow
    plane = [(links.across, 3 - h, 3), (links.along_x, y * 2 + 1 - x, 1), (links.along_y, (1 - y) * 2 + x, 2)]

    def columns(start, size):
        return pl.ds(pl.multiple_of(start, 128), size)

    def block(p):
        return pl.ds(pl.multiple_of(p * rows, rows), rows)

    spread_out = Stage(
        links, [(d_rows.at[:, columns(p * narrow, narrow)], d_out.at[block(h), :], peer) for peer, p, _ in plane]
    )
    own = pltpu.make_async_copy(d_rows.at[:, columns(h * narrow, narrow)], d_out.at[block(h), :], local_sem.at[0])
    kinds = ("up_y", "up_x", "down", "all_x")
    sums = [
        Sum(links, partials[i], *scratch[5 * i : 5 * i + 5], local_sem.at[1 + i], kinds[i]) for i in range(4)
    ]
    back = [Stage(links, [(d_sent.at[rel - 1], d_got.at[rel - 1], peer)]) for peer, _, rel in plane]
    q_core = Stage(links, [(q_part.at[:, :, :, 1 - c], q_sib, links.sibling)])
    q_line = LineSum(links, lambda at: q_part.at[:, :, at, c], q_z)
    q_across = Stage(
        links, [(q_part.at[p // 2, p % 2, z, c], q_plane.at[h], peer) for peer, p, _ in plane]
    )
    small_core = Stage(links, [(small_own.at[0], small_got.at[0], links.sibling)])
    small_x = Stage(links, [(small_own.at[1], small_got.at[1], links.along_x)])
    small_y = Stage(links, [(small_own.at[2], small_got.at[2], links.along_y)])
    small_z = Stage(links, [(small_own.at[3], small_got.at[3 + z], peer) for peer in links.along_z])

    links.greet()
    spread_out.start()
    own.start()
    for entry in sums:
        entry.begin()
    small_own[0] = small_ref[...]
    small_core.start()
    own.wait()
    spread_out.wait()
    live = live_ref[0]
    key_live = lax.broadcasted_iota(jnp.int32, (slot_rows, 1), 0) < live
    up_y, up_x, down, out = sums
    assert links.count <= REAR_COPIES

    def small_step(stage, number, following):
        def run():
            stage.wait()
            small_own[number + 1] = small_own[number] + small_got[number]
            if number == 2:
                small_got[3 + z] = small_own[3]
            following.start()

        return run

    def both(*steps):
        def run():
            for step in steps:
                step()

        return run

    events = {
        0: up_y.run_first,
        1: up_x.run_first,
        2: down.run_first,
        3: small_step(small_core, 0, small_x),
        6: out.run_first,
        7: small_step(small_x, 1, small_y),
        8: both(up_y.run_second, up_x.run_second),
        9: small_step(small_y, 2, small_z),
        11: both(up_y.line.relay, up_x.line.relay),
        13: down.run_second,
        15: both(up_y.run_last, up_x.run_last),
    }

    def tile_body(slot, carry):
        number, turn = slot // 4, slot % 4
        at_slots(slot, events)
        at = block(turn)

        @pl.when(turn == 0)
        def _():
            grad_keys[...] = jnp.zeros_like(grad_keys)
            grad_values[...] = jnp.zeros_like(grad_values)

        queries = heads_ref[3 * number, at, :]
        keys = heads_ref[3 * number + 1]
        values = heads_ref[3 * number + 2]
        grads = d_heads[number, at, :]
        scores = lax.dot_general(keys, queries, (((1,), (1,)), ((), ())), preferred_element_type=jnp.float32)
        powers = scores * (scaling * LOG2E) - logsum[number, :, at]
        weights = jnp.where(key_live, jnp.exp2(powers), 0.0)
        grad_values[...] += jnp.dot(weights.astype(jnp.bfloat16), grads, preferred_element_type=jnp.float32)
        grad_weights = lax.dot_general(
            values, grads, (((1,), (1,)), ((), ())), preferred_element_type=jnp.float32
        )
        deltas = jnp.sum(grad_weights * weights, axis=0, keepdims=True)
        grad_scores = (weights * (grad_weights - deltas)).astype(jnp.bfloat16)
        grad_keys[...] += jnp.dot(grad_scores, queries, preferred_element_type=jnp.float32)
        grad_queries = lax.dot_general(
            keys, grad_scores, (((0,), (0,)), ((), ())), preferred_element_type=jnp.float32
        )
        d_heads[4 + 3 * number, at, :] = (grad_queries.T * scaling).astype(jnp.bfloat16)

        @pl.when(turn == 3)
        def _():
            d_heads[5 + 3 * number] = (grad_keys[...] * scaling).astype(jnp.bfloat16)
            d_heads[6 + 3 * number] = grad_values[...].astype(jnp.bfloat16)

        return carry

    for number in range(heads):
        d_heads[number] = d_out[:, number * DH : (number + 1) * DH]
    lax.fori_loop(0, SLOTS, tile_body, 0)
    for number in range(3 * heads):
        d_spread[:, number * DH : (number + 1) * DH] = d_heads[4 + number]
    per = features // 4
    for j in range(4):
        left = jnp.concatenate([rows_ref[p, :, j * per : (j + 1) * per] for p in range(4)], axis=0)
        piece = lax.dot_general(
            left, d_spread[...], (((0,), (0,)), ((), ())), preferred_element_type=jnp.float32
        ).astype(jnp.bfloat16)
        q_part[j // 2, j % 2] = piece.reshape(4, 2, per // 8, wide)
    q_core.start()
    weight = qkv[...].reshape(features, wide)
    for (_, p, rel), stage in zip(plane, back):
        piece = lax.dot_general(
            d_spread[block(p), :], weight, (((1,), (1,)), ((), ())), preferred_element_type=jnp.float32
        )
        d_sent[rel - 1] = piece.astype(jnp.bfloat16)
        stage.start()
    q_core.wait()

    def add_sib(i, carry):
        index = (i // 8, i // 4 % 2, i % 4)
        q_part[(*index, c)] = q_part[(*index, c)] + q_sib[index]
        return carry

    lax.fori_loop(0, 16, add_sib, 0)
    q_line.start()
    d_normed[...] = lax.dot_general(
        d_spread[block(h), :], weight, (((1,), (1,)), ((), ())), preferred_element_type=jnp.float32
    )
    down.line.relay()
    q_line.relay()
    out.run_second()
    out.run_third()

    def add_line(slot):
        for i in range(4):
            index = (i // 2, i % 2)
            q_part[(*index, z, c)] = q_part[(*index, z, c)] + q_z[(slot, *index)]

    q_line.collect(add_line)
    q_across.start()
    out.line.relay()
    small_z.wait()
    small_out[...] = (small_got[3] + small_got[4] + small_got[5] + small_got[6])[0:2, 0:CLS]
    down.finish(g_down)
    up_y.finish(g_up)
    up_x.finish(g_up)
    out.finish(g_out)
    q_across.wait()
    g_qkv[:, columns(h * wide, wide)] = q_part[y, x, z, c].astype(jnp.float32)
    for _, p, _ in plane:
        g_qkv[:, columns(p * wide, wide)] = q_plane[p].astype(jnp.float32)
    for stage in back:
        stage.wait()
    upstream = d_normed[...] + (
        d_got[0].astype(jnp.float32) + d_got[1].astype(jnp.float32) + d_got[2].astype(jnp.float32)
    )
    upstream = upstream * gains_ref[0:1, :]
    value = normal_one[...]
    middle = jnp.mean(upstream, axis=-1, keepdims=True)
    along = jnp.mean(upstream * value, axis=-1, keepdims=True)
    d_normed[...] = d_second[...] + inverse_one[:, 0:1] * (upstream - middle - value * along)
    links.drain()


def rear(live, d_rows, heads_qkv, logsum, rows_all, qkv, small, ending, partials, scaling):
    rows, features = d_rows.shape
    slot_rows = 4 * rows
    narrow = features // 4
    heads = narrow // DH
    wide = 3 * narrow
    vmem, hbm = pl.BlockSpec(memory_space=pltpu.VMEM), pl.BlockSpec(memory_space=pl.ANY)
    low = jnp.bfloat16
    up, _, down, _, *rest = [a.shape[-2:] for a in partials]
    shard = (features // 32, wide)
    buffers = []
    for _ in range(2):
        buffers += [(2, 2, 4) + up, (2, 2, 4) + up, (2, 4) + up, up, (5, 2) + up]
    buffers += [(2, 4) + down, (2, 4) + down, (4,) + down, (8, 128), (5,) + down]
    for shape in rest:
        buffers += [(2, 2, 4) + shape, (2, 2, 4) + shape, (2, 4) + shape, (4,) + shape, (5,) + shape]
    single = jnp.float32
    return pl.pallas_call(
        partial(rear_kernel, scaling),
        out_shape=[
            jax.ShapeDtypeStruct((rows, features), single),
            jax.ShapeDtypeStruct((features // 32, 4 * wide), single),
            jax.ShapeDtypeStruct((up[0], 4 * up[1]), single),
            jax.ShapeDtypeStruct(down, single),
        ]
        + [jax.ShapeDtypeStruct(shape, single) for shape in rest]
        + [jax.ShapeDtypeStruct((2, CLS), single)],
        in_specs=[pl.BlockSpec(memory_space=pltpu.SMEM)] + [vmem] * 10 + [hbm] * 5,
        out_specs=[vmem] * 6,
        scratch_shapes=[
            pltpu.VMEM((slot_rows, narrow), low),
            pltpu.VMEM((4 * heads, slot_rows, DH), low),
            pltpu.VMEM((slot_rows, wide), low),
            pltpu.VMEM((slot_rows, DH), single),
            pltpu.VMEM((slot_rows, DH), single),
            pltpu.VMEM((3, rows, features), low),
            pltpu.VMEM((3, rows, features), low),
            pltpu.VMEM((2, 2, 4, 2) + shard, low),
            pltpu.VMEM((2, 2, 4) + shard, low),
            pltpu.VMEM((5, 2, 2) + shard, low),
            pltpu.VMEM((4,) + shard, low),
            pltpu.VMEM((4,) + small.shape, single),
            pltpu.VMEM((7,) + small.shape, single),
            pltpu.SemaphoreType.DMA((REAR_COPIES,)),
            pltpu.SemaphoreType.DMA((REAR_COPIES,)),
            pltpu.SemaphoreType.DMA((7,)),
        ]
        + [pltpu.VMEM(shape, low) for shape in buffers],
        compiler_params=pltpu.CompilerParams(
            collective_id=2, has_side_effects=True, vmem_limit_bytes=58 * 2**20
        ),
        name="rear",
    )(live, d_rows, heads_qkv, logsum, rows_all, qkv, small, *ending, *partials)


def ending_kernel(*refs):
    count = (len(refs) - 6) // 2
    results, (w_qkv, w_up, gains) = refs[:count], refs[count : count + 3]
    outs, gain_out, gain_sums, sems = refs[count + 3 : 2 * count + 3], *refs[2 * count + 3 :]
    copies = [pltpu.make_async_copy(results[i], outs[i], sems.at[i]) for i in range(count)]
    for copy in copies:
        copy.start()
    for number, (weight, grad) in enumerate(((w_qkv, results[2]), (w_up, results[4]))):
        total = jnp.sum(weight[...].astype(jnp.float32) * grad[...], axis=1, keepdims=True)
        total = jnp.broadcast_to(total, (total.shape[0], 128)).T[0:1, :]
        gain_sums[number : number + 1, :] = total / gains[number : number + 1, :].astype(jnp.float32)
    last = pltpu.make_async_copy(gain_sums, gain_out, sems.at[count])
    last.start()
    for copy in copies:
        copy.wait()
    last.wait()


def ending_copies(results, w_qkv, w_up, gains):
    vmem, hbm = pl.BlockSpec(memory_space=pltpu.VMEM), pl.BlockSpec(memory_space=pl.ANY)
    count = len(results)
    shapes = [jax.ShapeDtypeStruct(a.shape, a.dtype) for a in results]
    return pl.pallas_call(
        ending_kernel,
        out_shape=shapes + [jax.ShapeDtypeStruct(gains.shape, jnp.float32)],
        in_specs=[vmem] * (count + 3),
        out_specs=[hbm] * (count + 1),
        scratch_shapes=[pltpu.VMEM(gains.shape, jnp.float32), pltpu.SemaphoreType.DMA((count + 1,))],
        name="ending",
    )(*results, w_qkv, w_up, gains)


def body_planned(
    tokens,
    patch_counts,
    w_qkv,
    w_out,
    w_up,
    w_down,
    w_patch,
    w_class,
    norm_gains,
    mask_norm,
    grad_masks,
):
    low = jnp.bfloat16
    h, s = lax.axis_index("head"), lax.axis_index("seq")
    tokens, grad_masks = tokens[0], grad_masks[0]
    row_count = tokens.shape[0]
    live = CLS + patch_counts
    scaling = DH ** (-0.5)

    outs = front(
        live,
        tokens,
        norm_gains,
        grad_masks,
        mask_norm,
        (w_qkv, w_out, w_up, w_down, w_patch, w_class),
        scaling,
    )
    attended, heads_qkv, logsum, rows_all, gains, qkv, class_masks, mask_sums = outs[:8]
    normal_one, inverse_one, normed_two, active, d_branch, d_hidden = outs[8:14]
    d_mix, d_second, d_attended, g_patch, g_class = outs[14:]
    grad_down = [matmul_tn(active[k], d_branch[k]).astype(low) for k in range(2)]
    grad_up = [matmul_tn(normed_two[k], d_hidden[k]).astype(low) for k in range(2)]
    grad_out = matmul_tn(attended, d_mix).astype(low)

    def parted(value):
        return value.reshape(2, 2, 4, 2, value.shape[0] // 32, value.shape[1])

    partials = (
        parted(grad_up[0]),
        parted(grad_up[1]),
        grad_down[0].reshape(2, 4, 128, 1024),
        grad_down[1].reshape(2, 4, 128, 1024),
        parted(grad_out),
    )
    ending = (normal_one, inverse_one, d_second, gains)
    grad_inputs, g_qkv, g_up, g_down, g_out, sums = rear(
        live, d_attended, heads_qkv, logsum, rows_all, qkv, mask_sums, ending, partials, scaling
    )
    results = ending_copies(
        (class_masks, grad_inputs, g_qkv, g_out, g_up, g_down, g_patch, g_class, sums), w_qkv, w_up, norm_gains
    )
    return (results[0][None], results[1][None], *results[2:8], results[9], results[8])


def solution(mesh):
    planned = dict(mesh.shape) == {"head": 4, "seq": 8}
    return jax.shard_map(
        body_planned if planned else body_general,
        mesh=mesh,
        in_specs=(
            P("seq", "head", None),
            P("seq"),
            P(("head", "seq"), None),
            P(("head", "seq"), None),
            P(("head", "seq"), None),
            P(("head", "seq"), None),
            P(("head", "seq"), None),
            P(("head", "seq"), None),
            P(None, ("head", "seq")),
            P(),
            P("seq", "head", None),
        ),
        out_specs=(
            P("seq", "head", None),
            P("seq", "head", None),
            P(("head", "seq"), None),
            P(("head", "seq"), None),
            P(("head", "seq"), None),
            P(("head", "seq"), None),
            P(("head", "seq"), None),
            P(("head", "seq"), None),
            P(None, ("head", "seq")),
            P(),
        ),
        check_vma=False,
    )
```

```python
from functools import partial

import jax
import jax.numpy as jnp
from jax import lax
from jax.experimental import pallas as pl
from jax.experimental.pallas import tpu as pltpu
from jax.sharding import PartitionSpec as P

HEADS = 16
DH = 64
CLS = 150


def spread_2(value, axis, source):
    kept = jnp.where(lax.axis_index(axis) == source, value, 0).astype(value.dtype)
    return lax.psum(kept, axis)


def standardize(values):
    center = values - jnp.mean(values, axis=-1, keepdims=True)
    inverse = lax.rsqrt(jnp.mean(center * center, axis=-1, keepdims=True) + 1e-05)
    return (center * inverse, inverse)


def standard_back(normal, inverse, upstream):
    middle = jnp.mean(upstream, axis=-1, keepdims=True)
    along = jnp.mean(upstream * normal, axis=-1, keepdims=True)
    return inverse * (upstream - middle - normal * along)


def unit_scale(values):
    return lax.rsqrt(jnp.sum(values * values, axis=-1, keepdims=True) + 1e-06)


def unit_back(values, upstream):
    factor = unit_scale(values)
    direct = values * factor
    return factor * (upstream - direct * jnp.sum(upstream * direct, axis=-1, keepdims=True))


def block_scores(query_block, key_rows, key_live, scaling):
    scores = (
        jnp.einsum("qd,kd->qk", query_block, key_rows, preferred_element_type=jnp.float32) * scaling
    )
    return jnp.where(key_live, scores, -1e30)


def attend_head(queries, key_rows, values, key_live, scaling, blocks):
    head_width = queries.shape[-1]

    def single(query_block):
        scores = block_scores(query_block, key_rows, key_live, scaling)
        highest = jnp.max(scores, axis=-1, keepdims=True)
        weights_raw = jnp.exp(scores - highest)
        totals = jnp.sum(weights_raw, axis=-1, keepdims=True)
        weights = (weights_raw / totals).astype(jnp.bfloat16)
        output = jnp.einsum("qk,kd->qd", weights, values, preferred_element_type=jnp.float32)
        return (output.astype(jnp.bfloat16), (highest + jnp.log(totals))[:, 0])

    outputs, logsum = lax.map(single, queries.reshape(blocks, -1, head_width))
    return (outputs.reshape(-1, head_width), logsum.reshape(-1))


def attend_back(queries, key_rows, values, grad_out, logsum, key_live, scaling, blocks):
    head_width = queries.shape[-1]

    def single(running, pieces):
        grad_keys, grad_values = running
        query_block, grad_block, logsum_block = pieces
        scores = block_scores(query_block, key_rows, key_live, scaling)
        weights = jnp.exp(scores - logsum_block[:, None])
        grad_values = grad_values + jnp.einsum(
            "qk,qd->kd",
            weights.astype(jnp.bfloat16),
            grad_block,
            preferred_element_type=jnp.float32,
        )
        grad_weights = jnp.einsum(
            "qd,kd->qk", grad_block, values, preferred_element_type=jnp.float32
        )
        deltas = jnp.sum(grad_weights * weights, axis=-1, keepdims=True)
        grad_scores = (weights * (grad_weights - deltas)).astype(jnp.bfloat16)
        grad_query = (
            jnp.einsum("qk,kd->qd", grad_scores, key_rows, preferred_element_type=jnp.float32)
            * scaling
        )
        grad_keys = (
            grad_keys
            + jnp.einsum("qk,qd->kd", grad_scores, query_block, preferred_element_type=jnp.float32)
            * scaling
        )
        return ((grad_keys, grad_values), grad_query)

    zero_state = jnp.zeros(key_rows.shape, jnp.float32)
    pieces = (
        queries.reshape(blocks, -1, head_width),
        grad_out.reshape(blocks, -1, head_width),
        logsum.reshape(blocks, -1),
    )
    (grad_keys, grad_values), grad_queries = lax.scan(single, (zero_state, zero_state), pieces)
    return (grad_queries.reshape(-1, head_width), grad_keys, grad_values)


def body_general(
    tokens,
    patch_counts,
    w_qkv,
    w_out,
    w_up,
    w_down,
    w_patch,
    w_class,
    norm_gains,
    mask_norm,
    grad_masks,
):
    gains_rows = norm_gains.T
    gathered = (
        lax.all_gather(w_qkv, ("head", "seq"), axis=0, tiled=True),
        lax.all_gather(w_out, ("head", "seq"), axis=0, tiled=True),
        lax.all_gather(w_up, ("head", "seq"), axis=0, tiled=True),
        lax.all_gather(w_down, ("head", "seq"), axis=0, tiled=True),
        lax.all_gather(w_patch, ("head", "seq"), axis=0, tiled=True),
        lax.all_gather(w_class, ("head", "seq"), axis=0, tiled=True),
        lax.all_gather(gains_rows, ("head", "seq"), axis=0, tiled=True),
    )
    full_qkv, full_out, full_up, full_down, full_patch, full_class, full_gains = gathered
    gain_one = full_gains[:, 0].astype(jnp.float32)
    gain_two = full_gains[:, 1].astype(jnp.float32)
    image_count = tokens.shape[0]
    row_count = tokens.shape[1]
    groups = lax.axis_size("head")
    slot_rows = row_count * groups
    local_heads = HEADS // groups
    position = lax.axis_index("head") * row_count + jnp.arange(row_count, dtype=jnp.int32)
    live_limit = CLS + patch_counts
    patch_rows = ((position[None, :] >= CLS) & (position[None, :] < live_limit[:, None])).astype(
        jnp.float32
    )[:, :, None]
    key_live = (jnp.arange(slot_rows, dtype=jnp.int32)[None, :] < live_limit[:, None])[:, None, :]
    root_flag = (lax.axis_index("head") == 0).astype(jnp.float32)
    scaling = DH ** (-0.5)
    blocks = slot_rows // 512
    normal_one, inverse_one = standardize(tokens)
    normed_one = (normal_one * gain_one).astype(jnp.bfloat16)
    triple = jnp.einsum(
        "ird,dt->irt", normed_one, full_qkv, preferred_element_type=jnp.float32
    ).astype(jnp.bfloat16)
    spread = lax.all_to_all(triple, "head", split_axis=2, concat_axis=1, tiled=True).reshape(
        image_count, slot_rows, local_heads, 3, DH
    )
    image = 0
    outputs = []
    image_logsums = []
    for number in range(local_heads):
        output, logsum = attend_head(
            spread[image, :, number, 0],
            spread[image, :, number, 1],
            spread[image, :, number, 2],
            key_live[image],
            scaling,
            blocks,
        )
        outputs.append(output)
        image_logsums.append(logsum)
    image_outputs = [jnp.stack(outputs, axis=1).reshape(slot_rows, local_heads * DH)]
    logsums = [image_logsums]
    attended_heads = jnp.stack(image_outputs, axis=0)
    attended = lax.all_to_all(attended_heads, "head", split_axis=1, concat_axis=2, tiled=True)
    second = tokens + jnp.einsum(
        "ire,ed->ird", attended, full_out, preferred_element_type=jnp.float32
    )
    normal_two, inverse_two = standardize(second)
    normed_two = (normal_two * gain_two).astype(jnp.bfloat16)
    hidden = jnp.einsum("ird,df->irf", normed_two, full_up, preferred_element_type=jnp.float32)
    gelu_exact = partial(jax.nn.gelu, approximate=False)
    active = gelu_exact(hidden).astype(jnp.bfloat16)
    residual = second + jnp.einsum(
        "irf,fd->ird", active, full_down, preferred_element_type=jnp.float32
    )
    rounded = residual.astype(jnp.bfloat16)
    patch_proj = jnp.einsum("ird,de->ire", rounded, full_patch, preferred_element_type=jnp.float32)
    patch_unit = (patch_proj * unit_scale(patch_proj)).astype(jnp.bfloat16)
    class_proj = jnp.einsum(
        "ird,de->ire", rounded[:, :CLS], full_class, preferred_element_type=jnp.float32
    )
    class_unit = (class_proj * unit_scale(class_proj)).astype(jnp.bfloat16)
    classes = spread_2(class_unit, "head", 0)
    products = jnp.einsum("ird,icd->irc", patch_unit, classes, preferred_element_type=jnp.float32)
    normal_mask, inverse_mask = standardize(products)
    class_masks = (normal_mask * mask_norm[0] + mask_norm[1]) * patch_rows
    upstream = grad_masks * patch_rows
    norm_grads = lax.psum(
        jnp.stack([jnp.sum(upstream * normal_mask, axis=(0, 1)), jnp.sum(upstream, axis=(0, 1))]),
        ("head", "seq"),
    )
    d_products = standard_back(normal_mask, inverse_mask, upstream * mask_norm[0]).astype(
        jnp.bfloat16
    )
    d_patch_unit = jnp.einsum(
        "irc,icd->ird", d_products, classes, preferred_element_type=jnp.float32
    )
    class_part = jnp.einsum(
        "irc,ird->icd", d_products, patch_unit, preferred_element_type=jnp.float32
    )
    d_class_unit = lax.psum(class_part.astype(jnp.bfloat16), "head").astype(jnp.float32)
    d_patch_proj = unit_back(patch_proj, d_patch_unit).astype(jnp.bfloat16)
    d_class_proj = (unit_back(class_proj, d_class_unit) * root_flag).astype(jnp.bfloat16)
    regathered = (
        lax.all_gather(w_qkv, ("head", "seq"), axis=0, tiled=True),
        lax.all_gather(w_out, ("head", "seq"), axis=0, tiled=True),
        lax.all_gather(w_up, ("head", "seq"), axis=0, tiled=True),
        lax.all_gather(w_down, ("head", "seq"), axis=0, tiled=True),
        lax.all_gather(w_patch, ("head", "seq"), axis=0, tiled=True),
        lax.all_gather(w_class, ("head", "seq"), axis=0, tiled=True),
        lax.all_gather(gains_rows, ("head", "seq"), axis=0, tiled=True),
    )
    back_qkv, back_out, back_up, back_down, back_patch, back_class, back_gains = regathered
    back_one = back_gains[:, 0].astype(jnp.float32)
    back_two = back_gains[:, 1].astype(jnp.float32)
    grad_patch = jnp.einsum(
        "ird,ire->de", rounded, d_patch_proj, preferred_element_type=jnp.float32
    )
    grad_class = jnp.einsum(
        "ird,ire->de", rounded[:, :CLS], d_class_proj, preferred_element_type=jnp.float32
    )
    d_residual = jnp.einsum(
        "ire,de->ird", d_patch_proj, back_patch, preferred_element_type=jnp.float32
    )
    class_term = jnp.einsum(
        "ire,de->ird", d_class_proj, back_class, preferred_element_type=jnp.float32
    )
    d_residual = d_residual.at[:, :CLS].add(class_term)
    d_branch = d_residual.astype(jnp.bfloat16)
    grad_down = jnp.einsum("irf,ird->fd", active, d_branch, preferred_element_type=jnp.float32)
    d_active = jnp.einsum("ird,fd->irf", d_branch, back_down, preferred_element_type=jnp.float32)
    gelu_pull = jax.vjp(gelu_exact, hidden)[1]
    d_hidden = gelu_pull(d_active)[0].astype(jnp.bfloat16)
    grad_up = jnp.einsum("ird,irf->df", normed_two, d_hidden, preferred_element_type=jnp.float32)
    d_normed_two = jnp.einsum("irf,df->ird", d_hidden, back_up, preferred_element_type=jnp.float32)
    d_second = d_residual + standard_back(normal_two, inverse_two, d_normed_two * back_two)
    grad_gain_two = jnp.sum(d_normed_two * normal_two, axis=(0, 1))
    d_mix = d_second.astype(jnp.bfloat16)
    grad_out = jnp.einsum("ire,ird->ed", attended, d_mix, preferred_element_type=jnp.float32)
    d_attended = jnp.einsum(
        "ird,ed->ire", d_mix, back_out, preferred_element_type=jnp.float32
    ).astype(jnp.bfloat16)
    d_heads = lax.all_to_all(d_attended, "head", split_axis=2, concat_axis=1, tiled=True).reshape(
        image_count, slot_rows, local_heads, DH
    )
    image = 0
    head_grads = []
    for number in range(local_heads):
        grad_queries, grad_keys, grad_values = attend_back(
            spread[image, :, number, 0],
            spread[image, :, number, 1],
            spread[image, :, number, 2],
            d_heads[image, :, number],
            logsums[image][number],
            key_live[image],
            scaling,
            blocks,
        )
        head_grads.append(jnp.stack([grad_queries, grad_keys, grad_values], axis=1))
    image_grads = [jnp.stack(head_grads, axis=1).reshape(slot_rows, local_heads * 3 * DH)]
    d_spread = jnp.stack(image_grads, axis=0).astype(jnp.bfloat16)
    d_triple = lax.all_to_all(d_spread, "head", split_axis=1, concat_axis=2, tiled=True)
    grad_qkv = jnp.einsum("ird,irt->dt", normed_one, d_triple, preferred_element_type=jnp.float32)
    d_normed_one = jnp.einsum("irt,dt->ird", d_triple, back_qkv, preferred_element_type=jnp.float32)
    grad_inputs = d_second + standard_back(normal_one, inverse_one, d_normed_one * back_one)
    grad_gain_one = jnp.sum(d_normed_one * normal_one, axis=(0, 1))
    grad_gains = jnp.stack([grad_gain_one, grad_gain_two], axis=1)
    reduced = (
        lax.psum_scatter(grad_qkv, ("head", "seq"), scatter_dimension=0, tiled=True),
        lax.psum_scatter(grad_out, ("head", "seq"), scatter_dimension=0, tiled=True),
        lax.psum_scatter(grad_up, ("head", "seq"), scatter_dimension=0, tiled=True),
        lax.psum_scatter(grad_down, ("head", "seq"), scatter_dimension=0, tiled=True),
        lax.psum_scatter(grad_patch, ("head", "seq"), scatter_dimension=0, tiled=True),
        lax.psum_scatter(grad_class, ("head", "seq"), scatter_dimension=0, tiled=True),
        lax.psum_scatter(grad_gains, ("head", "seq"), scatter_dimension=0, tiled=True),
    )
    return (
        class_masks,
        grad_inputs,
        reduced[0],
        reduced[1],
        reduced[2],
        reduced[3],
        reduced[4],
        reduced[5],
        reduced[6].T,
        norm_grads,
    )


MESH = pl.DeviceIdType.MESH
LOG2E = 1.4426950408889634
SLOTS = 16
FRONT_COPIES = 160
REAR_COPIES = 88


def matmul(left, right):
    return jnp.dot(left, right, preferred_element_type=jnp.float32)


def matmul_nt(left, right):
    return lax.dot_general(left, right, (((1,), (1,)), ((), ())), preferred_element_type=jnp.float32)


def matmul_tn(left, right):
    return lax.dot_general(left, right, (((0,), (0,)), ((), ())), preferred_element_type=jnp.float32)


def norm(values):
    center = values - jnp.mean(values, axis=-1, keepdims=True)
    inverse = lax.rsqrt(jnp.mean(center * center, axis=-1, keepdims=True) + 1e-05)
    return center * inverse, inverse


def device(y, x, z, c):
    return (y * 2 + x, z * 2 + c)


class Links:
    def __init__(self, send_sem, recv_sem):
        head, seq = lax.axis_index("head"), lax.axis_index("seq")
        self.y, self.x, self.z, self.c = head // 2, head % 2, seq // 2, seq % 2
        y, x, z, c = self.y, self.x, self.z, self.c
        self.sibling = device(y, x, z, 1 - c)
        self.along_x = device(y, 1 - x, z, c)
        self.along_y = device(1 - y, x, z, c)
        self.across = device(1 - y, 1 - x, z, c)
        self.along_z = [device(y, x, (z + k) % 4, c) for k in (1, 2, 3)]
        self.send_sem, self.recv_sem, self.count, self.made, self.lines = send_sem, recv_sem, 0, [], []

    def greet(self):
        barrier = pltpu.get_barrier_semaphore()
        peers = [self.sibling, self.along_x, self.along_y, self.across] + self.along_z
        for peer in peers:
            pl.semaphore_signal(barrier, inc=1, device_id=peer, device_id_type=MESH)
        pl.semaphore_wait(barrier, len(peers))

    def plan(self, source, target, peer, sends=None, again=False):
        number = self.count - again
        self.count = number + 1
        copy = pltpu.make_async_remote_copy(
            src_ref=source,
            dst_ref=target,
            send_sem=self.send_sem.at[number],
            recv_sem=self.recv_sem.at[number],
            device_id=peer,
            device_id_type=MESH,
        )
        if not again:
            self.made.append((copy, sends))
        return copy

    def drain(self):
        for copy, sends in self.made:
            if sends is None:
                copy.wait_send()
            else:
                pl.when(sends)(copy.wait_send)
        for line in self.lines:
            line.drain()


class Stage:
    def __init__(self, links, moves, again=False):
        self.copies = [links.plan(*move, again=again) for move in moves]

    def start(self):
        for copy in self.copies:
            copy.start()

    def wait(self):
        for copy in self.copies:
            copy.wait_recv()


class Line:
    def __init__(self, links, piece, source=None):
        self.links, self.piece = links, piece
        self.source = piece(links.z) if source is None else source
        self.base = links.count
        links.count += 5
        links.lines.append(self)

    def copy(self, source, target, sent, landed):
        links = self.links
        return pltpu.make_async_remote_copy(
            src_ref=source,
            dst_ref=self.piece(landed),
            send_sem=links.send_sem.at[self.base + sent],
            recv_sem=links.recv_sem.at[self.base + landed],
            device_id=device(links.y, links.x, target, links.c),
            device_id_type=MESH,
        )

    def direct(self, target):
        z = self.links.z
        return (z != target) if target in (1, 2) else (z != target) & (z != 3 - target)

    def start(self):
        for target in (1, 2, 0, 3):

            @pl.when(self.direct(target))
            def _(target=target):
                self.copy(self.source, target, target, self.links.z).start()

    def relay(self):
        for at, end in ((2, 0), (1, 3)):

            @pl.when(self.links.z == at)
            def _(end=end):
                self.copy(self.source, 3 - end, 4, end).wait_recv()
                self.copy(self.piece(end), 3 - end, 4, end).start()

    def wait(self):
        z = self.links.z
        for origin in range(4):
            pending = z != origin
            if origin in (0, 3):
                pending = pending & (z != (2 if origin == 0 else 1))

            @pl.when(pending)
            def _(origin=origin):
                self.copy(self.source, 0, 0, origin).wait_recv()

    def drain(self):
        for target in range(4):

            @pl.when(self.direct(target))
            def _(target=target):
                self.copy(self.source, target, target, self.links.z).wait_send()

        @pl.when((self.links.z == 1) | (self.links.z == 2))
        def _():
            self.copy(self.source, 0, 4, 0).wait_send()


def at_slots(slot, events):
    for number, event in events.items():
        pl.when(slot == number)(event)


def weight_gradient(target, left, right):
    per = left.shape[1] // 4
    for j in range(4):
        piece = matmul_tn(left[:, j * per : (j + 1) * per], right[...]).astype(jnp.bfloat16)
        if len(target.shape) == 6:
            target[j // 2, j % 2] = piece.reshape(target.shape[2:])
        else:
            pair = target.shape[1] // 2
            at = (j % 2) * pair
            target[j // 2, at : at + pair] = piece.reshape((pair,) + target.shape[2:])


class LineSum:
    def __init__(self, links, piece, got):
        self.links, self.piece, self.got = links, piece, got
        self.base = links.count
        links.count += 5
        links.lines.append(self)

    def copy(self, piece, target, slot, sent):
        links = self.links
        return pltpu.make_async_remote_copy(
            src_ref=self.piece(piece),
            dst_ref=self.got.at[slot],
            send_sem=links.send_sem.at[self.base + sent],
            recv_sem=links.recv_sem.at[self.base + slot],
            device_id=device(links.y, links.x, target, links.c),
            device_id_type=MESH,
        )

    def start(self):
        z = self.links.z
        for target, end, middle in ((3, 0, 1), (0, 3, 2)):

            @pl.when(z == end)
            def _(target=target, middle=middle):
                self.copy(target, middle, 4, target).start()

        for target in range(4):
            direct = z != target
            if target in (0, 3):
                direct = z == (1 if target == 0 else 2)

            @pl.when(direct)
            def _(target=target):
                self.copy(target, target, z, target).start()

    def relay(self):
        z = self.links.z
        for target, middle in ((3, 1), (0, 2)):

            @pl.when(z == middle)
            def _(target=target, middle=middle):
                self.copy(target, target, 4, target).wait_recv()
                own = self.piece(target)
                own[...] = own[...] + self.got[4]
                self.copy(target, target, middle, target).start()

    def collect(self, add):
        z = self.links.z
        for origin in range(4):
            comes = z != origin
            if origin in (0, 3):
                comes = comes & (z != 3 - origin)

            @pl.when(comes)
            def _(origin=origin):
                self.copy(0, 0, origin, 0).wait_recv()
                add(origin)

    def drain(self):
        for target in range(4):

            @pl.when(self.links.z != target)
            def _(target=target):
                self.copy(target, target, 0, target).wait_send()


class Sum:
    def __init__(self, links, partial_ref, sib, one, two, three, kind):
        y, x, z, c = links.y, links.x, links.z, links.c
        self.links, self.sib, self.one, self.two, self.three = links, sib, one, two, three
        self.kind = kind
        self.q = y * (1 - c) + x * c
        lead = () if kind == "down" else (slice(None),) * 3
        total = self.total = partial_ref.at[(*lead, c)]
        self.core = Stage(links, [(partial_ref.at[(*lead, 1 - c)], sib, links.sibling)])
        if kind in ("up_y", "all_y"):
            self.first = Stage(links, [(total.at[1 - y], one, links.along_y)])
            self.kept = lambda i, j: (y, i, j)
        elif kind in ("up_x", "all_x"):
            self.first = Stage(links, [(total.at[:, 1 - x], one, links.along_x)])
            self.kept = lambda i, j: (i, x, j)
        else:
            turned = device(y + (1 - c) * (1 - 2 * y), x + c * (1 - 2 * x), z, c)
            self.first = Stage(links, [(total.at[1 - self.q], one, turned)])
            self.line = LineSum(links, lambda at: total.at[self.q, at], three)
        if kind == "up_y":
            self.line = LineSum(links, lambda at: total.at[y, :, at], three)
            self.last = Stage(links, [(total.at[y, 1 - x, z], two, links.along_x)])
        elif kind == "up_x":
            self.line = LineSum(links, lambda at: total.at[:, x, at], three)
            self.last = Stage(links, [(total.at[1 - y, x, z], two, links.along_y)])
        elif kind == "all_x":
            self.second = Stage(links, [(total.at[1 - y, x], two, links.along_y)])
        elif kind == "all_y":
            self.second = Stage(links, [(total.at[y, 1 - x], two, links.along_x)])
        if kind in ("all_x", "all_y"):
            self.line = LineSum(links, lambda at: total.at[y, x, at], three)

    def begin(self):
        self.core.start()

    def add(self, pairs, count):
        total = self.total

        def body(i, carry):
            index, extra = pairs(i)
            total[index] = total[index] + extra
            return carry

        lax.fori_loop(0, count, body, 0)

    def run_first(self):
        self.core.wait()
        sib = self.sib
        if self.kind == "down":
            self.add(lambda i: ((i // 4, i % 4), sib[i // 4, i % 4]), 8)
        else:
            self.add(lambda i: ((i // 8, i // 4 % 2, i % 4), sib[i // 8, i // 4 % 2, i % 4]), 16)
        self.first.start()

    def run_second(self):
        self.first.wait()
        one = self.one
        if self.kind == "down":
            self.add(lambda i: ((self.q, i), one[i]), 4)
        else:
            self.add(lambda i: (self.kept(i // 4, i % 4), one[i // 4, i % 4]), 8)
        if self.kind in ("all_x", "all_y"):
            self.second.start()
        else:
            self.line.start()

    def run_third(self):
        self.second.wait()
        y, x, two = self.links.y, self.links.x, self.two
        self.add(lambda i: ((y, x, i), two[i]), 4)
        self.line.start()

    def run_last(self):
        z, total, got = self.links.z, self.total, self.three

        def add(slot):
            for i in range(2):
                index = self.kept(i, z)
                total[index] = total[index] + got[slot, i]

        self.line.collect(add)
        self.last.start()

    def finish(self, out):
        y, x, z = self.links.y, self.links.x, self.links.z
        if self.kind in ("up_y", "up_x"):
            self.last.wait()
            along_x = self.kind == "up_y"
            mine = x if along_x else y
            for number, part in ((mine, self.total[y, x, z]), (1 - mine, self.two[...])):
                for j in range(8):
                    place = (j // 4 * 2 + number) if along_x else (number * 2 + j // 4)
                    start = (place * 4 + j % 4) * 256 + (0 if along_x else 128)
                    at = pl.ds(pl.multiple_of(start, 128), 128)
                    out[:, at] = part[:, j * 128 : (j + 1) * 128].astype(jnp.float32)
            return
        out[...] = (self.total[self.q, z] if self.kind == "down" else self.total[y, x, z]).astype(jnp.float32)

        def add(slot):
            out[...] = out[...] + self.three[slot].astype(jnp.float32)

        self.line.collect(add)


def front_kernel(scaling, *refs):
    live_ref, tokens, norm_gains, grad_masks, mask_norm = refs[:5]
    qkv_shard, out_shard, up_given, down_shard, patch_shard, class_shard = refs[5:11]
    attended, heads_ref, logsum, rows_ref, gains_ref, qkv, class_masks, mask_sums = refs[11:19]
    normal_one, inverse_one, normed_two, active, d_branch, d_hidden = refs[19:25]
    d_mix, d_second, d_attended, g_patch, g_class = refs[25:30]
    refs = refs[30:]
    full_out, ups, downs, full_patch, full_class, tiles, staged = refs[:7]
    slope, stream, normal_two, inverse_two, patch_proj, class_proj, classes = refs[7:14]
    part_sent, part_got, back_sent, back_got, class_sent, class_got = refs[14:20]
    term_sent, term_got, mask_in, tile, up_shard = refs[20:25]
    rounded, d_patch, class_rows, d_class = refs[25:29]
    patch_parts, class_parts = refs[29:34], refs[34:39]
    send_sem, recv_sem, local_sem = refs[39:]
    second = residual = d_residual = stream
    links = Links(send_sem, recv_sem)
    y, x, z, c = links.y, links.x, links.z, links.c
    h = y * 2 + x
    q = y * (1 - c) + x * c
    rows, features = tokens.shape
    wide = qkv.shape[-1]
    narrow = staged.shape[1]
    heads = narrow // DH
    block = ups.shape[-1]
    slot_rows = rows * 4
    plane = [(links.across, 3 - h, 3), (links.along_x, y * 2 + 1 - x, 1), (links.along_y, (1 - y) * 2 + x, 2)]
    at_x, at_y = plane[1][1], plane[2][1]

    def columns(start, size):
        return pl.ds(pl.multiple_of(start, 128), size)

    def up_block(number):
        return up_shard.at[:, columns(number * block, block)]

    local = [
        pltpu.make_async_copy(source, target, local_sem.at[number])
        for number, (source, target) in zip(
            (0, 1, 2, 3, 4, 5, 7, 8),
            [
                (tile, tiles.at[y, x, z, c]),
                (qkv_shard.at[:, columns(h * wide, wide)], qkv.at[y, x, z, c]),
                (out_shard, full_out.at[y, x, z, c]),
                (down_shard, downs.at[c, q, z]),
                (up_block(x), ups.at[0, y, x, z, c]),
                (up_block(2 + y), ups.at[1, y, x, z, c]),
                (patch_shard, full_patch.at[y, x, z, c]),
                (class_shard, full_class.at[y, x, z, c]),
            ]
        )
    ]
    gain_core = Stage(links, [(tile, tiles.at[y, x, z, c], links.sibling)])
    gain_z = Stage(links, [(tiles.at[y, x, z], tiles.at[y, x, z], peer) for peer in links.along_z])
    gain_plane = Stage(links, [(tiles.at[y, x], tiles.at[y, x], peer) for peer, _, _ in plane])
    qkv_plane = Stage(
        links, [(qkv_shard.at[:, columns(p * wide, wide)], qkv.at[y, x, z, c], peer) for peer, p, _ in plane]
    )
    part = qkv.shape[4] // 2
    qkv_z = [Line(links, lambda at, k=k: qkv.at[:, :, at, c, k * part : (k + 1) * part]) for k in range(2)]
    qkv_core = Stage(links, [(qkv.at[:, :, :, c], qkv.at[:, :, :, c], links.sibling)])
    up_split = [
        Stage(links, [(up_block(1 - x), ups.at[0, y, x, z, c], links.along_x)]),
        Stage(links, [(up_block(2 + 1 - y), ups.at[1, y, x, z, c], links.along_y)]),
    ]
    up_z = [
        Line(links, lambda at: ups.at[0, y, :, at, c]),
        Line(links, lambda at: ups.at[1, :, x, at, c]),
    ]
    up_on = [
        Stage(links, [(ups.at[0, y, :, :, c], ups.at[0, y, :, :, c], links.along_y)]),
        Stage(links, [(ups.at[1, :, x, :, c], ups.at[1, :, x, :, c], links.along_x)]),
    ]
    up_core = [
        Stage(links, [(ups.at[k, :, :, :, c], ups.at[k, :, :, :, c], links.sibling)]) for k in range(2)
    ]
    some = down_shard.shape[0] // 4
    turned = device(y + (1 - c) * (1 - 2 * y), x + c * (1 - 2 * x), z, c)
    spans = [slice(k * some, (k + 1) * some) for k in range(4)]
    down_turn = [Stage(links, [(down_shard.at[spans[k]], downs.at[c, q, z, spans[k]], turned)]) for k in (0, 1)]
    down_z = [Line(links, lambda at, k=k: downs.at[c, :, at, spans[k]]) for k in (0, 1)] + [
        Line(links, lambda at, k=k: downs.at[c, q, at, spans[k]], down_shard.at[spans[k]]) for k in (2, 3)
    ]
    down_on = [Stage(links, [(downs.at[c, q, :, spans[k]],) * 2 + (turned,)]) for k in (2, 3)]
    down_core = [
        Stage(links, [(downs.at[c, :, :, span], downs.at[c, :, :, span], links.sibling)])
        for span in (slice(0, 2 * some), slice(2 * some, 4 * some))
    ]
    patch_sum = Sum(links, *patch_parts, "all_x")
    class_sum = Sum(links, *class_parts, "all_y")
    part = out_shard.shape[0] // 2

    def square(full, shard):
        first = [full.at[y, x, :, c, 0:part], full.at[y, x, :, c, part:]]
        second = [full.at[:, x, :, c, 0:part], full.at[y, :, :, c, part:]]
        return (
            Line(links, lambda at: full.at[y, x, at, c], shard),
            Stage(links, [(first[0], first[0], links.along_y), (first[1], first[1], links.along_x)]),
            Stage(links, [(second[0], second[0], links.along_x), (second[1], second[1], links.along_y)]),
            Stage(links, [(full.at[:, :, :, c],) * 2 + (links.sibling,)]),
        )

    out_z, out_one, out_two, out_core = square(full_out, out_shard)
    near, far = slice(0, part), slice(part, 2 * part)
    patch_x = Stage(links, [(patch_shard.at[far], full_patch.at[y, x, z, c, far], links.along_x)])
    patch_y = Stage(links, [(full_patch.at[y, :, z, c, far],) * 2 + (links.along_y,)])
    patch_first = Line(links, lambda at: full_patch.at[y, x, at, c, near], patch_shard.at[near])
    patch_one = Stage(links, [(full_patch.at[y, x, :, c, near],) * 2 + (links.along_y,)])
    patch_two = Stage(links, [(full_patch.at[:, x, :, c, near],) * 2 + (links.along_x,)])
    class_y = Stage(links, [(class_shard, full_class.at[y, x, z, c], links.along_y)])
    class_x = Stage(links, [(full_class.at[:, x, z, c],) * 2 + (links.along_x,)])
    halves = [slice(k * part, (k + 1) * part) for k in range(2)]
    class_z = [Line(links, lambda at, k=k: full_class.at[:, :, at, c, k * part : (k + 1) * part]) for k in range(2)]
    halves = [slice(part + k * part // 2, part + (k + 1) * part // 2) for k in range(2)]
    patch_z = [Line(links, lambda at, k=k: full_patch.at[:, :, at, c, halves[k]]) for k in range(2)]
    patch_core = Stage(links, [(full_patch.at[:, :, :, c],) * 2 + (links.sibling,)])
    class_core = Stage(links, [(full_class.at[:, :, :, c],) * 2 + (links.sibling,)])
    beside = (links.along_x, links.along_y)
    here = slice(0, rows)
    few = class_proj.shape[0]
    tall = -(-CLS // 16) * 16
    parts = (slice(0, tall), slice(tall, rows))
    theirs = [slice(rows + at.start, rows + at.stop) for at in parts]

    def exchange(sent, got, sent_at, got_at):
        return [
            [Stage(links, [(sent.at[k, sent_at[i]], got.at[k, got_at[i]], beside[k])]) for i in range(2)]
            for k in range(2)
        ]

    normed_out = exchange(normed_two, normed_two, parts, theirs)
    branch_out = exchange(d_branch, d_branch, parts, theirs)
    part_back = exchange(part_sent, part_got, parts, parts)
    grad_back = exchange(back_sent, back_got, parts, parts)
    sizes = {1: few, 2: few, 3: tall - 3 * few}
    class_out = [
        links.plan(
            rounded.at[few * rel : few * rel + sizes[rel]], class_rows.at[0 : sizes[rel]], peer, h == 0
        )
        for peer, _, rel in plane
    ]
    mine = pl.ds(pl.multiple_of(h * few, few), few)
    unit_out = Stage(links, [(classes.at[mine], classes.at[mine], peer) for peer, _, _ in plane])
    class_back = Stage(links, [(class_sent.at[p], class_got.at[rel - 1], peer) for peer, p, rel in plane])
    term_back = [
        links.plan(term_sent.at[0 : sizes[rel]], term_got.at[rel - 1, 0 : sizes[rel]], peer, h == rel)
        for peer, _, rel in plane
    ]
    middle = rows // 2
    strips = [slice(0, middle), slice(middle, rows)]
    rows_x = [Stage(links, [(rows_ref.at[h, strips[k]],) * 2 + (links.along_x,)]) for k in (0, 1)]
    rows_y = [Stage(links, [(rows_ref.at[h, strips[k]],) * 2 + (links.along_y,)]) for k in (1, 0)]
    piece_a, piece_b = rows_ref.at[at_x, strips[0]], rows_ref.at[at_y, strips[1]]
    relay_y = Stage(links, [(piece_a, piece_a, links.along_y)])
    relay_x = Stage(links, [(piece_b, piece_b, links.along_x)])

    share = norm_gains.shape[1]
    tile[...] = jnp.zeros_like(tile)
    for i in range(4):

        @pl.when((z * 2 + c) % 4 == i)
        def _(i=i):
            tile[0:2, i * share : (i + 1) * share] = norm_gains[...].astype(jnp.float32)

    for number in range(4):
        for j in range(8):
            at = (j // 4 * 2 + number) if number < 2 else ((number - 2) * 2 + j // 4)
            at = (at * 4 + j % 4) * 256 + (0 if number < 2 else 128)
            up_shard[:, number * block + j * 128 : number * block + (j + 1) * 128] = up_given[:, at : at + 128]
    for copy in local:
        copy.start()
    class_rows[...] = jnp.zeros_like(class_rows)
    links.greet()
    for stage in (gain_core, qkv_plane, *up_split, *down_turn, class_y, patch_x, out_z, patch_first):
        stage.start()
    value, inverse = norm(tokens[...])
    normal_one[...] = value
    inverse_one[...] = jnp.broadcast_to(inverse, inverse_one.shape)
    local[0].wait()
    gain_core.wait()
    gain_z.start()
    gain_z.wait()
    gain_plane.start()
    local[1].wait()
    qkv_plane.wait()
    for line in qkv_z:
        line.start()
    gain_plane.wait()
    for j in range(8):
        piece = tiles[j // 4, j // 2 % 2, (j % 2) * 2, 0].astype(jnp.float32)
        for i in range(1, 4):
            piece = piece + tiles[j // 4, j // 2 % 2, (j % 2) * 2 + i // 2, i % 2].astype(jnp.float32)
        gains_ref[:, j * 128 : (j + 1) * 128] = piece[0:8]
    rows_ref[h] = (normal_one[...] * gains_ref[0:1, :]).astype(jnp.bfloat16)
    for stage in (rows_x[0], rows_y[0], rows_x[1], rows_y[1]):
        stage.start()
    for line in (out_z, patch_first, *qkv_z):
        line.relay()
    rows_x[0].wait()
    relay_y.start()
    rows_y[0].wait()
    relay_x.start()
    local[6].wait()
    patch_x.wait()
    patch_y.start()
    local[7].wait()
    class_y.wait()
    class_x.start()
    for line in qkv_z:
        line.wait()
    qkv_core.start()
    for k in range(2):
        local[4 + k].wait()
        up_split[k].wait()
        up_z[k].start()
    out_z.wait()
    patch_first.wait()
    for number in (2, 3):
        local[number].wait()

    def project(p):
        weight = qkv[...].reshape(rows * 4, wide)
        piece = jnp.dot(rows_ref[p], weight, preferred_element_type=jnp.float32).astype(jnp.bfloat16)
        at = pl.ds(pl.multiple_of(p * rows, rows), rows)
        for number in range(3 * heads):
            heads_ref[number, at, :] = piece[:, number * DH : (number + 1) * DH]

    qkv_core.wait()
    project(h)
    rows_x[1].wait()
    project(at_x)
    rows_y[1].wait()
    project(at_y)
    out_one.start()
    patch_one.start()
    relay_y.wait()
    relay_x.wait()
    project(3 - h)

    live = live_ref[0]
    key_live = lax.broadcasted_iota(jnp.int32, (slot_rows, 1), 0) < live
    returned = links.count - 1
    assert returned + 4 <= FRONT_COPIES

    def back(rel):
        peer = h + (rel % 2) * (1 - 2 * x) + (rel // 2) * (2 - 4 * y)
        return pltpu.make_async_remote_copy(
            src_ref=staged.at[pl.ds(pl.multiple_of(peer * rows, rows), rows), :],
            dst_ref=attended.at[:, columns(h * narrow, narrow)],
            send_sem=send_sem.at[returned + rel],
            recv_sem=recv_sem.at[returned + rel],
            device_id=(peer, z * 2 + c),
            device_id_type=MESH,
        )

    def up_next(k):
        up_z[k].wait()
        up_on[k].start()

    def up_end(k):
        up_on[k].wait()
        up_core[k].start()

    def out_next():
        out_one.wait()
        out_two.start()

    def out_end():
        out_two.wait()
        out_core.start()

    def patch_next():
        patch_one.wait()
        patch_two.start()

    def down_late():
        down_z[2].start()
        down_z[3].start()

    def down_early():
        for stage in down_turn:
            stage.wait()
        down_z[0].start()
        down_z[1].start()

    def down_relays():
        down_z[2].relay()
        down_z[3].relay()

    events = {
        0: up_z[0].relay,
        3: out_next,
        5: up_z[1].relay,
        6: down_late,
        11: down_early,
        12: out_end,
        14: down_relays,
    }

    def tile_body(slot, carry):
        turn, number = slot // 4, slot % 4
        rel = 3 - turn
        peer = h + (rel % 2) * (1 - 2 * x) + (rel // 2) * (2 - 4 * y)
        at = pl.ds(pl.multiple_of(peer * rows, rows), rows)
        at_slots(slot, events)
        queries = heads_ref[3 * number, at, :]
        keys = heads_ref[3 * number + 1]
        values = heads_ref[3 * number + 2]
        scores = lax.dot_general(keys, queries, (((1,), (1,)), ((), ())), preferred_element_type=jnp.float32)
        scores = jnp.where(key_live, scores * (scaling * LOG2E), -1e30)
        highest = jnp.max(scores, axis=0, keepdims=True)
        raw = jnp.exp2(scores - highest)
        totals = jnp.sum(raw, axis=0, keepdims=True)
        weights = (raw * (1.0 / totals)).astype(jnp.bfloat16)
        mixed = lax.dot_general(
            values, weights, (((0,), (0,)), ((), ())), preferred_element_type=jnp.float32
        )
        mixed = mixed.T.astype(jnp.bfloat16)
        for which in range(4):

            @pl.when(number == which)
            def _(which=which):
                staged[at, which * DH : (which + 1) * DH] = mixed

        logsum[number, :, at] = highest + jnp.log2(totals)

        @pl.when((number == 3) & (rel > 0))
        def _():
            back(rel).start()

        return carry

    lax.fori_loop(0, SLOTS, tile_body, 0)
    own = pltpu.make_async_copy(
        staged.at[pl.ds(pl.multiple_of(h * rows, rows), rows), :],
        attended.at[:, columns(h * narrow, narrow)],
        local_sem.at[6],
    )
    own.start()
    class_x.wait()
    patch_y.wait()
    for line in (*class_z, *patch_z):
        line.start()
    up_next(0)
    up_next(1)
    for k in range(2):
        down_z[2 + k].wait()
        down_on[k].start()
    for rel in (3, 2, 1):
        back(rel).wait()
    own.wait()
    out_core.wait()
    down_z[0].relay()

    def whole(weight):
        return weight[...].reshape(-1, weight.shape[-1])

    second[...] = tokens[...] + matmul(attended[...], whole(full_out))
    value, inverse = norm(second[...])
    normal_two[...] = value
    inverse_two[...] = jnp.broadcast_to(inverse, inverse_two.shape)
    value = (value * gains_ref[1:2, :]).astype(jnp.bfloat16)
    for k in range(2):
        normed_two[k, here] = value
    for i in range(2):
        for k in range(2):
            normed_out[k][i].start()
    down_z[1].relay()
    patch_next()
    up_end(0)
    up_end(1)
    for k in range(2):
        up_core[k].wait()
    wide_step = 256

    def forward(k, at, size):
        def step(j, carry):
            span = pl.ds(pl.multiple_of(j * wide_step, wide_step), wide_step)
            weight = ups[k, :, :, :, :, :, span].reshape(features, wide_step)
            hidden = matmul(normed_two[k, at], weight)
            spread = 0.5 + 0.5 * lax.erf(hidden * 0.7071067811865476)
            density = jnp.exp(hidden * hidden * -0.5) * 0.3989422804014327
            active[k, at, span] = (hidden * spread).astype(jnp.bfloat16)
            slope[k, at, span] = spread + hidden * density
            return carry

        lax.fori_loop(0, block // wide_step, step, 0)

    forward(0, here, rows)
    for stage in down_on:
        stage.wait()
    down_core[1].start()
    forward(1, here, rows)
    for line in down_z[:2]:
        line.wait()
    down_core[0].start()
    for stage in down_core:
        stage.wait()
    for i in range(2):
        for k in range(2):
            normed_out[k][i].wait()
            forward(k, theirs[i], parts[i].stop - parts[i].start)
            part_sent[k, parts[i]] = matmul(active[k, theirs[i]], whole(downs.at[k])).astype(jnp.bfloat16)
            part_back[k][i].start()
        if i == 0:
            for line in class_z:
                line.relay()
    residual[...] = second[...] + (
        matmul(active[0, here], whole(downs.at[0])) + matmul(active[1, here], whole(downs.at[1]))
    )
    for line in patch_z:
        line.relay()

    def complete(at):
        for k in range(2):
            part_back[k][0 if at.start == 0 else 1].wait()
        value = residual[at] + (part_got[0, at].astype(jnp.float32) + part_got[1, at].astype(jnp.float32))
        rounded[at] = value.astype(jnp.bfloat16)

    complete(parts[0])

    @pl.when(h == 0)
    def _():
        for copy in class_out:
            copy.start()
        class_rows[...] = rounded[0:few]

    for line in class_z:
        line.wait()
    class_core.start()
    complete(parts[1])
    for line in patch_z:
        line.wait()
    patch_two.wait()
    patch_core.start()
    patch_core.wait()

    patch_proj[...] = matmul(rounded[...], whole(full_patch))
    factor = unit_scale(patch_proj[...])
    patch_unit = (patch_proj[...] * factor).astype(jnp.bfloat16)
    classes[4 * few :] = jnp.zeros((classes.shape[0] - 4 * few, features), jnp.bfloat16)
    for copy, (_, _, rel) in zip(class_out, plane):
        pl.when(h == rel)(copy.wait_recv)
    class_core.wait()
    class_live = h * few + lax.broadcasted_iota(jnp.int32, (few, 1), 0) < CLS
    value = matmul(class_rows[...], whole(full_class))
    class_proj[...] = value
    classes[mine] = jnp.where(class_live, value * unit_scale(value), 0.0).astype(jnp.bfloat16)
    unit_out.start()
    mask_in[...] = jnp.zeros_like(mask_in)
    mask_in[0:rows, 0:CLS] = grad_masks[...]
    mask_in[rows : rows + 2, 0:CLS] = mask_norm[...]
    mask_gain, mask_bias = mask_in[rows : rows + 1, :], mask_in[rows + 1 : rows + 2, :]
    unit_out.wait()
    products = matmul_nt(patch_unit, classes[...])
    lane = lax.broadcasted_iota(jnp.int32, products.shape, 1)
    position = h * rows + lax.broadcasted_iota(jnp.int32, (rows, 1), 0)
    patch_rows = ((position >= CLS) & (position < live)).astype(jnp.float32)

    def class_mean(values):
        return jnp.sum(values, axis=-1, keepdims=True) * (1.0 / CLS)

    center = jnp.where(lane < CLS, products - class_mean(products), 0.0)
    inverse = lax.rsqrt(class_mean(center * center) + 1e-05)
    mask_normal = center * inverse
    class_masks[...] = ((mask_normal * mask_gain + mask_bias) * patch_rows)[:, 0:CLS]
    upstream = mask_in[0:rows, :] * patch_rows
    mask_sums[...] = jnp.zeros_like(mask_sums)
    mask_sums[0:1, :] = jnp.sum(upstream * mask_normal, axis=0, keepdims=True)
    mask_sums[1:2, :] = jnp.sum(upstream, axis=0, keepdims=True)
    upstream = upstream * mask_gain
    upstream = inverse * (upstream - class_mean(upstream) - mask_normal * class_mean(upstream * mask_normal))
    d_products = jnp.where(lane < CLS, upstream, 0.0).astype(jnp.bfloat16)
    class_part = matmul_tn(d_products, patch_unit)
    for p in range(4):
        class_sent[p] = class_part[few * p : few * (p + 1)].astype(jnp.bfloat16)
    class_back.start()
    upstream = matmul(d_products, classes[...])
    direct = patch_proj[...] * factor
    upstream = factor * (upstream - direct * jnp.sum(upstream * direct, axis=-1, keepdims=True))
    d_patch[...] = upstream.astype(jnp.bfloat16)
    d_residual[...] = matmul_nt(d_patch[...], whole(full_patch))

    def branch(i):
        value = d_residual[parts[i]].astype(jnp.bfloat16)
        for k in range(2):
            d_branch[k, parts[i]] = value
            branch_out[k][i].start()

    branch(1)

    weight_gradient(patch_parts[0], rounded, d_patch)
    patch_sum.begin()
    class_back.wait()
    upstream = class_sent[h].astype(jnp.float32)
    for number in range(3):
        upstream = upstream + class_got[number].astype(jnp.float32)
    d_class[...] = jnp.where(class_live, unit_back(class_proj[...], upstream), 0.0).astype(jnp.bfloat16)
    term = matmul_nt(d_class[...], whole(full_class))
    term_sent[...] = term.astype(jnp.bfloat16)
    for copy, (_, _, rel) in zip(term_back, plane):
        pl.when(h == rel)(copy.start)
    weight_gradient(class_parts[0], class_rows, d_class)
    class_sum.begin()

    def backward(k, at):
        for j in range(block // wide_step):
            weight = downs[k, j // 2, 2 * (j % 2) : 2 * (j % 2) + 2].reshape(wide_step, features)
            span = slice(j * wide_step, (j + 1) * wide_step)
            d_hidden[k, at, span] = (matmul_nt(d_branch[k, at], weight) * slope[k, at, span]).astype(jnp.bfloat16)


    def returned_rows(i):
        for k in range(2):
            branch_out[k][i].wait()
            backward(k, theirs[i])
            back_sent[k, parts[i]] = matmul_nt(d_hidden[k, theirs[i]], whole(ups.at[k])).astype(jnp.bfloat16)
            grad_back[k][i].start()

    for k in range(2):
        backward(k, parts[1])
    returned_rows(1)

    @pl.when(h == 0)
    def _():
        d_residual[0:few] = d_residual[0:few] + term_sent[...].astype(jnp.float32)
        for copy, (_, _, rel) in zip(term_back, plane):
            copy.wait_recv()
            at = slice(few * rel, few * rel + sizes[rel])
            d_residual[at] = d_residual[at] + term_got[rel - 1, 0 : sizes[rel]].astype(jnp.float32)

    branch(0)
    patch_sum.run_first()
    class_sum.run_first()
    for k in range(2):
        backward(k, parts[0])
    returned_rows(0)
    upstream = matmul_nt(d_hidden[0, here], whole(ups.at[0])) + matmul_nt(d_hidden[1, here], whole(ups.at[1]))
    patch_sum.run_second()
    class_sum.run_second()
    for k in range(2):
        for stage in grad_back[k]:
            stage.wait()
    upstream = upstream + (back_got[0].astype(jnp.float32) + back_got[1].astype(jnp.float32))
    upstream = upstream * gains_ref[1:2, :]
    value = normal_two[...]
    middle = jnp.mean(upstream, axis=-1, keepdims=True)
    along = jnp.mean(upstream * value, axis=-1, keepdims=True)
    d_second[...] = d_residual[...] + inverse_two[:, 0:1] * (upstream - middle - value * along)
    patch_sum.run_third()
    class_sum.run_third()
    d_mix[...] = d_second[...].astype(jnp.bfloat16)
    d_attended[...] = matmul_nt(d_mix[...], whole(full_out)).astype(jnp.bfloat16)
    patch_sum.line.relay()
    class_sum.line.relay()
    patch_sum.finish(g_patch)
    class_sum.finish(g_class)
    links.drain()


def front(live, tokens, norm_gains, grad_masks, mask_norm, shards, scaling):
    rows, features = tokens.shape
    vmem, hbm = pl.BlockSpec(memory_space=pltpu.VMEM), pl.BlockSpec(memory_space=pl.ANY)
    w_qkv, w_out, w_up, w_down, w_patch, w_class = shards
    wide = w_qkv.shape[1] // 4
    heads = wide // (3 * DH)
    block = w_up.shape[1] // 4
    lanes = 256
    few = -(-CLS // 64) * 16
    low, single = jnp.bfloat16, jnp.float32
    outs = [
        ((rows, features), low),
        ((3 * heads, 4 * rows, DH), low),
        ((heads, 1, 4 * rows), single),
        ((4, rows, features), low),
        ((8, features), single),
        ((2, 2, 4, 2, w_qkv.shape[0], wide), low),
        (grad_masks.shape, single),
        ((8, lanes), single),
        ((rows, features), single),
        ((rows, 128), single),
        ((2, 2 * rows, features), low),
        ((2, 2 * rows, block), low),
        ((2, 2 * rows, features), low),
        ((2, 2 * rows, block), low),
        ((rows, features), low),
        ((rows, features), single),
        ((rows, features), low),
        (w_patch.shape, single),
        (w_class.shape, single),
    ]
    scratch = [
        ((2, 2, 4, 2) + w_out.shape, low),
        ((2, 2, 2, 4, 2, w_up.shape[0], block), low),
        ((2, 2, 4) + w_down.shape, low),
        ((2, 2, 4, 2) + w_patch.shape, low),
        ((2, 2, 4, 2) + w_class.shape, low),
        ((2, 2, 4, 2, 8, 128), single),
        ((4 * rows, wide // 3), low),
        ((2, 2 * rows, block), single),
        ((rows, features), single),
        ((rows, features), single),
        ((rows, 128), single),
        ((rows, features), single),
        ((few, features), single),
        ((lanes, features), low),
        ((2, rows, features), low),
        ((2, rows, features), low),
        ((2, rows, features), low),
        ((2, rows, features), low),
        ((4, few, features), low),
        ((3, few, features), low),
        ((few, features), low),
        ((3, few, features), low),
        ((rows + 8, lanes), single),
        ((8, 128), single),
        (w_up.shape, low),
        ((rows, features), low),
        ((rows, features), low),
        ((few, features), low),
        ((few, features), low),
    ]
    for shape in (w_patch.shape, w_class.shape):
        for lead in ((2, 2, 4, 2), (2, 2, 4), (2, 4), (4,), (5,)):
            scratch.append((lead + shape, low))
    return pl.pallas_call(
        partial(front_kernel, scaling),
        out_shape=[jax.ShapeDtypeStruct(*out) for out in outs],
        in_specs=[pl.BlockSpec(memory_space=pltpu.SMEM)] + [vmem] * 4 + [hbm] * 2 + [vmem] + [hbm] * 3,
        out_specs=[vmem] * len(outs),
        scratch_shapes=[pltpu.VMEM(*shape) for shape in scratch]
        + [
            pltpu.SemaphoreType.DMA((FRONT_COPIES,)),
            pltpu.SemaphoreType.DMA((FRONT_COPIES,)),
            pltpu.SemaphoreType.DMA((9,)),
        ],
        compiler_params=pltpu.CompilerParams(
            collective_id=1, has_side_effects=True, vmem_limit_bytes=121 * 2**19
        ),
        name="front",
    )(live, tokens, norm_gains, grad_masks, mask_norm, *shards)


def rear_kernel(scaling, *refs):
    live_ref, d_rows, heads_ref, logsum, rows_ref, qkv, small_ref = refs[:7]
    normal_one, inverse_one, d_second, gains_ref = refs[7:11]
    refs = refs[:7] + refs[11:]
    normed_two, active, d_branch, d_hidden, attended, d_mix = refs[7:13]
    d_normed, g_qkv, g_up, g_down, g_out, small_out = refs[13:19]
    at = 19
    d_out, d_heads, d_spread, grad_keys, grad_values = refs[at : at + 5]
    d_sent, d_got, q_part, q_sib, q_z, q_plane = refs[at + 5 : at + 11]
    small_own, small_got, send_sem, recv_sem, local_sem = refs[at + 11 : at + 16]
    scratch = refs[at + 16 :]
    links = Links(send_sem, recv_sem)
    y, x, z, c = links.y, links.x, links.z, links.c
    h = y * 2 + x
    rows, features = d_rows.shape
    slot_rows = rows * 4
    narrow = d_out.shape[1]
    heads = narrow // DH
    wide = 3 * narrow
    plane = [(links.across, 3 - h, 3), (links.along_x, y * 2 + 1 - x, 1), (links.along_y, (1 - y) * 2 + x, 2)]

    def columns(start, size):
        return pl.ds(pl.multiple_of(start, 128), size)

    def block(p):
        return pl.ds(pl.multiple_of(p * rows, rows), rows)

    spread_out = Stage(
        links, [(d_rows.at[:, columns(p * narrow, narrow)], d_out.at[block(h), :], peer) for peer, p, _ in plane]
    )
    own = pltpu.make_async_copy(d_rows.at[:, columns(h * narrow, narrow)], d_out.at[block(h), :], local_sem.at[0])
    kinds = ("up_y", "up_x", "down", "all_x")
    sums = [
        Sum(links, *scratch[5 * i : 5 * i + 5], kinds[i]) for i in range(4)
    ]
    back = [Stage(links, [(d_sent.at[rel - 1], d_got.at[rel - 1], peer)]) for peer, _, rel in plane]
    q_core = Stage(links, [(q_part.at[:, :, :, 1 - c], q_sib, links.sibling)])
    q_line = LineSum(links, lambda at: q_part.at[:, :, at, c], q_z)
    q_across = Stage(
        links, [(q_part.at[p // 2, p % 2, z, c], q_plane.at[h], peer) for peer, p, _ in plane]
    )
    small_core = Stage(links, [(small_own.at[0], small_got.at[0], links.sibling)])
    small_x = Stage(links, [(small_own.at[1], small_got.at[1], links.along_x)])
    small_y = Stage(links, [(small_own.at[2], small_got.at[2], links.along_y)])
    small_z = Stage(links, [(small_own.at[3], small_got.at[3 + z], peer) for peer in links.along_z])

    links.greet()
    spread_out.start()
    own.start()
    small_own[0] = small_ref[...]
    small_core.start()
    parts = [scratch[5 * i] for i in range(4)]
    for k in range(2):
        weight_gradient(parts[k], normed_two.at[k], d_hidden.at[k])
        sums[k].begin()
    for k in range(2):
        weight_gradient(parts[2].at[k], active.at[k], d_branch.at[k])
    sums[2].begin()
    weight_gradient(parts[3], attended, d_mix)
    sums[3].begin()
    own.wait()
    spread_out.wait()
    live = live_ref[0]
    key_live = lax.broadcasted_iota(jnp.int32, (slot_rows, 1), 0) < live
    up_y, up_x, down, out = sums
    assert links.count <= REAR_COPIES

    def small_step(stage, number, following):
        def run():
            stage.wait()
            small_own[number + 1] = small_own[number] + small_got[number]
            if number == 2:
                small_got[3 + z] = small_own[3]
            following.start()

        return run

    def both(*steps):
        def run():
            for step in steps:
                step()

        return run

    events = {
        0: up_y.run_first,
        1: up_x.run_first,
        2: down.run_first,
        3: small_step(small_core, 0, small_x),
        6: out.run_first,
        7: small_step(small_x, 1, small_y),
        8: both(up_y.run_second, up_x.run_second),
        9: small_step(small_y, 2, small_z),
        11: both(up_y.line.relay, up_x.line.relay),
        13: down.run_second,
        15: both(up_y.run_last, up_x.run_last),
    }

    def tile_body(slot, carry):
        number, turn = slot // 4, slot % 4
        at_slots(slot, events)
        at = block(turn)

        @pl.when(turn == 0)
        def _():
            grad_keys[...] = jnp.zeros_like(grad_keys)
            grad_values[...] = jnp.zeros_like(grad_values)

        queries = heads_ref[3 * number, at, :]
        keys = heads_ref[3 * number + 1]
        values = heads_ref[3 * number + 2]
        grads = d_heads[number, at, :]
        scores = lax.dot_general(keys, queries, (((1,), (1,)), ((), ())), preferred_element_type=jnp.float32)
        powers = scores * (scaling * LOG2E) - logsum[number, :, at]
        weights = jnp.where(key_live, jnp.exp2(powers), 0.0)
        grad_values[...] += jnp.dot(weights.astype(jnp.bfloat16), grads, preferred_element_type=jnp.float32)
        grad_weights = lax.dot_general(
            values, grads, (((1,), (1,)), ((), ())), preferred_element_type=jnp.float32
        )
        deltas = jnp.sum(grad_weights * weights, axis=0, keepdims=True)
        grad_scores = (weights * (grad_weights - deltas)).astype(jnp.bfloat16)
        grad_keys[...] += jnp.dot(grad_scores, queries, preferred_element_type=jnp.float32)
        grad_queries = lax.dot_general(
            keys, grad_scores, (((0,), (0,)), ((), ())), preferred_element_type=jnp.float32
        )
        d_heads[4 + 3 * number, at, :] = (grad_queries.T * scaling).astype(jnp.bfloat16)

        @pl.when(turn == 3)
        def _():
            d_heads[5 + 3 * number] = (grad_keys[...] * scaling).astype(jnp.bfloat16)
            d_heads[6 + 3 * number] = grad_values[...].astype(jnp.bfloat16)

        return carry

    for number in range(heads):
        d_heads[number] = d_out[:, number * DH : (number + 1) * DH]
    lax.fori_loop(0, SLOTS, tile_body, 0)
    for number in range(3 * heads):
        d_spread[:, number * DH : (number + 1) * DH] = d_heads[4 + number]
    per = features // 4
    for j in range(4):
        left = jnp.concatenate([rows_ref[p, :, j * per : (j + 1) * per] for p in range(4)], axis=0)
        piece = lax.dot_general(
            left, d_spread[...], (((0,), (0,)), ((), ())), preferred_element_type=jnp.float32
        ).astype(jnp.bfloat16)
        q_part[j // 2, j % 2] = piece.reshape(4, 2, per // 8, wide)
    q_core.start()
    weight = qkv[...].reshape(features, wide)
    for (_, p, rel), stage in zip(plane, back):
        piece = lax.dot_general(
            d_spread[block(p), :], weight, (((1,), (1,)), ((), ())), preferred_element_type=jnp.float32
        )
        d_sent[rel - 1] = piece.astype(jnp.bfloat16)
        stage.start()
    q_core.wait()

    def add_sib(i, carry):
        index = (i // 8, i // 4 % 2, i % 4)
        q_part[(*index, c)] = q_part[(*index, c)] + q_sib[index]
        return carry

    lax.fori_loop(0, 16, add_sib, 0)
    q_line.start()
    d_normed[...] = lax.dot_general(
        d_spread[block(h), :], weight, (((1,), (1,)), ((), ())), preferred_element_type=jnp.float32
    )
    down.line.relay()
    q_line.relay()
    out.run_second()
    out.run_third()

    def add_line(slot):
        for i in range(4):
            index = (i // 2, i % 2)
            q_part[(*index, z, c)] = q_part[(*index, z, c)] + q_z[(slot, *index)]

    q_line.collect(add_line)
    q_across.start()
    out.line.relay()
    small_z.wait()
    small_out[...] = (small_got[3] + small_got[4] + small_got[5] + small_got[6])[0:2, 0:CLS]
    down.finish(g_down)
    up_y.finish(g_up)
    up_x.finish(g_up)
    out.finish(g_out)
    q_across.wait()
    g_qkv[:, columns(h * wide, wide)] = q_part[y, x, z, c].astype(jnp.float32)
    for _, p, _ in plane:
        g_qkv[:, columns(p * wide, wide)] = q_plane[p].astype(jnp.float32)
    for stage in back:
        stage.wait()
    upstream = d_normed[...] + (
        d_got[0].astype(jnp.float32) + d_got[1].astype(jnp.float32) + d_got[2].astype(jnp.float32)
    )
    upstream = upstream * gains_ref[0:1, :]
    value = normal_one[...]
    middle = jnp.mean(upstream, axis=-1, keepdims=True)
    along = jnp.mean(upstream * value, axis=-1, keepdims=True)
    d_normed[...] = d_second[...] + inverse_one[:, 0:1] * (upstream - middle - value * along)
    links.drain()


def rear(live, d_rows, heads_qkv, logsum, rows_all, qkv, small, ending, factors, scaling):
    rows, features = d_rows.shape
    slot_rows = 4 * rows
    narrow = features // 4
    heads = narrow // DH
    wide = 3 * narrow
    vmem, hbm = pl.BlockSpec(memory_space=pltpu.VMEM), pl.BlockSpec(memory_space=pl.ANY)
    low = jnp.bfloat16
    up, down = (features // 32, features), (features // 8, features)
    shard = (features // 32, wide)
    buffers = []
    for _ in range(2):
        buffers += [(2, 2, 4, 2) + up, (2, 2, 4) + up, (2, 4) + up, up, (5, 2) + up]
    buffers += [(2, 2, 4) + down, (2, 4) + down, (4,) + down, (8, 128), (5,) + down]
    buffers += [(2, 2, 4, 2) + up, (2, 2, 4) + up, (2, 4) + up, (4,) + up, (5,) + up]
    single = jnp.float32
    return pl.pallas_call(
        partial(rear_kernel, scaling),
        out_shape=[
            jax.ShapeDtypeStruct((rows, features), single),
            jax.ShapeDtypeStruct((features // 32, 4 * wide), single),
            jax.ShapeDtypeStruct((up[0], 4 * up[1]), single),
            jax.ShapeDtypeStruct(down, single),
        ]
        + [jax.ShapeDtypeStruct(up, single)]
        + [jax.ShapeDtypeStruct((2, CLS), single)],
        in_specs=[pl.BlockSpec(memory_space=pltpu.SMEM)] + [vmem] * 16,
        out_specs=[vmem] * 6,
        scratch_shapes=[
            pltpu.VMEM((slot_rows, narrow), low),
            pltpu.VMEM((4 * heads, slot_rows, DH), low),
            pltpu.VMEM((slot_rows, wide), low),
            pltpu.VMEM((slot_rows, DH), single),
            pltpu.VMEM((slot_rows, DH), single),
            pltpu.VMEM((3, rows, features), low),
            pltpu.VMEM((3, rows, features), low),
            pltpu.VMEM((2, 2, 4, 2) + shard, low),
            pltpu.VMEM((2, 2, 4) + shard, low),
            pltpu.VMEM((5, 2, 2) + shard, low),
            pltpu.VMEM((4,) + shard, low),
            pltpu.VMEM((4,) + small.shape, single),
            pltpu.VMEM((7,) + small.shape, single),
            pltpu.SemaphoreType.DMA((REAR_COPIES,)),
            pltpu.SemaphoreType.DMA((REAR_COPIES,)),
            pltpu.SemaphoreType.DMA((7,)),
        ]
        + [pltpu.VMEM(shape, low) for shape in buffers],
        compiler_params=pltpu.CompilerParams(
            collective_id=2, has_side_effects=True, vmem_limit_bytes=121 * 2**19
        ),
        name="rear",
    )(live, d_rows, heads_qkv, logsum, rows_all, qkv, small, *ending, *factors)


def ending_kernel(*refs):
    count = (len(refs) - 6) // 2
    results, (w_qkv, w_up, gains) = refs[:count], refs[count : count + 3]
    outs, gain_out, gain_sums, sems = refs[count + 3 : 2 * count + 3], *refs[2 * count + 3 :]
    copies = [pltpu.make_async_copy(results[i], outs[i], sems.at[i]) for i in range(count)]
    for copy in copies:
        copy.start()
    for number, (weight, grad) in enumerate(((w_qkv, results[2]), (w_up, results[4]))):
        total = jnp.sum(weight[...].astype(jnp.float32) * grad[...], axis=1, keepdims=True)
        total = jnp.broadcast_to(total, (total.shape[0], 128)).T[0:1, :]
        gain_sums[number : number + 1, :] = total / gains[number : number + 1, :].astype(jnp.float32)
    last = pltpu.make_async_copy(gain_sums, gain_out, sems.at[count])
    last.start()
    for copy in copies:
        copy.wait()
    last.wait()


def ending_copies(results, w_qkv, w_up, gains):
    vmem, hbm = pl.BlockSpec(memory_space=pltpu.VMEM), pl.BlockSpec(memory_space=pl.ANY)
    count = len(results)
    shapes = [jax.ShapeDtypeStruct(a.shape, a.dtype) for a in results]
    return pl.pallas_call(
        ending_kernel,
        out_shape=shapes + [jax.ShapeDtypeStruct(gains.shape, jnp.float32)],
        in_specs=[vmem] * (count + 3),
        out_specs=[hbm] * (count + 1),
        scratch_shapes=[pltpu.VMEM(gains.shape, jnp.float32), pltpu.SemaphoreType.DMA((count + 1,))],
        name="ending",
    )(*results, w_qkv, w_up, gains)


def body_planned(
    tokens,
    patch_counts,
    w_qkv,
    w_out,
    w_up,
    w_down,
    w_patch,
    w_class,
    norm_gains,
    mask_norm,
    grad_masks,
):
    low = jnp.bfloat16
    h, s = lax.axis_index("head"), lax.axis_index("seq")
    tokens, grad_masks = tokens[0], grad_masks[0]
    row_count = tokens.shape[0]
    live = CLS + patch_counts
    scaling = DH ** (-0.5)

    outs = front(
        live,
        tokens,
        norm_gains,
        grad_masks,
        mask_norm,
        (w_qkv, w_out, w_up, w_down, w_patch, w_class),
        scaling,
    )
    attended, heads_qkv, logsum, rows_all, gains, qkv, class_masks, mask_sums = outs[:8]
    normal_one, inverse_one, normed_two, active, d_branch, d_hidden = outs[8:14]
    d_mix, d_second, d_attended, g_patch, g_class = outs[14:]
    factors = (normed_two, active, d_branch, d_hidden, attended, d_mix)
    ending = (normal_one, inverse_one, d_second, gains)
    grad_inputs, g_qkv, g_up, g_down, g_out, sums = rear(
        live, d_attended, heads_qkv, logsum, rows_all, qkv, mask_sums, ending, factors, scaling
    )
    results = ending_copies(
        (class_masks, grad_inputs, g_qkv, g_out, g_up, g_down, g_patch, g_class, sums), w_qkv, w_up, norm_gains
    )
    return (results[0][None], results[1][None], *results[2:8], results[9], results[8])


def solution(mesh):
    planned = dict(mesh.shape) == {"head": 4, "seq": 8}
    return jax.shard_map(
        body_planned if planned else body_general,
        mesh=mesh,
        in_specs=(
            P("seq", "head", None),
            P("seq"),
            P(("head", "seq"), None),
            P(("head", "seq"), None),
            P(("head", "seq"), None),
            P(("head", "seq"), None),
            P(("head", "seq"), None),
            P(("head", "seq"), None),
            P(None, ("head", "seq")),
            P(),
            P("seq", "head", None),
        ),
        out_specs=(
            P("seq", "head", None),
            P("seq", "head", None),
            P(("head", "seq"), None),
            P(("head", "seq"), None),
            P(("head", "seq"), None),
            P(("head", "seq"), None),
            P(("head", "seq"), None),
            P(("head", "seq"), None),
            P(None, ("head", "seq")),
            P(),
        ),
        check_vma=False,
    )
```

```python
from functools import partial

import jax
import jax.numpy as jnp
from jax import lax
from jax.experimental import pallas as pl
from jax.experimental.pallas import tpu as pltpu
from jax.sharding import PartitionSpec as P

HEADS = 16
DH = 64
CLS = 150


def spread_2(value, axis, source):
    kept = jnp.where(lax.axis_index(axis) == source, value, 0).astype(value.dtype)
    return lax.psum(kept, axis)


def standardize(values):
    center = values - jnp.mean(values, axis=-1, keepdims=True)
    inverse = lax.rsqrt(jnp.mean(center * center, axis=-1, keepdims=True) + 1e-05)
    return (center * inverse, inverse)


def standard_back(normal, inverse, upstream):
    middle = jnp.mean(upstream, axis=-1, keepdims=True)
    along = jnp.mean(upstream * normal, axis=-1, keepdims=True)
    return inverse * (upstream - middle - normal * along)


def unit_scale(values):
    return lax.rsqrt(jnp.sum(values * values, axis=-1, keepdims=True) + 1e-06)


def unit_back(values, upstream):
    factor = unit_scale(values)
    direct = values * factor
    return factor * (upstream - direct * jnp.sum(upstream * direct, axis=-1, keepdims=True))


def block_scores(query_block, key_rows, key_live, scaling):
    scores = (
        jnp.einsum("qd,kd->qk", query_block, key_rows, preferred_element_type=jnp.float32) * scaling
    )
    return jnp.where(key_live, scores, -1e30)


def attend_head(queries, key_rows, values, key_live, scaling, blocks):
    head_width = queries.shape[-1]

    def single(query_block):
        scores = block_scores(query_block, key_rows, key_live, scaling)
        highest = jnp.max(scores, axis=-1, keepdims=True)
        weights_raw = jnp.exp(scores - highest)
        totals = jnp.sum(weights_raw, axis=-1, keepdims=True)
        weights = (weights_raw / totals).astype(jnp.bfloat16)
        output = jnp.einsum("qk,kd->qd", weights, values, preferred_element_type=jnp.float32)
        return (output.astype(jnp.bfloat16), (highest + jnp.log(totals))[:, 0])

    outputs, logsum = lax.map(single, queries.reshape(blocks, -1, head_width))
    return (outputs.reshape(-1, head_width), logsum.reshape(-1))


def attend_back(queries, key_rows, values, grad_out, logsum, key_live, scaling, blocks):
    head_width = queries.shape[-1]

    def single(running, pieces):
        grad_keys, grad_values = running
        query_block, grad_block, logsum_block = pieces
        scores = block_scores(query_block, key_rows, key_live, scaling)
        weights = jnp.exp(scores - logsum_block[:, None])
        grad_values = grad_values + jnp.einsum(
            "qk,qd->kd",
            weights.astype(jnp.bfloat16),
            grad_block,
            preferred_element_type=jnp.float32,
        )
        grad_weights = jnp.einsum(
            "qd,kd->qk", grad_block, values, preferred_element_type=jnp.float32
        )
        deltas = jnp.sum(grad_weights * weights, axis=-1, keepdims=True)
        grad_scores = (weights * (grad_weights - deltas)).astype(jnp.bfloat16)
        grad_query = (
            jnp.einsum("qk,kd->qd", grad_scores, key_rows, preferred_element_type=jnp.float32)
            * scaling
        )
        grad_keys = (
            grad_keys
            + jnp.einsum("qk,qd->kd", grad_scores, query_block, preferred_element_type=jnp.float32)
            * scaling
        )
        return ((grad_keys, grad_values), grad_query)

    zero_state = jnp.zeros(key_rows.shape, jnp.float32)
    pieces = (
        queries.reshape(blocks, -1, head_width),
        grad_out.reshape(blocks, -1, head_width),
        logsum.reshape(blocks, -1),
    )
    (grad_keys, grad_values), grad_queries = lax.scan(single, (zero_state, zero_state), pieces)
    return (grad_queries.reshape(-1, head_width), grad_keys, grad_values)


def body_general(
    tokens,
    patch_counts,
    w_qkv,
    w_out,
    w_up,
    w_down,
    w_patch,
    w_class,
    norm_gains,
    mask_norm,
    grad_masks,
):
    gains_rows = norm_gains.T
    gathered = (
        lax.all_gather(w_qkv, ("head", "seq"), axis=0, tiled=True),
        lax.all_gather(w_out, ("head", "seq"), axis=0, tiled=True),
        lax.all_gather(w_up, ("head", "seq"), axis=0, tiled=True),
        lax.all_gather(w_down, ("head", "seq"), axis=0, tiled=True),
        lax.all_gather(w_patch, ("head", "seq"), axis=0, tiled=True),
        lax.all_gather(w_class, ("head", "seq"), axis=0, tiled=True),
        lax.all_gather(gains_rows, ("head", "seq"), axis=0, tiled=True),
    )
    full_qkv, full_out, full_up, full_down, full_patch, full_class, full_gains = gathered
    gain_one = full_gains[:, 0].astype(jnp.float32)
    gain_two = full_gains[:, 1].astype(jnp.float32)
    image_count = tokens.shape[0]
    row_count = tokens.shape[1]
    groups = lax.axis_size("head")
    slot_rows = row_count * groups
    local_heads = HEADS // groups
    position = lax.axis_index("head") * row_count + jnp.arange(row_count, dtype=jnp.int32)
    live_limit = CLS + patch_counts
    patch_rows = ((position[None, :] >= CLS) & (position[None, :] < live_limit[:, None])).astype(
        jnp.float32
    )[:, :, None]
    key_live = (jnp.arange(slot_rows, dtype=jnp.int32)[None, :] < live_limit[:, None])[:, None, :]
    root_flag = (lax.axis_index("head") == 0).astype(jnp.float32)
    scaling = DH ** (-0.5)
    blocks = slot_rows // 512
    normal_one, inverse_one = standardize(tokens)
    normed_one = (normal_one * gain_one).astype(jnp.bfloat16)
    triple = jnp.einsum(
        "ird,dt->irt", normed_one, full_qkv, preferred_element_type=jnp.float32
    ).astype(jnp.bfloat16)
    spread = lax.all_to_all(triple, "head", split_axis=2, concat_axis=1, tiled=True).reshape(
        image_count, slot_rows, local_heads, 3, DH
    )
    image = 0
    outputs = []
    image_logsums = []
    for number in range(local_heads):
        output, logsum = attend_head(
            spread[image, :, number, 0],
            spread[image, :, number, 1],
            spread[image, :, number, 2],
            key_live[image],
            scaling,
            blocks,
        )
        outputs.append(output)
        image_logsums.append(logsum)
    image_outputs = [jnp.stack(outputs, axis=1).reshape(slot_rows, local_heads * DH)]
    logsums = [image_logsums]
    attended_heads = jnp.stack(image_outputs, axis=0)
    attended = lax.all_to_all(attended_heads, "head", split_axis=1, concat_axis=2, tiled=True)
    second = tokens + jnp.einsum(
        "ire,ed->ird", attended, full_out, preferred_element_type=jnp.float32
    )
    normal_two, inverse_two = standardize(second)
    normed_two = (normal_two * gain_two).astype(jnp.bfloat16)
    hidden = jnp.einsum("ird,df->irf", normed_two, full_up, preferred_element_type=jnp.float32)
    gelu_exact = partial(jax.nn.gelu, approximate=False)
    active = gelu_exact(hidden).astype(jnp.bfloat16)
    residual = second + jnp.einsum(
        "irf,fd->ird", active, full_down, preferred_element_type=jnp.float32
    )
    rounded = residual.astype(jnp.bfloat16)
    patch_proj = jnp.einsum("ird,de->ire", rounded, full_patch, preferred_element_type=jnp.float32)
    patch_unit = (patch_proj * unit_scale(patch_proj)).astype(jnp.bfloat16)
    class_proj = jnp.einsum(
        "ird,de->ire", rounded[:, :CLS], full_class, preferred_element_type=jnp.float32
    )
    class_unit = (class_proj * unit_scale(class_proj)).astype(jnp.bfloat16)
    classes = spread_2(class_unit, "head", 0)
    products = jnp.einsum("ird,icd->irc", patch_unit, classes, preferred_element_type=jnp.float32)
    normal_mask, inverse_mask = standardize(products)
    class_masks = (normal_mask * mask_norm[0] + mask_norm[1]) * patch_rows
    upstream = grad_masks * patch_rows
    norm_grads = lax.psum(
        jnp.stack([jnp.sum(upstream * normal_mask, axis=(0, 1)), jnp.sum(upstream, axis=(0, 1))]),
        ("head", "seq"),
    )
    d_products = standard_back(normal_mask, inverse_mask, upstream * mask_norm[0]).astype(
        jnp.bfloat16
    )
    d_patch_unit = jnp.einsum(
        "irc,icd->ird", d_products, classes, preferred_element_type=jnp.float32
    )
    class_part = jnp.einsum(
        "irc,ird->icd", d_products, patch_unit, preferred_element_type=jnp.float32
    )
    d_class_unit = lax.psum(class_part.astype(jnp.bfloat16), "head").astype(jnp.float32)
    d_patch_proj = unit_back(patch_proj, d_patch_unit).astype(jnp.bfloat16)
    d_class_proj = (unit_back(class_proj, d_class_unit) * root_flag).astype(jnp.bfloat16)
    regathered = (
        lax.all_gather(w_qkv, ("head", "seq"), axis=0, tiled=True),
        lax.all_gather(w_out, ("head", "seq"), axis=0, tiled=True),
        lax.all_gather(w_up, ("head", "seq"), axis=0, tiled=True),
        lax.all_gather(w_down, ("head", "seq"), axis=0, tiled=True),
        lax.all_gather(w_patch, ("head", "seq"), axis=0, tiled=True),
        lax.all_gather(w_class, ("head", "seq"), axis=0, tiled=True),
        lax.all_gather(gains_rows, ("head", "seq"), axis=0, tiled=True),
    )
    back_qkv, back_out, back_up, back_down, back_patch, back_class, back_gains = regathered
    back_one = back_gains[:, 0].astype(jnp.float32)
    back_two = back_gains[:, 1].astype(jnp.float32)
    grad_patch = jnp.einsum(
        "ird,ire->de", rounded, d_patch_proj, preferred_element_type=jnp.float32
    )
    grad_class = jnp.einsum(
        "ird,ire->de", rounded[:, :CLS], d_class_proj, preferred_element_type=jnp.float32
    )
    d_residual = jnp.einsum(
        "ire,de->ird", d_patch_proj, back_patch, preferred_element_type=jnp.float32
    )
    class_term = jnp.einsum(
        "ire,de->ird", d_class_proj, back_class, preferred_element_type=jnp.float32
    )
    d_residual = d_residual.at[:, :CLS].add(class_term)
    d_branch = d_residual.astype(jnp.bfloat16)
    grad_down = jnp.einsum("irf,ird->fd", active, d_branch, preferred_element_type=jnp.float32)
    d_active = jnp.einsum("ird,fd->irf", d_branch, back_down, preferred_element_type=jnp.float32)
    gelu_pull = jax.vjp(gelu_exact, hidden)[1]
    d_hidden = gelu_pull(d_active)[0].astype(jnp.bfloat16)
    grad_up = jnp.einsum("ird,irf->df", normed_two, d_hidden, preferred_element_type=jnp.float32)
    d_normed_two = jnp.einsum("irf,df->ird", d_hidden, back_up, preferred_element_type=jnp.float32)
    d_second = d_residual + standard_back(normal_two, inverse_two, d_normed_two * back_two)
    grad_gain_two = jnp.sum(d_normed_two * normal_two, axis=(0, 1))
    d_mix = d_second.astype(jnp.bfloat16)
    grad_out = jnp.einsum("ire,ird->ed", attended, d_mix, preferred_element_type=jnp.float32)
    d_attended = jnp.einsum(
        "ird,ed->ire", d_mix, back_out, preferred_element_type=jnp.float32
    ).astype(jnp.bfloat16)
    d_heads = lax.all_to_all(d_attended, "head", split_axis=2, concat_axis=1, tiled=True).reshape(
        image_count, slot_rows, local_heads, DH
    )
    image = 0
    head_grads = []
    for number in range(local_heads):
        grad_queries, grad_keys, grad_values = attend_back(
            spread[image, :, number, 0],
            spread[image, :, number, 1],
            spread[image, :, number, 2],
            d_heads[image, :, number],
            logsums[image][number],
            key_live[image],
            scaling,
            blocks,
        )
        head_grads.append(jnp.stack([grad_queries, grad_keys, grad_values], axis=1))
    image_grads = [jnp.stack(head_grads, axis=1).reshape(slot_rows, local_heads * 3 * DH)]
    d_spread = jnp.stack(image_grads, axis=0).astype(jnp.bfloat16)
    d_triple = lax.all_to_all(d_spread, "head", split_axis=1, concat_axis=2, tiled=True)
    grad_qkv = jnp.einsum("ird,irt->dt", normed_one, d_triple, preferred_element_type=jnp.float32)
    d_normed_one = jnp.einsum("irt,dt->ird", d_triple, back_qkv, preferred_element_type=jnp.float32)
    grad_inputs = d_second + standard_back(normal_one, inverse_one, d_normed_one * back_one)
    grad_gain_one = jnp.sum(d_normed_one * normal_one, axis=(0, 1))
    grad_gains = jnp.stack([grad_gain_one, grad_gain_two], axis=1)
    reduced = (
        lax.psum_scatter(grad_qkv, ("head", "seq"), scatter_dimension=0, tiled=True),
        lax.psum_scatter(grad_out, ("head", "seq"), scatter_dimension=0, tiled=True),
        lax.psum_scatter(grad_up, ("head", "seq"), scatter_dimension=0, tiled=True),
        lax.psum_scatter(grad_down, ("head", "seq"), scatter_dimension=0, tiled=True),
        lax.psum_scatter(grad_patch, ("head", "seq"), scatter_dimension=0, tiled=True),
        lax.psum_scatter(grad_class, ("head", "seq"), scatter_dimension=0, tiled=True),
        lax.psum_scatter(grad_gains, ("head", "seq"), scatter_dimension=0, tiled=True),
    )
    return (
        class_masks,
        grad_inputs,
        reduced[0],
        reduced[1],
        reduced[2],
        reduced[3],
        reduced[4],
        reduced[5],
        reduced[6].T,
        norm_grads,
    )


MESH = pl.DeviceIdType.MESH
LOG2E = 1.4426950408889634
SLOTS = 16
FRONT_COPIES = 160
REAR_COPIES = 88


def matmul(left, right):
    return jnp.dot(left, right, preferred_element_type=jnp.float32)


def matmul_nt(left, right):
    return lax.dot_general(left, right, (((1,), (1,)), ((), ())), preferred_element_type=jnp.float32)


def matmul_tn(left, right):
    return lax.dot_general(left, right, (((0,), (0,)), ((), ())), preferred_element_type=jnp.float32)


def norm(values):
    center = values - jnp.mean(values, axis=-1, keepdims=True)
    inverse = lax.rsqrt(jnp.mean(center * center, axis=-1, keepdims=True) + 1e-05)
    return center * inverse, inverse


def device(y, x, z, c):
    return (y * 2 + x, z * 2 + c)


class Links:
    def __init__(self, send_sem, recv_sem):
        head, seq = lax.axis_index("head"), lax.axis_index("seq")
        self.y, self.x, self.z, self.c = head // 2, head % 2, seq // 2, seq % 2
        y, x, z, c = self.y, self.x, self.z, self.c
        self.sibling = device(y, x, z, 1 - c)
        self.along_x = device(y, 1 - x, z, c)
        self.along_y = device(1 - y, x, z, c)
        self.across = device(1 - y, 1 - x, z, c)
        self.along_z = [device(y, x, (z + k) % 4, c) for k in (1, 2, 3)]
        self.send_sem, self.recv_sem, self.count, self.made, self.lines = send_sem, recv_sem, 0, [], []

    def greet(self):
        barrier = pltpu.get_barrier_semaphore()
        peers = [self.sibling, self.along_x, self.along_y, self.across] + self.along_z
        for peer in peers:
            pl.semaphore_signal(barrier, inc=1, device_id=peer, device_id_type=MESH)
        pl.semaphore_wait(barrier, len(peers))

    def plan(self, source, target, peer, sends=None, again=False):
        number = self.count - again
        self.count = number + 1
        copy = pltpu.make_async_remote_copy(
            src_ref=source,
            dst_ref=target,
            send_sem=self.send_sem.at[number],
            recv_sem=self.recv_sem.at[number],
            device_id=peer,
            device_id_type=MESH,
        )
        if not again:
            self.made.append((copy, sends))
        return copy

    def drain(self):
        for copy, sends in self.made:
            if sends is None:
                copy.wait_send()
            else:
                pl.when(sends)(copy.wait_send)
        for line in self.lines:
            line.drain()


class Stage:
    def __init__(self, links, moves, again=False):
        self.copies = [links.plan(*move, again=again) for move in moves]

    def start(self):
        for copy in self.copies:
            copy.start()

    def wait(self):
        for copy in self.copies:
            copy.wait_recv()


class Line:
    def __init__(self, links, piece, source=None):
        self.links, self.piece = links, piece
        self.source = piece(links.z) if source is None else source
        self.base = links.count
        links.count += 5
        links.lines.append(self)

    def copy(self, source, target, sent, landed):
        links = self.links
        return pltpu.make_async_remote_copy(
            src_ref=source,
            dst_ref=self.piece(landed),
            send_sem=links.send_sem.at[self.base + sent],
            recv_sem=links.recv_sem.at[self.base + landed],
            device_id=device(links.y, links.x, target, links.c),
            device_id_type=MESH,
        )

    def direct(self, target):
        z = self.links.z
        return (z != target) if target in (1, 2) else (z != target) & (z != 3 - target)

    def start(self):
        for target in (1, 2, 0, 3):

            @pl.when(self.direct(target))
            def _(target=target):
                self.copy(self.source, target, target, self.links.z).start()

    def relay(self):
        for at, end in ((2, 0), (1, 3)):

            @pl.when(self.links.z == at)
            def _(end=end):
                self.copy(self.source, 3 - end, 4, end).wait_recv()
                self.copy(self.piece(end), 3 - end, 4, end).start()

    def wait(self):
        z = self.links.z
        for origin in range(4):
            pending = z != origin
            if origin in (0, 3):
                pending = pending & (z != (2 if origin == 0 else 1))

            @pl.when(pending)
            def _(origin=origin):
                self.copy(self.source, 0, 0, origin).wait_recv()

    def drain(self):
        for target in range(4):

            @pl.when(self.direct(target))
            def _(target=target):
                self.copy(self.source, target, target, self.links.z).wait_send()

        @pl.when((self.links.z == 1) | (self.links.z == 2))
        def _():
            self.copy(self.source, 0, 4, 0).wait_send()


def at_slots(slot, events):
    for number, event in events.items():
        pl.when(slot == number)(event)


def weight_gradient(target, left, right):
    per = left.shape[1] // 4
    for j in range(4):
        piece = matmul_tn(left[:, j * per : (j + 1) * per], right[...]).astype(jnp.bfloat16)
        if len(target.shape) == 6:
            target[j // 2, j % 2] = piece.reshape(target.shape[2:])
        else:
            pair = target.shape[1] // 2
            at = (j % 2) * pair
            target[j // 2, at : at + pair] = piece.reshape((pair,) + target.shape[2:])


class LineSum:
    def __init__(self, links, piece, got):
        self.links, self.piece, self.got = links, piece, got
        self.base = links.count
        links.count += 4
        links.lines.append(self)

    def copy(self, piece, target, slot, sent):
        links = self.links
        return pltpu.make_async_remote_copy(
            src_ref=self.piece(piece),
            dst_ref=self.got.at[slot],
            send_sem=links.send_sem.at[self.base + sent],
            recv_sem=links.recv_sem.at[self.base + slot],
            device_id=device(links.y, links.x, target, links.c),
            device_id_type=MESH,
        )

    def start(self):
        z = self.links.z
        for target, end, middle in ((3, 0, 1), (0, 3, 2)):

            @pl.when(z == end)
            def _(target=target, middle=middle):
                self.copy(target, middle, middle, target).start()

        for target in range(4):
            direct = z != target
            if target in (0, 3):
                direct = z == (1 if target == 0 else 2)

            @pl.when(direct)
            def _(target=target):
                self.copy(target, target, z, target).start()

    def relay(self):
        z = self.links.z
        for target, middle in ((3, 1), (0, 2)):

            @pl.when(z == middle)
            def _(target=target, middle=middle):
                self.copy(target, target, middle, target).wait_recv()
                own = self.piece(target)
                own[...] = own[...] + self.got[middle]
                self.copy(target, target, middle, target).start()

    def collect(self, add):
        z = self.links.z
        for origin in range(4):
            comes = z != origin
            if origin in (0, 3):
                comes = comes & (z != 3 - origin)

            @pl.when(comes)
            def _(origin=origin):
                self.copy(0, 0, origin, 0).wait_recv()
                add(origin)

    def drain(self):
        for target in range(4):

            @pl.when(self.links.z != target)
            def _(target=target):
                self.copy(target, target, 0, target).wait_send()


class Sum:
    def __init__(self, links, partial_ref, sib, one, two, three, kind):
        y, x, z, c = links.y, links.x, links.z, links.c
        self.links, self.sib, self.one, self.two, self.three = links, sib, one, two, three
        self.kind = kind
        self.q = y * (1 - c) + x * c
        lead = () if kind == "down" else (slice(None),) * 3
        total = self.total = partial_ref.at[(*lead, c)]
        self.core = Stage(links, [(partial_ref.at[(*lead, 1 - c)], sib, links.sibling)])
        if kind in ("up_y", "all_y"):
            self.first = Stage(links, [(total.at[1 - y], one, links.along_y)])
            self.kept = lambda i, j: (y, i, j)
        elif kind in ("up_x", "all_x"):
            self.first = Stage(links, [(total.at[:, 1 - x], one, links.along_x)])
            self.kept = lambda i, j: (i, x, j)
        else:
            turned = device(y + (1 - c) * (1 - 2 * y), x + c * (1 - 2 * x), z, c)
            self.first = Stage(links, [(total.at[1 - self.q], one, turned)])
            self.line = LineSum(links, lambda at: total.at[self.q, at], three)
        if kind == "up_y":
            self.line = LineSum(links, lambda at: total.at[y, :, at], three)
            self.last = Stage(links, [(total.at[y, 1 - x, z], two, links.along_x)])
        elif kind == "up_x":
            self.line = LineSum(links, lambda at: total.at[:, x, at], three)
            self.last = Stage(links, [(total.at[1 - y, x, z], two, links.along_y)])
        elif kind == "all_x":
            self.second = Stage(links, [(total.at[1 - y, x], two, links.along_y)])
        elif kind == "all_y":
            self.second = Stage(links, [(total.at[y, 1 - x], two, links.along_x)])
        if kind in ("all_x", "all_y") and three is not None:
            self.line = LineSum(links, lambda at: total.at[y, x, at], three)

    def begin(self):
        self.core.start()

    def add(self, pairs, count):
        total = self.total

        def body(i, carry):
            index, extra = pairs(i)
            total[index] = total[index] + extra
            return carry

        lax.fori_loop(0, count, body, 0)

    def run_first(self):
        self.core.wait()
        sib = self.sib
        if self.kind == "down":
            self.add(lambda i: ((i // 4, i % 4), sib[i // 4, i % 4]), 8)
        else:
            self.add(lambda i: ((i // 8, i // 4 % 2, i % 4), sib[i // 8, i // 4 % 2, i % 4]), 16)
        self.first.start()

    def run_second(self):
        self.first.wait()
        one = self.one
        if self.kind == "down":
            self.add(lambda i: ((self.q, i), one[i]), 4)
        else:
            self.add(lambda i: (self.kept(i // 4, i % 4), one[i // 4, i % 4]), 8)
        if self.kind in ("all_x", "all_y"):
            self.second.start()
        else:
            self.line.start()

    def run_third(self):
        self.second.wait()
        y, x, two = self.links.y, self.links.x, self.two
        self.add(lambda i: ((y, x, i), two[i]), 4)
        self.line.start()

    def hand_over(self, out):
        self.second.wait()
        y, x = self.links.y, self.links.x
        for i in range(4):
            out[i] = self.total[y, x, i] + self.two[i]

    def run_last(self):
        z, total, got = self.links.z, self.total, self.three

        def add(slot):
            for i in range(2):
                index = self.kept(i, z)
                total[index] = total[index] + got[slot, i]

        self.line.collect(add)
        self.last.start()

    def finish(self, out):
        y, x, z = self.links.y, self.links.x, self.links.z
        if self.kind in ("up_y", "up_x"):
            self.last.wait()
            along_x = self.kind == "up_y"
            mine = x if along_x else y
            for number, part in ((mine, self.total[y, x, z]), (1 - mine, self.two[...])):
                for j in range(8):
                    place = (j // 4 * 2 + number) if along_x else (number * 2 + j // 4)
                    start = (place * 4 + j % 4) * 256 + (0 if along_x else 128)
                    at = pl.ds(pl.multiple_of(start, 128), 128)
                    out[:, at] = part[:, j * 128 : (j + 1) * 128].astype(jnp.float32)
            return
        out[...] = (self.total[self.q, z] if self.kind == "down" else self.total[y, x, z]).astype(jnp.float32)

        def add(slot):
            out[...] = out[...] + self.three[slot].astype(jnp.float32)

        self.line.collect(add)


def front_kernel(scaling, *refs):
    live_ref, tokens, norm_gains, grad_masks, mask_norm = refs[:5]
    qkv_shard, out_shard, up_given, down_shard, patch_shard, class_shard = refs[5:11]
    attended, heads_ref, logsum, rows_ref, gains_ref, qkv, class_masks, mask_sums = refs[11:19]
    normal_one, inverse_one, normed_two, active, d_branch, d_hidden = refs[19:25]
    d_mix, d_second, d_attended, g_patch, g_class = refs[25:30]
    refs = refs[30:]
    full_out, ups, downs, full_patch, full_class, tiles, staged = refs[:7]
    slope, stream, normal_two, inverse_two, patch_proj, class_proj, classes = refs[7:14]
    part_sent, part_got, back_sent, back_got, class_sent, class_got = refs[14:20]
    term_sent, term_got, mask_in, tile, up_shard = refs[20:25]
    rounded, d_patch, class_rows, d_class = refs[25:29]
    patch_parts, class_parts = refs[29:33], refs[33:37]
    send_sem, recv_sem, local_sem = refs[37:]
    second = residual = d_residual = stream
    links = Links(send_sem, recv_sem)
    y, x, z, c = links.y, links.x, links.z, links.c
    h = y * 2 + x
    q = y * (1 - c) + x * c
    rows, features = tokens.shape
    wide = qkv.shape[-1]
    narrow = staged.shape[1]
    heads = narrow // DH
    block = ups.shape[-1]
    slot_rows = rows * 4
    plane = [(links.across, 3 - h, 3), (links.along_x, y * 2 + 1 - x, 1), (links.along_y, (1 - y) * 2 + x, 2)]
    at_x, at_y = plane[1][1], plane[2][1]

    def columns(start, size):
        return pl.ds(pl.multiple_of(start, 128), size)

    def up_block(number):
        return up_shard.at[:, columns(number * block, block)]

    local = [
        pltpu.make_async_copy(source, target, local_sem.at[number])
        for number, (source, target) in zip(
            (0, 1, 2, 3, 4, 5, 7, 8),
            [
                (tile, tiles.at[y, x, z, c]),
                (qkv_shard.at[:, columns(h * wide, wide)], qkv.at[y, x, z, c]),
                (out_shard, full_out.at[y, x, z, c]),
                (down_shard, downs.at[c, q, z]),
                (up_block(x), ups.at[0, y, x, z, c]),
                (up_block(2 + y), ups.at[1, y, x, z, c]),
                (patch_shard, full_patch.at[y, x, z, c]),
                (class_shard, full_class.at[y, x, z, c]),
            ]
        )
    ]
    gain_core = Stage(links, [(tile, tiles.at[y, x, z, c], links.sibling)])
    gain_z = Stage(links, [(tiles.at[y, x, z], tiles.at[y, x, z], peer) for peer in links.along_z])
    gain_plane = Stage(links, [(tiles.at[y, x], tiles.at[y, x], peer) for peer, _, _ in plane])
    qkv_plane = Stage(
        links, [(qkv_shard.at[:, columns(p * wide, wide)], qkv.at[y, x, z, c], peer) for peer, p, _ in plane]
    )
    part = qkv.shape[4] // 2
    qkv_z = [Line(links, lambda at, k=k: qkv.at[:, :, at, c, k * part : (k + 1) * part]) for k in range(2)]
    qkv_core = Stage(links, [(qkv.at[:, :, :, c], qkv.at[:, :, :, c], links.sibling)])
    up_split = [
        Stage(links, [(up_block(1 - x), ups.at[0, y, x, z, c], links.along_x)]),
        Stage(links, [(up_block(2 + 1 - y), ups.at[1, y, x, z, c], links.along_y)]),
    ]
    up_z = [
        Line(links, lambda at: ups.at[0, y, :, at, c]),
        Line(links, lambda at: ups.at[1, :, x, at, c]),
    ]
    up_on = [
        Stage(links, [(ups.at[0, y, :, :, c], ups.at[0, y, :, :, c], links.along_y)]),
        Stage(links, [(ups.at[1, :, x, :, c], ups.at[1, :, x, :, c], links.along_x)]),
    ]
    up_core = [
        Stage(links, [(ups.at[k, :, :, :, c], ups.at[k, :, :, :, c], links.sibling)]) for k in range(2)
    ]
    some = down_shard.shape[0] // 4
    turned = device(y + (1 - c) * (1 - 2 * y), x + c * (1 - 2 * x), z, c)
    spans = [slice(k * some, (k + 1) * some) for k in range(4)]
    down_turn = [Stage(links, [(down_shard.at[spans[k]], downs.at[c, q, z, spans[k]], turned)]) for k in (0, 1)]
    down_z = [Line(links, lambda at, k=k: downs.at[c, :, at, spans[k]]) for k in (0, 1)] + [
        Line(links, lambda at, k=k: downs.at[c, q, at, spans[k]], down_shard.at[spans[k]]) for k in (2, 3)
    ]
    down_on = [Stage(links, [(downs.at[c, q, :, spans[k]],) * 2 + (turned,)]) for k in (2, 3)]
    down_core = [
        Stage(links, [(downs.at[c, :, :, span], downs.at[c, :, :, span], links.sibling)])
        for span in (slice(0, 2 * some), slice(2 * some, 4 * some))
    ]
    patch_sum = Sum(links, *patch_parts, None, "all_x")
    class_sum = Sum(links, *class_parts, None, "all_y")
    part = out_shard.shape[0] // 2

    def square(full, shard):
        first = [full.at[y, x, :, c, 0:part], full.at[y, x, :, c, part:]]
        second = [full.at[:, x, :, c, 0:part], full.at[y, :, :, c, part:]]
        return (
            Line(links, lambda at: full.at[y, x, at, c], shard),
            Stage(links, [(first[0], first[0], links.along_y), (first[1], first[1], links.along_x)]),
            Stage(links, [(second[0], second[0], links.along_x), (second[1], second[1], links.along_y)]),
            Stage(links, [(full.at[:, :, :, c],) * 2 + (links.sibling,)]),
        )

    out_z, out_one, out_two, out_core = square(full_out, out_shard)
    near, far = slice(0, part), slice(part, 2 * part)
    patch_x = Stage(links, [(patch_shard.at[far], full_patch.at[y, x, z, c, far], links.along_x)])
    patch_y = Stage(links, [(full_patch.at[y, :, z, c, far],) * 2 + (links.along_y,)])
    patch_first = Line(links, lambda at: full_patch.at[y, x, at, c, near], patch_shard.at[near])
    patch_one = Stage(links, [(full_patch.at[y, x, :, c, near],) * 2 + (links.along_y,)])
    patch_two = Stage(links, [(full_patch.at[:, x, :, c, near],) * 2 + (links.along_x,)])
    class_y = Stage(links, [(class_shard, full_class.at[y, x, z, c], links.along_y)])
    class_x = Stage(links, [(full_class.at[:, x, z, c],) * 2 + (links.along_x,)])
    halves = [slice(k * part, (k + 1) * part) for k in range(2)]
    class_z = [Line(links, lambda at, k=k: full_class.at[:, :, at, c, k * part : (k + 1) * part]) for k in range(2)]
    halves = [slice(part + k * part // 2, part + (k + 1) * part // 2) for k in range(2)]
    patch_z = [Line(links, lambda at, k=k: full_patch.at[:, :, at, c, halves[k]]) for k in range(2)]
    patch_core = Stage(links, [(full_patch.at[:, :, :, c],) * 2 + (links.sibling,)])
    class_core = Stage(links, [(full_class.at[:, :, :, c],) * 2 + (links.sibling,)])
    beside = (links.along_x, links.along_y)
    here = slice(0, rows)
    few = class_proj.shape[0]
    tall = -(-CLS // 16) * 16
    parts = (slice(0, tall), slice(tall, rows))
    theirs = [slice(rows + at.start, rows + at.stop) for at in parts]

    def exchange(sent, got, sent_at, got_at):
        return [
            [Stage(links, [(sent.at[k, sent_at[i]], got.at[k, got_at[i]], beside[k])]) for i in range(2)]
            for k in range(2)
        ]

    normed_out = exchange(normed_two, normed_two, parts, theirs)
    branch_out = exchange(d_branch, d_branch, parts, theirs)
    part_back = exchange(part_sent, part_got, parts, parts)
    grad_back = exchange(back_sent, back_got, parts, parts)
    sizes = {1: few, 2: few, 3: tall - 3 * few}
    class_out = [
        links.plan(
            rounded.at[few * rel : few * rel + sizes[rel]], class_rows.at[0 : sizes[rel]], peer, h == 0
        )
        for peer, _, rel in plane
    ]
    mine = pl.ds(pl.multiple_of(h * few, few), few)
    unit_out = Stage(links, [(classes.at[mine], classes.at[mine], peer) for peer, _, _ in plane])
    class_back = Stage(links, [(class_sent.at[p], class_got.at[rel - 1], peer) for peer, p, rel in plane])
    term_back = [
        links.plan(term_sent.at[0 : sizes[rel]], term_got.at[rel - 1, 0 : sizes[rel]], peer, h == rel)
        for peer, _, rel in plane
    ]
    middle = rows // 2
    strips = [slice(0, middle), slice(middle, rows)]
    rows_x = [Stage(links, [(rows_ref.at[h, strips[k]],) * 2 + (links.along_x,)]) for k in (0, 1)]
    rows_y = [Stage(links, [(rows_ref.at[h, strips[k]],) * 2 + (links.along_y,)]) for k in (1, 0)]
    piece_a, piece_b = rows_ref.at[at_x, strips[0]], rows_ref.at[at_y, strips[1]]
    relay_y = Stage(links, [(piece_a, piece_a, links.along_y)])
    relay_x = Stage(links, [(piece_b, piece_b, links.along_x)])

    share = norm_gains.shape[1]
    tile[...] = jnp.zeros_like(tile)
    for i in range(4):

        @pl.when((z * 2 + c) % 4 == i)
        def _(i=i):
            tile[0:2, i * share : (i + 1) * share] = norm_gains[...].astype(jnp.float32)

    for number in range(4):
        for j in range(8):
            at = (j // 4 * 2 + number) if number < 2 else ((number - 2) * 2 + j // 4)
            at = (at * 4 + j % 4) * 256 + (0 if number < 2 else 128)
            up_shard[:, number * block + j * 128 : number * block + (j + 1) * 128] = up_given[:, at : at + 128]
    for copy in local:
        copy.start()
    class_rows[...] = jnp.zeros_like(class_rows)
    links.greet()
    for stage in (gain_core, qkv_plane, *up_split, *down_turn, class_y, patch_x, out_z, patch_first):
        stage.start()
    value, inverse = norm(tokens[...])
    normal_one[...] = value
    inverse_one[...] = jnp.broadcast_to(inverse, inverse_one.shape)
    local[0].wait()
    gain_core.wait()
    gain_z.start()
    gain_z.wait()
    gain_plane.start()
    local[1].wait()
    qkv_plane.wait()
    for line in qkv_z:
        line.start()
    gain_plane.wait()
    for j in range(8):
        piece = tiles[j // 4, j // 2 % 2, (j % 2) * 2, 0].astype(jnp.float32)
        for i in range(1, 4):
            piece = piece + tiles[j // 4, j // 2 % 2, (j % 2) * 2 + i // 2, i % 2].astype(jnp.float32)
        gains_ref[:, j * 128 : (j + 1) * 128] = piece[0:8]
    rows_ref[h] = (normal_one[...] * gains_ref[0:1, :]).astype(jnp.bfloat16)
    for stage in (rows_x[0], rows_y[0], rows_x[1], rows_y[1]):
        stage.start()
    for line in (out_z, patch_first, *qkv_z):
        line.relay()
    rows_x[0].wait()
    relay_y.start()
    rows_y[0].wait()
    relay_x.start()
    local[6].wait()
    patch_x.wait()
    patch_y.start()
    local[7].wait()
    class_y.wait()
    class_x.start()
    for line in qkv_z:
        line.wait()
    qkv_core.start()
    for k in range(2):
        local[4 + k].wait()
        up_split[k].wait()
        up_z[k].start()
    out_z.wait()
    patch_first.wait()
    for number in (2, 3):
        local[number].wait()

    def project(p):
        weight = qkv[...].reshape(rows * 4, wide)
        piece = jnp.dot(rows_ref[p], weight, preferred_element_type=jnp.float32).astype(jnp.bfloat16)
        at = pl.ds(pl.multiple_of(p * rows, rows), rows)
        for number in range(3 * heads):
            heads_ref[number, at, :] = piece[:, number * DH : (number + 1) * DH]

    qkv_core.wait()
    project(h)
    rows_x[1].wait()
    project(at_x)
    rows_y[1].wait()
    project(at_y)
    out_one.start()
    patch_one.start()
    relay_y.wait()
    relay_x.wait()
    project(3 - h)

    live = live_ref[0]
    key_live = lax.broadcasted_iota(jnp.int32, (slot_rows, 1), 0) < live
    returned = links.count - 1
    assert returned + 4 <= FRONT_COPIES

    def back(rel):
        peer = h + (rel % 2) * (1 - 2 * x) + (rel // 2) * (2 - 4 * y)
        return pltpu.make_async_remote_copy(
            src_ref=staged.at[pl.ds(pl.multiple_of(peer * rows, rows), rows), :],
            dst_ref=attended.at[:, columns(h * narrow, narrow)],
            send_sem=send_sem.at[returned + rel],
            recv_sem=recv_sem.at[returned + rel],
            device_id=(peer, z * 2 + c),
            device_id_type=MESH,
        )

    def up_next(k):
        up_z[k].wait()
        up_on[k].start()

    def up_end(k):
        up_on[k].wait()
        up_core[k].start()

    def out_next():
        out_one.wait()
        out_two.start()

    def out_end():
        out_two.wait()
        out_core.start()

    def patch_next():
        patch_one.wait()
        patch_two.start()

    def down_late():
        down_z[2].start()
        down_z[3].start()

    def down_early():
        for stage in down_turn:
            stage.wait()
        down_z[0].start()
        down_z[1].start()

    def down_relays():
        down_z[2].relay()
        down_z[3].relay()

    events = {
        0: up_z[0].relay,
        3: out_next,
        5: up_z[1].relay,
        6: down_late,
        11: down_early,
        12: out_end,
        14: down_relays,
    }

    def tile_body(slot, carry):
        turn, number = slot // 4, slot % 4
        rel = 3 - turn
        peer = h + (rel % 2) * (1 - 2 * x) + (rel // 2) * (2 - 4 * y)
        at = pl.ds(pl.multiple_of(peer * rows, rows), rows)
        at_slots(slot, events)
        queries = heads_ref[3 * number, at, :]
        keys = heads_ref[3 * number + 1]
        values = heads_ref[3 * number + 2]
        scores = lax.dot_general(keys, queries, (((1,), (1,)), ((), ())), preferred_element_type=jnp.float32)
        scores = jnp.where(key_live, scores * (scaling * LOG2E), -1e30)
        highest = jnp.max(scores, axis=0, keepdims=True)
        raw = jnp.exp2(scores - highest)
        totals = jnp.sum(raw, axis=0, keepdims=True)
        weights = (raw * (1.0 / totals)).astype(jnp.bfloat16)
        mixed = lax.dot_general(
            values, weights, (((0,), (0,)), ((), ())), preferred_element_type=jnp.float32
        )
        mixed = mixed.T.astype(jnp.bfloat16)
        for which in range(4):

            @pl.when(number == which)
            def _(which=which):
                staged[at, which * DH : (which + 1) * DH] = mixed

        logsum[number, :, at] = highest + jnp.log2(totals)

        @pl.when((number == 3) & (rel > 0))
        def _():
            back(rel).start()

        return carry

    lax.fori_loop(0, SLOTS, tile_body, 0)
    own = pltpu.make_async_copy(
        staged.at[pl.ds(pl.multiple_of(h * rows, rows), rows), :],
        attended.at[:, columns(h * narrow, narrow)],
        local_sem.at[6],
    )
    own.start()
    class_x.wait()
    patch_y.wait()
    for line in (*class_z, *patch_z):
        line.start()
    up_next(0)
    up_next(1)
    for k in range(2):
        down_z[2 + k].wait()
        down_on[k].start()
    for rel in (3, 2, 1):
        back(rel).wait()
    own.wait()
    out_core.wait()
    down_z[0].relay()

    def whole(weight):
        return weight[...].reshape(-1, weight.shape[-1])

    second[...] = tokens[...] + matmul(attended[...], whole(full_out))
    value, inverse = norm(second[...])
    normal_two[...] = value
    inverse_two[...] = jnp.broadcast_to(inverse, inverse_two.shape)
    value = (value * gains_ref[1:2, :]).astype(jnp.bfloat16)
    for k in range(2):
        normed_two[k, here] = value
    for i in range(2):
        for k in range(2):
            normed_out[k][i].start()
    down_z[1].relay()
    patch_next()
    up_end(0)
    up_end(1)
    for k in range(2):
        up_core[k].wait()
    wide_step = 256

    def forward(k, at, size):
        def step(j, carry):
            span = pl.ds(pl.multiple_of(j * wide_step, wide_step), wide_step)
            weight = ups[k, :, :, :, :, :, span].reshape(features, wide_step)
            hidden = matmul(normed_two[k, at], weight)
            spread = 0.5 + 0.5 * lax.erf(hidden * 0.7071067811865476)
            density = jnp.exp(hidden * hidden * -0.5) * 0.3989422804014327
            active[k, at, span] = (hidden * spread).astype(jnp.bfloat16)
            slope[k, at, span] = spread + hidden * density
            return carry

        lax.fori_loop(0, block // wide_step, step, 0)

    forward(0, here, rows)
    for stage in down_on:
        stage.wait()
    down_core[1].start()
    forward(1, here, rows)
    for line in down_z[:2]:
        line.wait()
    down_core[0].start()
    for stage in down_core:
        stage.wait()
    for i in range(2):
        for k in range(2):
            normed_out[k][i].wait()
            forward(k, theirs[i], parts[i].stop - parts[i].start)
            part_sent[k, parts[i]] = matmul(active[k, theirs[i]], whole(downs.at[k])).astype(jnp.bfloat16)
            part_back[k][i].start()
        if i == 0:
            for line in class_z:
                line.relay()
    residual[...] = second[...] + (
        matmul(active[0, here], whole(downs.at[0])) + matmul(active[1, here], whole(downs.at[1]))
    )
    for line in patch_z:
        line.relay()

    def complete(at):
        for k in range(2):
            part_back[k][0 if at.start == 0 else 1].wait()
        value = residual[at] + (part_got[0, at].astype(jnp.float32) + part_got[1, at].astype(jnp.float32))
        rounded[at] = value.astype(jnp.bfloat16)

    complete(parts[0])

    @pl.when(h == 0)
    def _():
        for copy in class_out:
            copy.start()
        class_rows[...] = rounded[0:few]

    for line in class_z:
        line.wait()
    class_core.start()
    complete(parts[1])
    for line in patch_z:
        line.wait()
    patch_two.wait()
    patch_core.start()
    patch_core.wait()

    patch_proj[...] = matmul(rounded[...], whole(full_patch))
    factor = unit_scale(patch_proj[...])
    patch_unit = (patch_proj[...] * factor).astype(jnp.bfloat16)
    classes[4 * few :] = jnp.zeros((classes.shape[0] - 4 * few, features), jnp.bfloat16)
    for copy, (_, _, rel) in zip(class_out, plane):
        pl.when(h == rel)(copy.wait_recv)
    class_core.wait()
    class_live = h * few + lax.broadcasted_iota(jnp.int32, (few, 1), 0) < CLS
    value = matmul(class_rows[...], whole(full_class))
    class_proj[...] = value
    classes[mine] = jnp.where(class_live, value * unit_scale(value), 0.0).astype(jnp.bfloat16)
    unit_out.start()
    mask_in[...] = jnp.zeros_like(mask_in)
    mask_in[0:rows, 0:CLS] = grad_masks[...]
    mask_in[rows : rows + 2, 0:CLS] = mask_norm[...]
    mask_gain, mask_bias = mask_in[rows : rows + 1, :], mask_in[rows + 1 : rows + 2, :]
    unit_out.wait()
    products = matmul_nt(patch_unit, classes[...])
    lane = lax.broadcasted_iota(jnp.int32, products.shape, 1)
    position = h * rows + lax.broadcasted_iota(jnp.int32, (rows, 1), 0)
    patch_rows = ((position >= CLS) & (position < live)).astype(jnp.float32)

    def class_mean(values):
        return jnp.sum(values, axis=-1, keepdims=True) * (1.0 / CLS)

    center = jnp.where(lane < CLS, products - class_mean(products), 0.0)
    inverse = lax.rsqrt(class_mean(center * center) + 1e-05)
    mask_normal = center * inverse
    class_masks[...] = ((mask_normal * mask_gain + mask_bias) * patch_rows)[:, 0:CLS]
    upstream = mask_in[0:rows, :] * patch_rows
    mask_sums[...] = jnp.zeros_like(mask_sums)
    mask_sums[0:1, :] = jnp.sum(upstream * mask_normal, axis=0, keepdims=True)
    mask_sums[1:2, :] = jnp.sum(upstream, axis=0, keepdims=True)
    upstream = upstream * mask_gain
    upstream = inverse * (upstream - class_mean(upstream) - mask_normal * class_mean(upstream * mask_normal))
    d_products = jnp.where(lane < CLS, upstream, 0.0).astype(jnp.bfloat16)
    class_part = matmul_tn(d_products, patch_unit)
    for p in range(4):
        class_sent[p] = class_part[few * p : few * (p + 1)].astype(jnp.bfloat16)
    class_back.start()
    upstream = matmul(d_products, classes[...])
    direct = patch_proj[...] * factor
    upstream = factor * (upstream - direct * jnp.sum(upstream * direct, axis=-1, keepdims=True))
    d_patch[...] = upstream.astype(jnp.bfloat16)
    d_residual[...] = matmul_nt(d_patch[...], whole(full_patch))

    def branch(i):
        value = d_residual[parts[i]].astype(jnp.bfloat16)
        for k in range(2):
            d_branch[k, parts[i]] = value
            branch_out[k][i].start()

    branch(1)

    weight_gradient(patch_parts[0], rounded, d_patch)
    patch_sum.begin()
    class_back.wait()
    upstream = class_sent[h].astype(jnp.float32)
    for number in range(3):
        upstream = upstream + class_got[number].astype(jnp.float32)
    d_class[...] = jnp.where(class_live, unit_back(class_proj[...], upstream), 0.0).astype(jnp.bfloat16)
    term = matmul_nt(d_class[...], whole(full_class))
    term_sent[...] = term.astype(jnp.bfloat16)
    for copy, (_, _, rel) in zip(term_back, plane):
        pl.when(h == rel)(copy.start)
    weight_gradient(class_parts[0], class_rows, d_class)
    class_sum.begin()

    def backward(k, at):
        for j in range(block // wide_step):
            weight = downs[k, j // 2, 2 * (j % 2) : 2 * (j % 2) + 2].reshape(wide_step, features)
            span = slice(j * wide_step, (j + 1) * wide_step)
            d_hidden[k, at, span] = (matmul_nt(d_branch[k, at], weight) * slope[k, at, span]).astype(jnp.bfloat16)


    def returned_rows(i):
        for k in range(2):
            branch_out[k][i].wait()
            backward(k, theirs[i])
            back_sent[k, parts[i]] = matmul_nt(d_hidden[k, theirs[i]], whole(ups.at[k])).astype(jnp.bfloat16)
            grad_back[k][i].start()

    for k in range(2):
        backward(k, parts[1])
    returned_rows(1)

    @pl.when(h == 0)
    def _():
        d_residual[0:few] = d_residual[0:few] + term_sent[...].astype(jnp.float32)
        for copy, (_, _, rel) in zip(term_back, plane):
            copy.wait_recv()
            at = slice(few * rel, few * rel + sizes[rel])
            d_residual[at] = d_residual[at] + term_got[rel - 1, 0 : sizes[rel]].astype(jnp.float32)

    branch(0)
    patch_sum.run_first()
    class_sum.run_first()
    for k in range(2):
        backward(k, parts[0])
    returned_rows(0)
    upstream = matmul_nt(d_hidden[0, here], whole(ups.at[0])) + matmul_nt(d_hidden[1, here], whole(ups.at[1]))
    patch_sum.run_second()
    class_sum.run_second()
    for k in range(2):
        for stage in grad_back[k]:
            stage.wait()
    upstream = upstream + (back_got[0].astype(jnp.float32) + back_got[1].astype(jnp.float32))
    upstream = upstream * gains_ref[1:2, :]
    value = normal_two[...]
    middle = jnp.mean(upstream, axis=-1, keepdims=True)
    along = jnp.mean(upstream * value, axis=-1, keepdims=True)
    d_second[...] = d_residual[...] + inverse_two[:, 0:1] * (upstream - middle - value * along)
    d_mix[...] = d_second[...].astype(jnp.bfloat16)
    d_attended[...] = matmul_nt(d_mix[...], whole(full_out)).astype(jnp.bfloat16)
    patch_sum.hand_over(g_patch)
    class_sum.hand_over(g_class)
    links.drain()


def front(live, tokens, norm_gains, grad_masks, mask_norm, shards, scaling):
    rows, features = tokens.shape
    vmem, hbm = pl.BlockSpec(memory_space=pltpu.VMEM), pl.BlockSpec(memory_space=pl.ANY)
    w_qkv, w_out, w_up, w_down, w_patch, w_class = shards
    wide = w_qkv.shape[1] // 4
    heads = wide // (3 * DH)
    block = w_up.shape[1] // 4
    lanes = 256
    few = -(-CLS // 64) * 16
    low, single = jnp.bfloat16, jnp.float32
    outs = [
        ((rows, features), low),
        ((3 * heads, 4 * rows, DH), low),
        ((heads, 1, 4 * rows), single),
        ((4, rows, features), low),
        ((8, features), single),
        ((2, 2, 4, 2, w_qkv.shape[0], wide), low),
        (grad_masks.shape, single),
        ((8, lanes), single),
        ((rows, features), single),
        ((rows, 128), single),
        ((2, 2 * rows, features), low),
        ((2, 2 * rows, block), low),
        ((2, 2 * rows, features), low),
        ((2, 2 * rows, block), low),
        ((rows, features), low),
        ((rows, features), single),
        ((rows, features), low),
        ((4,) + w_patch.shape, low),
        ((4,) + w_class.shape, low),
    ]
    scratch = [
        ((2, 2, 4, 2) + w_out.shape, low),
        ((2, 2, 2, 4, 2, w_up.shape[0], block), low),
        ((2, 2, 4) + w_down.shape, low),
        ((2, 2, 4, 2) + w_patch.shape, low),
        ((2, 2, 4, 2) + w_class.shape, low),
        ((2, 2, 4, 2, 8, 128), single),
        ((4 * rows, wide // 3), low),
        ((2, 2 * rows, block), single),
        ((rows, features), single),
        ((rows, features), single),
        ((rows, 128), single),
        ((rows, features), single),
        ((few, features), single),
        ((lanes, features), low),
        ((2, rows, features), low),
        ((2, rows, features), low),
        ((2, rows, features), low),
        ((2, rows, features), low),
        ((4, few, features), low),
        ((3, few, features), low),
        ((few, features), low),
        ((3, few, features), low),
        ((rows + 8, lanes), single),
        ((8, 128), single),
        (w_up.shape, low),
        ((rows, features), low),
        ((rows, features), low),
        ((few, features), low),
        ((few, features), low),
    ]
    for shape in (w_patch.shape, w_class.shape):
        for lead in ((2, 2, 4, 2), (2, 2, 4), (2, 4), (4,)):
            scratch.append((lead + shape, low))
    return pl.pallas_call(
        partial(front_kernel, scaling),
        out_shape=[jax.ShapeDtypeStruct(*out) for out in outs],
        in_specs=[pl.BlockSpec(memory_space=pltpu.SMEM)] + [vmem] * 4 + [hbm] * 2 + [vmem] + [hbm] * 3,
        out_specs=[vmem] * len(outs),
        scratch_shapes=[pltpu.VMEM(*shape) for shape in scratch]
        + [
            pltpu.SemaphoreType.DMA((FRONT_COPIES,)),
            pltpu.SemaphoreType.DMA((FRONT_COPIES,)),
            pltpu.SemaphoreType.DMA((9,)),
        ],
        compiler_params=pltpu.CompilerParams(
            collective_id=1, has_side_effects=True, vmem_limit_bytes=121 * 2**19
        ),
        name="front",
    )(live, tokens, norm_gains, grad_masks, mask_norm, *shards)


def rear_kernel(scaling, *refs):
    live_ref, d_rows, heads_ref, logsum, rows_ref, qkv, small_ref = refs[:7]
    normal_one, inverse_one, d_second, gains_ref = refs[7:11]
    refs = refs[:7] + refs[11:]
    normed_two, active, d_branch, d_hidden, attended, d_mix = refs[7:13]
    handed = refs[13:15]
    d_normed, g_qkv, g_up, g_down, g_out, small_out, *g_handed = refs[15:23]
    at = 23
    d_out, d_heads, d_spread, grad_keys, grad_values = refs[at : at + 5]
    d_sent, d_got, q_part, q_sib, q_z, q_plane = refs[at + 5 : at + 11]
    small_own, small_got, send_sem, recv_sem, local_sem = refs[at + 11 : at + 16]
    handed_own, handed_got = refs[at + 16 : at + 18]
    scratch = refs[at + 18 :]
    links = Links(send_sem, recv_sem)
    y, x, z, c = links.y, links.x, links.z, links.c
    h = y * 2 + x
    rows, features = d_rows.shape
    slot_rows = rows * 4
    narrow = d_out.shape[1]
    heads = narrow // DH
    wide = 3 * narrow
    plane = [(links.across, 3 - h, 3), (links.along_x, y * 2 + 1 - x, 1), (links.along_y, (1 - y) * 2 + x, 2)]

    def columns(start, size):
        return pl.ds(pl.multiple_of(start, 128), size)

    def block(p):
        return pl.ds(pl.multiple_of(p * rows, rows), rows)

    spread_out = Stage(
        links, [(d_rows.at[:, columns(p * narrow, narrow)], d_out.at[block(h), :], peer) for peer, p, _ in plane]
    )
    own = pltpu.make_async_copy(d_rows.at[:, columns(h * narrow, narrow)], d_out.at[block(h), :], local_sem.at[0])
    kinds = ("up_y", "up_x", "down", "all_x")
    sums = [
        Sum(links, *scratch[5 * i : 5 * i + 5], kinds[i]) for i in range(4)
    ]
    back = [Stage(links, [(d_sent.at[rel - 1], d_got.at[rel - 1], peer)]) for peer, _, rel in plane]
    q_core = Stage(links, [(q_part.at[:, :, :, 1 - c], q_sib, links.sibling)])
    q_line = LineSum(links, lambda at: q_part.at[:, :, at, c], q_z)
    q_across = Stage(
        links, [(q_part.at[p // 2, p % 2, z, c], q_plane.at[h], peer) for peer, p, _ in plane]
    )
    small_core = Stage(links, [(small_own.at[0], small_got.at[0], links.sibling)])
    small_x = Stage(links, [(small_own.at[1], small_got.at[1], links.along_x)])
    small_y = Stage(links, [(small_own.at[2], small_got.at[2], links.along_y)])
    small_z = Stage(links, [(small_own.at[3], small_got.at[3 + z], peer) for peer in links.along_z])

    handed_z = [LineSum(links, lambda at, k=k: handed_own.at[k, at], handed_got.at[k]) for k in range(2)]
    for k in range(2):
        handed_own[k] = handed[k][...]
    links.greet()
    spread_out.start()
    own.start()
    small_own[0] = small_ref[...]
    small_core.start()
    for line in handed_z:
        line.start()
    parts = [scratch[5 * i] for i in range(4)]
    for k in range(2):
        weight_gradient(parts[k], normed_two.at[k], d_hidden.at[k])
        sums[k].begin()
    for k in range(2):
        weight_gradient(parts[2].at[k], active.at[k], d_branch.at[k])
    sums[2].begin()
    weight_gradient(parts[3], attended, d_mix)
    sums[3].begin()
    own.wait()
    spread_out.wait()
    live = live_ref[0]
    key_live = lax.broadcasted_iota(jnp.int32, (slot_rows, 1), 0) < live
    up_y, up_x, down, out = sums
    assert links.count <= REAR_COPIES

    def small_step(stage, number, following):
        def run():
            stage.wait()
            small_own[number + 1] = small_own[number] + small_got[number]
            if number == 2:
                small_got[3 + z] = small_own[3]
            following.start()

        return run

    def both(*steps):
        def run():
            for step in steps:
                step()

        return run

    def handed_end():
        for k in range(2):
            out_ref = g_handed[k]
            out_ref[...] = handed_own[k, z].astype(jnp.float32)

            def add(slot, k=k, out_ref=out_ref):
                out_ref[...] = out_ref[...] + handed_got[k, slot].astype(jnp.float32)

            handed_z[k].collect(add)

    events = {
        0: both(handed_z[0].relay, handed_z[1].relay, up_y.run_first),
        1: up_x.run_first,
        2: down.run_first,
        3: small_step(small_core, 0, small_x),
        5: handed_end,
        6: out.run_first,
        7: small_step(small_x, 1, small_y),
        10: both(up_y.run_second, up_x.run_second),
        11: small_step(small_y, 2, small_z),
        13: both(up_y.line.relay, up_x.line.relay),
        14: down.run_second,
    }

    def tile_body(slot, carry):
        number, turn = slot // 4, slot % 4
        at_slots(slot, events)
        at = block(turn)

        @pl.when(turn == 0)
        def _():
            grad_keys[...] = jnp.zeros_like(grad_keys)
            grad_values[...] = jnp.zeros_like(grad_values)

        queries = heads_ref[3 * number, at, :]
        keys = heads_ref[3 * number + 1]
        values = heads_ref[3 * number + 2]
        grads = d_heads[number, at, :]
        scores = lax.dot_general(keys, queries, (((1,), (1,)), ((), ())), preferred_element_type=jnp.float32)
        powers = scores * (scaling * LOG2E) - logsum[number, :, at]
        weights = jnp.where(key_live, jnp.exp2(powers), 0.0)
        grad_values[...] += jnp.dot(weights.astype(jnp.bfloat16), grads, preferred_element_type=jnp.float32)
        grad_weights = lax.dot_general(
            values, grads, (((1,), (1,)), ((), ())), preferred_element_type=jnp.float32
        )
        deltas = jnp.sum(grad_weights * weights, axis=0, keepdims=True)
        grad_scores = (weights * (grad_weights - deltas)).astype(jnp.bfloat16)
        grad_keys[...] += jnp.dot(grad_scores, queries, preferred_element_type=jnp.float32)
        grad_queries = lax.dot_general(
            keys, grad_scores, (((0,), (0,)), ((), ())), preferred_element_type=jnp.float32
        )
        d_heads[4 + 3 * number, at, :] = (grad_queries.T * scaling).astype(jnp.bfloat16)

        @pl.when(turn == 3)
        def _():
            d_heads[5 + 3 * number] = (grad_keys[...] * scaling).astype(jnp.bfloat16)
            d_heads[6 + 3 * number] = grad_values[...].astype(jnp.bfloat16)

        return carry

    for number in range(heads):
        d_heads[number] = d_out[:, number * DH : (number + 1) * DH]
    lax.fori_loop(0, SLOTS, tile_body, 0)
    for number in range(3 * heads):
        d_spread[:, number * DH : (number + 1) * DH] = d_heads[4 + number]
    per = features // 4
    for j in range(4):
        left = jnp.concatenate([rows_ref[p, :, j * per : (j + 1) * per] for p in range(4)], axis=0)
        piece = lax.dot_general(
            left, d_spread[...], (((0,), (0,)), ((), ())), preferred_element_type=jnp.float32
        ).astype(jnp.bfloat16)
        q_part[j // 2, j % 2] = piece.reshape(4, 2, per // 8, wide)
    q_core.start()
    weight = qkv[...].reshape(features, wide)
    for (_, p, rel), stage in zip(plane, back):
        piece = lax.dot_general(
            d_spread[block(p), :], weight, (((1,), (1,)), ((), ())), preferred_element_type=jnp.float32
        )
        d_sent[rel - 1] = piece.astype(jnp.bfloat16)
        stage.start()
    up_y.run_last()
    up_x.run_last()
    q_core.wait()

    def add_sib(i, carry):
        index = (i // 8, i // 4 % 2, i % 4)
        q_part[(*index, c)] = q_part[(*index, c)] + q_sib[index]
        return carry

    lax.fori_loop(0, 16, add_sib, 0)
    q_line.start()
    d_normed[...] = lax.dot_general(
        d_spread[block(h), :], weight, (((1,), (1,)), ((), ())), preferred_element_type=jnp.float32
    )
    down.line.relay()
    q_line.relay()
    out.run_second()
    out.run_third()

    def add_line(slot):
        for i in range(4):
            index = (i // 2, i % 2)
            q_part[(*index, z, c)] = q_part[(*index, z, c)] + q_z[(slot, *index)]

    q_line.collect(add_line)
    q_across.start()
    out.line.relay()
    small_z.wait()
    small_out[...] = (small_got[3] + small_got[4] + small_got[5] + small_got[6])[0:2, 0:CLS]
    down.finish(g_down)
    up_y.finish(g_up)
    up_x.finish(g_up)
    out.finish(g_out)
    q_across.wait()
    g_qkv[:, columns(h * wide, wide)] = q_part[y, x, z, c].astype(jnp.float32)
    for _, p, _ in plane:
        g_qkv[:, columns(p * wide, wide)] = q_plane[p].astype(jnp.float32)
    for stage in back:
        stage.wait()
    upstream = d_normed[...] + (
        d_got[0].astype(jnp.float32) + d_got[1].astype(jnp.float32) + d_got[2].astype(jnp.float32)
    )
    upstream = upstream * gains_ref[0:1, :]
    value = normal_one[...]
    middle = jnp.mean(upstream, axis=-1, keepdims=True)
    along = jnp.mean(upstream * value, axis=-1, keepdims=True)
    d_normed[...] = d_second[...] + inverse_one[:, 0:1] * (upstream - middle - value * along)
    links.drain()


def rear(live, d_rows, heads_qkv, logsum, rows_all, qkv, small, ending, factors, scaling):
    rows, features = d_rows.shape
    slot_rows = 4 * rows
    narrow = features // 4
    heads = narrow // DH
    wide = 3 * narrow
    vmem, hbm = pl.BlockSpec(memory_space=pltpu.VMEM), pl.BlockSpec(memory_space=pl.ANY)
    low = jnp.bfloat16
    up, down = (features // 32, features), (features // 8, features)
    shard = (features // 32, wide)
    buffers = []
    for _ in range(2):
        buffers += [(2, 2, 4, 2) + up, (2, 2, 4) + up, (2, 4) + up, up, (4, 2) + up]
    buffers += [(2, 2, 4) + down, (2, 4) + down, (4,) + down, (8, 128), (4,) + down]
    buffers += [(2, 2, 4, 2) + up, (2, 2, 4) + up, (2, 4) + up, (4,) + up, (4,) + up]
    single = jnp.float32
    return pl.pallas_call(
        partial(rear_kernel, scaling),
        out_shape=[
            jax.ShapeDtypeStruct((rows, features), single),
            jax.ShapeDtypeStruct((features // 32, 4 * wide), single),
            jax.ShapeDtypeStruct((up[0], 4 * up[1]), single),
            jax.ShapeDtypeStruct(down, single),
        ]
        + [jax.ShapeDtypeStruct(up, single)]
        + [jax.ShapeDtypeStruct((2, CLS), single)]
        + [jax.ShapeDtypeStruct(up, single)] * 2,
        in_specs=[pl.BlockSpec(memory_space=pltpu.SMEM)] + [vmem] * 18,
        out_specs=[vmem] * 8,
        scratch_shapes=[
            pltpu.VMEM((slot_rows, narrow), low),
            pltpu.VMEM((4 * heads, slot_rows, DH), low),
            pltpu.VMEM((slot_rows, wide), low),
            pltpu.VMEM((slot_rows, DH), single),
            pltpu.VMEM((slot_rows, DH), single),
            pltpu.VMEM((3, rows, features), low),
            pltpu.VMEM((3, rows, features), low),
            pltpu.VMEM((2, 2, 4, 2) + shard, low),
            pltpu.VMEM((2, 2, 4) + shard, low),
            pltpu.VMEM((4, 2, 2) + shard, low),
            pltpu.VMEM((4,) + shard, low),
            pltpu.VMEM((4,) + small.shape, single),
            pltpu.VMEM((7,) + small.shape, single),
            pltpu.SemaphoreType.DMA((REAR_COPIES,)),
            pltpu.SemaphoreType.DMA((REAR_COPIES,)),
            pltpu.SemaphoreType.DMA((7,)),
        ]
        + [pltpu.VMEM((2, 4) + up, low), pltpu.VMEM((2, 4) + up, low)]
        + [pltpu.VMEM(shape, low) for shape in buffers],
        compiler_params=pltpu.CompilerParams(
            collective_id=2, has_side_effects=True, vmem_limit_bytes=121 * 2**19
        ),
        name="rear",
    )(live, d_rows, heads_qkv, logsum, rows_all, qkv, small, *ending, *factors)


def ending_kernel(*refs):
    count = (len(refs) - 6) // 2
    results, (w_qkv, w_up, gains) = refs[:count], refs[count : count + 3]
    outs, gain_out, gain_sums, sems = refs[count + 3 : 2 * count + 3], *refs[2 * count + 3 :]
    copies = [pltpu.make_async_copy(results[i], outs[i], sems.at[i]) for i in range(count)]
    for copy in copies:
        copy.start()
    for number, (weight, grad) in enumerate(((w_qkv, results[2]), (w_up, results[4]))):
        total = jnp.sum(weight[...].astype(jnp.float32) * grad[...], axis=1, keepdims=True)
        total = jnp.broadcast_to(total, (total.shape[0], 128)).T[0:1, :]
        gain_sums[number : number + 1, :] = total / gains[number : number + 1, :].astype(jnp.float32)
    last = pltpu.make_async_copy(gain_sums, gain_out, sems.at[count])
    last.start()
    for copy in copies:
        copy.wait()
    last.wait()


def ending_copies(results, w_qkv, w_up, gains):
    vmem, hbm = pl.BlockSpec(memory_space=pltpu.VMEM), pl.BlockSpec(memory_space=pl.ANY)
    count = len(results)
    shapes = [jax.ShapeDtypeStruct(a.shape, a.dtype) for a in results]
    return pl.pallas_call(
        ending_kernel,
        out_shape=shapes + [jax.ShapeDtypeStruct(gains.shape, jnp.float32)],
        in_specs=[vmem] * (count + 3),
        out_specs=[hbm] * (count + 1),
        scratch_shapes=[pltpu.VMEM(gains.shape, jnp.float32), pltpu.SemaphoreType.DMA((count + 1,))],
        name="ending",
    )(*results, w_qkv, w_up, gains)


def body_planned(
    tokens,
    patch_counts,
    w_qkv,
    w_out,
    w_up,
    w_down,
    w_patch,
    w_class,
    norm_gains,
    mask_norm,
    grad_masks,
):
    low = jnp.bfloat16
    h, s = lax.axis_index("head"), lax.axis_index("seq")
    tokens, grad_masks = tokens[0], grad_masks[0]
    row_count = tokens.shape[0]
    live = CLS + patch_counts
    scaling = DH ** (-0.5)

    outs = front(
        live,
        tokens,
        norm_gains,
        grad_masks,
        mask_norm,
        (w_qkv, w_out, w_up, w_down, w_patch, w_class),
        scaling,
    )
    attended, heads_qkv, logsum, rows_all, gains, qkv, class_masks, mask_sums = outs[:8]
    normal_one, inverse_one, normed_two, active, d_branch, d_hidden = outs[8:14]
    d_mix, d_second, d_attended, *handed = outs[14:]
    factors = (normed_two, active, d_branch, d_hidden, attended, d_mix, *handed)
    ending = (normal_one, inverse_one, d_second, gains)
    grad_inputs, g_qkv, g_up, g_down, g_out, sums, g_patch, g_class = rear(
        live, d_attended, heads_qkv, logsum, rows_all, qkv, mask_sums, ending, factors, scaling
    )
    results = ending_copies(
        (class_masks, grad_inputs, g_qkv, g_out, g_up, g_down, g_patch, g_class, sums), w_qkv, w_up, norm_gains
    )
    return (results[0][None], results[1][None], *results[2:8], results[9], results[8])


def solution(mesh):
    planned = dict(mesh.shape) == {"head": 4, "seq": 8}
    return jax.shard_map(
        body_planned if planned else body_general,
        mesh=mesh,
        in_specs=(
            P("seq", "head", None),
            P("seq"),
            P(("head", "seq"), None),
            P(("head", "seq"), None),
            P(("head", "seq"), None),
            P(("head", "seq"), None),
            P(("head", "seq"), None),
            P(("head", "seq"), None),
            P(None, ("head", "seq")),
            P(),
            P("seq", "head", None),
        ),
        out_specs=(
            P("seq", "head", None),
            P("seq", "head", None),
            P(("head", "seq"), None),
            P(("head", "seq"), None),
            P(("head", "seq"), None),
            P(("head", "seq"), None),
            P(("head", "seq"), None),
            P(("head", "seq"), None),
            P(None, ("head", "seq")),
            P(),
        ),
        check_vma=False,
    )
```
